32 devices in a mesh: dp: 4 (over z), mp: 8 (over y, x, core).
Axes of the slice: x: 2, y: 2, z: 4, core: 2. Of those that a mesh axis runs over, the one named last changes fastest.
Arguments:
- block_input: bfloat16 [10752, 2048], P('dp'), may hold values from -6 to 6
- cotangent: bfloat16 [10752, 2048], P(('dp', 'mp')), may hold values from -6 to 6
- prefix_len: int32 [12], P('dp'), may hold values from 1 to 896
- cluster_id: int32 [12], replicated, may hold values from 0 to 5
- positions: int32 [10752], P('dp'), may hold values from 0 to 1790, as said below
- step_count: int32 [1], replicated, may hold values from 2 to 20
- master_qkv: float32 [3, 2048, 2048], P(None, 'dp', 'mp'), may hold values from -0.125 to 0.125
- first_qkv: float32 [3, 2048, 2048], P(None, 'dp', 'mp')
- second_qkv: float32 [3, 2048, 2048], P(None, 'dp', 'mp'), as said below
- master_out: float32 [2048, 2048], P('mp', 'dp'), may hold values from -3 to 3
- first_out: float32 [2048, 2048], P('mp', 'dp')
- second_out: float32 [2048, 2048], P('mp', 'dp'), as said below
- master_gateup: float32 [2, 2048, 5632], P(None, 'dp', 'mp'), as said below
- first_gateup: float32 [2, 2048, 5632], P(None, 'dp', 'mp'), as said below
- second_gateup: float32 [2, 2048, 5632], P(None, 'dp', 'mp'), as said below
- master_down: float32 [5632, 2048], P('mp', 'dp'), as said below
- first_down: float32 [5632, 2048], P('mp', 'dp'), as said below
- second_down: float32 [5632, 2048], P('mp', 'dp'), as said below
- master_norm: float32 [4, 2048], replicated, as said below
- first_norm: float32 [4, 2048], replicated
- second_norm: float32 [4, 2048], replicated, as said below
Outputs:
- block_output: bfloat16 [10752, 2048], P(('dp', 'mp'))
- grad_input: bfloat16 [10752, 2048], P(('dp', 'mp'))
- grad_qkv: float32 [3, 2048, 2048], P(None, 'dp', 'mp')
- new_qkv: float32 [3, 2048, 2048], P(None, 'dp', 'mp')
- new_first_qkv: float32 [3, 2048, 2048], P(None, 'dp', 'mp')
- new_second_qkv: float32 [3, 2048, 2048], P(None, 'dp', 'mp')
- grad_out: float32 [2048, 2048], P('mp', 'dp')
- new_out: float32 [2048, 2048], P('mp', 'dp')
- new_first_out: float32 [2048, 2048], P('mp', 'dp')
- new_second_out: float32 [2048, 2048], P('mp', 'dp')
- grad_gateup: float32 [2, 2048, 5632], P(None, 'dp', 'mp')
- new_gateup: float32 [2, 2048, 5632], P(None, 'dp', 'mp')
- new_first_gateup: float32 [2, 2048, 5632], P(None, 'dp', 'mp')
- new_second_gateup: float32 [2, 2048, 5632], P(None, 'dp', 'mp')
- grad_down: float32 [5632, 2048], P('mp', 'dp')
- new_down: float32 [5632, 2048], P('mp', 'dp')
- new_first_down: float32 [5632, 2048], P('mp', 'dp')
- new_second_down: float32 [5632, 2048], P('mp', 'dp')
- grad_norm: float32 [4, 2048], replicated
- new_norm: float32 [4, 2048], replicated
- new_first_norm: float32 [4, 2048], replicated
- new_second_norm: float32 [4, 2048], replicated
The draws below stay inside these ranges and needn't reach their ends.
Inputs may be any that keep to these rules, and one draw needn't show every extreme that they name: `positions`: within each protein of 896 tokens the first position is 0 and each next one is larger by 1 or 2; in one protein every step is 2. `master_gateup`: hidden units from 5461 on are zero. `master_down`: hidden units from 5461 on are zero. `first_gateup`: hidden units from 5461 on are zero. `second_gateup`: hidden units from 5461 on are zero, all others positive. `first_down`: hidden units from 5461 on are zero. `second_down`: hidden units from 5461 on are zero, all others positive. `second_qkv`: Positive. `second_out`: Positive. `second_norm`: Positive. `master_norm`: gains in rows 0 and 2 are positive.
All inputs are finite; a program needn't handle non-finite values.
Results may differ from the reference program's by a relative error of at most 0.022.
Values may be sent and summed in bfloat16 or wider, within the bound.
A program may use at most 256 MiB of HBM per device.

```python
import math
import jax
import jax.numpy as jnp
from jax import lax

D = 2048
HEADS = 16
HEAD_DIM = 128
FF = 5632
FF_LIVE = 5461
DEPTH = 24
LEN = 896
PROTEINS = 12
TOKENS = 10752


def rough_values(key, shape):
    return jnp.clip(jax.random.normal(key, shape, jnp.float32), -4.0, 4.0)


def live_units():
    return (jnp.arange(FF) < FF_LIVE).astype(jnp.float32)


def first_state(key, shape, grad_size):
    return 0.1 / 0.9 * grad_size * rough_values(key, shape)


def second_state(key, shape, grad_size):
    factor = jnp.exp(jax.random.uniform(key, shape, jnp.float32, math.log(0.5), math.log(8.0)))
    return 0.05 / 0.95 * grad_size * grad_size * factor


def token_root():
    return math.sqrt(TOKENS)


def draw_positions(key, part):
    stride = jax.random.randint(key, (PROTEINS, LEN), 1, 3)
    chosen = jax.random.randint(jax.random.fold_in(key, 7), (), 0, PROTEINS)
    stride = jnp.where(jnp.arange(PROTEINS)[:, None] == chosen, 2, stride)
    column = jnp.arange(LEN)[None, :]
    stride = jnp.where(column == 0, 0, stride)
    return jnp.cumsum(stride, axis=1).reshape(TOKENS).astype(jnp.int32)


def draw_first_qkv(key, part):
    return first_state(key, (3, D, HEADS * HEAD_DIM), 0.4 * token_root())


def draw_second_qkv(key, part):
    return second_state(key, (3, D, HEADS * HEAD_DIM), 0.4 * token_root())


def draw_first_out(key, part):
    return first_state(key, (HEADS * HEAD_DIM, D), 0.02 * token_root())


def draw_second_out(key, part):
    return second_state(key, (HEADS * HEAD_DIM, D), 0.02 * token_root())


def draw_master_gateup(key, part):
    return rough_values(key, (2, D, FF)) * D ** (-0.5) * live_units()[None, None, :]


def draw_first_gateup(key, part):
    return first_state(key, (2, D, FF), 0.27 * token_root()) * live_units()[None, None, :]


def draw_second_gateup(key, part):
    return second_state(key, (2, D, FF), 0.27 * token_root()) * live_units()[None, None, :]


def draw_master_down(key, part):
    return rough_values(key, (FF, D)) * max(FF // 64, 1) ** (-0.5) * live_units()[:, None]


def draw_first_down(key, part):
    return first_state(key, (FF, D), 0.06 * token_root()) * live_units()[:, None]


def draw_second_down(key, part):
    return second_state(key, (FF, D), 0.06 * token_root()) * live_units()[:, None]


def draw_master_norm(key, part):
    noise = rough_values(key, (4, D))
    is_gain = (jnp.arange(4) % 2 == 0)[:, None]
    return jnp.where(is_gain, 1.0 + 0.1 * noise, 0.3 * noise)


def draw_first_norm(key, part):
    return first_state(key, (4, D), 0.8 * token_root())


def draw_second_norm(key, part):
    return second_state(key, (4, D), 0.8 * token_root())


def with_ends(result, rng, smallest, largest):
    index_at = [jax.random.randint(jax.random.fold_in(rng, axis), (), 0, length) for axis, length in enumerate(result.shape)]
    longest = result.shape.index(max(result.shape))
    next_to = index_at[:longest] + [(index_at[longest] + 1) % result.shape[longest]] + index_at[longest + 1:]
    return result.at[tuple(index_at)].set(smallest).at[tuple(next_to)].set(largest)


def levels(own_key, shape, shards, least, largest):
    def one(position, parts):
        heights = jax.random.uniform(jax.random.fold_in(jax.random.fold_in(own_key, 6), position), (parts,), jnp.float32, least / len(shards), largest / len(shards))
        return jnp.repeat(jnp.exp(heights), shape[position] // parts).reshape((-1,) + (1,) * (len(shape) - position - 1))

    level = one(*shards[0])
    for cut in shards[1:]:
        level = level * one(*cut)
    return level


def gaussian(rng, dims, scale, most, shards=(), held_as=jnp.bfloat16):
    result = jax.random.normal(rng, dims, jnp.float32) * scale
    if len(shards) > 0:
        result = levels(rng, dims, shards, -0.22, 0.18) * result
    return jnp.clip(result, min=-most, max=most).astype(held_as)


def setup_inputs(seed: int = 0) -> dict:
    key_of = jax.random.split(jax.random.key(seed), 22)
    block_input = gaussian(key_of[0], (TOKENS, D), 1.0, 6.0, ((0, 4),))
    cotangent = gaussian(key_of[1], (TOKENS, D), 1.0, 6.0, ((0, 32),))
    prefix_len = with_ends(jax.random.randint(key_of[2], (PROTEINS,), 1, LEN + 1), jax.random.fold_in(key_of[2], 1), 1, LEN).astype(jnp.int32)
    cluster_id = with_ends(jax.random.randint(key_of[3], (PROTEINS,), 0, PROTEINS // 2), jax.random.fold_in(key_of[3], 1), 0, (PROTEINS // 2) - 1).astype(jnp.int32)
    positions = draw_positions(jax.random.fold_in(key_of[21], 71), 0)
    step_count = jax.random.randint(key_of[5], (1,), 2, 21).astype(jnp.int32)
    master_qkv = gaussian(key_of[6], (3, D, HEADS * HEAD_DIM), D ** -0.5, 0.125, ((1, 4), (2, 8)), jnp.float32)
    first_qkv = draw_first_qkv(jax.random.fold_in(key_of[21], 71), 0)
    second_qkv = draw_second_qkv(jax.random.fold_in(key_of[21], 71), 0)
    master_out = gaussian(key_of[9], (HEADS * HEAD_DIM, D), (max(HEADS * HEAD_DIM // 512, 1)) ** -0.5, 3.0, ((0, 8), (1, 4)), jnp.float32)
    first_out = draw_first_out(jax.random.fold_in(key_of[21], 71), 0)
    second_out = draw_second_out(jax.random.fold_in(key_of[21], 71), 0)
    master_gateup = draw_master_gateup(jax.random.fold_in(key_of[21], 71), 0)
    first_gateup = draw_first_gateup(jax.random.fold_in(key_of[21], 71), 0)
    second_gateup = draw_second_gateup(jax.random.fold_in(key_of[21], 71), 0)
    master_down = draw_master_down(jax.random.fold_in(key_of[21], 71), 0)
    first_down = draw_first_down(jax.random.fold_in(key_of[21], 71), 0)
    second_down = draw_second_down(jax.random.fold_in(key_of[21], 71), 0)
    master_norm = draw_master_norm(jax.random.fold_in(key_of[21], 71), 0)
    first_norm = draw_first_norm(jax.random.fold_in(key_of[21], 71), 0)
    second_norm = draw_second_norm(jax.random.fold_in(key_of[21], 71), 0)
    return dict(block_input=block_input, cotangent=cotangent, prefix_len=prefix_len, cluster_id=cluster_id, positions=positions, step_count=step_count, master_qkv=master_qkv, first_qkv=first_qkv, second_qkv=second_qkv, master_out=master_out, first_out=first_out, second_out=second_out, master_gateup=master_gateup, first_gateup=first_gateup, second_gateup=second_gateup, master_down=master_down, first_down=first_down, second_down=second_down, master_norm=master_norm, first_norm=first_norm, second_norm=second_norm)


@jax.custom_vjp
def low(v):
    return lax.optimization_barrier(v.astype(jnp.bfloat16)).astype(jnp.float32)

@jax.custom_vjp
def low_back(v):
    return v

def low_keep(v):
    return (low(v), None)

def low_pass(kept, grad):
    return (grad,)

def back_keep(v):
    return (v, None)

def back_low(kept, grad):
    return (low(grad),)
low.defvjp(low_keep, low_pass)
low_back.defvjp(back_keep, back_low)
HIGH_PRECISION = lax.Precision.HIGHEST
beta_one = 0.9
beta_two = 0.95
adam_epsilon = 1e-08
decay_weight = 0.1
norm_epsilon = 1e-05

def layer_norm(hidden_rows, gain, offset):
    centre = hidden_rows - lax.optimization_barrier(jnp.mean(hidden_rows, axis=-1, keepdims=True))
    spread = lax.optimization_barrier(jnp.mean(centre * centre, axis=-1, keepdims=True))
    return centre * lax.rsqrt(spread + norm_epsilon) * gain + offset

def rotate_half(values):
    middle = values.shape[-1] // 2
    return jnp.concatenate([-values[..., middle:], values[..., :middle]], axis=-1)

def rope_tables(positions):
    ladder = jnp.arange(HEAD_DIM // 2, dtype=jnp.float32)
    inverse = jnp.exp(ladder * (-2.0 * math.log(10000.0) / HEAD_DIM))
    angles = positions.astype(jnp.float32)[:, None] * inverse[None, :]
    cos_half = jnp.cos(angles)
    sin_half = jnp.sin(angles)
    return (jnp.concatenate([cos_half, cos_half], axis=-1), jnp.concatenate([sin_half, sin_half], axis=-1))

def apply_rope(values, cos_table, sin_table):
    return values * cos_table[:, None, :] + rotate_half(values) * sin_table[:, None, :]

def gelu_tanh(values):
    return jax.nn.gelu(values, approximate=True)

def layer_block(block_rows, cos_table, sin_table, prefixes, weights):
    w_qkv, w_out, w_gateup, w_down, w_norm = weights
    token_count = block_rows.shape[0]
    protein_count = token_count // LEN
    head_count = w_qkv.shape[2] // HEAD_DIM
    deep_alpha = math.sqrt(2.0 * DEPTH)
    score_scale = 1.0 / math.sqrt(HEAD_DIM)
    projected = [low_back(jnp.dot(block_rows, w_qkv[member], precision=HIGH_PRECISION)).reshape(token_count, head_count, HEAD_DIM) for member in range(3)]
    queries = low(apply_rope(projected[0], cos_table, sin_table) * score_scale).reshape(protein_count, LEN, head_count, HEAD_DIM)
    key_rows = low(apply_rope(projected[1], cos_table, sin_table)).reshape(protein_count, LEN, head_count, HEAD_DIM)
    value_rows = low(projected[2]).reshape(protein_count, LEN, head_count, HEAD_DIM)
    scores = low_back(jnp.einsum('bqhd,bkhd->bhqk', queries, key_rows, precision=HIGH_PRECISION))
    row_ids = jnp.arange(LEN)[:, None]
    col_ids = jnp.arange(LEN)[None, :]
    visible = (col_ids[None, :, :] < prefixes[:, None, None]) | (col_ids <= row_ids)[None, :, :]
    scores = jnp.where(visible[:, None, :, :], scores, -1e+30)
    attn_probs = low(jax.nn.softmax(scores, axis=-1))
    attended = jnp.einsum('bhqk,bkhd->bqhd', attn_probs, value_rows, precision=HIGH_PRECISION).reshape(token_count, head_count * HEAD_DIM)
    attended = low(low_back(attended))
    attn_branch = low_back(jnp.dot(attended, w_out, precision=HIGH_PRECISION))
    middle_rows = layer_norm(deep_alpha * block_rows + attn_branch, w_norm[0], w_norm[1])
    middle_low = low(middle_rows)
    gate_rows = low_back(jnp.dot(middle_low, w_gateup[0], precision=HIGH_PRECISION))
    up_rows = low_back(jnp.dot(middle_low, w_gateup[1], precision=HIGH_PRECISION))
    hidden = low(gelu_tanh(gate_rows) * up_rows)
    ffn_branch = low_back(jnp.dot(hidden, w_down, precision=HIGH_PRECISION))
    return layer_norm(deep_alpha * middle_rows + ffn_branch, w_norm[2], w_norm[3])

def adamw_step(old_master, old_first, old_second, grad_sum, learn_rate, step_value):
    first_new = beta_one * old_first + (1.0 - beta_one) * grad_sum
    second_new = beta_two * old_second + (1.0 - beta_two) * grad_sum * grad_sum
    fix_first = 1.0 - jnp.power(beta_one, step_value)
    fix_second = 1.0 - jnp.power(beta_two, step_value)
    update = first_new / fix_first / (jnp.sqrt(second_new / fix_second) + adam_epsilon) + decay_weight * old_master
    return (old_master - learn_rate * update, first_new, second_new)

def reference(block_input, cotangent, prefix_len, cluster_id, positions, step_count, master_qkv, first_qkv, second_qkv, master_out, first_out, second_out, master_gateup, first_gateup, second_gateup, master_down, first_down, second_down, master_norm, first_norm, second_norm):
    group_size = math.gcd(PROTEINS, 4)
    block_count = PROTEINS // group_size
    block_rows = group_size * LEN
    cos_table, sin_table = rope_tables(positions)

    def forward(input_rows, qkv_master, out_master, gateup_master, down_master, norm_master):
        weights = (low(qkv_master), low(out_master), low(gateup_master), low(down_master), low(norm_master))

        def block_apply(rows_here, cos_here, sin_here, prefix_here):
            return layer_block(rows_here, cos_here, sin_here, prefix_here, weights)
        checked = jax.checkpoint(block_apply)

        def one_block(pieces):
            return checked(pieces[0], pieces[1], pieces[2], pieces[3])
        outputs = lax.map(one_block, (input_rows.reshape(block_count, block_rows, D), cos_table.reshape(block_count, block_rows, HEAD_DIM), sin_table.reshape(block_count, block_rows, HEAD_DIM), prefix_len.reshape(block_count, group_size)))
        return outputs.reshape(TOKENS, D)
    matches = (cluster_id[:, None] == cluster_id[None, :]).astype(jnp.float32)
    protein_weight = 1.0 / lax.optimization_barrier(jnp.sum(matches, axis=1))
    token_weight = jnp.repeat(protein_weight, LEN)
    seed_grad = cotangent.astype(jnp.float32) * token_weight[:, None]
    output_rows, pull_back = jax.vjp(forward, block_input.astype(jnp.float32), master_qkv, master_out, master_gateup, master_down, master_norm)
    grads = pull_back(seed_grad)
    step_value = step_count[0].astype(jnp.float32)
    rate_qkv = D ** (-0.5)
    rate_out = max(HEADS * HEAD_DIM // 512, 1) ** (-0.5)
    rate_gateup = D ** (-0.5)
    rate_down = max(FF // 64, 1) ** (-0.5)
    rate_norm = 1.0
    new_qkv, new_first_qkv, new_second_qkv = adamw_step(master_qkv, first_qkv, second_qkv, grads[1], rate_qkv, step_value)
    new_out, new_first_out, new_second_out = adamw_step(master_out, first_out, second_out, grads[2], rate_out, step_value)
    new_gateup, new_first_gateup, new_second_gateup = adamw_step(master_gateup, first_gateup, second_gateup, grads[3], rate_gateup, step_value)
    new_down, new_first_down, new_second_down = adamw_step(master_down, first_down, second_down, grads[4], rate_down, step_value)
    new_norm, new_first_norm, new_second_norm = adamw_step(master_norm, first_norm, second_norm, grads[5], rate_norm, step_value)
    return (output_rows.astype(jnp.bfloat16), grads[0].astype(jnp.bfloat16), grads[1], new_qkv, new_first_qkv, new_second_qkv, grads[2], new_out, new_first_out, new_second_out, grads[3], new_gateup, new_first_gateup, new_second_gateup, grads[4], new_down, new_first_down, new_second_down, grads[5], new_norm, new_first_norm, new_second_norm)
```

```python
import functools
import math

import jax
import jax.numpy as jnp
from jax import lax
from jax.experimental import pallas as pl
from jax.experimental.pallas import tpu as pltpu
from jax.sharding import PartitionSpec as P

D = 2048
HEADS = 16
HEAD_DIM = 128
FF = 5632
DEPTH = 24
LEN = 896


beta_one = 0.9
beta_two = 0.95
adam_epsilon = 1e-08
decay_weight = 0.1
norm_epsilon = 1e-05


def norm_forward(hidden_rows, gain, offset):
    centre = hidden_rows - jnp.mean(hidden_rows, axis=-1, keepdims=True)
    inv_std = lax.rsqrt(jnp.mean(centre * centre, axis=-1, keepdims=True) + norm_epsilon)
    normed = centre * inv_std
    return (normed * gain + offset, normed, inv_std)


def norm_backward(grad_rows, normed, inv_std, gain):
    grad_normed = grad_rows * gain
    first_term = jnp.mean(grad_normed, axis=-1, keepdims=True)
    second_term = jnp.mean(grad_normed * normed, axis=-1, keepdims=True)
    grad_hidden = inv_std * (grad_normed - first_term - normed * second_term)
    return (grad_hidden, jnp.sum(grad_rows * normed, axis=0), jnp.sum(grad_rows, axis=0))


def rotate_half(values):
    middle = values.shape[-1] // 2
    return jnp.concatenate([-values[..., middle:], values[..., :middle]], axis=-1)


def rotate_back(values):
    middle = values.shape[-1] // 2
    return jnp.concatenate([values[..., middle:], -values[..., :middle]], axis=-1)


def rope_tables(positions):
    ladder = jnp.arange(HEAD_DIM // 2, dtype=jnp.float32)
    inverse = jnp.exp(ladder * (-2.0 * math.log(10000.0) / HEAD_DIM))
    angles = positions.astype(jnp.float32)[:, None] * inverse[None, :]
    cos_half = jnp.cos(angles)
    sin_half = jnp.sin(angles)
    return (
        jnp.concatenate([cos_half, cos_half], axis=-1),
        jnp.concatenate([sin_half, sin_half], axis=-1),
    )


def apply_rope(values, cos_table, sin_table):
    return values * cos_table[:, None, :] + rotate_half(values) * sin_table[:, None, :]


def rope_back(grads, cos_table, sin_table):
    return grads * cos_table[:, None, :] + rotate_back(grads * sin_table[:, None, :])


def gelu_tanh(values):
    return jax.nn.gelu(values, approximate=True)


def adamw_step(old_master, old_first, old_second, grad_sum, learn_rate, step_value):
    first_new = beta_one * old_first + (1.0 - beta_one) * grad_sum
    second_new = beta_two * old_second + (1.0 - beta_two) * grad_sum * grad_sum
    fix_first = 1.0 - jnp.power(beta_one, step_value)
    fix_second = 1.0 - jnp.power(beta_two, step_value)
    update = (
        first_new / fix_first / (jnp.sqrt(second_new / fix_second) + adam_epsilon)
        + decay_weight * old_master
    )
    return (old_master - learn_rate * update, first_new, second_new)


def body_plain(
    block_input,
    cotangent,
    prefix_len,
    cluster_id,
    positions,
    step_count,
    master_qkv,
    first_qkv,
    second_qkv,
    master_out,
    first_out,
    second_out,
    master_gateup,
    first_gateup,
    second_gateup,
    master_down,
    first_down,
    second_down,
    master_norm,
    first_norm,
    second_norm,
):
    w_qkv, w_out, w_gateup, w_down = (
        lax.all_gather(master_qkv.astype(jnp.bfloat16), "dp", axis=1, tiled=True),
        lax.all_gather(master_out.astype(jnp.bfloat16), "dp", axis=1, tiled=True),
        lax.all_gather(master_gateup.astype(jnp.bfloat16), "dp", axis=1, tiled=True),
        lax.all_gather(master_down.astype(jnp.bfloat16), "dp", axis=1, tiled=True),
    )
    w_norm = lax.optimization_barrier(master_norm.astype(jnp.bfloat16)).astype(jnp.float32)
    token_count = block_input.shape[0]
    protein_count = token_count // LEN
    share_rows = cotangent.shape[0]
    share_start = lax.axis_index("mp") * share_rows
    head_count = w_qkv.shape[2] // HEAD_DIM
    width_heads = head_count * HEAD_DIM
    deep_alpha = math.sqrt(2.0 * DEPTH)
    score_scale = 1.0 / math.sqrt(HEAD_DIM)
    cos_table, sin_table = rope_tables(positions)
    projected = jnp.einsum("td,jdc->jtc", block_input, w_qkv, preferred_element_type=jnp.float32)
    shaped = projected.reshape(3, token_count, head_count, HEAD_DIM)
    queries = (apply_rope(shaped[0], cos_table, sin_table) * score_scale).astype(jnp.bfloat16)
    key_rows = apply_rope(shaped[1], cos_table, sin_table).astype(jnp.bfloat16)
    value_rows = shaped[2].astype(jnp.bfloat16)
    row_ids = jnp.arange(LEN)[:, None]
    col_ids = jnp.arange(LEN)[None, :]
    attended_parts = []
    log_totals = []
    for protein in range(protein_count):
        row_slice = slice(protein * LEN, (protein + 1) * LEN)
        visible = (col_ids < prefix_len[protein]) | (col_ids <= row_ids)
        scores = jnp.einsum(
            "qhd,khd->hqk",
            queries[row_slice],
            key_rows[row_slice],
            preferred_element_type=jnp.float32,
        )
        scores = jnp.where(visible[None], scores, -1e30)
        row_peak = jnp.max(scores, axis=-1, keepdims=True)
        expo_rows = jnp.exp(scores - row_peak)
        totals = jnp.sum(expo_rows, axis=-1, keepdims=True)
        attn_probs = (expo_rows / totals).astype(jnp.bfloat16)
        attended_parts.append(
            jnp.einsum(
                "hqk,khd->qhd",
                attn_probs,
                value_rows[row_slice],
                preferred_element_type=jnp.float32,
            )
        )
        log_totals.append(row_peak + jnp.log(totals))
    attended = (
        jnp.concatenate(attended_parts, axis=0)
        .reshape(token_count, width_heads)
        .astype(jnp.bfloat16)
    )
    attn_part = jnp.dot(attended, w_out, preferred_element_type=jnp.float32)
    input_share = lax.dynamic_slice_in_dim(block_input, share_start, share_rows, 0).astype(
        jnp.float32
    )
    attn_share = lax.psum_scatter(
        attn_part.astype(jnp.bfloat16), "mp", scatter_dimension=0, tiled=True
    ).astype(jnp.float32)
    middle_share, normed_one, inv_one = norm_forward(
        deep_alpha * input_share + attn_share, w_norm[0], w_norm[1]
    )
    middle_low = lax.all_gather(middle_share.astype(jnp.bfloat16), "mp", axis=0, tiled=True)
    gateup = jnp.einsum("td,jdf->jtf", middle_low, w_gateup, preferred_element_type=jnp.float32)
    gate_rows = gateup[0]
    up_rows = gateup[1]
    activated, gelu_pull = jax.vjp(gelu_tanh, gate_rows)
    hidden = (activated * up_rows).astype(jnp.bfloat16)
    ffn_part = jnp.dot(hidden, w_down, preferred_element_type=jnp.float32)
    ffn_share = lax.psum_scatter(
        ffn_part.astype(jnp.bfloat16), "mp", scatter_dimension=0, tiled=True
    ).astype(jnp.float32)
    out_share, normed_two, inv_two = norm_forward(
        deep_alpha * middle_share + ffn_share, w_norm[2], w_norm[3]
    )
    block_output = out_share.astype(jnp.bfloat16)
    matches = (cluster_id[:, None] == cluster_id[None, :]).astype(jnp.float32)
    counts = jnp.sum(matches, axis=1)
    group_counts = lax.dynamic_slice_in_dim(
        counts, lax.axis_index("dp") * protein_count, protein_count, 0
    )
    row_protein = (share_start + jnp.arange(share_rows)) // LEN
    one_hot = (row_protein[:, None] == jnp.arange(protein_count)[None, :]).astype(jnp.float32)
    row_weight = jnp.sum(one_hot * (1.0 / group_counts)[None, :], axis=1)
    grad_output = cotangent.astype(jnp.float32) * row_weight[:, None]
    grad_h2, grad_gain_two, grad_bias_two = norm_backward(
        grad_output, normed_two, inv_two, w_norm[2]
    )
    ffn_grad_full = lax.all_gather(grad_h2.astype(jnp.bfloat16), "mp", axis=0, tiled=True)
    grad_down_part = jnp.einsum(
        "tf,td->fd", hidden, ffn_grad_full, preferred_element_type=jnp.float32
    )
    grad_hidden = jnp.einsum("td,fd->tf", ffn_grad_full, w_down, preferred_element_type=jnp.float32)
    grad_gate = gelu_pull(grad_hidden * up_rows)[0]
    grad_up = grad_hidden * activated
    grad_gateup_rows = jnp.stack([grad_gate, grad_up]).astype(jnp.bfloat16)
    grad_gateup_part = jnp.einsum(
        "td,jtf->jdf", middle_low, grad_gateup_rows, preferred_element_type=jnp.float32
    )
    middle_grad_part = jnp.einsum(
        "jtf,jdf->td", grad_gateup_rows, w_gateup, preferred_element_type=jnp.float32
    )
    middle_grad = (
        lax.psum_scatter(
            middle_grad_part.astype(jnp.bfloat16), "mp", scatter_dimension=0, tiled=True
        ).astype(jnp.float32)
        + deep_alpha * grad_h2
    )
    grad_h1, grad_gain_one, grad_bias_one = norm_backward(
        middle_grad, normed_one, inv_one, w_norm[0]
    )
    attn_grad_full = lax.all_gather(grad_h1.astype(jnp.bfloat16), "mp", axis=0, tiled=True)
    grad_out_part = jnp.einsum(
        "tc,td->cd", attended, attn_grad_full, preferred_element_type=jnp.float32
    )
    grad_attended = (
        jnp.einsum("td,cd->tc", attn_grad_full, w_out, preferred_element_type=jnp.float32)
        .astype(jnp.bfloat16)
        .reshape(token_count, head_count, HEAD_DIM)
    )
    query_grads = []
    key_grads = []
    value_grads = []
    for protein in range(protein_count):
        row_slice = slice(protein * LEN, (protein + 1) * LEN)
        visible = (col_ids < prefix_len[protein]) | (col_ids <= row_ids)
        scores = jnp.einsum(
            "qhd,khd->hqk",
            queries[row_slice],
            key_rows[row_slice],
            preferred_element_type=jnp.float32,
        )
        scores = jnp.where(visible[None], scores, -1e30)
        probs_full = jnp.exp(scores - log_totals[protein])
        probs_low = probs_full.astype(jnp.bfloat16)
        grad_slice = grad_attended[row_slice]
        value_grads.append(
            jnp.einsum("hqk,qhd->khd", probs_low, grad_slice, preferred_element_type=jnp.float32)
        )
        prob_grads = jnp.einsum(
            "qhd,khd->hqk", grad_slice, value_rows[row_slice], preferred_element_type=jnp.float32
        )
        centre_term = jnp.sum(probs_full * prob_grads, axis=-1, keepdims=True)
        score_grads = (probs_full * (prob_grads - centre_term)).astype(jnp.bfloat16)
        query_grads.append(
            jnp.einsum(
                "hqk,khd->qhd", score_grads, key_rows[row_slice], preferred_element_type=jnp.float32
            )
        )
        key_grads.append(
            jnp.einsum(
                "hqk,qhd->khd", score_grads, queries[row_slice], preferred_element_type=jnp.float32
            )
        )
    grad_query = rope_back(jnp.concatenate(query_grads, axis=0), cos_table, sin_table) * score_scale
    grad_key = rope_back(jnp.concatenate(key_grads, axis=0), cos_table, sin_table)
    grad_value = jnp.concatenate(value_grads, axis=0)
    grad_proj = (
        jnp.stack([grad_query, grad_key, grad_value])
        .reshape(3, token_count, width_heads)
        .astype(jnp.bfloat16)
    )
    grad_qkv_part = jnp.einsum(
        "td,jtc->jdc", block_input, grad_proj, preferred_element_type=jnp.float32
    )
    input_grad_part = jnp.einsum(
        "jtc,jdc->td", grad_proj, w_qkv, preferred_element_type=jnp.float32
    )
    input_grad = (
        lax.psum_scatter(
            input_grad_part.astype(jnp.bfloat16), "mp", scatter_dimension=0, tiled=True
        ).astype(jnp.float32)
        + deep_alpha * grad_h1
    )
    grad_input = input_grad.astype(jnp.bfloat16)
    norm_terms = jnp.stack([grad_gain_one, grad_bias_one, grad_gain_two, grad_bias_two])
    grad_norm = lax.psum(norm_terms, ("dp", "mp"))
    red_qkv, red_out, red_gateup, red_down = (
        lax.psum_scatter(
            grad_qkv_part.astype(jnp.bfloat16), "dp", scatter_dimension=1, tiled=True
        ).astype(jnp.float32),
        lax.psum_scatter(
            grad_out_part.astype(jnp.bfloat16), "dp", scatter_dimension=1, tiled=True
        ).astype(jnp.float32),
        lax.psum_scatter(
            grad_gateup_part.astype(jnp.bfloat16), "dp", scatter_dimension=1, tiled=True
        ).astype(jnp.float32),
        lax.psum_scatter(
            grad_down_part.astype(jnp.bfloat16), "dp", scatter_dimension=1, tiled=True
        ).astype(jnp.float32),
    )
    step_value = step_count[0].astype(jnp.float32)
    rate_qkv = D ** (-0.5)
    rate_out = max(HEADS * HEAD_DIM // 512, 1) ** (-0.5)
    rate_gateup = D ** (-0.5)
    rate_down = max(FF // 64, 1) ** (-0.5)
    rate_norm = 1.0
    new_qkv, new_first_qkv, new_second_qkv = adamw_step(
        master_qkv, first_qkv, second_qkv, red_qkv, rate_qkv, step_value
    )
    new_out, new_first_out, new_second_out = adamw_step(
        master_out, first_out, second_out, red_out, rate_out, step_value
    )
    new_gateup, new_first_gateup, new_second_gateup = adamw_step(
        master_gateup, first_gateup, second_gateup, red_gateup, rate_gateup, step_value
    )
    new_down, new_first_down, new_second_down = adamw_step(
        master_down, first_down, second_down, red_down, rate_down, step_value
    )
    new_norm, new_first_norm, new_second_norm = adamw_step(
        master_norm, first_norm, second_norm, grad_norm, rate_norm, step_value
    )
    return (
        block_output,
        grad_input,
        red_qkv,
        new_qkv,
        new_first_qkv,
        new_second_qkv,
        red_out,
        new_out,
        new_first_out,
        new_second_out,
        red_gateup,
        new_gateup,
        new_first_gateup,
        new_second_gateup,
        red_down,
        new_down,
        new_first_down,
        new_second_down,
        grad_norm,
        new_norm,
        new_first_norm,
        new_second_norm,
    )


MESH = pl.DeviceIdType.MESH
VMEM_BYTES = 61 * 1024 * 1024
BF16 = jnp.bfloat16
F32 = jnp.float32
NT = (((1,), (1,)), ((), ()))
ANY = pl.BlockSpec(memory_space=pl.ANY)
VM = pl.BlockSpec(memory_space=pltpu.VMEM)
PLUS = [(0, 1), (1, 2), (2, 3), (3, 0)]
MINUS = [(1, 0), (2, 1), (3, 2), (0, 3)]


def nt_dot(left, right):
    return lax.dot_general(left, right, NT, preferred_element_type=F32)


def ring_gather(first, second):
    left = (lax.ppermute(first, "dp", PLUS), lax.ppermute(second, "dp", PLUS))
    right = (lax.ppermute(first, "dp", MINUS), lax.ppermute(second, "dp", MINUS))
    far = (lax.ppermute(left[0], "dp", PLUS), lax.ppermute(right[1], "dp", MINUS))
    return (first, second) + left + right + far


def ring_scatter(shard_of):
    here = lax.axis_index("dp")
    far = shard_of((here + 2) % 4)
    nxt = shard_of((here + 1) % 4)
    prv = shard_of((here + 3) % 4)
    own = shard_of(here)
    plus_far = lax.ppermute(far[0], "dp", PLUS)
    minus_far = lax.ppermute(far[1], "dp", MINUS)
    plus_b = lax.ppermute(nxt[1], "dp", PLUS)
    minus_a = lax.ppermute(prv[0], "dp", MINUS)
    plus_a = lax.ppermute((nxt[0].astype(F32) + plus_far.astype(F32)).astype(BF16), "dp", PLUS)
    minus_b = lax.ppermute((prv[1].astype(F32) + minus_far.astype(F32)).astype(BF16), "dp", MINUS)
    return (
        own[0].astype(F32) + plus_a.astype(F32) + minus_a.astype(F32),
        own[1].astype(F32) + plus_b.astype(F32) + minus_b.astype(F32),
    )


class Square:
    def __init__(self, send, recv, rows):
        me = lax.axis_index("mp")
        self.core = me % 2
        self.x = (me // 2) % 2
        self.y = me // 4
        self.xn = (self.y * 2 + (1 - self.x)) * 2 + self.core
        self.yn = ((1 - self.y) * 2 + self.x) * 2 + self.core
        self.peer = (self.y * 2 + self.x) * 2 + (1 - self.core)
        self.own = self.y * 2 + self.x
        self.xc = self.y * 2 + (1 - self.x)
        self.yc = (1 - self.y) * 2 + self.x
        self.dc = (1 - self.y) * 2 + (1 - self.x)
        self.send, self.recv = send, recv
        cut = rows // 2 // 16 * 16
        self.rows = rows
        self.a = pl.ds(0, cut)
        self.b = pl.ds(cut, rows - cut)
        self.na, self.nb, self.cut = cut, rows - cut, cut

    def barrier(self):
        sem = pltpu.get_barrier_semaphore()
        for other in (self.xn, self.yn, self.peer):
            pl.semaphore_signal(sem, inc=1, device_id={"mp": other}, device_id_type=MESH)
        pl.semaphore_wait(sem, 3)

    def copy(self, k, src, dst, other):
        return pltpu.make_async_remote_copy(
            src_ref=src,
            dst_ref=dst,
            send_sem=self.send.at[k],
            recv_sem=self.recv.at[k],
            device_id={"mp": other},
            device_id_type=MESH,
        )


def add_rows(dst, src, count):
    def step(i, carry):
        rows = pl.ds(pl.multiple_of(i * 16, 16), 16)
        dst[rows, :] = (dst[rows, :].astype(F32) + src[rows, :].astype(F32)).astype(BF16)
        return carry

    lax.fori_loop(0, count // 16, step, 0)


def square_kernel(rows, gather, scatter, compute, share, full, gbuf, pbuf, bufs, out, send, recv, lsem):
    sq = Square(send, recv, rows)
    core = sq.core
    sq.barrier()
    if gather:
        c_own = sq.copy(0, share, gbuf.at[sq.own, core], sq.peer)
        x_a = sq.copy(1, share.at[sq.a], gbuf.at[sq.own, core, sq.a], sq.xn)
        y_b = sq.copy(2, share.at[sq.b], gbuf.at[sq.own, core, sq.b], sq.yn)
        f_x = sq.copy(3, gbuf.at[sq.yc, core, sq.b], gbuf.at[sq.yc, core, sq.b], sq.xn)
        f_y = sq.copy(4, gbuf.at[sq.xc, core, sq.a], gbuf.at[sq.xc, core, sq.a], sq.yn)
        x_b = sq.copy(5, share.at[sq.b], gbuf.at[sq.own, core, sq.b], sq.xn)
        y_a = sq.copy(6, share.at[sq.a], gbuf.at[sq.own, core, sq.a], sq.yn)
        c_d = sq.copy(7, gbuf.at[sq.dc, core], gbuf.at[sq.dc, core], sq.peer)
        c_x = sq.copy(8, gbuf.at[sq.xc, core], gbuf.at[sq.xc, core], sq.peer)
        c_y = sq.copy(9, gbuf.at[sq.yc, core], gbuf.at[sq.yc, core], sq.peer)
        local = pltpu.make_async_copy(share, gbuf.at[sq.own, core], lsem.at[8])
        x_a.start()
        y_b.start()
        c_own.start()
        local.start()
    if scatter:
        rcore, rxd, ryd, rx, ry = bufs
        x_d = sq.copy(14, pbuf.at[sq.dc, core, sq.a], rxd, sq.xn)
        y_d = sq.copy(15, pbuf.at[sq.dc, core, sq.b], ryd, sq.yn)
        x_ra = sq.copy(16, pbuf.at[sq.xc, core, sq.a], rx.at[sq.a], sq.xn)
        y_rb = sq.copy(17, pbuf.at[sq.yc, core, sq.b], ry.at[sq.b], sq.yn)
        x_rb = sq.copy(18, pbuf.at[sq.xc, core, sq.b], rx.at[sq.b], sq.xn)
        y_ra = sq.copy(19, pbuf.at[sq.yc, core, sq.a], ry.at[sq.a], sq.yn)

    def step(t, carry):
        unit = t // 2
        turn = t % 2
        rel = unit if gather else (unit + 1) % 4
        chip_y = (sq.y + rel % 2) % 2
        chip_x = (sq.x + ((rel + 1) // 2) % 2) % 2
        chip = chip_y * 2 + chip_x
        which = (1 - core + turn) % 2
        if gather:

            @pl.when(t == 0)
            def _():
                c_own.wait_recv()
                local.wait()

            @pl.when(t == 2)
            def _():
                x_a.wait_recv()
                y_b.wait_recv()
                f_x.start()
                f_y.start()
                x_b.start()
                y_a.start()
                f_x.wait_recv()
                f_y.wait_recv()
                c_d.start()
                c_d.wait_recv()

            @pl.when(t == 4)
            def _():
                x_b.wait_recv()
                y_a.wait_recv()
                c_x.start()
                c_y.start()
                c_x.wait_recv()
                c_y.wait_recv()

            if full is not None:
                pltpu.make_async_copy(gbuf.at[chip, which], full.at[chip, which], lsem.at[t]).start()
        compute(t, chip, which)
        if scatter:

            @pl.when(turn == 0)
            def _():
                sq.copy(10 + rel, pbuf.at[chip, which], rcore.at[chip], sq.peer).start()

            @pl.when(turn == 1)
            def _():
                sq.copy(10 + rel, pbuf.at[chip, which], rcore.at[chip], sq.peer).wait_recv()
                add_rows(pbuf.at[chip, which], rcore.at[chip], rows)

            @pl.when((turn == 1) & (rel == 1))
            def _():
                x_d.start()
                y_d.start()

            @pl.when((turn == 1) & (rel == 2))
            def _():
                x_ra.start()

            @pl.when((turn == 1) & (rel == 3))
            def _():
                y_rb.start()

        return carry

    lax.fori_loop(0, 8, step, 0)
    if scatter:
        x_d.wait_recv()
        add_rows(pbuf.at[sq.yc, core, sq.a], rxd, sq.na)
        y_ra.start()
        y_d.wait_recv()
        add_rows(pbuf.at[sq.xc, core, sq.b], ryd, sq.nb)
        x_rb.start()
        x_ra.wait_recv()
        y_rb.wait_recv()
        y_ra.wait_recv()
        x_rb.wait_recv()

        def last(i, carry):
            part = pl.ds(pl.multiple_of(i * 16, 16), 16)
            out[part, :] = (
                pbuf[sq.own, core, part, :].astype(F32)
                + rx[part, :].astype(F32)
                + ry[part, :].astype(F32)
            )
            return carry

        lax.fori_loop(0, rows // 16, last, 0)
        for k in range(4):
            sq.copy(10 + k, pbuf.at[0, 0], rcore.at[0], sq.peer).wait_send()
        for copy in (x_d, y_d, x_ra, y_rb, x_rb, y_ra):
            copy.wait_send()
    if gather:
        for copy in (c_own, x_a, y_b, f_x, f_y, x_b, y_a, c_d, c_x, c_y):
            copy.wait_send()
        if full is not None:
            for t in range(8):
                pltpu.make_async_copy(gbuf.at[0, 0], full.at[0, 0], lsem.at[t]).wait()


def scatter_scratch(rows, width):
    cut = rows // 2 // 16 * 16
    return [
        pltpu.VMEM((4, 2, rows, width), BF16),
        pltpu.VMEM((4, rows, width), BF16),
        pltpu.VMEM((cut, width), BF16),
        pltpu.VMEM((rows - cut, width), BF16),
        pltpu.VMEM((rows, width), BF16),
        pltpu.VMEM((rows, width), BF16),
    ]


SEMS = [
    pltpu.SemaphoreType.DMA((20,)),
    pltpu.SemaphoreType.DMA((20,)),
    pltpu.SemaphoreType.DMA((9,)),
]


def params(collective_id):
    return pltpu.CompilerParams(
        collective_id=collective_id, has_side_effects=True, vmem_limit_bytes=VMEM_BYTES
    )


def weight_copies(pieces, place, sem):
    here = lax.axis_index("dp")
    owners = (here, (here + 3) % 4, (here + 1) % 4, (here + 2) % 4)
    copies = []
    for k, piece in enumerate(pieces):
        copies.append(pltpu.make_async_copy(piece, place(owners[k // 2], k % 2), sem.at[k]))
    return copies


def row_place(buf, depth):
    half = depth // 2

    def place(owner, part):
        return buf.at[:, pl.ds(pl.multiple_of(owner * depth + part * half, half), half), :]

    return place


def plane_place(buf, depth):
    def place(owner, part):
        return buf.at[part, pl.ds(pl.multiple_of(owner * depth, depth), depth), :]

    return place


def column_place(buf, depth):
    half = buf.shape[0] // 2

    def place(owner, part):
        return buf.at[pl.ds(part * half, half), pl.ds(pl.multiple_of(owner * depth, depth), depth)]

    return place


def qkv_call(block_input, pieces, cos_table, sin_table):
    tokens, width = block_input.shape
    cols = pieces[0].shape[2]
    depth = pieces[0].shape[1] * 2
    rows = 336
    heads = cols // HEAD_DIM
    scale = 1.0 / math.sqrt(HEAD_DIM)

    def kernel(x_ref, cos_ref, sin_ref, *rest):
        piece_refs, (q_ref, k_ref, v_ref, w_buf, sem) = rest[:8], rest[8:]

        @pl.when(pl.program_id(0) == 0)
        def _():
            copies = weight_copies(piece_refs, row_place(w_buf, depth), sem)
            for copy in copies:
                copy.start()
            for copy in copies:
                copy.wait()

        x = x_ref[...]
        for j, ref in enumerate((q_ref, k_ref)):
            a = jnp.dot(x, w_buf[j], preferred_element_type=F32)
            for h in range(heads):
                part = a[:, h * HEAD_DIM : (h + 1) * HEAD_DIM]
                turned = part * cos_ref[...] + pltpu.roll(part, HEAD_DIM // 2, 1) * sin_ref[...]
                if j == 0:
                    turned = turned * scale
                ref[:, h * HEAD_DIM : (h + 1) * HEAD_DIM] = turned.astype(BF16)
        v_ref[...] = jnp.dot(x, w_buf[2], preferred_element_type=F32).astype(BF16)

    tile = lambda n: pl.BlockSpec((rows, n), lambda i: (i, 0))
    return pl.pallas_call(
        kernel,
        grid=(tokens // rows,),
        out_shape=[jax.ShapeDtypeStruct((tokens, cols), BF16)] * 3,
        in_specs=[tile(width), tile(HEAD_DIM), tile(HEAD_DIM)] + [ANY] * 8,
        out_specs=[tile(cols)] * 3,
        scratch_shapes=[pltpu.VMEM((3, width, cols), BF16), pltpu.SemaphoreType.DMA((8,))],
        compiler_params=pltpu.CompilerParams(vmem_limit_bytes=VMEM_BYTES),
        cost_estimate=pl.CostEstimate(
            flops=6 * tokens * width * cols, bytes_accessed=20 << 20, transcendentals=0
        ),
        name="qkv",
    )(block_input, cos_table, sin_table, *pieces)


BLOCK = 128


def attention_call(queries, key_rows, value_rows, prefix_len):
    tokens, cols = queries.shape
    proteins = tokens // LEN
    heads = cols // HEAD_DIM

    def kernel(pre_ref, q_ref, k_ref, v_ref, o_ref, p_ref):
        prefix = pre_ref[pl.program_id(0)]

        def step(i, carry):
            rows = pl.ds(pl.multiple_of(i * BLOCK, BLOCK), BLOCK)
            s = nt_dot(q_ref[rows, :], k_ref[...])
            col = lax.broadcasted_iota(jnp.int32, s.shape, 1)
            row = lax.broadcasted_iota(jnp.int32, s.shape, 0) + i * BLOCK
            s = jnp.where(col < jnp.maximum(prefix, row + 1), s, -1e30)
            e = jnp.exp(s - jnp.max(s, axis=-1, keepdims=True))
            p = (e / jnp.sum(e, axis=-1, keepdims=True)).astype(BF16)
            p_ref[0, 0, rows, :] = p
            o_ref[rows, :] = jnp.dot(p, v_ref[...], preferred_element_type=F32).astype(BF16)
            return carry

        lax.fori_loop(0, LEN // BLOCK, step, 0)

    tile = pl.BlockSpec((LEN, HEAD_DIM), lambda p, h, *_: (p, h))
    return pl.pallas_call(
        kernel,
        grid_spec=pltpu.PrefetchScalarGridSpec(
            num_scalar_prefetch=1,
            grid=(proteins, heads),
            in_specs=[tile] * 3,
            out_specs=[tile, pl.BlockSpec((1, 1, LEN, LEN), lambda p, h, *_: (p, h, 0, 0))],
        ),
        out_shape=[
            jax.ShapeDtypeStruct((tokens, cols), BF16),
            jax.ShapeDtypeStruct((proteins, heads, LEN, LEN), BF16),
        ],
        compiler_params=pltpu.CompilerParams(vmem_limit_bytes=VMEM_BYTES),
        cost_estimate=pl.CostEstimate(
            flops=4 * tokens * LEN * cols, bytes_accessed=16 << 20, transcendentals=tokens * LEN * heads
        ),
        name="attention",
    )(prefix_len, queries, key_rows, value_rows)


def attention_back_call(queries, key_rows, value_rows, probs, attended, grad_attended, cos_table, sin_table):
    tokens, cols = queries.shape
    proteins = tokens // LEN
    heads = cols // HEAD_DIM
    scale = 1.0 / math.sqrt(HEAD_DIM)
    TN = (((0,), (0,)), ((), ()))

    def kernel(q_ref, k_ref, v_ref, p_ref, o_ref, do_ref, cos_ref, sin_ref, da_ref, dk_acc, dv_acc):
        dk_acc[...] = jnp.zeros_like(dk_acc)
        dv_acc[...] = jnp.zeros_like(dv_acc)

        def step(i, carry):
            rows = pl.ds(pl.multiple_of(i * BLOCK, BLOCK), BLOCK)
            do = do_ref[rows, :]
            p = p_ref[0, 0, rows, :]
            delta = jnp.sum(do.astype(F32) * o_ref[rows, :].astype(F32), axis=-1, keepdims=True)
            dp = nt_dot(do, v_ref[...])
            ds = (p.astype(F32) * (dp - delta)).astype(BF16)
            dv_acc[...] += lax.dot_general(p, do, TN, preferred_element_type=F32)
            dk_acc[...] += lax.dot_general(ds, q_ref[rows, :], TN, preferred_element_type=F32)
            dq = jnp.dot(ds, k_ref[...], preferred_element_type=F32)
            turned = dq * cos_ref[rows, :] - pltpu.roll(dq, HEAD_DIM // 2, 1) * sin_ref[rows, :]
            da_ref[0, rows, :] = (turned * scale).astype(BF16)
            return carry

        lax.fori_loop(0, LEN // BLOCK, step, 0)
        dk = dk_acc[...]
        turned = dk * cos_ref[...] - pltpu.roll(dk, HEAD_DIM // 2, 1) * sin_ref[...]
        da_ref[1] = turned.astype(BF16)
        da_ref[2] = dv_acc[...].astype(BF16)

    tile = pl.BlockSpec((LEN, HEAD_DIM), lambda p, h: (p, h))
    table = pl.BlockSpec((LEN, HEAD_DIM), lambda p, h: (p, 0))
    return pl.pallas_call(
        kernel,
        grid=(proteins, heads),
        in_specs=[tile] * 3
        + [pl.BlockSpec((1, 1, LEN, LEN), lambda p, h: (p, h, 0, 0)), tile, tile, table, table],
        out_specs=pl.BlockSpec((3, LEN, HEAD_DIM), lambda p, h: (0, p, h)),
        out_shape=jax.ShapeDtypeStruct((3, tokens, cols), BF16),
        scratch_shapes=[pltpu.VMEM((LEN, HEAD_DIM), F32), pltpu.VMEM((LEN, HEAD_DIM), F32)],
        compiler_params=pltpu.CompilerParams(vmem_limit_bytes=VMEM_BYTES),
        cost_estimate=pl.CostEstimate(
            flops=8 * tokens * LEN * cols, bytes_accessed=20 << 20, transcendentals=0
        ),
        name="attention_back",
    )(queries, key_rows, value_rows, probs, attended, grad_attended, cos_table, sin_table)


def out_call(attended, pieces, rows):
    cols = attended.shape[1]
    depth = pieces[0].shape[1]

    def kernel(o_ref, *rest):
        piece_refs, (out, w_buf, pbuf, rcore, rxd, ryd, rx, ry, wsem, send, recv, lsem) = rest[:8], rest[8:]
        copies = weight_copies(piece_refs, column_place(w_buf, depth), wsem)
        for copy in copies:
            copy.start()
        for copy in copies:
            copy.wait()

        def compute(t, chip, which):
            part = jnp.dot(o_ref[chip, which], w_buf[...], preferred_element_type=F32)
            pbuf[chip, which] = part.astype(BF16)

        square_kernel(
            rows, False, True, compute, None, None, None, pbuf, (rcore, rxd, ryd, rx, ry), out, send, recv, lsem
        )

    return pl.pallas_call(
        kernel,
        out_shape=jax.ShapeDtypeStruct((rows, D), F32),
        in_specs=[VM] + [ANY] * 8,
        out_specs=VM,
        scratch_shapes=[pltpu.VMEM((cols, D), BF16)]
        + scatter_scratch(rows, D)
        + [pltpu.SemaphoreType.DMA((8,))]
        + SEMS,
        compiler_params=params(0),
        cost_estimate=pl.CostEstimate(flops=40 << 30, bytes_accessed=100 << 20, transcendentals=0),
        name="out_reduce",
    )(attended.reshape(4, 2, rows, cols), *pieces)


def ffn_call(middle_low, gateup_pieces, down_pieces):
    rows = middle_low.shape[0]
    live = gateup_pieces[0].shape[-1]
    depth = gateup_pieces[0].shape[0]
    curve = math.sqrt(2.0 / math.pi)

    def kernel(share, *rest):
        g_refs, d_refs = rest[:8], rest[8:16]
        (out, full, hid_ref, act_ref, pull_ref) = rest[16:21]
        (w_g, w_d, gbuf, stage, pbuf, rcore, rxd, ryd, rx, ry, gsem, dsem, osem, send, recv, lsem) = rest[21:]
        copies = weight_copies(g_refs, plane_place(w_g, depth), gsem)
        copies += weight_copies(d_refs, column_place(w_d, depth), dsem)
        for copy in copies:
            copy.start()
        outs = (hid_ref, act_ref, pull_ref)

        def compute(t, chip, which):
            slot = t % 2

            @pl.when(t == 0)
            def _():
                for copy in copies:
                    copy.wait()

            @pl.when(t >= 2)
            def _():
                for k, ref in enumerate(outs):
                    pltpu.make_async_copy(stage.at[slot, k], ref.at[chip, which], osem.at[slot, k]).wait()

            tile = gbuf[chip, which]
            gate = jnp.dot(tile, w_g[0], preferred_element_type=F32)
            up = jnp.dot(tile, w_g[1], preferred_element_type=F32)
            square = gate * gate
            bent = jnp.tanh(curve * gate * (1.0 + 0.044715 * square))
            half = 0.5 * (1.0 + bent)
            act = gate * half
            slope = half + 0.5 * curve * gate * (1.0 - bent * bent) * (1.0 + 3.0 * 0.044715 * square)
            hid = (act * up).astype(BF16)
            stage[slot, 0] = hid
            stage[slot, 1] = act.astype(BF16)
            stage[slot, 2] = (slope * up).astype(BF16)
            for k, ref in enumerate(outs):
                pltpu.make_async_copy(stage.at[slot, k], ref.at[chip, which], osem.at[slot, k]).start()
            pbuf[chip, which] = jnp.dot(hid, w_d[...], preferred_element_type=F32).astype(BF16)

        square_kernel(
            rows, True, True, compute, share, full, gbuf, pbuf, (rcore, rxd, ryd, rx, ry), out, send, recv, lsem
        )
        for slot in range(2):
            for k, ref in enumerate(outs):
                pltpu.make_async_copy(stage.at[slot, k], ref.at[0, 0], osem.at[slot, k]).wait()

    kept = jax.ShapeDtypeStruct((4, 2, rows, live), BF16)
    return pl.pallas_call(
        kernel,
        out_shape=[
            jax.ShapeDtypeStruct((rows, D), F32),
            jax.ShapeDtypeStruct((4, 2, rows, D), BF16),
            kept,
            kept,
            kept,
        ],
        in_specs=[ANY] * 17,
        out_specs=[VM, ANY, ANY, ANY, ANY],
        scratch_shapes=[
            pltpu.VMEM((2, D, live), BF16),
            pltpu.VMEM((live, D), BF16),
            pltpu.VMEM((4, 2, rows, D), BF16),
            pltpu.VMEM((2, 3, rows, live), BF16),
        ]
        + scatter_scratch(rows, D)
        + [pltpu.SemaphoreType.DMA((8,)), pltpu.SemaphoreType.DMA((8,)), pltpu.SemaphoreType.DMA((2, 3))]
        + SEMS,
        compiler_params=params(1),
        cost_estimate=pl.CostEstimate(flops=100 << 30, bytes_accessed=300 << 20, transcendentals=0),
        name="ffn",
    )(middle_low, *gateup_pieces, *down_pieces)


def ffn_back_call(ffn_grad, act, pull, gateup_pieces, down_pieces):
    rows = ffn_grad.shape[0]
    live = gateup_pieces[0].shape[-1]
    depth = gateup_pieces[0].shape[0]

    def kernel(share, act_ref, pull_ref, *rest):
        g_refs, d_refs = rest[:8], rest[8:16]
        (out, full, dg_ref) = rest[16:19]
        (w_g, w_d, gbuf, load, stage, pbuf, rcore, rxd, ryd, rx, ry, gsem, dsem, isem, osem, send, recv, lsem) = rest[
            19:
        ]
        copies = weight_copies(g_refs, plane_place(w_g, depth), gsem)
        copies += weight_copies(d_refs, column_place(w_d, depth), dsem)
        for copy in copies:
            copy.start()

        def compute(t, chip, which):
            slot = t % 2

            @pl.when(t == 0)
            def _():
                for copy in copies:
                    copy.wait()

            loads = [
                pltpu.make_async_copy(ref.at[chip, which], load.at[k], isem.at[k])
                for k, ref in enumerate((act_ref, pull_ref))
            ]
            stores = [
                pltpu.make_async_copy(stage.at[slot, k], dg_ref.at[k, chip, which], osem.at[slot, k])
                for k in range(2)
            ]
            for copy in loads:
                copy.start()

            @pl.when(t >= 2)
            def _():
                for copy in stores:
                    copy.wait()

            dh = nt_dot(gbuf[chip, which], w_d[...])
            for copy in loads:
                copy.wait()
            d_gate = (dh * load[1].astype(F32)).astype(BF16)
            d_up = (dh * load[0].astype(F32)).astype(BF16)
            stage[slot, 0] = d_gate
            stage[slot, 1] = d_up
            for copy in stores:
                copy.start()
            pbuf[chip, which] = (nt_dot(d_gate, w_g[0]) + nt_dot(d_up, w_g[1])).astype(BF16)

        square_kernel(
            rows, True, True, compute, share, full, gbuf, pbuf, (rcore, rxd, ryd, rx, ry), out, send, recv, lsem
        )
        for slot in range(2):
            for k in range(2):
                pltpu.make_async_copy(stage.at[slot, k], dg_ref.at[k, 0, 0], osem.at[slot, k]).wait()

    return pl.pallas_call(
        kernel,
        out_shape=[
            jax.ShapeDtypeStruct((rows, D), F32),
            jax.ShapeDtypeStruct((4, 2, rows, D), BF16),
            jax.ShapeDtypeStruct((2, 4, 2, rows, live), BF16),
        ],
        in_specs=[ANY] * 19,
        out_specs=[VM, ANY, ANY],
        scratch_shapes=[
            pltpu.VMEM((2, D, live), BF16),
            pltpu.VMEM((live, D), BF16),
            pltpu.VMEM((4, 2, rows, D), BF16),
            pltpu.VMEM((2, rows, live), BF16),
            pltpu.VMEM((2, 2, rows, live), BF16),
        ]
        + scatter_scratch(rows, D)
        + [
            pltpu.SemaphoreType.DMA((8,)),
            pltpu.SemaphoreType.DMA((8,)),
            pltpu.SemaphoreType.DMA((2,)),
            pltpu.SemaphoreType.DMA((2, 2)),
        ]
        + SEMS,
        compiler_params=params(2),
        cost_estimate=pl.CostEstimate(flops=100 << 30, bytes_accessed=300 << 20, transcendentals=0),
        name="ffn_back",
    )(ffn_grad, act, pull, *gateup_pieces, *down_pieces)


def out_back_call(attn_grad, pieces):
    rows = attn_grad.shape[0]
    cols = pieces[0].shape[0] * 2
    depth = pieces[0].shape[1]

    def kernel(share, *rest):
        piece_refs, (full, dout, w_buf, gbuf, wsem, send, recv, lsem) = rest[:8], rest[8:]
        copies = weight_copies(piece_refs, column_place(w_buf, depth), wsem)
        for copy in copies:
            copy.start()
        for copy in copies:
            copy.wait()

        def compute(t, chip, which):
            dout[chip, which] = nt_dot(gbuf[chip, which], w_buf[...]).astype(BF16)

        square_kernel(rows, True, False, compute, share, full, gbuf, None, None, None, send, recv, lsem)

    return pl.pallas_call(
        kernel,
        out_shape=[
            jax.ShapeDtypeStruct((4, 2, rows, D), BF16),
            jax.ShapeDtypeStruct((4, 2, rows, cols), BF16),
        ],
        in_specs=[ANY] * 9,
        out_specs=[ANY, VM],
        scratch_shapes=[
            pltpu.VMEM((cols, D), BF16),
            pltpu.VMEM((4, 2, rows, D), BF16),
            pltpu.SemaphoreType.DMA((8,)),
        ]
        + SEMS,
        compiler_params=params(3),
        cost_estimate=pl.CostEstimate(flops=40 << 30, bytes_accessed=100 << 20, transcendentals=0),
        name="out_back",
    )(attn_grad, *pieces)


def input_back_call(grad_proj, pieces, rows):
    cols = grad_proj.shape[2]
    depth = pieces[0].shape[1] * 2

    def kernel(da_ref, *rest):
        piece_refs, (out, w_buf, pbuf, rcore, rxd, ryd, rx, ry, wsem, send, recv, lsem) = rest[:8], rest[8:]
        copies = weight_copies(piece_refs, row_place(w_buf, depth), wsem)
        for copy in copies:
            copy.start()
        for copy in copies:
            copy.wait()

        def compute(t, chip, which):
            part = nt_dot(da_ref[0, chip, which], w_buf[0])
            part += nt_dot(da_ref[1, chip, which], w_buf[1])
            part += nt_dot(da_ref[2, chip, which], w_buf[2])
            pbuf[chip, which] = part.astype(BF16)

        square_kernel(
            rows, False, True, compute, None, None, None, pbuf, (rcore, rxd, ryd, rx, ry), out, send, recv, lsem
        )

    return pl.pallas_call(
        kernel,
        out_shape=jax.ShapeDtypeStruct((rows, D), F32),
        in_specs=[VM] + [ANY] * 8,
        out_specs=VM,
        scratch_shapes=[pltpu.VMEM((3, D, cols), BF16)]
        + scatter_scratch(rows, D)
        + [pltpu.SemaphoreType.DMA((8,))]
        + SEMS,
        compiler_params=params(4),
        cost_estimate=pl.CostEstimate(flops=50 << 30, bytes_accessed=100 << 20, transcendentals=0),
        name="input_back",
    )(grad_proj.reshape(3, 4, 2, rows, cols), *pieces)


def body_ring(
    block_input,
    cotangent,
    prefix_len,
    cluster_id,
    positions,
    step_count,
    master_qkv,
    first_qkv,
    second_qkv,
    master_out,
    first_out,
    second_out,
    master_gateup,
    first_gateup,
    second_gateup,
    master_down,
    first_down,
    second_down,
    master_norm,
    first_norm,
    second_norm,
):
    token_count = block_input.shape[0]
    protein_count = token_count // LEN
    share_rows = cotangent.shape[0]
    share_start = lax.axis_index("mp") * share_rows
    deep_alpha = math.sqrt(2.0 * DEPTH)
    depth = master_qkv.shape[1]
    half = depth // 2

    low_qkv = master_qkv.astype(BF16)
    qkv_pieces = ring_gather(low_qkv[:, :half], low_qkv[:, half:])
    low_out = master_out.astype(BF16)
    out_half = low_out.shape[0] // 2
    out_pieces = ring_gather(low_out[:out_half], low_out[out_half:])
    low_gateup = master_gateup.astype(BF16)
    gateup_pieces = ring_gather(low_gateup[0], low_gateup[1])
    low_down = master_down.astype(BF16)
    down_half = low_down.shape[0] // 2
    down_pieces = ring_gather(low_down[:down_half], low_down[down_half:])
    w_norm = lax.optimization_barrier(master_norm.astype(BF16)).astype(F32)

    cos_table, sin_table = rope_tables(positions)
    sign = jnp.where(jnp.arange(HEAD_DIM) < HEAD_DIM // 2, -1.0, 1.0).astype(F32)
    sin_table = sin_table * sign[None, :]
    queries, key_rows, value_rows = qkv_call(block_input, qkv_pieces, cos_table, sin_table)
    attended, probs = attention_call(queries, key_rows, value_rows, prefix_len)
    attn_share = out_call(attended, out_pieces, share_rows)
    input_share = lax.dynamic_slice_in_dim(block_input, share_start, share_rows, 0).astype(F32)
    middle_share, normed_one, inv_one = norm_forward(
        deep_alpha * input_share + attn_share, w_norm[0], w_norm[1]
    )
    ffn_share, middle_low, hidden, act, pull = ffn_call(
        middle_share.astype(BF16), gateup_pieces, down_pieces
    )
    out_share, normed_two, inv_two = norm_forward(
        deep_alpha * middle_share + ffn_share, w_norm[2], w_norm[3]
    )
    block_output = out_share.astype(BF16)
    matches = (cluster_id[:, None] == cluster_id[None, :]).astype(F32)
    counts = jnp.sum(matches, axis=1)
    group_counts = lax.dynamic_slice_in_dim(
        counts, lax.axis_index("dp") * protein_count, protein_count, 0
    )
    row_protein = (share_start + jnp.arange(share_rows)) // LEN
    one_hot = (row_protein[:, None] == jnp.arange(protein_count)[None, :]).astype(F32)
    row_weight = jnp.sum(one_hot * (1.0 / group_counts)[None, :], axis=1)
    grad_output = cotangent.astype(F32) * row_weight[:, None]
    grad_h2, grad_gain_two, grad_bias_two = norm_backward(
        grad_output, normed_two, inv_two, w_norm[2]
    )
    middle_grad, ffn_grad, grad_gateup_rows = ffn_back_call(
        grad_h2.astype(BF16), act, pull, gateup_pieces, down_pieces
    )
    hidden = hidden.reshape(token_count, -1)
    middle_low = middle_low.reshape(token_count, D)
    ffn_grad = ffn_grad.reshape(token_count, D)
    grad_gateup_rows = grad_gateup_rows.reshape(2, token_count, -1)
    grad_down_part = jnp.einsum("tf,td->fd", hidden, ffn_grad, preferred_element_type=F32).astype(BF16)
    grad_gateup_part = jnp.einsum(
        "td,jtf->jdf", middle_low, grad_gateup_rows, preferred_element_type=F32
    ).astype(BF16)
    middle_grad = middle_grad + deep_alpha * grad_h2
    grad_h1, grad_gain_one, grad_bias_one = norm_backward(
        middle_grad, normed_one, inv_one, w_norm[0]
    )
    attn_grad, grad_attended = out_back_call(grad_h1.astype(BF16), out_pieces)
    attn_grad = attn_grad.reshape(token_count, D)
    grad_attended = grad_attended.reshape(token_count, -1)
    grad_out_part = jnp.einsum("tc,td->cd", attended, attn_grad, preferred_element_type=F32).astype(BF16)
    grad_proj = attention_back_call(
        queries, key_rows, value_rows, probs, attended, grad_attended, cos_table, sin_table
    )
    grad_qkv_part = jnp.einsum("td,jtc->jdc", block_input, grad_proj, preferred_element_type=F32).astype(BF16)
    input_share_grad = input_back_call(grad_proj, qkv_pieces, share_rows)
    grad_input = (input_share_grad + deep_alpha * grad_h1).astype(BF16)
    norm_terms = jnp.stack([grad_gain_one, grad_bias_one, grad_gain_two, grad_bias_two])
    grad_norm = lax.psum(norm_terms, ("dp", "mp"))

    def down_shard(owner):
        part = lax.dynamic_slice_in_dim(grad_down_part, owner * depth, depth, 1)
        return part[:down_half], part[down_half:]

    def gateup_shard(owner):
        part = lax.dynamic_slice_in_dim(grad_gateup_part, owner * depth, depth, 1)
        return part[0], part[1]

    def out_shard(owner):
        part = lax.dynamic_slice_in_dim(grad_out_part, owner * depth, depth, 1)
        return part[:out_half], part[out_half:]

    def qkv_shard(owner):
        part = lax.dynamic_slice_in_dim(grad_qkv_part, owner * depth, depth, 1)
        return part[:, :half], part[:, half:]

    red_down = jnp.concatenate(ring_scatter(down_shard), axis=0)
    red_gateup = jnp.stack(ring_scatter(gateup_shard))
    red_out = jnp.concatenate(ring_scatter(out_shard), axis=0)
    red_qkv = jnp.concatenate(ring_scatter(qkv_shard), axis=1)

    step_value = step_count[0].astype(F32)
    rate_qkv = D ** (-0.5)
    rate_out = max(HEADS * HEAD_DIM // 512, 1) ** (-0.5)
    rate_gateup = D ** (-0.5)
    rate_down = max(FF // 64, 1) ** (-0.5)
    rate_norm = 1.0
    new_qkv, new_first_qkv, new_second_qkv = adamw_step(
        master_qkv, first_qkv, second_qkv, red_qkv, rate_qkv, step_value
    )
    new_out, new_first_out, new_second_out = adamw_step(
        master_out, first_out, second_out, red_out, rate_out, step_value
    )
    new_gateup, new_first_gateup, new_second_gateup = adamw_step(
        master_gateup, first_gateup, second_gateup, red_gateup, rate_gateup, step_value
    )
    new_down, new_first_down, new_second_down = adamw_step(
        master_down, first_down, second_down, red_down, rate_down, step_value
    )
    new_norm, new_first_norm, new_second_norm = adamw_step(
        master_norm, first_norm, second_norm, grad_norm, rate_norm, step_value
    )
    return (
        block_output,
        grad_input,
        red_qkv,
        new_qkv,
        new_first_qkv,
        new_second_qkv,
        red_out,
        new_out,
        new_first_out,
        new_second_out,
        red_gateup,
        new_gateup,
        new_first_gateup,
        new_second_gateup,
        red_down,
        new_down,
        new_first_down,
        new_second_down,
        grad_norm,
        new_norm,
        new_first_norm,
        new_second_norm,
    )


def solution(mesh):
    placed = (
        P("dp", None),
        P(("dp", "mp"), None),
        P("dp"),
        P(),
        P("dp"),
        P(),
        P(None, "dp", "mp"),
        P(None, "dp", "mp"),
        P(None, "dp", "mp"),
        P("mp", "dp"),
        P("mp", "dp"),
        P("mp", "dp"),
        P(None, "dp", "mp"),
        P(None, "dp", "mp"),
        P(None, "dp", "mp"),
        P("mp", "dp"),
        P("mp", "dp"),
        P("mp", "dp"),
        P(),
        P(),
        P(),
    )
    ring = mesh.shape["dp"] == 4 and mesh.shape["mp"] == 8
    return jax.shard_map(
        body_ring if ring else body_plain,
        mesh=mesh,
        in_specs=placed,
        out_specs=(
            P(("dp", "mp"), None),
            P(("dp", "mp"), None),
            P(None, "dp", "mp"),
            P(None, "dp", "mp"),
            P(None, "dp", "mp"),
            P(None, "dp", "mp"),
            P("mp", "dp"),
            P("mp", "dp"),
            P("mp", "dp"),
            P("mp", "dp"),
            P(None, "dp", "mp"),
            P(None, "dp", "mp"),
            P(None, "dp", "mp"),
            P(None, "dp", "mp"),
            P("mp", "dp"),
            P("mp", "dp"),
            P("mp", "dp"),
            P("mp", "dp"),
            P(),
            P(),
            P(),
            P(),
        ),
        check_vma=False,
    )
```

```python
import functools
import math

import jax
import jax.numpy as jnp
from jax import lax
from jax.experimental import pallas as pl
from jax.experimental.pallas import tpu as pltpu
from jax.sharding import PartitionSpec as P

D = 2048
HEADS = 16
HEAD_DIM = 128
FF = 5632
DEPTH = 24
LEN = 896


beta_one = 0.9
beta_two = 0.95
adam_epsilon = 1e-08
decay_weight = 0.1
norm_epsilon = 1e-05


def norm_forward(hidden_rows, gain, offset):
    centre = hidden_rows - jnp.mean(hidden_rows, axis=-1, keepdims=True)
    inv_std = lax.rsqrt(jnp.mean(centre * centre, axis=-1, keepdims=True) + norm_epsilon)
    normed = centre * inv_std
    return (normed * gain + offset, normed, inv_std)


def norm_backward(grad_rows, normed, inv_std, gain):
    grad_normed = grad_rows * gain
    first_term = jnp.mean(grad_normed, axis=-1, keepdims=True)
    second_term = jnp.mean(grad_normed * normed, axis=-1, keepdims=True)
    grad_hidden = inv_std * (grad_normed - first_term - normed * second_term)
    return (grad_hidden, jnp.sum(grad_rows * normed, axis=0), jnp.sum(grad_rows, axis=0))


def rotate_half(values):
    middle = values.shape[-1] // 2
    return jnp.concatenate([-values[..., middle:], values[..., :middle]], axis=-1)


def rotate_back(values):
    middle = values.shape[-1] // 2
    return jnp.concatenate([values[..., middle:], -values[..., :middle]], axis=-1)


def rope_tables(positions):
    ladder = jnp.arange(HEAD_DIM // 2, dtype=jnp.float32)
    inverse = jnp.exp(ladder * (-2.0 * math.log(10000.0) / HEAD_DIM))
    angles = positions.astype(jnp.float32)[:, None] * inverse[None, :]
    cos_half = jnp.cos(angles)
    sin_half = jnp.sin(angles)
    return (
        jnp.concatenate([cos_half, cos_half], axis=-1),
        jnp.concatenate([sin_half, sin_half], axis=-1),
    )


def apply_rope(values, cos_table, sin_table):
    return values * cos_table[:, None, :] + rotate_half(values) * sin_table[:, None, :]


def rope_back(grads, cos_table, sin_table):
    return grads * cos_table[:, None, :] + rotate_back(grads * sin_table[:, None, :])


def gelu_tanh(values):
    return jax.nn.gelu(values, approximate=True)


def adamw_step(old_master, old_first, old_second, grad_sum, learn_rate, step_value):
    first_new = beta_one * old_first + (1.0 - beta_one) * grad_sum
    second_new = beta_two * old_second + (1.0 - beta_two) * grad_sum * grad_sum
    fix_first = 1.0 - jnp.power(beta_one, step_value)
    fix_second = 1.0 - jnp.power(beta_two, step_value)
    update = (
        first_new / fix_first / (jnp.sqrt(second_new / fix_second) + adam_epsilon)
        + decay_weight * old_master
    )
    return (old_master - learn_rate * update, first_new, second_new)


def body_plain(
    block_input,
    cotangent,
    prefix_len,
    cluster_id,
    positions,
    step_count,
    master_qkv,
    first_qkv,
    second_qkv,
    master_out,
    first_out,
    second_out,
    master_gateup,
    first_gateup,
    second_gateup,
    master_down,
    first_down,
    second_down,
    master_norm,
    first_norm,
    second_norm,
):
    w_qkv, w_out, w_gateup, w_down = (
        lax.all_gather(master_qkv.astype(jnp.bfloat16), "dp", axis=1, tiled=True),
        lax.all_gather(master_out.astype(jnp.bfloat16), "dp", axis=1, tiled=True),
        lax.all_gather(master_gateup.astype(jnp.bfloat16), "dp", axis=1, tiled=True),
        lax.all_gather(master_down.astype(jnp.bfloat16), "dp", axis=1, tiled=True),
    )
    w_norm = lax.optimization_barrier(master_norm.astype(jnp.bfloat16)).astype(jnp.float32)
    token_count = block_input.shape[0]
    protein_count = token_count // LEN
    share_rows = cotangent.shape[0]
    share_start = lax.axis_index("mp") * share_rows
    head_count = w_qkv.shape[2] // HEAD_DIM
    width_heads = head_count * HEAD_DIM
    deep_alpha = math.sqrt(2.0 * DEPTH)
    score_scale = 1.0 / math.sqrt(HEAD_DIM)
    cos_table, sin_table = rope_tables(positions)
    projected = jnp.einsum("td,jdc->jtc", block_input, w_qkv, preferred_element_type=jnp.float32)
    shaped = projected.reshape(3, token_count, head_count, HEAD_DIM)
    queries = (apply_rope(shaped[0], cos_table, sin_table) * score_scale).astype(jnp.bfloat16)
    key_rows = apply_rope(shaped[1], cos_table, sin_table).astype(jnp.bfloat16)
    value_rows = shaped[2].astype(jnp.bfloat16)
    row_ids = jnp.arange(LEN)[:, None]
    col_ids = jnp.arange(LEN)[None, :]
    attended_parts = []
    log_totals = []
    for protein in range(protein_count):
        row_slice = slice(protein * LEN, (protein + 1) * LEN)
        visible = (col_ids < prefix_len[protein]) | (col_ids <= row_ids)
        scores = jnp.einsum(
            "qhd,khd->hqk",
            queries[row_slice],
            key_rows[row_slice],
            preferred_element_type=jnp.float32,
        )
        scores = jnp.where(visible[None], scores, -1e30)
        row_peak = jnp.max(scores, axis=-1, keepdims=True)
        expo_rows = jnp.exp(scores - row_peak)
        totals = jnp.sum(expo_rows, axis=-1, keepdims=True)
        attn_probs = (expo_rows / totals).astype(jnp.bfloat16)
        attended_parts.append(
            jnp.einsum(
                "hqk,khd->qhd",
                attn_probs,
                value_rows[row_slice],
                preferred_element_type=jnp.float32,
            )
        )
        log_totals.append(row_peak + jnp.log(totals))
    attended = (
        jnp.concatenate(attended_parts, axis=0)
        .reshape(token_count, width_heads)
        .astype(jnp.bfloat16)
    )
    attn_part = jnp.dot(attended, w_out, preferred_element_type=jnp.float32)
    input_share = lax.dynamic_slice_in_dim(block_input, share_start, share_rows, 0).astype(
        jnp.float32
    )
    attn_share = lax.psum_scatter(
        attn_part.astype(jnp.bfloat16), "mp", scatter_dimension=0, tiled=True
    ).astype(jnp.float32)
    middle_share, normed_one, inv_one = norm_forward(
        deep_alpha * input_share + attn_share, w_norm[0], w_norm[1]
    )
    middle_low = lax.all_gather(middle_share.astype(jnp.bfloat16), "mp", axis=0, tiled=True)
    gateup = jnp.einsum("td,jdf->jtf", middle_low, w_gateup, preferred_element_type=jnp.float32)
    gate_rows = gateup[0]
    up_rows = gateup[1]
    activated, gelu_pull = jax.vjp(gelu_tanh, gate_rows)
    hidden = (activated * up_rows).astype(jnp.bfloat16)
    ffn_part = jnp.dot(hidden, w_down, preferred_element_type=jnp.float32)
    ffn_share = lax.psum_scatter(
        ffn_part.astype(jnp.bfloat16), "mp", scatter_dimension=0, tiled=True
    ).astype(jnp.float32)
    out_share, normed_two, inv_two = norm_forward(
        deep_alpha * middle_share + ffn_share, w_norm[2], w_norm[3]
    )
    block_output = out_share.astype(jnp.bfloat16)
    matches = (cluster_id[:, None] == cluster_id[None, :]).astype(jnp.float32)
    counts = jnp.sum(matches, axis=1)
    group_counts = lax.dynamic_slice_in_dim(
        counts, lax.axis_index("dp") * protein_count, protein_count, 0
    )
    row_protein = (share_start + jnp.arange(share_rows)) // LEN
    one_hot = (row_protein[:, None] == jnp.arange(protein_count)[None, :]).astype(jnp.float32)
    row_weight = jnp.sum(one_hot * (1.0 / group_counts)[None, :], axis=1)
    grad_output = cotangent.astype(jnp.float32) * row_weight[:, None]
    grad_h2, grad_gain_two, grad_bias_two = norm_backward(
        grad_output, normed_two, inv_two, w_norm[2]
    )
    ffn_grad_full = lax.all_gather(grad_h2.astype(jnp.bfloat16), "mp", axis=0, tiled=True)
    grad_down_part = jnp.einsum(
        "tf,td->fd", hidden, ffn_grad_full, preferred_element_type=jnp.float32
    )
    grad_hidden = jnp.einsum("td,fd->tf", ffn_grad_full, w_down, preferred_element_type=jnp.float32)
    grad_gate = gelu_pull(grad_hidden * up_rows)[0]
    grad_up = grad_hidden * activated
    grad_gateup_rows = jnp.stack([grad_gate, grad_up]).astype(jnp.bfloat16)
    grad_gateup_part = jnp.einsum(
        "td,jtf->jdf", middle_low, grad_gateup_rows, preferred_element_type=jnp.float32
    )
    middle_grad_part = jnp.einsum(
        "jtf,jdf->td", grad_gateup_rows, w_gateup, preferred_element_type=jnp.float32
    )
    middle_grad = (
        lax.psum_scatter(
            middle_grad_part.astype(jnp.bfloat16), "mp", scatter_dimension=0, tiled=True
        ).astype(jnp.float32)
        + deep_alpha * grad_h2
    )
    grad_h1, grad_gain_one, grad_bias_one = norm_backward(
        middle_grad, normed_one, inv_one, w_norm[0]
    )
    attn_grad_full = lax.all_gather(grad_h1.astype(jnp.bfloat16), "mp", axis=0, tiled=True)
    grad_out_part = jnp.einsum(
        "tc,td->cd", attended, attn_grad_full, preferred_element_type=jnp.float32
    )
    grad_attended = (
        jnp.einsum("td,cd->tc", attn_grad_full, w_out, preferred_element_type=jnp.float32)
        .astype(jnp.bfloat16)
        .reshape(token_count, head_count, HEAD_DIM)
    )
    query_grads = []
    key_grads = []
    value_grads = []
    for protein in range(protein_count):
        row_slice = slice(protein * LEN, (protein + 1) * LEN)
        visible = (col_ids < prefix_len[protein]) | (col_ids <= row_ids)
        scores = jnp.einsum(
            "qhd,khd->hqk",
            queries[row_slice],
            key_rows[row_slice],
            preferred_element_type=jnp.float32,
        )
        scores = jnp.where(visible[None], scores, -1e30)
        probs_full = jnp.exp(scores - log_totals[protein])
        probs_low = probs_full.astype(jnp.bfloat16)
        grad_slice = grad_attended[row_slice]
        value_grads.append(
            jnp.einsum("hqk,qhd->khd", probs_low, grad_slice, preferred_element_type=jnp.float32)
        )
        prob_grads = jnp.einsum(
            "qhd,khd->hqk", grad_slice, value_rows[row_slice], preferred_element_type=jnp.float32
        )
        centre_term = jnp.sum(probs_full * prob_grads, axis=-1, keepdims=True)
        score_grads = (probs_full * (prob_grads - centre_term)).astype(jnp.bfloat16)
        query_grads.append(
            jnp.einsum(
                "hqk,khd->qhd", score_grads, key_rows[row_slice], preferred_element_type=jnp.float32
            )
        )
        key_grads.append(
            jnp.einsum(
                "hqk,qhd->khd", score_grads, queries[row_slice], preferred_element_type=jnp.float32
            )
        )
    grad_query = rope_back(jnp.concatenate(query_grads, axis=0), cos_table, sin_table) * score_scale
    grad_key = rope_back(jnp.concatenate(key_grads, axis=0), cos_table, sin_table)
    grad_value = jnp.concatenate(value_grads, axis=0)
    grad_proj = (
        jnp.stack([grad_query, grad_key, grad_value])
        .reshape(3, token_count, width_heads)
        .astype(jnp.bfloat16)
    )
    grad_qkv_part = jnp.einsum(
        "td,jtc->jdc", block_input, grad_proj, preferred_element_type=jnp.float32
    )
    input_grad_part = jnp.einsum(
        "jtc,jdc->td", grad_proj, w_qkv, preferred_element_type=jnp.float32
    )
    input_grad = (
        lax.psum_scatter(
            input_grad_part.astype(jnp.bfloat16), "mp", scatter_dimension=0, tiled=True
        ).astype(jnp.float32)
        + deep_alpha * grad_h1
    )
    grad_input = input_grad.astype(jnp.bfloat16)
    norm_terms = jnp.stack([grad_gain_one, grad_bias_one, grad_gain_two, grad_bias_two])
    grad_norm = lax.psum(norm_terms, ("dp", "mp"))
    red_qkv, red_out, red_gateup, red_down = (
        lax.psum_scatter(
            grad_qkv_part.astype(jnp.bfloat16), "dp", scatter_dimension=1, tiled=True
        ).astype(jnp.float32),
        lax.psum_scatter(
            grad_out_part.astype(jnp.bfloat16), "dp", scatter_dimension=1, tiled=True
        ).astype(jnp.float32),
        lax.psum_scatter(
            grad_gateup_part.astype(jnp.bfloat16), "dp", scatter_dimension=1, tiled=True
        ).astype(jnp.float32),
        lax.psum_scatter(
            grad_down_part.astype(jnp.bfloat16), "dp", scatter_dimension=1, tiled=True
        ).astype(jnp.float32),
    )
    step_value = step_count[0].astype(jnp.float32)
    rate_qkv = D ** (-0.5)
    rate_out = max(HEADS * HEAD_DIM // 512, 1) ** (-0.5)
    rate_gateup = D ** (-0.5)
    rate_down = max(FF // 64, 1) ** (-0.5)
    rate_norm = 1.0
    new_qkv, new_first_qkv, new_second_qkv = adamw_step(
        master_qkv, first_qkv, second_qkv, red_qkv, rate_qkv, step_value
    )
    new_out, new_first_out, new_second_out = adamw_step(
        master_out, first_out, second_out, red_out, rate_out, step_value
    )
    new_gateup, new_first_gateup, new_second_gateup = adamw_step(
        master_gateup, first_gateup, second_gateup, red_gateup, rate_gateup, step_value
    )
    new_down, new_first_down, new_second_down = adamw_step(
        master_down, first_down, second_down, red_down, rate_down, step_value
    )
    new_norm, new_first_norm, new_second_norm = adamw_step(
        master_norm, first_norm, second_norm, grad_norm, rate_norm, step_value
    )
    return (
        block_output,
        grad_input,
        red_qkv,
        new_qkv,
        new_first_qkv,
        new_second_qkv,
        red_out,
        new_out,
        new_first_out,
        new_second_out,
        red_gateup,
        new_gateup,
        new_first_gateup,
        new_second_gateup,
        red_down,
        new_down,
        new_first_down,
        new_second_down,
        grad_norm,
        new_norm,
        new_first_norm,
        new_second_norm,
    )


MESH = pl.DeviceIdType.MESH
VMEM_BYTES = 61 * 1024 * 1024
BF16 = jnp.bfloat16
F32 = jnp.float32
NT = (((1,), (1,)), ((), ()))
ANY = pl.BlockSpec(memory_space=pl.ANY)
VM = pl.BlockSpec(memory_space=pltpu.VMEM)


LIGHT = pl.CostEstimate(flops=1 << 20, bytes_accessed=1 << 16, transcendentals=0)


def nt_dot(left, right):
    return lax.dot_general(left, right, NT, preferred_element_type=F32)


class Ring:
    def __init__(self, send, recv, local):
        self.here = lax.axis_index("dp")
        self.right = (self.here + 1) % 4
        self.left = (self.here + 3) % 4
        self.far = (self.here + 2) % 4
        self.send, self.recv, self.local = send, recv, local

    def copy(self, k, src, dst, other):
        return pltpu.make_async_remote_copy(
            src_ref=src,
            dst_ref=dst,
            send_sem=self.send.at[k],
            recv_sem=self.recv.at[k],
            device_id={"dp": other},
            device_id_type=MESH,
        )


class RingGather:
    def __init__(self, ring, first, half_of, place):
        self.plus_0 = ring.copy(first, half_of(0), place(ring.here, 0), ring.right)
        self.minus_1 = ring.copy(first + 1, half_of(1), place(ring.here, 1), ring.left)
        self.plus_1 = ring.copy(first + 2, half_of(1), place(ring.here, 1), ring.right)
        self.minus_0 = ring.copy(first + 3, half_of(0), place(ring.here, 0), ring.left)
        self.far_0 = ring.copy(first + 4, place(ring.left, 0), place(ring.left, 0), ring.right)
        self.far_1 = ring.copy(first + 5, place(ring.right, 1), place(ring.right, 1), ring.left)
        self.own = [
            pltpu.make_async_copy(half_of(h), place(ring.here, h), ring.local.at[first + h])
            for h in range(2)
        ]
        self.remote = (self.plus_0, self.minus_1, self.plus_1, self.minus_0, self.far_0, self.far_1)

    def start(self):
        for copy in self.remote[:4]:
            copy.start()
        for copy in self.own:
            copy.start()

    def forward(self):
        self.plus_0.wait_recv()
        self.far_0.start()
        self.minus_1.wait_recv()
        self.far_1.start()

    def near(self):
        self.plus_1.wait_recv()
        self.minus_0.wait_recv()

    def far(self):
        self.far_0.wait_recv()
        self.far_1.wait_recv()

    def drain(self):
        for copy in self.remote:
            copy.wait_send()

    def finish(self):
        for copy in self.own:
            copy.wait()
        self.near()
        self.far()
        self.drain()


class RingScatter:
    def __init__(self, ring, first, half_at, buf, out):
        self.buf, self.out = buf, out
        self.plus_far = ring.copy(first, half_at(ring.far, 0), buf.at[0], ring.right)
        self.minus_far = ring.copy(first + 1, half_at(ring.far, 1), buf.at[1], ring.left)
        self.plus_near = ring.copy(first + 2, half_at(ring.right, 1), buf.at[2], ring.right)
        self.minus_near = ring.copy(first + 3, half_at(ring.left, 0), buf.at[3], ring.left)
        self.plus_sum = ring.copy(first + 4, buf.at[6], buf.at[4], ring.right)
        self.minus_sum = ring.copy(first + 5, buf.at[7], buf.at[5], ring.left)
        places = ((ring.right, 0), (ring.left, 1), (ring.here, 0), (ring.here, 1))
        self.loads = [
            pltpu.make_async_copy(half_at(*place), buf.at[6 + k], ring.local.at[first + k])
            for k, place in enumerate(places)
        ]
        self.remote = (
            self.plus_far,
            self.minus_far,
            self.plus_near,
            self.minus_near,
            self.plus_sum,
            self.minus_sum,
        )

    def start(self):
        for copy in self.remote[:4]:
            copy.start()
        for copy in self.loads:
            copy.start()

    def forward(self):
        for copy in self.loads:
            copy.wait()
        self.plus_far.wait_recv()
        for_rows(self.buf.shape[1:], lambda at: add_at(self.buf, 6, 0, at))
        self.plus_sum.start()
        self.minus_far.wait_recv()
        for_rows(self.buf.shape[1:], lambda at: add_at(self.buf, 7, 1, at))
        self.minus_sum.start()

    def finish(self):
        for copy in self.remote[2:]:
            copy.wait_recv()
        buf = self.buf
        for half, terms in enumerate(((8, 3, 4), (9, 2, 5))):
            out = self.out(half)

            def total(at, out=out, terms=terms):
                out[at] = sum(buf[(k,) + at].astype(F32) for k in terms)

            for_rows(buf.shape[1:], total)
        for copy in self.remote:
            copy.wait_send()


def add_at(buf, dst, src, at):
    buf[(dst,) + at] = (buf[(dst,) + at].astype(F32) + buf[(src,) + at].astype(F32)).astype(BF16)


def for_rows(shape, visit):
    def step(i, carry):
        rows = pl.ds(pl.multiple_of(i * 16, 16), 16)
        if len(shape) == 2:
            visit((rows, slice(None)))
        else:
            for j in range(shape[0]):
                visit((j, rows, slice(None)))
        return carry

    lax.fori_loop(0, shape[-2] // 16, step, 0)


def ring_sems(count):
    return [pltpu.SemaphoreType.DMA((count,)) for _ in range(3)]


def row_halves(depth):
    half = depth // 2

    def place(ref):
        def at(owner, part):
            return ref.at[:, pl.ds(pl.multiple_of(owner * depth + part * half, half), half), :]

        return at

    return place


def plane_columns(depth):
    def place(ref):
        def at(owner, part):
            return ref.at[part, :, pl.ds(pl.multiple_of(owner * depth, depth), depth)]

        return at

    return place


def column_halves(depth):
    def place(ref):
        half = ref.shape[0] // 2

        def at(owner, part):
            columns = pl.ds(pl.multiple_of(owner * depth, depth), depth)
            return ref.at[pl.ds(part * half, half), columns]

        return at

    return place


def span_scatter(ring, first, ref, span, buf, out):
    at = plane_columns(ref.shape[2] // 4)(ref.at[:, pl.ds(*span), :])
    return RingScatter(ring, first, at, buf, lambda h: out.at[h])


def each(items, name):
    for item in items:
        getattr(item, name)()


def greet(others):
    sem = pltpu.get_barrier_semaphore()
    for other in others:
        pl.semaphore_signal(sem, inc=1, device_id=other, device_id_type=MESH)
    pl.semaphore_wait(sem, len(others))


class Square:
    def __init__(self, send, recv, rows):
        me = lax.axis_index("mp")
        self.core = me % 2
        self.x = (me // 2) % 2
        self.y = me // 4
        self.xn = (self.y * 2 + (1 - self.x)) * 2 + self.core
        self.yn = ((1 - self.y) * 2 + self.x) * 2 + self.core
        self.peer = (self.y * 2 + self.x) * 2 + (1 - self.core)
        self.own = self.y * 2 + self.x
        self.xc = self.y * 2 + (1 - self.x)
        self.yc = (1 - self.y) * 2 + self.x
        self.dc = (1 - self.y) * 2 + (1 - self.x)
        self.send, self.recv = send, recv
        cut = rows // 2 // 16 * 16
        self.rows = rows
        self.a = pl.ds(0, cut)
        self.b = pl.ds(cut, rows - cut)
        self.na, self.nb, self.cut = cut, rows - cut, cut

        self.others = [{"mp": self.xn}, {"mp": self.yn}, {"mp": self.peer}]

    def copy(self, k, src, dst, other):
        return pltpu.make_async_remote_copy(
            src_ref=src,
            dst_ref=dst,
            send_sem=self.send.at[k],
            recv_sem=self.recv.at[k],
            device_id={"mp": other},
            device_id_type=MESH,
        )


def add_rows(dst, src, count):
    def step(i, carry):
        rows = pl.ds(pl.multiple_of(i * 16, 16), 16)
        dst[rows, :] = (dst[rows, :].astype(F32) + src[rows, :].astype(F32)).astype(BF16)
        return carry

    lax.fori_loop(0, count // 16, step, 0)


def nothing():
    pass


def square_kernel(
    rows,
    sems,
    gather=None,
    scatter=None,
    ring=None,
    start=nothing,
    first=nothing,
    early=nothing,
    later=nothing,
    between=nothing,
    middle=nothing,
    end=nothing,
):
    send, recv, lsem = sems
    sq = Square(send, recv, rows)
    core = sq.core
    greet(sq.others + ([{"dp": ring.left}, {"dp": ring.right}] if ring is not None else []))

    def place(rel, turn):
        chip_y = (sq.y + rel % 2) % 2
        chip_x = (sq.x + ((rel + 1) // 2) % 2) % 2
        return chip_y * 2 + chip_x, (1 - core + turn) % 2

    if gather is not None:
        compute, share, full, gbuf = gather
        c_own = sq.copy(0, share, gbuf.at[sq.own, core], sq.peer)
        x_a = sq.copy(1, share.at[sq.a], gbuf.at[sq.own, core, sq.a], sq.xn)
        y_b = sq.copy(2, share.at[sq.b], gbuf.at[sq.own, core, sq.b], sq.yn)
        f_x = sq.copy(3, gbuf.at[sq.yc, core, sq.b], gbuf.at[sq.yc, core, sq.b], sq.xn)
        f_y = sq.copy(4, gbuf.at[sq.xc, core, sq.a], gbuf.at[sq.xc, core, sq.a], sq.yn)
        x_b = sq.copy(5, share.at[sq.b], gbuf.at[sq.own, core, sq.b], sq.xn)
        y_a = sq.copy(6, share.at[sq.a], gbuf.at[sq.own, core, sq.a], sq.yn)
        c_d = sq.copy(7, gbuf.at[sq.dc, core], gbuf.at[sq.dc, core], sq.peer)
        c_x = sq.copy(8, gbuf.at[sq.xc, core], gbuf.at[sq.xc, core], sq.peer)
        c_y = sq.copy(9, gbuf.at[sq.yc, core], gbuf.at[sq.yc, core], sq.peer)
        local = pltpu.make_async_copy(share, gbuf.at[sq.own, core], lsem.at[8])
        x_a.start()
        y_b.start()
        c_own.start()
        local.start()
    start()
    if gather is not None:

        def gather_step(t, carry):
            chip, which = place(t // 2, t % 2)

            @pl.when(t == 0)
            def _():
                c_own.wait_recv()
                local.wait()
                first()

            @pl.when(t == 2)
            def _():
                x_a.wait_recv()
                y_b.wait_recv()
                f_x.start()
                f_y.start()
                x_b.start()
                y_a.start()
                early()
                f_x.wait_recv()
                f_y.wait_recv()
                c_d.start()
                c_d.wait_recv()

            @pl.when(t == 4)
            def _():
                x_b.wait_recv()
                y_a.wait_recv()
                c_x.start()
                c_y.start()
                later()
                c_x.wait_recv()
                c_y.wait_recv()

            pltpu.make_async_copy(gbuf.at[chip, which], full.at[chip, which], lsem.at[t]).start()
            compute(t, chip, which)
            return carry

        lax.fori_loop(0, 8, gather_step, 0)
    between()
    if scatter is not None:
        finish_tile, pbuf, (rcore, rxd, ryd, rx, ry), out = scatter
        x_d = sq.copy(14, pbuf.at[sq.dc, core, sq.a], rxd, sq.xn)
        y_d = sq.copy(15, pbuf.at[sq.dc, core, sq.b], ryd, sq.yn)
        x_ra = sq.copy(16, pbuf.at[sq.xc, core, sq.a], rx.at[sq.a], sq.xn)
        y_rb = sq.copy(17, pbuf.at[sq.yc, core, sq.b], ry.at[sq.b], sq.yn)
        x_rb = sq.copy(18, pbuf.at[sq.xc, core, sq.b], rx.at[sq.b], sq.xn)
        y_ra = sq.copy(19, pbuf.at[sq.yc, core, sq.a], ry.at[sq.a], sq.yn)

        def scatter_step(t, carry):
            turn = t % 2
            rel = (t // 2 + 1) % 4
            chip, which = place(rel, turn)
            finish_tile(t, chip, which)
            to_peer = sq.copy(10 + rel, pbuf.at[chip, which], rcore.at[chip], sq.peer)

            @pl.when(turn == 0)
            def _():
                to_peer.start()

            @pl.when(turn == 1)
            def _():
                to_peer.wait_recv()
                add_rows(pbuf.at[chip, which], rcore.at[chip], rows)

            @pl.when(t == 1)
            def _():
                x_d.start()
                y_d.start()

            @pl.when(t == 3)
            def _():
                x_ra.start()

            @pl.when(t == 5)
            def _():
                y_rb.start()

            return carry

        lax.fori_loop(0, 8, scatter_step, 0)
        x_d.wait_recv()
        add_rows(pbuf.at[sq.yc, core, sq.a], rxd, sq.na)
        y_ra.start()
        y_d.wait_recv()
        add_rows(pbuf.at[sq.xc, core, sq.b], ryd, sq.nb)
        x_rb.start()
        middle()
        x_ra.wait_recv()
        y_rb.wait_recv()
        y_ra.wait_recv()
        x_rb.wait_recv()

        def last(i, carry):
            part = pl.ds(pl.multiple_of(i * 16, 16), 16)
            out[part, :] = (
                pbuf[sq.own, core, part, :].astype(F32)
                + rx[part, :].astype(F32)
                + ry[part, :].astype(F32)
            )
            return carry

        lax.fori_loop(0, rows // 16, last, 0)
        for k in range(4):
            sq.copy(10 + k, pbuf.at[0, 0], rcore.at[0], sq.peer).wait_send()
        for copy in (x_d, y_d, x_ra, y_rb, x_rb, y_ra):
            copy.wait_send()
    end()
    if gather is not None:
        for copy in (c_own, x_a, y_b, f_x, f_y, x_b, y_a, c_d, c_x, c_y):
            copy.wait_send()
        for t in range(8):
            pltpu.make_async_copy(gbuf.at[0, 0], full.at[0, 0], lsem.at[t]).wait()


def scatter_scratch(rows, width):
    cut = rows // 2 // 16 * 16
    return [
        pltpu.VMEM((4, 2, rows, width), BF16),
        pltpu.VMEM((4, rows, width), BF16),
        pltpu.VMEM((cut, width), BF16),
        pltpu.VMEM((rows - cut, width), BF16),
        pltpu.VMEM((rows, width), BF16),
        pltpu.VMEM((rows, width), BF16),
    ]


SEMS = [
    pltpu.SemaphoreType.DMA((20,)),
    pltpu.SemaphoreType.DMA((20,)),
    pltpu.SemaphoreType.DMA((9,)),
]


def params(collective_id):
    return pltpu.CompilerParams(
        collective_id=collective_id, has_side_effects=True, vmem_limit_bytes=VMEM_BYTES
    )


def whole(shape):
    return pl.BlockSpec(shape, lambda *_: (0,) * len(shape))


def qkv_call(block_input, low_qkv, positions, rows):
    tokens, width = block_input.shape
    depth, cols = low_qkv.shape[1:]
    tiles = tokens // rows
    heads = cols // HEAD_DIM
    scale = 1.0 / math.sqrt(HEAD_DIM)
    half = depth // 2

    def kernel(
        x_ref, low_ref, pos_ref, q_ref, k_ref, v_ref, cos_ref, sin_ref, w_ref,
        x_buf, w_buf, acc, xsem, osem, send, recv, local,
    ):
        ring = Ring(send, recv, local)
        gather = RingGather(
            ring, 0, lambda h: low_ref.at[:, pl.ds(h * half, half), :], row_halves(depth)(w_buf)
        )

        def x_copy(t, k):
            return pltpu.make_async_copy(
                x_ref.at[t, :, pl.ds(k * depth, depth)], x_buf.at[t, k], xsem.at[t, k]
            )

        def start_tile(t, carry):
            for k in range(4):
                x_copy(t, k).start()
            return carry

        lax.fori_loop(0, tiles, start_tile, 0)
        greet([{"dp": ring.left}, {"dp": ring.right}])
        gather.start()
        for copy in gather.own:
            copy.wait()

        def part(t, j, owner):
            depths = pl.ds(pl.multiple_of(owner * depth, depth), depth)
            return jnp.dot(x_buf[t, owner], w_buf[j, depths, :], preferred_element_type=F32)

        def own_tile(t, carry):
            for k in range(4):
                x_copy(t, k).wait()
            for j in range(3):
                acc[t, j] = part(t, j, ring.here)
            return carry

        lax.fori_loop(0, tiles, own_tile, 0)
        lane = lax.broadcasted_iota(jnp.int32, (1, HEAD_DIM), 1)
        ladder = (lane % (HEAD_DIM // 2)).astype(F32)
        inverse = jnp.exp(ladder * (-2.0 * math.log(10000.0) / HEAD_DIM))
        sign = jnp.where(lane < HEAD_DIM // 2, -1.0, 1.0)

        def table_tile(t, carry):
            angles = pos_ref[t].astype(F32) * inverse
            cos_ref[t] = jnp.cos(angles)
            sin_ref[t] = jnp.sin(angles) * sign
            return carry

        lax.fori_loop(0, tiles // 2, table_tile, 0)
        gather.forward()
        lax.fori_loop(tiles // 2, tiles, table_tile, 0)
        gather.near()

        def near_tile(t, carry):
            for j in range(3):
                acc[t, j] += part(t, j, ring.left) + part(t, j, ring.right)
            return carry

        lax.fori_loop(0, tiles, near_tile, 0)
        gather.far()
        keep = pltpu.make_async_copy(w_buf, w_ref, osem.at[0])
        keep.start()

        def far_tile(t, carry):
            for j, ref in enumerate((q_ref, k_ref)):
                a = acc[t, j] + part(t, j, ring.far)
                for h in range(heads):
                    cut = slice(h * HEAD_DIM, (h + 1) * HEAD_DIM)
                    turned = a[:, cut] * cos_ref[t] + pltpu.roll(a[:, cut], HEAD_DIM // 2, 1) * sin_ref[t]
                    if j == 0:
                        turned = turned * scale
                    ref[t, :, cut] = turned.astype(BF16)
            v_ref[t] = (acc[t, 2] + part(t, 2, ring.far)).astype(BF16)
            return carry

        lax.fori_loop(0, tiles, far_tile, 0)
        keep.wait()
        gather.drain()

    tile = jax.ShapeDtypeStruct((tiles, rows, cols), BF16)
    return pl.pallas_call(
        kernel,
        out_shape=[tile] * 3
        + [jax.ShapeDtypeStruct((tiles, rows, HEAD_DIM), F32)] * 2
        + [jax.ShapeDtypeStruct((3, width, cols), BF16)],
        in_specs=[ANY, ANY, VM],
        out_specs=[VM] * 5 + [ANY],
        scratch_shapes=[
            pltpu.VMEM((tiles, 4, rows, depth), BF16),
            pltpu.VMEM((3, width, cols), BF16),
            pltpu.VMEM((tiles, 3, rows, cols), F32),
            pltpu.SemaphoreType.DMA((tiles, 4)),
            pltpu.SemaphoreType.DMA((1,)),
        ]
        + ring_sems(6),
        compiler_params=params(5),
        cost_estimate=LIGHT,
        name="qkv",
    )(
        block_input.reshape(tiles, rows, width),
        low_qkv,
        positions.reshape(tiles, rows, 1),
    )


BLOCK = 128


def attention_call(queries, key_rows, value_rows, prefix_len, low_out, low_unit):
    tokens, cols = queries.shape
    proteins = tokens // LEN
    heads = cols // HEAD_DIM
    depth = low_out.shape[1]
    last = proteins * heads - 1

    def kernel(pre_ref, q_ref, k_ref, v_ref, lo_ref, lu_ref, o_ref, p_ref, wo_ref, wu_ref, send, recv, local):
        prefix = pre_ref[pl.program_id(0)]
        step = pl.program_id(0) * heads + pl.program_id(1)
        ring = Ring(send, recv, local)
        half = lo_ref.shape[0] // 2
        gathers = [
            RingGather(ring, 0, lambda h: lo_ref.at[pl.ds(h * half, half), :], column_halves(depth)(wo_ref)),
            RingGather(ring, 6, lambda h: lu_ref.at[h], plane_columns(depth)(wu_ref)),
        ]

        @pl.when(step == 0)
        def _():
            greet([{"dp": ring.left}, {"dp": ring.right}])
            for gather in gathers:
                gather.start()

        for i in range(LEN // BLOCK):
            rows = slice(i * BLOCK, (i + 1) * BLOCK)
            s = nt_dot(q_ref[rows, :], k_ref[...])
            col = lax.broadcasted_iota(jnp.int32, s.shape, 1)
            row = lax.broadcasted_iota(jnp.int32, (BLOCK, 1), 0) + i * BLOCK
            s = jnp.where(col < jnp.maximum(prefix, row + 1), s, -1e30)
            e = jnp.exp(s - jnp.max(s, axis=-1, keepdims=True))
            p = (e * (1.0 / jnp.sum(e, axis=-1, keepdims=True))).astype(BF16)
            p_ref[0, 0, rows, :] = p
            o_ref[rows, :] = jnp.dot(p, v_ref[...], preferred_element_type=F32).astype(BF16)

        @pl.when(step == last // 2)
        def _():
            for gather in gathers:
                gather.forward()

        @pl.when(step == last)
        def _():
            for gather in gathers:
                for copy in gather.own:
                    copy.wait()
                gather.near()
                gather.far()
                gather.drain()

    tile = pl.BlockSpec((LEN, HEAD_DIM), lambda p, h, *_: (p, h))
    return pl.pallas_call(
        kernel,
        grid_spec=pltpu.PrefetchScalarGridSpec(
            num_scalar_prefetch=1,
            grid=(proteins, heads),
            in_specs=[tile] * 3 + [ANY, ANY],
            out_specs=[tile, pl.BlockSpec((1, 1, LEN, LEN), lambda p, h, *_: (p, h, 0, 0)), ANY, ANY],
            scratch_shapes=ring_sems(12),
        ),
        out_shape=[
            jax.ShapeDtypeStruct((tokens, cols), BF16),
            jax.ShapeDtypeStruct((proteins, heads, LEN, LEN), BF16),
            jax.ShapeDtypeStruct((low_out.shape[0], 4 * depth), BF16),
            jax.ShapeDtypeStruct(low_unit.shape[:2] + (4 * depth,), BF16),
        ],
        compiler_params=params(6),
        cost_estimate=LIGHT,
        name="attention",
    )(prefix_len, queries, key_rows, value_rows, low_out, low_unit)


TN = (((0,), (0,)), ((), ()))


def attention_back_call(
    queries, key_rows, value_rows, probs, attended, grad_attended, cos_table, sin_table, norm_terms,
    grad_gateup_part, span,
):
    tokens, cols = queries.shape
    proteins = tokens // LEN
    heads = cols // HEAD_DIM
    scale = 1.0 / math.sqrt(HEAD_DIM)
    last = proteins * heads - 1
    depth = grad_gateup_part.shape[2] // 4

    def kernel(
        q_ref, k_ref, v_ref, p_ref, o_ref, do_ref, cos_ref, sin_ref, nt_ref, gg_ref,
        da_ref, norm_ref, red_ref,
        dk_acc, dv_acc, sums, got, nsend, nrecv, buf, send, recv, local,
    ):
        step = pl.program_id(0) * heads + pl.program_id(1)
        ring = Ring(send, recv, local)
        side = span_scatter(ring, 0, gg_ref, span, buf, red_ref)
        sq = Square(nsend, nrecv, 32)
        partners = [
            {"mp": sq.peer},
            {"mp": sq.xn},
            {"mp": sq.yn},
            {"dp": ring.here + 1 - 2 * (ring.here % 2)},
            {"dp": 3 - ring.here},
        ]
        swaps = [
            pltpu.make_async_remote_copy(
                src_ref=sums.at[k],
                dst_ref=got.at[k],
                send_sem=nsend.at[k],
                recv_sem=nrecv.at[k],
                device_id=other,
                device_id_type=MESH,
            )
            for k, other in enumerate(partners)
        ]

        @pl.when(step == 0)
        def _():
            sums[0] = nt_ref[...]
            greet(sq.others + [{"dp": ring.left}, {"dp": ring.right}])
            side.start()
            swaps[0].start()

        for k in range(5):

            @pl.when(step == k + 1)
            def _():
                swaps[k].wait()
                if k < 4:
                    sums[k + 1] = sums[k] + got[k]
                    swaps[k + 1].start()
                else:
                    norm_ref[...] = sums[k] + got[k]

        @pl.when(step == last // 2)
        def _():
            side.forward()

        for i in range(LEN // BLOCK):
            rows = slice(i * BLOCK, (i + 1) * BLOCK)
            do = do_ref[rows, :]
            p = p_ref[0, 0, rows, :]
            delta = jnp.sum(do.astype(F32) * o_ref[rows, :].astype(F32), axis=-1, keepdims=True)
            dp = nt_dot(do, v_ref[...])
            ds = (p.astype(F32) * (dp - delta)).astype(BF16)
            dv = lax.dot_general(p, do, TN, preferred_element_type=F32)
            dk = lax.dot_general(ds, q_ref[rows, :], TN, preferred_element_type=F32)
            if i == 0:
                dv_acc[...] = dv
                dk_acc[...] = dk
            else:
                dv_acc[...] += dv
                dk_acc[...] += dk
            dq = jnp.dot(ds, k_ref[...], preferred_element_type=F32)
            turned = dq * cos_ref[rows, :] - pltpu.roll(dq, HEAD_DIM // 2, 1) * sin_ref[rows, :]
            da_ref[0, rows, :] = (turned * scale).astype(BF16)
        dk = dk_acc[...]
        turned = dk * cos_ref[...] - pltpu.roll(dk, HEAD_DIM // 2, 1) * sin_ref[...]
        da_ref[1] = turned.astype(BF16)
        da_ref[2] = dv_acc[...].astype(BF16)

        @pl.when(step == last)
        def _():
            side.finish()

    tile = pl.BlockSpec((LEN, HEAD_DIM), lambda p, h: (p, h))
    table = pl.BlockSpec((LEN, HEAD_DIM), lambda p, h: (p, 0))
    return pl.pallas_call(
        kernel,
        grid=(proteins, heads),
        in_specs=[tile] * 3
        + [pl.BlockSpec((1, 1, LEN, LEN), lambda p, h: (p, h, 0, 0)), tile, tile, table, table]
        + [whole(norm_terms.shape), ANY],
        out_specs=[
            pl.BlockSpec((3, LEN, HEAD_DIM), lambda p, h: (0, p, h)),
            whole(norm_terms.shape),
            whole((2, span[1], depth)),
        ],
        out_shape=[
            jax.ShapeDtypeStruct((3, tokens, cols), BF16),
            jax.ShapeDtypeStruct(norm_terms.shape, F32),
            jax.ShapeDtypeStruct((2, span[1], depth), F32),
        ],
        scratch_shapes=[
            pltpu.VMEM((LEN, HEAD_DIM), F32),
            pltpu.VMEM((LEN, HEAD_DIM), F32),
            pltpu.VMEM((5,) + norm_terms.shape, F32),
            pltpu.VMEM((5,) + norm_terms.shape, F32),
            pltpu.SemaphoreType.DMA((5,)),
            pltpu.SemaphoreType.DMA((5,)),
            pltpu.VMEM((10, span[1], depth), BF16),
        ]
        + ring_sems(6),
        compiler_params=params(7),
        cost_estimate=LIGHT,
        name="attention_back",
    )(
        queries,
        key_rows,
        value_rows,
        probs,
        attended,
        grad_attended,
        cos_table,
        sin_table,
        norm_terms,
        grad_gateup_part,
    )


def out_call(attended, w_out, low_units, rows):
    cols = attended.shape[1]
    count = len(low_units)
    depth = low_units[0].shape[2]

    def kernel(o_ref, w_ref, *rest):
        low_refs, (out, *unit_refs), rest = rest[:count], rest[count : 2 * count + 1], rest[2 * count + 1 :]
        w_buf, pbuf, rcore, rxd, ryd, rx, ry, wsem, send, recv, lsem, zsend, zrecv, zlocal = rest
        ring = Ring(zsend, zrecv, zlocal)
        gathers = [
            RingGather(ring, 6 * k, lambda h, low=low: low.at[h], plane_columns(depth)(unit))
            for k, (low, unit) in enumerate(zip(low_refs, unit_refs))
        ]
        weight = pltpu.make_async_copy(w_ref, w_buf, wsem.at[0])
        weight.start()

        def start():
            gathers[0].start()
            weight.wait()

        def between():
            gathers[0].forward()
            for gather in gathers[1:]:
                gather.start()

        def middle():
            for gather in gathers[1:]:
                gather.forward()

        def end():
            for gather in gathers:
                gather.finish()

        def compute(t, chip, which):
            part = jnp.dot(o_ref[chip, which], w_buf[...], preferred_element_type=F32)
            pbuf[chip, which] = part.astype(BF16)

        square_kernel(
            rows,
            (send, recv, lsem),
            scatter=(compute, pbuf, (rcore, rxd, ryd, rx, ry), out),
            ring=ring,
            start=start,
            between=nothing,
            middle=lambda: (between(), middle()),
            end=end,
        )

    return pl.pallas_call(
        kernel,
        out_shape=[jax.ShapeDtypeStruct((rows, D), F32)]
        + [jax.ShapeDtypeStruct(low.shape[:2] + (D,), BF16) for low in low_units],
        in_specs=[VM, ANY] + [ANY] * count,
        out_specs=[VM] + [ANY] * count,
        scratch_shapes=[pltpu.VMEM((cols, D), BF16)]
        + scatter_scratch(rows, D)
        + [pltpu.SemaphoreType.DMA((1,))]
        + SEMS
        + ring_sems(6 * count),
        compiler_params=params(0),
        cost_estimate=LIGHT,
        name="out_reduce",
    )(attended.reshape(4, 2, rows, cols), w_out, *low_units)


def ffn_call(middle_low, units, low_unit, low_down):
    rows = middle_low.shape[0]
    live, depth = low_down.shape
    count = len(units)
    rest_rows = low_unit.shape[1]
    curve = math.sqrt(2.0 / math.pi)

    def kernel(share, lu_ref, ld_ref, *rest):
        unit_refs, rest = rest[:count], rest[count:]
        out, full, hid_ref, act_ref, pull_ref, wg_ref, wd_ref = rest[:7]
        (w_g, w_d, gbuf, hid_buf, stage, pbuf, rcore, rxd, ryd, rx, ry) = rest[7:18]
        wsem, osem, hsem, send, recv, lsem, zsend, zrecv, zlocal = rest[18:]
        ring = Ring(zsend, zrecv, zlocal)
        tail = w_g.at[:, pl.ds(live - rest_rows, rest_rows), :]
        gather_g = RingGather(ring, 0, lambda h: lu_ref.at[h], plane_columns(depth)(tail))
        half = live // 2
        gather_d = RingGather(ring, 6, lambda h: ld_ref.at[pl.ds(h * half, half), :], column_halves(depth)(w_d))
        copies = []
        offset = 0
        for k, ref in enumerate(unit_refs):
            size = ref.shape[1]
            copies.append(pltpu.make_async_copy(ref, w_g.at[:, pl.ds(offset, size), :], wsem.at[k]))
            offset += size
        for copy in copies:
            copy.start()
        keep_g = pltpu.make_async_copy(w_g, wg_ref, wsem.at[count])
        keep_d = pltpu.make_async_copy(w_d, wd_ref, wsem.at[count + 1])
        outs = (act_ref, pull_ref)

        def first():
            gather_g.forward()
            gather_d.start()
            for copy in copies:
                copy.wait()
            for copy in gather_g.own:
                copy.wait()
            gather_g.near()
            gather_g.far()
            keep_g.start()

        def later():
            gather_d.forward()

        def between():
            for copy in gather_d.own:
                copy.wait()
            gather_d.near()
            gather_d.far()
            keep_d.start()

        def compute(t, chip, which):
            slot = t % 2

            @pl.when(t >= 2)
            def _():
                for k, ref in enumerate(outs):
                    pltpu.make_async_copy(stage.at[slot, k], ref.at[chip, which], osem.at[slot, k]).wait()

            tile = gbuf[chip, which]
            gate = nt_dot(tile, w_g[0])
            up = nt_dot(tile, w_g[1])
            square = gate * gate
            bent = jnp.tanh(curve * gate * (1.0 + 0.044715 * square))
            half = 0.5 * (1.0 + bent)
            act = gate * half
            slope = half + 0.5 * curve * gate * (1.0 - bent * bent) * (1.0 + 3.0 * 0.044715 * square)
            hid_buf[chip, which] = (act * up).astype(BF16)
            stage[slot, 0] = act.astype(BF16)
            stage[slot, 1] = (slope * up).astype(BF16)
            for k, ref in enumerate(outs):
                pltpu.make_async_copy(stage.at[slot, k], ref.at[chip, which], osem.at[slot, k]).start()
            pltpu.make_async_copy(hid_buf.at[chip, which], hid_ref.at[chip, which], hsem.at[t]).start()

        def finish_tile(t, chip, which):
            part = jnp.dot(hid_buf[chip, which], w_d[...], preferred_element_type=F32)
            pbuf[chip, which] = part.astype(BF16)

        def end():
            for slot in range(2):
                for k, ref in enumerate(outs):
                    pltpu.make_async_copy(stage.at[slot, k], ref.at[0, 0], osem.at[slot, k]).wait()
            for t in range(8):
                pltpu.make_async_copy(hid_buf.at[0, 0], hid_ref.at[0, 0], hsem.at[t]).wait()
            keep_g.wait()
            keep_d.wait()
            gather_g.drain()
            gather_d.drain()

        square_kernel(
            rows,
            (send, recv, lsem),
            gather=(compute, share, full, gbuf),
            scatter=(finish_tile, pbuf, (rcore, rxd, ryd, rx, ry), out),
            ring=ring,
            start=gather_g.start,
            first=first,
            later=later,
            between=between,
            end=end,
        )

    kept = jax.ShapeDtypeStruct((4, 2, rows, live), BF16)
    return pl.pallas_call(
        kernel,
        out_shape=[
            jax.ShapeDtypeStruct((rows, D), F32),
            jax.ShapeDtypeStruct((4, 2, rows, D), BF16),
            kept,
            kept,
            kept,
            jax.ShapeDtypeStruct((2, live, D), BF16),
            jax.ShapeDtypeStruct((live, D), BF16),
        ],
        in_specs=[ANY] * (3 + count),
        out_specs=[VM] + [ANY] * 6,
        scratch_shapes=[
            pltpu.VMEM((2, live, D), BF16),
            pltpu.VMEM((live, D), BF16),
            pltpu.VMEM((4, 2, rows, D), BF16),
            pltpu.VMEM((4, 2, rows, live), BF16),
            pltpu.VMEM((2, 2, rows, live), BF16),
        ]
        + scatter_scratch(rows, D)
        + [
            pltpu.SemaphoreType.DMA((count + 2,)),
            pltpu.SemaphoreType.DMA((2, 2)),
            pltpu.SemaphoreType.DMA((8,)),
        ]
        + SEMS
        + ring_sems(12),
        compiler_params=params(1),
        cost_estimate=LIGHT,
        name="ffn",
    )(middle_low, low_unit, low_down, *units)


def ffn_back_call(ffn_grad, act, pull, w_down):
    rows = ffn_grad.shape[0]
    live = w_down.shape[0]

    def kernel(share, act_ref, pull_ref, wd_ref, full, dg_ref, w_d, gbuf, load, stage, wsem, isem, osem, send, recv, lsem):
        weight = pltpu.make_async_copy(wd_ref, w_d, wsem.at[0])
        weight.start()

        def compute(t, chip, which):
            slot = t % 2
            loads = [
                pltpu.make_async_copy(ref.at[chip, which], load.at[k], isem.at[k])
                for k, ref in enumerate((act_ref, pull_ref))
            ]
            stores = [
                pltpu.make_async_copy(stage.at[slot, k], dg_ref.at[k, chip, which], osem.at[slot, k])
                for k in range(2)
            ]
            for copy in loads:
                copy.start()

            @pl.when(t >= 2)
            def _():
                for copy in stores:
                    copy.wait()

            dh = nt_dot(gbuf[chip, which], w_d[...])
            for copy in loads:
                copy.wait()
            stage[slot, 0] = (dh * load[1].astype(F32)).astype(BF16)
            stage[slot, 1] = (dh * load[0].astype(F32)).astype(BF16)
            for copy in stores:
                copy.start()

        def end():
            for slot in range(2):
                for k in range(2):
                    pltpu.make_async_copy(stage.at[slot, k], dg_ref.at[k, 0, 0], osem.at[slot, k]).wait()

        square_kernel(
            rows, (send, recv, lsem), gather=(compute, share, full, gbuf), first=weight.wait, end=end
        )

    return pl.pallas_call(
        kernel,
        out_shape=[
            jax.ShapeDtypeStruct((4, 2, rows, D), BF16),
            jax.ShapeDtypeStruct((2, 4, 2, rows, live), BF16),
        ],
        in_specs=[ANY] * 4,
        out_specs=[ANY, ANY],
        scratch_shapes=[
            pltpu.VMEM((live, D), BF16),
            pltpu.VMEM((4, 2, rows, D), BF16),
            pltpu.VMEM((2, rows, live), BF16),
            pltpu.VMEM((2, 2, rows, live), BF16),
            pltpu.SemaphoreType.DMA((1,)),
            pltpu.SemaphoreType.DMA((2,)),
            pltpu.SemaphoreType.DMA((2, 2)),
        ]
        + SEMS,
        compiler_params=params(2),
        cost_estimate=LIGHT,
        name="ffn_back",
    )(ffn_grad, act, pull, w_down)


def middle_back_call(grad_gateup_rows, w_gateup, grad_down_part, grad_gateup_part, span, rows):
    live, width = grad_down_part.shape
    depth = width // 4

    def kernel(
        dg_ref, wg_ref, gd_ref, gg_ref, out, red_d, red_g,
        w_g, load, buf_d, buf_g, pbuf, rcore, rxd, ryd, rx, ry, wsem, isem, send, recv, lsem, zsend, zrecv, zlocal,
    ):
        ring = Ring(zsend, zrecv, zlocal)
        half = live // 2
        sides = (
            RingScatter(ring, 0, column_halves(depth)(gd_ref), buf_d, lambda h: red_d.at[pl.ds(h * half, half), :]),
            span_scatter(ring, 6, gg_ref, span, buf_g, red_g),
        )
        weight = pltpu.make_async_copy(wg_ref, w_g, wsem.at[0])
        weight.start()
        me = lax.axis_index("mp")
        core, x, y = me % 2, (me // 2) % 2, me // 4

        def loads(t):
            rel = (t // 2 + 1) % 4
            chip = ((y + rel % 2) % 2) * 2 + (x + ((rel + 1) // 2) % 2) % 2
            which = (1 - core + t % 2) % 2
            return [
                pltpu.make_async_copy(dg_ref.at[k, chip, which], load.at[t % 2, k], isem.at[t % 2, k])
                for k in range(2)
            ]

        for copy in loads(0):
            copy.start()

        def compute(t, chip, which):
            @pl.when(t < 7)
            def _():
                for copy in loads(t + 1):
                    copy.start()

            for copy in loads(t):
                copy.wait()
            slot = t % 2
            part = jnp.dot(load[slot, 0], w_g[0], preferred_element_type=F32)
            part += jnp.dot(load[slot, 1], w_g[1], preferred_element_type=F32)
            pbuf[chip, which] = part.astype(BF16)

        square_kernel(
            rows,
            (send, recv, lsem),
            scatter=(compute, pbuf, (rcore, rxd, ryd, rx, ry), out),
            ring=ring,
            start=lambda: (each(sides, "start"), weight.wait()),
            middle=lambda: each(sides, "forward"),
            end=lambda: each(sides, "finish"),
        )

    return pl.pallas_call(
        kernel,
        out_shape=[
            jax.ShapeDtypeStruct((rows, D), F32),
            jax.ShapeDtypeStruct((live, depth), F32),
            jax.ShapeDtypeStruct((2, span[1], depth), F32),
        ],
        in_specs=[ANY] * 4,
        out_specs=[VM] * 3,
        scratch_shapes=[
            pltpu.VMEM((2, live, D), BF16),
            pltpu.VMEM((2, 2, rows, live), BF16),
            pltpu.VMEM((10, live // 2, depth), BF16),
            pltpu.VMEM((10, span[1], depth), BF16),
        ]
        + scatter_scratch(rows, D)
        + [pltpu.SemaphoreType.DMA((1,)), pltpu.SemaphoreType.DMA((2, 2))]
        + SEMS
        + ring_sems(12),
        compiler_params=params(8),
        cost_estimate=LIGHT,
        name="middle_back",
    )(grad_gateup_rows, w_gateup, grad_down_part, grad_gateup_part)


def out_back_call(attn_grad, w_out, grad_gateup_part, span):
    rows = attn_grad.shape[0]
    cols = w_out.shape[0]
    depth = grad_gateup_part.shape[2] // 4

    def kernel(
        share, w_ref, gg_ref, full, dout, red, w_buf, gbuf, buf, wsem, send, recv, lsem, zsend, zrecv, zlocal
    ):
        ring = Ring(zsend, zrecv, zlocal)
        side = span_scatter(ring, 0, gg_ref, span, buf, red)
        weight = pltpu.make_async_copy(w_ref, w_buf, wsem.at[0])
        weight.start()

        def compute(t, chip, which):
            dout[chip, which] = nt_dot(gbuf[chip, which], w_buf[...]).astype(BF16)

        square_kernel(
            rows,
            (send, recv, lsem),
            gather=(compute, share, full, gbuf),
            ring=ring,
            start=side.start,
            first=weight.wait,
            early=side.forward,
            end=side.finish,
        )

    return pl.pallas_call(
        kernel,
        out_shape=[
            jax.ShapeDtypeStruct((4, 2, rows, D), BF16),
            jax.ShapeDtypeStruct((4, 2, rows, cols), BF16),
            jax.ShapeDtypeStruct((2, span[1], depth), F32),
        ],
        in_specs=[ANY] * 3,
        out_specs=[ANY, VM, VM],
        scratch_shapes=[
            pltpu.VMEM((cols, D), BF16),
            pltpu.VMEM((4, 2, rows, D), BF16),
            pltpu.VMEM((10, span[1], depth), BF16),
            pltpu.SemaphoreType.DMA((1,)),
        ]
        + SEMS
        + ring_sems(6),
        compiler_params=params(3),
        cost_estimate=LIGHT,
        name="out_back",
    )(attn_grad, w_out, grad_gateup_part)


def input_back_call(grad_proj, w_qkv, grad_qkv_part, grad_out_part, rows):
    width, cols = w_qkv.shape[1:]
    depth = width // 4

    def kernel(
        da_ref, w_ref, gq_ref, go_ref, out, red_q, red_o,
        w_buf, buf_q, buf_o, pbuf, rcore, rxd, ryd, rx, ry, wsem, send, recv, lsem, zsend, zrecv, zlocal,
    ):
        ring = Ring(zsend, zrecv, zlocal)
        half = depth // 2
        part = cols // 2
        sides = (
            RingScatter(
                ring, 0, row_halves(depth)(gq_ref), buf_q, lambda h: red_q.at[:, pl.ds(h * half, half), :]
            ),
            RingScatter(
                ring, 6, column_halves(depth)(go_ref), buf_o, lambda h: red_o.at[pl.ds(h * part, part), :]
            ),
        )
        weight = pltpu.make_async_copy(w_ref, w_buf, wsem.at[0])
        weight.start()

        def start():
            each(sides, "start")
            weight.wait()

        def compute(t, chip, which):
            part = nt_dot(da_ref[0, chip, which], w_buf[0])
            part += nt_dot(da_ref[1, chip, which], w_buf[1])
            part += nt_dot(da_ref[2, chip, which], w_buf[2])
            pbuf[chip, which] = part.astype(BF16)

        square_kernel(
            rows,
            (send, recv, lsem),
            scatter=(compute, pbuf, (rcore, rxd, ryd, rx, ry), out),
            ring=ring,
            start=start,
            middle=lambda: each(sides, "forward"),
            end=lambda: each(sides, "finish"),
        )

    return pl.pallas_call(
        kernel,
        out_shape=[
            jax.ShapeDtypeStruct((rows, D), F32),
            jax.ShapeDtypeStruct((3, depth, cols), F32),
            jax.ShapeDtypeStruct((cols, depth), F32),
        ],
        in_specs=[VM, ANY, ANY, ANY],
        out_specs=[VM, VM, VM],
        scratch_shapes=[
            pltpu.VMEM((3, D, cols), BF16),
            pltpu.VMEM((10, 3, depth // 2, cols), BF16),
            pltpu.VMEM((10, cols // 2, depth), BF16),
        ]
        + scatter_scratch(rows, D)
        + [pltpu.SemaphoreType.DMA((1,))]
        + SEMS
        + ring_sems(12),
        compiler_params=params(4),
        cost_estimate=LIGHT,
        name="input_back",
    )(grad_proj.reshape(3, 4, 2, rows, cols), w_qkv, grad_qkv_part, grad_out_part)


SPANS = ((0, 96), (96, 416), (512, 192))


def body_ring(
    block_input,
    cotangent,
    prefix_len,
    cluster_id,
    positions,
    step_count,
    master_qkv,
    first_qkv,
    second_qkv,
    master_out,
    first_out,
    second_out,
    master_gateup,
    first_gateup,
    second_gateup,
    master_down,
    first_down,
    second_down,
    master_norm,
    first_norm,
    second_norm,
):
    token_count = block_input.shape[0]
    protein_count = token_count // LEN
    share_rows = cotangent.shape[0]
    share_start = lax.axis_index("mp") * share_rows
    deep_alpha = math.sqrt(2.0 * DEPTH)

    low_qkv = master_qkv.astype(BF16)
    low_out = master_out.astype(BF16)
    low_gateup = jnp.swapaxes(master_gateup, 1, 2).astype(BF16)
    unit = low_gateup.shape[1] // 4
    low_units = [low_gateup[:, k * unit : (k + 1) * unit] for k in range(4)]
    low_down = master_down.astype(BF16)
    w_norm = lax.optimization_barrier(master_norm.astype(BF16)).astype(F32)

    queries, key_rows, value_rows, cos_table, sin_table, w_qkv = qkv_call(
        block_input, low_qkv, positions, share_rows
    )
    cos_table = cos_table.reshape(token_count, HEAD_DIM)
    sin_table = sin_table.reshape(token_count, HEAD_DIM)
    queries, key_rows, value_rows = (
        part.reshape(token_count, -1) for part in (queries, key_rows, value_rows)
    )
    attended, probs, w_out, unit_0 = attention_call(
        queries, key_rows, value_rows, prefix_len, low_out, low_units[0]
    )
    attn_share, unit_1, unit_2 = out_call(attended, w_out, low_units[1:3], share_rows)
    input_share = lax.dynamic_slice_in_dim(block_input, share_start, share_rows, 0).astype(F32)
    middle_share, normed_one, inv_one = norm_forward(
        deep_alpha * input_share + attn_share, w_norm[0], w_norm[1]
    )
    ffn_share, middle_low, hidden, act, pull, w_gateup, w_down = ffn_call(
        middle_share.astype(BF16), (unit_0, unit_1, unit_2), low_units[3], low_down
    )
    out_share, normed_two, inv_two = norm_forward(
        deep_alpha * middle_share + ffn_share, w_norm[2], w_norm[3]
    )
    block_output = out_share.astype(BF16)
    matches = (cluster_id[:, None] == cluster_id[None, :]).astype(F32)
    counts = jnp.sum(matches, axis=1)
    group_counts = lax.dynamic_slice_in_dim(
        counts, lax.axis_index("dp") * protein_count, protein_count, 0
    )
    row_protein = (share_start + jnp.arange(share_rows)) // LEN
    one_hot = (row_protein[:, None] == jnp.arange(protein_count)[None, :]).astype(F32)
    row_weight = jnp.sum(one_hot * (1.0 / group_counts)[None, :], axis=1)
    grad_output = cotangent.astype(F32) * row_weight[:, None]
    grad_h2, grad_gain_two, grad_bias_two = norm_backward(
        grad_output, normed_two, inv_two, w_norm[2]
    )
    ffn_grad, grad_gateup_rows = ffn_back_call(grad_h2.astype(BF16), act, pull, w_down)
    hidden = hidden.reshape(token_count, -1)
    middle_low = middle_low.reshape(token_count, D)
    ffn_grad = ffn_grad.reshape(token_count, D)
    gateup_rows = grad_gateup_rows.reshape(2, token_count, -1)
    grad_down_part = jnp.einsum("tf,td->fd", hidden, ffn_grad, preferred_element_type=F32).astype(BF16)
    grad_gateup_part = jnp.einsum(
        "jtf,td->jfd", gateup_rows, middle_low, preferred_element_type=F32
    ).astype(BF16)
    grad_down_part, grad_gateup_part, grad_gateup_rows = lax.optimization_barrier(
        (grad_down_part, grad_gateup_part, grad_gateup_rows)
    )
    middle_grad, red_down, red_gateup_0 = middle_back_call(
        grad_gateup_rows, w_gateup, grad_down_part, grad_gateup_part, SPANS[0], share_rows
    )
    middle_grad = middle_grad + deep_alpha * grad_h2
    grad_h1, grad_gain_one, grad_bias_one = norm_backward(
        middle_grad, normed_one, inv_one, w_norm[0]
    )
    attn_grad, grad_attended, red_gateup_1 = out_back_call(
        grad_h1.astype(BF16), w_out, grad_gateup_part, SPANS[1]
    )
    attn_grad = attn_grad.reshape(token_count, D)
    grad_attended = grad_attended.reshape(token_count, -1)
    grad_out_part = jnp.einsum("tc,td->cd", attended, attn_grad, preferred_element_type=F32).astype(BF16)
    grad_out_part, grad_attended = lax.optimization_barrier((grad_out_part, grad_attended))
    norm_terms = jnp.stack([grad_gain_one, grad_bias_one, grad_gain_two, grad_bias_two])
    grad_proj, grad_norm, red_gateup_2 = attention_back_call(
        queries,
        key_rows,
        value_rows,
        probs,
        attended,
        grad_attended,
        cos_table,
        sin_table,
        norm_terms,
        grad_gateup_part,
        SPANS[2],
    )
    red_gateup = jnp.swapaxes(
        jnp.concatenate([red_gateup_0, red_gateup_1, red_gateup_2], axis=1), 1, 2
    )
    grad_qkv_part = jnp.einsum("td,jtc->jdc", block_input, grad_proj, preferred_element_type=F32).astype(BF16)
    input_share_grad, red_qkv, red_out = input_back_call(
        grad_proj, w_qkv, grad_qkv_part, grad_out_part, share_rows
    )
    grad_input = (input_share_grad + deep_alpha * grad_h1).astype(BF16)

    step_value = step_count[0].astype(F32)
    rate_qkv = D ** (-0.5)
    rate_out = max(HEADS * HEAD_DIM // 512, 1) ** (-0.5)
    rate_gateup = D ** (-0.5)
    rate_down = max(FF // 64, 1) ** (-0.5)
    rate_norm = 1.0
    new_qkv, new_first_qkv, new_second_qkv = adamw_step(
        master_qkv, first_qkv, second_qkv, red_qkv, rate_qkv, step_value
    )
    new_out, new_first_out, new_second_out = adamw_step(
        master_out, first_out, second_out, red_out, rate_out, step_value
    )
    new_gateup, new_first_gateup, new_second_gateup = adamw_step(
        master_gateup, first_gateup, second_gateup, red_gateup, rate_gateup, step_value
    )
    new_down, new_first_down, new_second_down = adamw_step(
        master_down, first_down, second_down, red_down, rate_down, step_value
    )
    new_norm, new_first_norm, new_second_norm = adamw_step(
        master_norm, first_norm, second_norm, grad_norm, rate_norm, step_value
    )
    return (
        block_output,
        grad_input,
        red_qkv,
        new_qkv,
        new_first_qkv,
        new_second_qkv,
        red_out,
        new_out,
        new_first_out,
        new_second_out,
        red_gateup,
        new_gateup,
        new_first_gateup,
        new_second_gateup,
        red_down,
        new_down,
        new_first_down,
        new_second_down,
        grad_norm,
        new_norm,
        new_first_norm,
        new_second_norm,
    )


def solution(mesh):
    placed = (
        P("dp", None),
        P(("dp", "mp"), None),
        P("dp"),
        P(),
        P("dp"),
        P(),
        P(None, "dp", "mp"),
        P(None, "dp", "mp"),
        P(None, "dp", "mp"),
        P("mp", "dp"),
        P("mp", "dp"),
        P("mp", "dp"),
        P(None, "dp", "mp"),
        P(None, "dp", "mp"),
        P(None, "dp", "mp"),
        P("mp", "dp"),
        P("mp", "dp"),
        P("mp", "dp"),
        P(),
        P(),
        P(),
    )
    ring = mesh.shape["dp"] == 4 and mesh.shape["mp"] == 8
    return jax.shard_map(
        body_ring if ring else body_plain,
        mesh=mesh,
        in_specs=placed,
        out_specs=(
            P(("dp", "mp"), None),
            P(("dp", "mp"), None),
            P(None, "dp", "mp"),
            P(None, "dp", "mp"),
            P(None, "dp", "mp"),
            P(None, "dp", "mp"),
            P("mp", "dp"),
            P("mp", "dp"),
            P("mp", "dp"),
            P("mp", "dp"),
            P(None, "dp", "mp"),
            P(None, "dp", "mp"),
            P(None, "dp", "mp"),
            P(None, "dp", "mp"),
            P("mp", "dp"),
            P("mp", "dp"),
            P("mp", "dp"),
            P("mp", "dp"),
            P(),
            P(),
            P(),
            P(),
        ),
        check_vma=False,
    )
```

```python
import functools
import math

import jax
import jax.numpy as jnp
from jax import lax
from jax.experimental import pallas as pl
from jax.experimental.pallas import tpu as pltpu
from jax.sharding import PartitionSpec as P

D = 2048
HEADS = 16
HEAD_DIM = 128
FF = 5632
DEPTH = 24
LEN = 896


beta_one = 0.9
beta_two = 0.95
adam_epsilon = 1e-08
decay_weight = 0.1
norm_epsilon = 1e-05


def norm_forward(hidden_rows, gain, offset):
    centre = hidden_rows - jnp.mean(hidden_rows, axis=-1, keepdims=True)
    inv_std = lax.rsqrt(jnp.mean(centre * centre, axis=-1, keepdims=True) + norm_epsilon)
    normed = centre * inv_std
    return (normed * gain + offset, normed, inv_std)


def norm_backward(grad_rows, normed, inv_std, gain):
    grad_normed = grad_rows * gain
    first_term = jnp.mean(grad_normed, axis=-1, keepdims=True)
    second_term = jnp.mean(grad_normed * normed, axis=-1, keepdims=True)
    grad_hidden = inv_std * (grad_normed - first_term - normed * second_term)
    return (grad_hidden, jnp.sum(grad_rows * normed, axis=0), jnp.sum(grad_rows, axis=0))


def rotate_half(values):
    middle = values.shape[-1] // 2
    return jnp.concatenate([-values[..., middle:], values[..., :middle]], axis=-1)


def rotate_back(values):
    middle = values.shape[-1] // 2
    return jnp.concatenate([values[..., middle:], -values[..., :middle]], axis=-1)


def rope_tables(positions):
    ladder = jnp.arange(HEAD_DIM // 2, dtype=jnp.float32)
    inverse = jnp.exp(ladder * (-2.0 * math.log(10000.0) / HEAD_DIM))
    angles = positions.astype(jnp.float32)[:, None] * inverse[None, :]
    cos_half = jnp.cos(angles)
    sin_half = jnp.sin(angles)
    return (
        jnp.concatenate([cos_half, cos_half], axis=-1),
        jnp.concatenate([sin_half, sin_half], axis=-1),
    )


def apply_rope(values, cos_table, sin_table):
    return values * cos_table[:, None, :] + rotate_half(values) * sin_table[:, None, :]


def rope_back(grads, cos_table, sin_table):
    return grads * cos_table[:, None, :] + rotate_back(grads * sin_table[:, None, :])


def gelu_tanh(values):
    return jax.nn.gelu(values, approximate=True)


def adamw_step(old_master, old_first, old_second, grad_sum, learn_rate, step_value):
    first_new = beta_one * old_first + (1.0 - beta_one) * grad_sum
    second_new = beta_two * old_second + (1.0 - beta_two) * grad_sum * grad_sum
    fix_first = 1.0 - jnp.power(beta_one, step_value)
    fix_second = 1.0 - jnp.power(beta_two, step_value)
    update = (
        first_new / fix_first / (jnp.sqrt(second_new / fix_second) + adam_epsilon)
        + decay_weight * old_master
    )
    return (old_master - learn_rate * update, first_new, second_new)


def body_plain(
    block_input,
    cotangent,
    prefix_len,
    cluster_id,
    positions,
    step_count,
    master_qkv,
    first_qkv,
    second_qkv,
    master_out,
    first_out,
    second_out,
    master_gateup,
    first_gateup,
    second_gateup,
    master_down,
    first_down,
    second_down,
    master_norm,
    first_norm,
    second_norm,
):
    w_qkv, w_out, w_gateup, w_down = (
        lax.all_gather(master_qkv.astype(jnp.bfloat16), "dp", axis=1, tiled=True),
        lax.all_gather(master_out.astype(jnp.bfloat16), "dp", axis=1, tiled=True),
        lax.all_gather(master_gateup.astype(jnp.bfloat16), "dp", axis=1, tiled=True),
        lax.all_gather(master_down.astype(jnp.bfloat16), "dp", axis=1, tiled=True),
    )
    w_norm = lax.optimization_barrier(master_norm.astype(jnp.bfloat16)).astype(jnp.float32)
    token_count = block_input.shape[0]
    protein_count = token_count // LEN
    share_rows = cotangent.shape[0]
    share_start = lax.axis_index("mp") * share_rows
    head_count = w_qkv.shape[2] // HEAD_DIM
    width_heads = head_count * HEAD_DIM
    deep_alpha = math.sqrt(2.0 * DEPTH)
    score_scale = 1.0 / math.sqrt(HEAD_DIM)
    cos_table, sin_table = rope_tables(positions)
    projected = jnp.einsum("td,jdc->jtc", block_input, w_qkv, preferred_element_type=jnp.float32)
    shaped = projected.reshape(3, token_count, head_count, HEAD_DIM)
    queries = (apply_rope(shaped[0], cos_table, sin_table) * score_scale).astype(jnp.bfloat16)
    key_rows = apply_rope(shaped[1], cos_table, sin_table).astype(jnp.bfloat16)
    value_rows = shaped[2].astype(jnp.bfloat16)
    row_ids = jnp.arange(LEN)[:, None]
    col_ids = jnp.arange(LEN)[None, :]
    attended_parts = []
    log_totals = []
    for protein in range(protein_count):
        row_slice = slice(protein * LEN, (protein + 1) * LEN)
        visible = (col_ids < prefix_len[protein]) | (col_ids <= row_ids)
        scores = jnp.einsum(
            "qhd,khd->hqk",
            queries[row_slice],
            key_rows[row_slice],
            preferred_element_type=jnp.float32,
        )
        scores = jnp.where(visible[None], scores, -1e30)
        row_peak = jnp.max(scores, axis=-1, keepdims=True)
        expo_rows = jnp.exp(scores - row_peak)
        totals = jnp.sum(expo_rows, axis=-1, keepdims=True)
        attn_probs = (expo_rows / totals).astype(jnp.bfloat16)
        attended_parts.append(
            jnp.einsum(
                "hqk,khd->qhd",
                attn_probs,
                value_rows[row_slice],
                preferred_element_type=jnp.float32,
            )
        )
        log_totals.append(row_peak + jnp.log(totals))
    attended = (
        jnp.concatenate(attended_parts, axis=0)
        .reshape(token_count, width_heads)
        .astype(jnp.bfloat16)
    )
    attn_part = jnp.dot(attended, w_out, preferred_element_type=jnp.float32)
    input_share = lax.dynamic_slice_in_dim(block_input, share_start, share_rows, 0).astype(
        jnp.float32
    )
    attn_share = lax.psum_scatter(
        attn_part.astype(jnp.bfloat16), "mp", scatter_dimension=0, tiled=True
    ).astype(jnp.float32)
    middle_share, normed_one, inv_one = norm_forward(
        deep_alpha * input_share + attn_share, w_norm[0], w_norm[1]
    )
    middle_low = lax.all_gather(middle_share.astype(jnp.bfloat16), "mp", axis=0, tiled=True)
    gateup = jnp.einsum("td,jdf->jtf", middle_low, w_gateup, preferred_element_type=jnp.float32)
    gate_rows = gateup[0]
    up_rows = gateup[1]
    activated, gelu_pull = jax.vjp(gelu_tanh, gate_rows)
    hidden = (activated * up_rows).astype(jnp.bfloat16)
    ffn_part = jnp.dot(hidden, w_down, preferred_element_type=jnp.float32)
    ffn_share = lax.psum_scatter(
        ffn_part.astype(jnp.bfloat16), "mp", scatter_dimension=0, tiled=True
    ).astype(jnp.float32)
    out_share, normed_two, inv_two = norm_forward(
        deep_alpha * middle_share + ffn_share, w_norm[2], w_norm[3]
    )
    block_output = out_share.astype(jnp.bfloat16)
    matches = (cluster_id[:, None] == cluster_id[None, :]).astype(jnp.float32)
    counts = jnp.sum(matches, axis=1)
    group_counts = lax.dynamic_slice_in_dim(
        counts, lax.axis_index("dp") * protein_count, protein_count, 0
    )
    row_protein = (share_start + jnp.arange(share_rows)) // LEN
    one_hot = (row_protein[:, None] == jnp.arange(protein_count)[None, :]).astype(jnp.float32)
    row_weight = jnp.sum(one_hot * (1.0 / group_counts)[None, :], axis=1)
    grad_output = cotangent.astype(jnp.float32) * row_weight[:, None]
    grad_h2, grad_gain_two, grad_bias_two = norm_backward(
        grad_output, normed_two, inv_two, w_norm[2]
    )
    ffn_grad_full = lax.all_gather(grad_h2.astype(jnp.bfloat16), "mp", axis=0, tiled=True)
    grad_down_part = jnp.einsum(
        "tf,td->fd", hidden, ffn_grad_full, preferred_element_type=jnp.float32
    )
    grad_hidden = jnp.einsum("td,fd->tf", ffn_grad_full, w_down, preferred_element_type=jnp.float32)
    grad_gate = gelu_pull(grad_hidden * up_rows)[0]
    grad_up = grad_hidden * activated
    grad_gateup_rows = jnp.stack([grad_gate, grad_up]).astype(jnp.bfloat16)
    grad_gateup_part = jnp.einsum(
        "td,jtf->jdf", middle_low, grad_gateup_rows, preferred_element_type=jnp.float32
    )
    middle_grad_part = jnp.einsum(
        "jtf,jdf->td", grad_gateup_rows, w_gateup, preferred_element_type=jnp.float32
    )
    middle_grad = (
        lax.psum_scatter(
            middle_grad_part.astype(jnp.bfloat16), "mp", scatter_dimension=0, tiled=True
        ).astype(jnp.float32)
        + deep_alpha * grad_h2
    )
    grad_h1, grad_gain_one, grad_bias_one = norm_backward(
        middle_grad, normed_one, inv_one, w_norm[0]
    )
    attn_grad_full = lax.all_gather(grad_h1.astype(jnp.bfloat16), "mp", axis=0, tiled=True)
    grad_out_part = jnp.einsum(
        "tc,td->cd", attended, attn_grad_full, preferred_element_type=jnp.float32
    )
    grad_attended = (
        jnp.einsum("td,cd->tc", attn_grad_full, w_out, preferred_element_type=jnp.float32)
        .astype(jnp.bfloat16)
        .reshape(token_count, head_count, HEAD_DIM)
    )
    query_grads = []
    key_grads = []
    value_grads = []
    for protein in range(protein_count):
        row_slice = slice(protein * LEN, (protein + 1) * LEN)
        visible = (col_ids < prefix_len[protein]) | (col_ids <= row_ids)
        scores = jnp.einsum(
            "qhd,khd->hqk",
            queries[row_slice],
            key_rows[row_slice],
            preferred_element_type=jnp.float32,
        )
        scores = jnp.where(visible[None], scores, -1e30)
        probs_full = jnp.exp(scores - log_totals[protein])
        probs_low = probs_full.astype(jnp.bfloat16)
        grad_slice = grad_attended[row_slice]
        value_grads.append(
            jnp.einsum("hqk,qhd->khd", probs_low, grad_slice, preferred_element_type=jnp.float32)
        )
        prob_grads = jnp.einsum(
            "qhd,khd->hqk", grad_slice, value_rows[row_slice], preferred_element_type=jnp.float32
        )
        centre_term = jnp.sum(probs_full * prob_grads, axis=-1, keepdims=True)
        score_grads = (probs_full * (prob_grads - centre_term)).astype(jnp.bfloat16)
        query_grads.append(
            jnp.einsum(
                "hqk,khd->qhd", score_grads, key_rows[row_slice], preferred_element_type=jnp.float32
            )
        )
        key_grads.append(
            jnp.einsum(
                "hqk,qhd->khd", score_grads, queries[row_slice], preferred_element_type=jnp.float32
            )
        )
    grad_query = rope_back(jnp.concatenate(query_grads, axis=0), cos_table, sin_table) * score_scale
    grad_key = rope_back(jnp.concatenate(key_grads, axis=0), cos_table, sin_table)
    grad_value = jnp.concatenate(value_grads, axis=0)
    grad_proj = (
        jnp.stack([grad_query, grad_key, grad_value])
        .reshape(3, token_count, width_heads)
        .astype(jnp.bfloat16)
    )
    grad_qkv_part = jnp.einsum(
        "td,jtc->jdc", block_input, grad_proj, preferred_element_type=jnp.float32
    )
    input_grad_part = jnp.einsum(
        "jtc,jdc->td", grad_proj, w_qkv, preferred_element_type=jnp.float32
    )
    input_grad = (
        lax.psum_scatter(
            input_grad_part.astype(jnp.bfloat16), "mp", scatter_dimension=0, tiled=True
        ).astype(jnp.float32)
        + deep_alpha * grad_h1
    )
    grad_input = input_grad.astype(jnp.bfloat16)
    norm_terms = jnp.stack([grad_gain_one, grad_bias_one, grad_gain_two, grad_bias_two])
    grad_norm = lax.psum(norm_terms, ("dp", "mp"))
    red_qkv, red_out, red_gateup, red_down = (
        lax.psum_scatter(
            grad_qkv_part.astype(jnp.bfloat16), "dp", scatter_dimension=1, tiled=True
        ).astype(jnp.float32),
        lax.psum_scatter(
            grad_out_part.astype(jnp.bfloat16), "dp", scatter_dimension=1, tiled=True
        ).astype(jnp.float32),
        lax.psum_scatter(
            grad_gateup_part.astype(jnp.bfloat16), "dp", scatter_dimension=1, tiled=True
        ).astype(jnp.float32),
        lax.psum_scatter(
            grad_down_part.astype(jnp.bfloat16), "dp", scatter_dimension=1, tiled=True
        ).astype(jnp.float32),
    )
    step_value = step_count[0].astype(jnp.float32)
    rate_qkv = D ** (-0.5)
    rate_out = max(HEADS * HEAD_DIM // 512, 1) ** (-0.5)
    rate_gateup = D ** (-0.5)
    rate_down = max(FF // 64, 1) ** (-0.5)
    rate_norm = 1.0
    new_qkv, new_first_qkv, new_second_qkv = adamw_step(
        master_qkv, first_qkv, second_qkv, red_qkv, rate_qkv, step_value
    )
    new_out, new_first_out, new_second_out = adamw_step(
        master_out, first_out, second_out, red_out, rate_out, step_value
    )
    new_gateup, new_first_gateup, new_second_gateup = adamw_step(
        master_gateup, first_gateup, second_gateup, red_gateup, rate_gateup, step_value
    )
    new_down, new_first_down, new_second_down = adamw_step(
        master_down, first_down, second_down, red_down, rate_down, step_value
    )
    new_norm, new_first_norm, new_second_norm = adamw_step(
        master_norm, first_norm, second_norm, grad_norm, rate_norm, step_value
    )
    return (
        block_output,
        grad_input,
        red_qkv,
        new_qkv,
        new_first_qkv,
        new_second_qkv,
        red_out,
        new_out,
        new_first_out,
        new_second_out,
        red_gateup,
        new_gateup,
        new_first_gateup,
        new_second_gateup,
        red_down,
        new_down,
        new_first_down,
        new_second_down,
        grad_norm,
        new_norm,
        new_first_norm,
        new_second_norm,
    )


MESH = pl.DeviceIdType.MESH
VMEM_BYTES = 61 * 1024 * 1024
BF16 = jnp.bfloat16
F32 = jnp.float32
NT = (((1,), (1,)), ((), ()))
ANY = pl.BlockSpec(memory_space=pl.ANY)
VM = pl.BlockSpec(memory_space=pltpu.VMEM)


LIGHT = pl.CostEstimate(flops=1 << 20, bytes_accessed=1 << 16, transcendentals=0)


def nt_dot(left, right):
    return lax.dot_general(left, right, NT, preferred_element_type=F32)


class Ring:
    def __init__(self, send, recv, local):
        self.here = lax.axis_index("dp")
        self.right = (self.here + 1) % 4
        self.left = (self.here + 3) % 4
        self.far = (self.here + 2) % 4
        self.send, self.recv, self.local = send, recv, local

    def copy(self, k, src, dst, other):
        return pltpu.make_async_remote_copy(
            src_ref=src,
            dst_ref=dst,
            send_sem=self.send.at[k],
            recv_sem=self.recv.at[k],
            device_id={"dp": other},
            device_id_type=MESH,
        )


class RingGather:
    def __init__(self, ring, first, half_of, place):
        self.plus_0 = ring.copy(first, half_of(0), place(ring.here, 0), ring.right)
        self.minus_1 = ring.copy(first + 1, half_of(1), place(ring.here, 1), ring.left)
        self.plus_1 = ring.copy(first + 2, half_of(1), place(ring.here, 1), ring.right)
        self.minus_0 = ring.copy(first + 3, half_of(0), place(ring.here, 0), ring.left)
        self.far_0 = ring.copy(first + 4, place(ring.left, 0), place(ring.left, 0), ring.right)
        self.far_1 = ring.copy(first + 5, place(ring.right, 1), place(ring.right, 1), ring.left)
        self.own = [
            pltpu.make_async_copy(half_of(h), place(ring.here, h), ring.local.at[first + h])
            for h in range(2)
        ]
        self.remote = (self.plus_0, self.minus_1, self.plus_1, self.minus_0, self.far_0, self.far_1)

    def start(self):
        for copy in self.remote[:4]:
            copy.start()
        for copy in self.own:
            copy.start()

    def forward(self):
        self.plus_0.wait_recv()
        self.far_0.start()
        self.minus_1.wait_recv()
        self.far_1.start()

    def near(self):
        self.plus_1.wait_recv()
        self.minus_0.wait_recv()

    def far(self):
        self.far_0.wait_recv()
        self.far_1.wait_recv()

    def drain(self):
        for copy in self.remote:
            copy.wait_send()

    def finish(self):
        for copy in self.own:
            copy.wait()
        self.near()
        self.far()
        self.drain()


class RingScatter:
    def __init__(self, ring, first, half_at, buf, out):
        self.buf, self.out = buf, out
        self.plus_far = ring.copy(first, half_at(ring.far, 0), buf.at[0], ring.right)
        self.minus_far = ring.copy(first + 1, half_at(ring.far, 1), buf.at[1], ring.left)
        self.plus_near = ring.copy(first + 2, half_at(ring.right, 1), buf.at[2], ring.right)
        self.minus_near = ring.copy(first + 3, half_at(ring.left, 0), buf.at[3], ring.left)
        self.plus_sum = ring.copy(first + 4, buf.at[6], buf.at[4], ring.right)
        self.minus_sum = ring.copy(first + 5, buf.at[7], buf.at[5], ring.left)
        places = ((ring.right, 0), (ring.left, 1), (ring.here, 0), (ring.here, 1))
        self.loads = [
            pltpu.make_async_copy(half_at(*place), buf.at[6 + k], ring.local.at[first + k])
            for k, place in enumerate(places)
        ]
        self.remote = (
            self.plus_far,
            self.minus_far,
            self.plus_near,
            self.minus_near,
            self.plus_sum,
            self.minus_sum,
        )

    def start(self):
        for copy in self.remote[:4]:
            copy.start()
        for copy in self.loads:
            copy.start()

    def forward(self):
        for copy in self.loads:
            copy.wait()
        self.plus_far.wait_recv()
        for_rows(self.buf.shape[1:], lambda at: add_at(self.buf, 6, 0, at))
        self.plus_sum.start()
        self.minus_far.wait_recv()
        for_rows(self.buf.shape[1:], lambda at: add_at(self.buf, 7, 1, at))
        self.minus_sum.start()

    def finish(self):
        for copy in self.remote[2:]:
            copy.wait_recv()
        buf = self.buf
        for half, terms in enumerate(((8, 3, 4), (9, 2, 5))):
            out = self.out(half)

            def total(at, out=out, terms=terms):
                out[at] = sum(buf[(k,) + at].astype(F32) for k in terms)

            for_rows(buf.shape[1:], total)
        for copy in self.remote:
            copy.wait_send()


def add_at(buf, dst, src, at):
    buf[(dst,) + at] = (buf[(dst,) + at].astype(F32) + buf[(src,) + at].astype(F32)).astype(BF16)


def for_rows(shape, visit):
    def step(i, carry):
        rows = pl.ds(pl.multiple_of(i * 16, 16), 16)
        if len(shape) == 2:
            visit((rows, slice(None)))
        else:
            for j in range(shape[0]):
                visit((j, rows, slice(None)))
        return carry

    lax.fori_loop(0, shape[-2] // 16, step, 0)


def ring_sems(count):
    return [pltpu.SemaphoreType.DMA((count,)) for _ in range(3)]


def row_halves(depth):
    half = depth // 2

    def place(ref):
        def at(owner, part):
            return ref.at[:, pl.ds(pl.multiple_of(owner * depth + part * half, half), half), :]

        return at

    return place


def plane_columns(depth):
    def place(ref):
        def at(owner, part):
            return ref.at[part, :, pl.ds(pl.multiple_of(owner * depth, depth), depth)]

        return at

    return place


def column_halves(depth):
    def place(ref):
        half = ref.shape[0] // 2

        def at(owner, part):
            columns = pl.ds(pl.multiple_of(owner * depth, depth), depth)
            return ref.at[pl.ds(part * half, half), columns]

        return at

    return place


def span_scatter(ring, first, ref, span, buf, out):
    at = plane_columns(ref.shape[2] // 4)(ref.at[:, pl.ds(*span), :])
    return RingScatter(ring, first, at, buf, lambda h: out.at[h])


def greet(others):
    sem = pltpu.get_barrier_semaphore()
    for other in others:
        pl.semaphore_signal(sem, inc=1, device_id=other, device_id_type=MESH)
    pl.semaphore_wait(sem, len(others))


class Square:
    def __init__(self, send, recv, rows):
        me = lax.axis_index("mp")
        self.core = me % 2
        self.x = (me // 2) % 2
        self.y = me // 4
        self.xn = (self.y * 2 + (1 - self.x)) * 2 + self.core
        self.yn = ((1 - self.y) * 2 + self.x) * 2 + self.core
        self.peer = (self.y * 2 + self.x) * 2 + (1 - self.core)
        self.own = self.y * 2 + self.x
        self.xc = self.y * 2 + (1 - self.x)
        self.yc = (1 - self.y) * 2 + self.x
        self.dc = (1 - self.y) * 2 + (1 - self.x)
        self.send, self.recv = send, recv
        cut = rows // 2 // 16 * 16
        self.rows = rows
        self.a = pl.ds(0, cut)
        self.b = pl.ds(cut, rows - cut)
        self.na, self.nb, self.cut = cut, rows - cut, cut

        self.others = [{"mp": self.xn}, {"mp": self.yn}, {"mp": self.peer}]

    def copy(self, k, src, dst, other):
        return pltpu.make_async_remote_copy(
            src_ref=src,
            dst_ref=dst,
            send_sem=self.send.at[k],
            recv_sem=self.recv.at[k],
            device_id={"mp": other},
            device_id_type=MESH,
        )


def add_rows(dst, src, count):
    def step(i, carry):
        rows = pl.ds(pl.multiple_of(i * 16, 16), 16)
        dst[rows, :] = (dst[rows, :].astype(F32) + src[rows, :].astype(F32)).astype(BF16)
        return carry

    lax.fori_loop(0, count // 16, step, 0)


def nothing():
    pass


def square_kernel(
    rows,
    sems,
    gather=None,
    scatter=None,
    ring=None,
    start=nothing,
    first=nothing,
    early=nothing,
    later=nothing,
    between=nothing,
    middle=nothing,
    end=nothing,
    near_first=False,
):
    send, recv, lsem = sems
    sq = Square(send, recv, rows)
    core = sq.core
    greet(sq.others + ([{"dp": ring.left}, {"dp": ring.right}] if ring is not None else []))

    def place(rel, turn):
        chip_y = (sq.y + rel % 2) % 2
        chip_x = (sq.x + ((rel + 1) // 2) % 2) % 2
        return chip_y * 2 + chip_x, (1 - core + turn) % 2

    if gather is not None:
        compute, share, full, gbuf = gather
        c_own = sq.copy(0, share, gbuf.at[sq.own, core], sq.peer)
        x_a = sq.copy(1, share.at[sq.a], gbuf.at[sq.own, core, sq.a], sq.xn)
        y_b = sq.copy(2, share.at[sq.b], gbuf.at[sq.own, core, sq.b], sq.yn)
        f_x = sq.copy(3, gbuf.at[sq.yc, core, sq.b], gbuf.at[sq.yc, core, sq.b], sq.xn)
        f_y = sq.copy(4, gbuf.at[sq.xc, core, sq.a], gbuf.at[sq.xc, core, sq.a], sq.yn)
        x_b = sq.copy(5, share.at[sq.b], gbuf.at[sq.own, core, sq.b], sq.xn)
        y_a = sq.copy(6, share.at[sq.a], gbuf.at[sq.own, core, sq.a], sq.yn)
        c_d = sq.copy(7, gbuf.at[sq.dc, core], gbuf.at[sq.dc, core], sq.peer)
        c_x = sq.copy(8, gbuf.at[sq.xc, core], gbuf.at[sq.xc, core], sq.peer)
        c_y = sq.copy(9, gbuf.at[sq.yc, core], gbuf.at[sq.yc, core], sq.peer)
        local = pltpu.make_async_copy(share, gbuf.at[sq.own, core], lsem.at[8])
        x_a.start()
        y_b.start()
        if near_first:
            x_b.start()
            y_a.start()
        c_own.start()
        local.start()
    start()
    if gather is not None:

        def take_own():
            c_own.wait_recv()
            local.wait()
            first()

        def forward():
            x_a.wait_recv()
            y_b.wait_recv()
            f_x.start()
            f_y.start()
            if not near_first:
                x_b.start()
                y_a.start()
            early()

        def take_far():
            f_x.wait_recv()
            f_y.wait_recv()
            c_d.start()
            c_d.wait_recv()

        def take_near():
            x_b.wait_recv()
            y_a.wait_recv()
            c_x.start()
            c_y.start()
            later()
            c_x.wait_recv()
            c_y.wait_recv()

        def gather_step(t, carry):
            unit = t // 2
            if near_first:
                chip_y = (sq.y + unit // 2) % 2
                chip_x = (sq.x + unit % 2) % 2
                chip, which = chip_y * 2 + chip_x, (1 - core + t % 2) % 2
            else:
                chip, which = place(unit, t % 2)

            pl.when(t == 0)(take_own)

            @pl.when(t == 2)
            def _():
                forward()
                if near_first:
                    take_near()
                else:
                    take_far()

            pl.when(t == (6 if near_first else 4))(take_far if near_first else take_near)

            if full is not None:
                pltpu.make_async_copy(gbuf.at[chip, which], full.at[chip, which], lsem.at[t]).start()
            compute(t, chip, which)
            return carry

        lax.fori_loop(0, 8 if scatter is None else 6, gather_step, 0)
    between()
    if scatter is not None:
        finish_tile, pbuf, (rcore, rxd, ryd, rx, ry), out = scatter
        x_d = sq.copy(14, pbuf.at[sq.dc, core, sq.a], rxd, sq.xn)
        y_d = sq.copy(15, pbuf.at[sq.dc, core, sq.b], ryd, sq.yn)
        x_ra = sq.copy(16, pbuf.at[sq.xc, core, sq.a], rx.at[sq.a], sq.xn)
        y_rb = sq.copy(17, pbuf.at[sq.yc, core, sq.b], ry.at[sq.b], sq.yn)
        x_rb = sq.copy(18, pbuf.at[sq.xc, core, sq.b], rx.at[sq.b], sq.xn)
        y_ra = sq.copy(19, pbuf.at[sq.yc, core, sq.a], ry.at[sq.a], sq.yn)

        def scatter_step(t, carry):
            turn = t % 2
            rel = (t // 2 + 1) % 4
            chip, which = place(rel, turn)
            finish_tile(t, chip, which)
            to_peer = sq.copy(10 + rel, pbuf.at[chip, which], rcore.at[chip], sq.peer)

            @pl.when(turn == 0)
            def _():
                to_peer.start()

            @pl.when(turn == 1)
            def _():
                to_peer.wait_recv()
                add_rows(pbuf.at[chip, which], rcore.at[chip], rows)

            @pl.when(t == 1)
            def _():
                x_d.start()
                y_d.start()

            @pl.when(t == 3)
            def _():
                x_ra.start()

            @pl.when(t == 5)
            def _():
                y_rb.start()

            return carry

        if gather is None:
            lax.fori_loop(0, 8, scatter_step, 0)
        else:
            lax.fori_loop(0, 2, scatter_step, 0)
            lax.fori_loop(6, 8, gather_step, 0)
            lax.fori_loop(2, 8, scatter_step, 0)
        x_d.wait_recv()
        add_rows(pbuf.at[sq.yc, core, sq.a], rxd, sq.na)
        y_ra.start()
        y_d.wait_recv()
        add_rows(pbuf.at[sq.xc, core, sq.b], ryd, sq.nb)
        x_rb.start()
        middle()
        x_ra.wait_recv()
        y_rb.wait_recv()
        y_ra.wait_recv()
        x_rb.wait_recv()

        def last(i, carry):
            part = pl.ds(pl.multiple_of(i * 16, 16), 16)
            out[part, :] = (
                pbuf[sq.own, core, part, :].astype(F32)
                + rx[part, :].astype(F32)
                + ry[part, :].astype(F32)
            )
            return carry

        lax.fori_loop(0, rows // 16, last, 0)
        for k in range(4):
            sq.copy(10 + k, pbuf.at[0, 0], rcore.at[0], sq.peer).wait_send()
        for copy in (x_d, y_d, x_ra, y_rb, x_rb, y_ra):
            copy.wait_send()
    end()
    if gather is not None:
        for copy in (c_own, x_a, y_b, f_x, f_y, x_b, y_a, c_d, c_x, c_y):
            copy.wait_send()
        if full is not None:
            for t in range(8):
                pltpu.make_async_copy(gbuf.at[0, 0], full.at[0, 0], lsem.at[t]).wait()


def scatter_scratch(rows, width):
    cut = rows // 2 // 16 * 16
    return [
        pltpu.VMEM((4, 2, rows, width), BF16),
        pltpu.VMEM((4, rows, width), BF16),
        pltpu.VMEM((cut, width), BF16),
        pltpu.VMEM((rows - cut, width), BF16),
        pltpu.VMEM((rows, width), BF16),
        pltpu.VMEM((rows, width), BF16),
    ]


SEMS = [
    pltpu.SemaphoreType.DMA((20,)),
    pltpu.SemaphoreType.DMA((20,)),
    pltpu.SemaphoreType.DMA((9,)),
]


def params(collective_id):
    return pltpu.CompilerParams(
        collective_id=collective_id, has_side_effects=True, vmem_limit_bytes=VMEM_BYTES
    )


def whole(shape):
    return pl.BlockSpec(shape, lambda *_: (0,) * len(shape))


def qkv_call(block_input, low_qkv, low_out, positions, rows):
    tokens, width = block_input.shape
    depth, cols = low_qkv.shape[1:]
    tiles = tokens // rows
    heads = cols // HEAD_DIM
    scale = 1.0 / math.sqrt(HEAD_DIM)
    half = depth // 2

    def kernel(
        x_ref, low_ref, lo_ref, pos_ref, q_ref, k_ref, v_ref, cos_ref, sin_ref, w_ref, wo_ref,
        x_buf, w_buf, acc, xsem, osem, send, recv, local,
    ):
        ring = Ring(send, recv, local)
        gather = RingGather(
            ring, 0, lambda h: low_ref.at[:, pl.ds(h * half, half), :], row_halves(depth)(w_buf)
        )

        out_half = lo_ref.shape[0] // 2
        gather_out = RingGather(
            ring, 6, lambda h: lo_ref.at[pl.ds(h * out_half, out_half), :], column_halves(depth)(wo_ref)
        )

        def x_copy(t, k):
            return pltpu.make_async_copy(
                x_ref.at[t, :, pl.ds(k * depth, depth)], x_buf.at[t, k], xsem.at[t, k]
            )

        def start_tile(t, carry):
            for k in range(4):
                x_copy(t, k).start()
            return carry

        lax.fori_loop(0, tiles, start_tile, 0)
        greet([{"dp": ring.left}, {"dp": ring.right}])
        gather.start()
        for copy in gather.own:
            copy.wait()

        def part(t, j, owner):
            depths = pl.ds(pl.multiple_of(owner * depth, depth), depth)
            return jnp.dot(x_buf[t, owner], w_buf[j, depths, :], preferred_element_type=F32)

        def own_tile(t, carry):
            for k in range(4):
                x_copy(t, k).wait()
            for j in range(3):
                acc[t, j] = part(t, j, ring.here)
            return carry

        lax.fori_loop(0, tiles, own_tile, 0)
        lane = lax.broadcasted_iota(jnp.int32, (1, HEAD_DIM), 1)
        ladder = (lane % (HEAD_DIM // 2)).astype(F32)
        inverse = jnp.exp(ladder * (-2.0 * math.log(10000.0) / HEAD_DIM))
        sign = jnp.where(lane < HEAD_DIM // 2, -1.0, 1.0)

        def table_tile(t, carry):
            angles = pos_ref[t].astype(F32) * inverse
            cos_ref[t] = jnp.cos(angles)
            sin_ref[t] = jnp.sin(angles) * sign
            return carry

        lax.fori_loop(0, tiles // 2, table_tile, 0)
        gather.forward()
        gather_out.start()
        lax.fori_loop(tiles // 2, tiles, table_tile, 0)
        gather.near()

        def near_tile(t, carry):
            for j in range(3):
                acc[t, j] += part(t, j, ring.left) + part(t, j, ring.right)
            return carry

        lax.fori_loop(0, tiles, near_tile, 0)
        gather.far()
        keep = pltpu.make_async_copy(w_buf, w_ref, osem.at[0])
        keep.start()

        def far_tile(t, carry):
            for j, ref in enumerate((q_ref, k_ref)):
                a = acc[t, j] + part(t, j, ring.far)
                for h in range(heads):
                    cut = slice(h * HEAD_DIM, (h + 1) * HEAD_DIM)
                    turned = a[:, cut] * cos_ref[t] + pltpu.roll(a[:, cut], HEAD_DIM // 2, 1) * sin_ref[t]
                    if j == 0:
                        turned = turned * scale
                    ref[t, :, cut] = turned.astype(BF16)
            v_ref[t] = (acc[t, 2] + part(t, 2, ring.far)).astype(BF16)
            return carry

        lax.fori_loop(0, tiles, far_tile, 0)
        gather_out.forward()
        keep.wait()
        gather.drain()
        gather_out.finish()

    tile = jax.ShapeDtypeStruct((tiles, rows, cols), BF16)
    return pl.pallas_call(
        kernel,
        out_shape=[tile] * 3
        + [jax.ShapeDtypeStruct((tiles, rows, HEAD_DIM), F32)] * 2
        + [jax.ShapeDtypeStruct((3, width, cols), BF16), jax.ShapeDtypeStruct((cols, 4 * depth), BF16)],
        in_specs=[ANY, ANY, ANY, VM],
        out_specs=[VM] * 5 + [ANY, ANY],
        scratch_shapes=[
            pltpu.VMEM((tiles, 4, rows, depth), BF16),
            pltpu.VMEM((3, width, cols), BF16),
            pltpu.VMEM((tiles, 3, rows, cols), F32),
            pltpu.SemaphoreType.DMA((tiles, 4)),
            pltpu.SemaphoreType.DMA((1,)),
        ]
        + ring_sems(12),
        compiler_params=params(5),
        cost_estimate=LIGHT,
        name="qkv",
    )(
        block_input.reshape(tiles, rows, width),
        low_qkv,
        low_out,
        positions.reshape(tiles, rows, 1),
    )


BLOCK = 128


def attention_call(queries, key_rows, value_rows, prefix_len, low_unit):
    tokens, cols = queries.shape
    proteins = tokens // LEN
    heads = cols // HEAD_DIM
    depth = low_unit.shape[2]
    last = proteins * heads - 1

    def kernel(pre_ref, q_ref, k_ref, v_ref, lu_ref, o_ref, p_ref, wu_ref, send, recv, local):
        prefix = pre_ref[pl.program_id(0)]
        step = pl.program_id(0) * heads + pl.program_id(1)
        ring = Ring(send, recv, local)
        gather = RingGather(ring, 0, lambda h: lu_ref.at[h], plane_columns(depth)(wu_ref))

        @pl.when(step == 0)
        def _():
            greet([{"dp": ring.left}, {"dp": ring.right}])
            gather.start()

        for i in range(LEN // BLOCK):
            rows = slice(i * BLOCK, (i + 1) * BLOCK)
            s = nt_dot(q_ref[rows, :], k_ref[...])
            col = lax.broadcasted_iota(jnp.int32, s.shape, 1)
            row = lax.broadcasted_iota(jnp.int32, (BLOCK, 1), 0) + i * BLOCK
            s = jnp.where(col < jnp.maximum(prefix, row + 1), s, -1e30)
            e = jnp.exp(s - jnp.max(s, axis=-1, keepdims=True))
            p = (e * (1.0 / jnp.sum(e, axis=-1, keepdims=True))).astype(BF16)
            p_ref[0, 0, rows, :] = p
            o_ref[rows, :] = jnp.dot(p, v_ref[...], preferred_element_type=F32).astype(BF16)

        @pl.when(step == last - 1)
        def _():
            gather.forward()

        @pl.when(step == last)
        def _():
            gather.finish()

    tile = pl.BlockSpec((LEN, HEAD_DIM), lambda p, h, *_: (p, h))
    return pl.pallas_call(
        kernel,
        grid_spec=pltpu.PrefetchScalarGridSpec(
            num_scalar_prefetch=1,
            grid=(proteins, heads),
            in_specs=[tile] * 3 + [ANY],
            out_specs=[tile, pl.BlockSpec((1, 1, LEN, LEN), lambda p, h, *_: (p, h, 0, 0)), ANY],
            scratch_shapes=ring_sems(6),
        ),
        out_shape=[
            jax.ShapeDtypeStruct((tokens, cols), BF16),
            jax.ShapeDtypeStruct((proteins, heads, LEN, LEN), BF16),
            jax.ShapeDtypeStruct(low_unit.shape[:2] + (4 * depth,), BF16),
        ],
        compiler_params=params(6),
        cost_estimate=LIGHT,
        name="attention",
    )(prefix_len, queries, key_rows, value_rows, low_unit)


TN = (((0,), (0,)), ((), ()))


def attention_back_call(
    queries, key_rows, value_rows, probs, attended, grad_attended, cos_table, sin_table, norm_terms,
    grad_out_part, grad_gateup_part, span,
):
    tokens, cols = queries.shape
    proteins = tokens // LEN
    heads = cols // HEAD_DIM
    scale = 1.0 / math.sqrt(HEAD_DIM)
    last = proteins * heads - 1
    depth = grad_gateup_part.shape[2] // 4

    def kernel(
        q_ref, k_ref, v_ref, p_ref, o_ref, do_ref, cos_ref, sin_ref, nt_ref, go_ref, gg_ref,
        da_ref, norm_ref, red_o, red_g,
        dk_acc, dv_acc, sums, got, nsend, nrecv, buf_o, buf_g, send, recv, local,
    ):
        step = pl.program_id(0) * heads + pl.program_id(1)
        ring = Ring(send, recv, local)
        part = cols // 2
        sides = (
            span_scatter(ring, 0, gg_ref, span, buf_g, red_g),
            RingScatter(
                ring, 6, column_halves(depth)(go_ref), buf_o, lambda h: red_o.at[pl.ds(h * part, part), :]
            ),
        )
        sq = Square(nsend, nrecv, 32)
        partners = [
            {"mp": sq.peer},
            {"mp": sq.xn},
            {"mp": sq.yn},
            {"dp": ring.here + 1 - 2 * (ring.here % 2)},
            {"dp": 3 - ring.here},
        ]
        swaps = [
            pltpu.make_async_remote_copy(
                src_ref=sums.at[k],
                dst_ref=got.at[k],
                send_sem=nsend.at[k],
                recv_sem=nrecv.at[k],
                device_id=other,
                device_id_type=MESH,
            )
            for k, other in enumerate(partners)
        ]

        @pl.when(step == 0)
        def _():
            sums[0] = nt_ref[...]
            greet(sq.others + [{"dp": ring.left}, {"dp": ring.right}])
            for side in sides:
                side.start()
            swaps[0].start()

        for k in range(5):

            @pl.when(step == k + 1)
            def _():
                swaps[k].wait()
                if k < 4:
                    sums[k + 1] = sums[k] + got[k]
                    swaps[k + 1].start()
                else:
                    norm_ref[...] = sums[k] + got[k]

        @pl.when(step == last - 1)
        def _():
            for side in sides:
                side.forward()

        for i in range(LEN // BLOCK):
            rows = slice(i * BLOCK, (i + 1) * BLOCK)
            do = do_ref[rows, :]
            p = p_ref[0, 0, rows, :]
            delta = jnp.sum(do.astype(F32) * o_ref[rows, :].astype(F32), axis=-1, keepdims=True)
            dp = nt_dot(do, v_ref[...])
            ds = (p.astype(F32) * (dp - delta)).astype(BF16)
            dv = lax.dot_general(p, do, TN, preferred_element_type=F32)
            dk = lax.dot_general(ds, q_ref[rows, :], TN, preferred_element_type=F32)
            if i == 0:
                dv_acc[...] = dv
                dk_acc[...] = dk
            else:
                dv_acc[...] += dv
                dk_acc[...] += dk
            dq = jnp.dot(ds, k_ref[...], preferred_element_type=F32)
            turned = dq * cos_ref[rows, :] - pltpu.roll(dq, HEAD_DIM // 2, 1) * sin_ref[rows, :]
            da_ref[0, rows, :] = (turned * scale).astype(BF16)
        dk = dk_acc[...]
        turned = dk * cos_ref[...] - pltpu.roll(dk, HEAD_DIM // 2, 1) * sin_ref[...]
        da_ref[1] = turned.astype(BF16)
        da_ref[2] = dv_acc[...].astype(BF16)

        @pl.when(step == last)
        def _():
            for side in sides:
                side.finish()

    tile = pl.BlockSpec((LEN, HEAD_DIM), lambda p, h: (p, h))
    table = pl.BlockSpec((LEN, HEAD_DIM), lambda p, h: (p, 0))
    return pl.pallas_call(
        kernel,
        grid=(proteins, heads),
        in_specs=[tile] * 3
        + [pl.BlockSpec((1, 1, LEN, LEN), lambda p, h: (p, h, 0, 0)), tile, tile, table, table]
        + [whole(norm_terms.shape), ANY, ANY],
        out_specs=[
            pl.BlockSpec((3, LEN, HEAD_DIM), lambda p, h: (0, p, h)),
            whole(norm_terms.shape),
            whole((cols, depth)),
            whole((2, span[1], depth)),
        ],
        out_shape=[
            jax.ShapeDtypeStruct((3, tokens, cols), BF16),
            jax.ShapeDtypeStruct(norm_terms.shape, F32),
            jax.ShapeDtypeStruct((cols, depth), F32),
            jax.ShapeDtypeStruct((2, span[1], depth), F32),
        ],
        scratch_shapes=[
            pltpu.VMEM((LEN, HEAD_DIM), F32),
            pltpu.VMEM((LEN, HEAD_DIM), F32),
            pltpu.VMEM((5,) + norm_terms.shape, F32),
            pltpu.VMEM((5,) + norm_terms.shape, F32),
            pltpu.SemaphoreType.DMA((5,)),
            pltpu.SemaphoreType.DMA((5,)),
            pltpu.VMEM((10, cols // 2, depth), BF16),
            pltpu.VMEM((10, span[1], depth), BF16),
        ]
        + ring_sems(12),
        compiler_params=params(7),
        cost_estimate=LIGHT,
        name="attention_back",
    )(
        queries,
        key_rows,
        value_rows,
        probs,
        attended,
        grad_attended,
        cos_table,
        sin_table,
        norm_terms,
        grad_out_part,
        grad_gateup_part,
    )


def out_call(attended, w_out, low_units, rows):
    cols = attended.shape[1]
    count = len(low_units)
    depth = low_units[0].shape[2]

    def kernel(o_ref, w_ref, *rest):
        low_refs, (out, *unit_refs), rest = rest[:count], rest[count : 2 * count + 1], rest[2 * count + 1 :]
        w_buf, pbuf, rcore, rxd, ryd, rx, ry, wsem, send, recv, lsem, zsend, zrecv, zlocal = rest
        ring = Ring(zsend, zrecv, zlocal)
        gathers = [
            RingGather(ring, 6 * k, lambda h, low=low: low.at[h], plane_columns(depth)(unit))
            for k, (low, unit) in enumerate(zip(low_refs, unit_refs))
        ]
        weight = pltpu.make_async_copy(w_ref, w_buf, wsem.at[0])
        weight.start()

        def start():
            gathers[0].start()
            weight.wait()

        def between():
            gathers[0].forward()
            for gather in gathers[1:]:
                gather.start()

        def middle():
            for gather in gathers[1:]:
                gather.forward()

        def end():
            for gather in gathers:
                gather.finish()

        def compute(t, chip, which):
            part = jnp.dot(o_ref[chip, which], w_buf[...], preferred_element_type=F32)
            pbuf[chip, which] = part.astype(BF16)

        square_kernel(
            rows,
            (send, recv, lsem),
            scatter=(compute, pbuf, (rcore, rxd, ryd, rx, ry), out),
            ring=ring,
            start=start,
            between=nothing,
            middle=lambda: (between(), middle()),
            end=end,
        )

    return pl.pallas_call(
        kernel,
        out_shape=[jax.ShapeDtypeStruct((rows, D), F32)]
        + [jax.ShapeDtypeStruct(low.shape[:2] + (D,), BF16) for low in low_units],
        in_specs=[VM, ANY] + [ANY] * count,
        out_specs=[VM] + [ANY] * count,
        scratch_shapes=[pltpu.VMEM((cols, D), BF16)]
        + scatter_scratch(rows, D)
        + [pltpu.SemaphoreType.DMA((1,))]
        + SEMS
        + ring_sems(6 * count),
        compiler_params=params(0),
        cost_estimate=LIGHT,
        name="out_reduce",
    )(attended.reshape(4, 2, rows, cols), w_out, *low_units)


def ffn_call(middle_low, units, low_down):
    rows = middle_low.shape[0]
    live, depth = low_down.shape
    count = len(units)
    curve = math.sqrt(2.0 / math.pi)

    def kernel(share, ld_ref, *rest):
        unit_refs, rest = rest[:count], rest[count:]
        out, full, hid_ref, act_ref, pull_ref, wg_ref, wd_ref = rest[:7]
        (w_g, w_d, gbuf, hid_buf, stage, pbuf, rcore, rxd, ryd, rx, ry) = rest[7:18]
        wsem, osem, hsem, send, recv, lsem, zsend, zrecv, zlocal = rest[18:]
        ring = Ring(zsend, zrecv, zlocal)
        half = live // 2
        gather_d = RingGather(ring, 0, lambda h: ld_ref.at[pl.ds(h * half, half), :], column_halves(depth)(w_d))
        copies = []
        offset = 0
        for k, ref in enumerate(unit_refs):
            size = ref.shape[1]
            copies.append(pltpu.make_async_copy(ref, w_g.at[:, pl.ds(offset, size), :], wsem.at[k]))
            offset += size
        for copy in copies:
            copy.start()
        keep_g = pltpu.make_async_copy(w_g, wg_ref, wsem.at[count])
        keep_d = pltpu.make_async_copy(w_d, wd_ref, wsem.at[count + 1])
        outs = (act_ref, pull_ref)

        def first():
            for copy in copies:
                copy.wait()
            keep_g.start()

        def between():
            for copy in gather_d.own:
                copy.wait()
            gather_d.near()
            gather_d.far()
            keep_d.start()

        def compute(t, chip, which):
            slot = t % 2

            @pl.when(t >= 2)
            def _():
                for k, ref in enumerate(outs):
                    pltpu.make_async_copy(stage.at[slot, k], ref.at[chip, which], osem.at[slot, k]).wait()

            tile = gbuf[chip, which]
            gate = nt_dot(tile, w_g[0])
            up = nt_dot(tile, w_g[1])
            square = gate * gate
            bent = jnp.tanh(curve * gate * (1.0 + 0.044715 * square))
            half = 0.5 * (1.0 + bent)
            act = gate * half
            slope = half + 0.5 * curve * gate * (1.0 - bent * bent) * (1.0 + 3.0 * 0.044715 * square)
            hid_buf[chip, which] = (act * up).astype(BF16)
            stage[slot, 0] = act.astype(BF16)
            stage[slot, 1] = (slope * up).astype(BF16)
            for k, ref in enumerate(outs):
                pltpu.make_async_copy(stage.at[slot, k], ref.at[chip, which], osem.at[slot, k]).start()
            pltpu.make_async_copy(hid_buf.at[chip, which], hid_ref.at[chip, which], hsem.at[t]).start()

        def finish_tile(t, chip, which):
            part = jnp.dot(hid_buf[chip, which], w_d[...], preferred_element_type=F32)
            pbuf[chip, which] = part.astype(BF16)

        def end():
            for slot in range(2):
                for k, ref in enumerate(outs):
                    pltpu.make_async_copy(stage.at[slot, k], ref.at[0, 0], osem.at[slot, k]).wait()
            for t in range(8):
                pltpu.make_async_copy(hid_buf.at[0, 0], hid_ref.at[0, 0], hsem.at[t]).wait()
            keep_g.wait()
            keep_d.wait()
            gather_d.drain()

        square_kernel(
            rows,
            (send, recv, lsem),
            gather=(compute, share, full, gbuf),
            scatter=(finish_tile, pbuf, (rcore, rxd, ryd, rx, ry), out),
            ring=ring,
            start=gather_d.start,
            first=first,
            early=gather_d.forward,
            between=between,
            end=end,
        )

    kept = jax.ShapeDtypeStruct((4, 2, rows, live), BF16)
    return pl.pallas_call(
        kernel,
        out_shape=[
            jax.ShapeDtypeStruct((rows, D), F32),
            jax.ShapeDtypeStruct((4, 2, rows, D), BF16),
            kept,
            kept,
            kept,
            jax.ShapeDtypeStruct((2, live, D), BF16),
            jax.ShapeDtypeStruct((live, D), BF16),
        ],
        in_specs=[ANY] * (2 + count),
        out_specs=[VM] + [ANY] * 6,
        scratch_shapes=[
            pltpu.VMEM((2, live, D), BF16),
            pltpu.VMEM((live, D), BF16),
            pltpu.VMEM((4, 2, rows, D), BF16),
            pltpu.VMEM((4, 2, rows, live), BF16),
            pltpu.VMEM((2, 2, rows, live), BF16),
        ]
        + scatter_scratch(rows, D)
        + [
            pltpu.SemaphoreType.DMA((count + 2,)),
            pltpu.SemaphoreType.DMA((2, 2)),
            pltpu.SemaphoreType.DMA((8,)),
        ]
        + SEMS
        + ring_sems(6),
        compiler_params=params(1),
        cost_estimate=LIGHT,
        name="ffn",
    )(middle_low, low_down, *units)


def ffn_back_call(ffn_grad, act, pull, w_down):
    rows = ffn_grad.shape[0]
    live = w_down.shape[0]

    def kernel(share, act_ref, pull_ref, wd_ref, full, dg_ref, w_d, gbuf, load, stage, wsem, isem, osem, send, recv, lsem):
        weight = pltpu.make_async_copy(wd_ref, w_d, wsem.at[0])
        weight.start()

        def compute(t, chip, which):
            slot = t % 2
            loads = [
                pltpu.make_async_copy(ref.at[chip, which], load.at[k], isem.at[k])
                for k, ref in enumerate((act_ref, pull_ref))
            ]
            stores = [
                pltpu.make_async_copy(stage.at[slot, k], dg_ref.at[k, chip, which], osem.at[slot, k])
                for k in range(2)
            ]
            for copy in loads:
                copy.start()

            @pl.when(t >= 2)
            def _():
                for copy in stores:
                    copy.wait()

            dh = nt_dot(gbuf[chip, which], w_d[...])
            for copy in loads:
                copy.wait()
            stage[slot, 0] = (dh * load[1].astype(F32)).astype(BF16)
            stage[slot, 1] = (dh * load[0].astype(F32)).astype(BF16)
            for copy in stores:
                copy.start()

        def end():
            for slot in range(2):
                for k in range(2):
                    pltpu.make_async_copy(stage.at[slot, k], dg_ref.at[k, 0, 0], osem.at[slot, k]).wait()

        square_kernel(
            rows,
            (send, recv, lsem),
            gather=(compute, share, full, gbuf),
            first=weight.wait,
            end=end,
            near_first=True,
        )

    return pl.pallas_call(
        kernel,
        out_shape=[
            jax.ShapeDtypeStruct((4, 2, rows, D), BF16),
            jax.ShapeDtypeStruct((2, 4, 2, rows, live), BF16),
        ],
        in_specs=[ANY] * 4,
        out_specs=[ANY, ANY],
        scratch_shapes=[
            pltpu.VMEM((live, D), BF16),
            pltpu.VMEM((4, 2, rows, D), BF16),
            pltpu.VMEM((2, rows, live), BF16),
            pltpu.VMEM((2, 2, rows, live), BF16),
            pltpu.SemaphoreType.DMA((1,)),
            pltpu.SemaphoreType.DMA((2,)),
            pltpu.SemaphoreType.DMA((2, 2)),
        ]
        + SEMS,
        compiler_params=params(2),
        cost_estimate=LIGHT,
        name="ffn_back",
    )(ffn_grad, act, pull, w_down)


def middle_back_call(grad_gateup_rows, w_gateup, grad_gateup_part, span, rows):
    live, width = grad_gateup_part.shape[1:]
    depth = width // 4

    def kernel(
        dg_ref, wg_ref, gg_ref, out, red_g,
        w_g, load, buf_g, pbuf, rcore, rxd, ryd, rx, ry, wsem, isem, send, recv, lsem, zsend, zrecv, zlocal,
    ):
        ring = Ring(zsend, zrecv, zlocal)
        side = span_scatter(ring, 0, gg_ref, span, buf_g, red_g)
        weight = pltpu.make_async_copy(wg_ref, w_g, wsem.at[0])
        weight.start()
        me = lax.axis_index("mp")
        core, x, y = me % 2, (me // 2) % 2, me // 4

        def loads(t):
            rel = (t // 2 + 1) % 4
            chip = ((y + rel % 2) % 2) * 2 + (x + ((rel + 1) // 2) % 2) % 2
            which = (1 - core + t % 2) % 2
            return [
                pltpu.make_async_copy(dg_ref.at[k, chip, which], load.at[t % 2, k], isem.at[t % 2, k])
                for k in range(2)
            ]

        for copy in loads(0):
            copy.start()

        def compute(t, chip, which):
            @pl.when(t < 7)
            def _():
                for copy in loads(t + 1):
                    copy.start()

            for copy in loads(t):
                copy.wait()
            slot = t % 2
            part = jnp.dot(load[slot, 0], w_g[0], preferred_element_type=F32)
            part += jnp.dot(load[slot, 1], w_g[1], preferred_element_type=F32)
            pbuf[chip, which] = part.astype(BF16)

        square_kernel(
            rows,
            (send, recv, lsem),
            scatter=(compute, pbuf, (rcore, rxd, ryd, rx, ry), out),
            ring=ring,
            start=lambda: (side.start(), weight.wait()),
            middle=side.forward,
            end=side.finish,
        )

    return pl.pallas_call(
        kernel,
        out_shape=[
            jax.ShapeDtypeStruct((rows, D), F32),
            jax.ShapeDtypeStruct((2, span[1], depth), F32),
        ],
        in_specs=[ANY] * 3,
        out_specs=[VM] * 2,
        scratch_shapes=[
            pltpu.VMEM((2, live, D), BF16),
            pltpu.VMEM((2, 2, rows, live), BF16),
            pltpu.VMEM((10, span[1], depth), BF16),
        ]
        + scatter_scratch(rows, D)
        + [pltpu.SemaphoreType.DMA((1,)), pltpu.SemaphoreType.DMA((2, 2))]
        + SEMS
        + ring_sems(6),
        compiler_params=params(8),
        cost_estimate=LIGHT,
        name="middle_back",
    )(grad_gateup_rows, w_gateup, grad_gateup_part)


def out_back_call(attn_grad, w_out, attended, grad_gateup_part, span):
    rows = attn_grad.shape[0]
    cols = w_out.shape[0]
    depth = grad_gateup_part.shape[2] // 4

    def kernel(
        share, w_ref, o_ref, gg_ref, dout, go_ref, red,
        w_buf, gbuf, buf, acc, wsem, send, recv, lsem, zsend, zrecv, zlocal,
    ):
        ring = Ring(zsend, zrecv, zlocal)
        side = span_scatter(ring, 0, gg_ref, span, buf, red)
        weight = pltpu.make_async_copy(w_ref, w_buf, wsem.at[0])
        weight.start()

        def compute(t, chip, which):
            tile = gbuf[chip, which]
            dout[chip, which] = nt_dot(tile, w_buf[...]).astype(BF16)
            part = lax.dot_general(o_ref[chip, which], tile, TN, preferred_element_type=F32)

            @pl.when(t == 0)
            def _():
                acc[...] = part

            @pl.when(t > 0)
            def _():
                acc[...] += part

        def end():
            go_ref[...] = acc[...].astype(BF16)
            side.finish()

        square_kernel(
            rows,
            (send, recv, lsem),
            gather=(compute, share, None, gbuf),
            ring=ring,
            start=side.start,
            first=weight.wait,
            early=side.forward,
            end=end,
            near_first=True,
        )

    return pl.pallas_call(
        kernel,
        out_shape=[
            jax.ShapeDtypeStruct((4, 2, rows, cols), BF16),
            jax.ShapeDtypeStruct((cols, D), BF16),
            jax.ShapeDtypeStruct((2, span[1], depth), F32),
        ],
        in_specs=[ANY, ANY, VM, ANY],
        out_specs=[VM, VM, VM],
        scratch_shapes=[
            pltpu.VMEM((cols, D), BF16),
            pltpu.VMEM((4, 2, rows, D), BF16),
            pltpu.VMEM((10, span[1], depth), BF16),
            pltpu.VMEM((cols, D), F32),
            pltpu.SemaphoreType.DMA((1,)),
        ]
        + SEMS
        + ring_sems(6),
        compiler_params=params(3),
        cost_estimate=LIGHT,
        name="out_back",
    )(attn_grad, w_out, attended.reshape(4, 2, rows, cols), grad_gateup_part)


def input_back_call(grad_proj, w_qkv, grad_qkv_part, rows):
    width, cols = w_qkv.shape[1:]
    depth = width // 4

    def kernel(
        da_ref, w_ref, gq_ref, out, red_q,
        w_buf, buf_q, pbuf, rcore, rxd, ryd, rx, ry, wsem, send, recv, lsem, zsend, zrecv, zlocal,
    ):
        ring = Ring(zsend, zrecv, zlocal)
        half = depth // 2
        side = RingScatter(
            ring, 0, row_halves(depth)(gq_ref), buf_q, lambda h: red_q.at[:, pl.ds(h * half, half), :]
        )
        weight = pltpu.make_async_copy(w_ref, w_buf, wsem.at[0])
        weight.start()

        def start():
            side.start()
            weight.wait()

        def compute(t, chip, which):
            part = nt_dot(da_ref[0, chip, which], w_buf[0])
            part += nt_dot(da_ref[1, chip, which], w_buf[1])
            part += nt_dot(da_ref[2, chip, which], w_buf[2])
            pbuf[chip, which] = part.astype(BF16)

        square_kernel(
            rows,
            (send, recv, lsem),
            scatter=(compute, pbuf, (rcore, rxd, ryd, rx, ry), out),
            ring=ring,
            start=start,
            middle=side.forward,
            end=side.finish,
        )

    return pl.pallas_call(
        kernel,
        out_shape=[
            jax.ShapeDtypeStruct((rows, D), F32),
            jax.ShapeDtypeStruct((3, depth, cols), F32),
        ],
        in_specs=[VM, ANY, ANY],
        out_specs=[VM, VM],
        scratch_shapes=[
            pltpu.VMEM((3, D, cols), BF16),
            pltpu.VMEM((10, 3, depth // 2, cols), BF16),
        ]
        + scatter_scratch(rows, D)
        + [pltpu.SemaphoreType.DMA((1,))]
        + SEMS
        + ring_sems(6),
        compiler_params=params(4),
        cost_estimate=LIGHT,
        name="input_back",
    )(grad_proj.reshape(3, 4, 2, rows, cols), w_qkv, grad_qkv_part)


PARTS = ((0, 240), (240, 464))
SPANS = ((0, 176), (176, 416), (592, 112))


def body_ring(
    block_input,
    cotangent,
    prefix_len,
    cluster_id,
    positions,
    step_count,
    master_qkv,
    first_qkv,
    second_qkv,
    master_out,
    first_out,
    second_out,
    master_gateup,
    first_gateup,
    second_gateup,
    master_down,
    first_down,
    second_down,
    master_norm,
    first_norm,
    second_norm,
):
    token_count = block_input.shape[0]
    protein_count = token_count // LEN
    share_rows = cotangent.shape[0]
    share_start = lax.axis_index("mp") * share_rows
    deep_alpha = math.sqrt(2.0 * DEPTH)

    low_qkv = master_qkv.astype(BF16)
    low_out = master_out.astype(BF16)
    low_gateup = jnp.swapaxes(master_gateup, 1, 2).astype(BF16)
    low_units = [low_gateup[:, first : first + size] for first, size in PARTS]
    low_down = master_down.astype(BF16)
    w_norm = lax.optimization_barrier(master_norm.astype(BF16)).astype(F32)

    queries, key_rows, value_rows, cos_table, sin_table, w_qkv, w_out = qkv_call(
        block_input, low_qkv, low_out, positions, share_rows
    )
    cos_table = cos_table.reshape(token_count, HEAD_DIM)
    sin_table = sin_table.reshape(token_count, HEAD_DIM)
    queries, key_rows, value_rows = (
        part.reshape(token_count, -1) for part in (queries, key_rows, value_rows)
    )
    attended, probs, unit_0 = attention_call(queries, key_rows, value_rows, prefix_len, low_units[0])
    attn_share, unit_1 = out_call(attended, w_out, low_units[1:2], share_rows)
    input_share = lax.dynamic_slice_in_dim(block_input, share_start, share_rows, 0).astype(F32)
    middle_share, normed_one, inv_one = norm_forward(
        deep_alpha * input_share + attn_share, w_norm[0], w_norm[1]
    )
    ffn_share, middle_low, hidden, act, pull, w_gateup, w_down = ffn_call(
        middle_share.astype(BF16), (unit_0, unit_1), low_down
    )
    out_share, normed_two, inv_two = norm_forward(
        deep_alpha * middle_share + ffn_share, w_norm[2], w_norm[3]
    )
    block_output = out_share.astype(BF16)
    matches = (cluster_id[:, None] == cluster_id[None, :]).astype(F32)
    counts = jnp.sum(matches, axis=1)
    group_counts = lax.dynamic_slice_in_dim(
        counts, lax.axis_index("dp") * protein_count, protein_count, 0
    )
    row_protein = (share_start + jnp.arange(share_rows)) // LEN
    one_hot = (row_protein[:, None] == jnp.arange(protein_count)[None, :]).astype(F32)
    row_weight = jnp.sum(one_hot * (1.0 / group_counts)[None, :], axis=1)
    grad_output = cotangent.astype(F32) * row_weight[:, None]
    grad_h2, grad_gain_two, grad_bias_two = norm_backward(
        grad_output, normed_two, inv_two, w_norm[2]
    )
    ffn_grad, grad_gateup_rows = ffn_back_call(grad_h2.astype(BF16), act, pull, w_down)
    hidden = hidden.reshape(token_count, -1)
    middle_low = middle_low.reshape(token_count, D)
    ffn_grad = ffn_grad.reshape(token_count, D)
    gateup_rows = grad_gateup_rows.reshape(2, token_count, -1)
    grad_down_part = jnp.einsum("tf,td->fd", hidden, ffn_grad, preferred_element_type=F32).astype(BF16)
    red_down = lax.psum_scatter(grad_down_part, "dp", scatter_dimension=1, tiled=True).astype(F32)
    gateup_rows, grad_gateup_rows, grad_down_part = lax.optimization_barrier(
        (gateup_rows, grad_gateup_rows, grad_down_part)
    )
    grad_gateup_part = jnp.einsum(
        "jtf,td->jfd", gateup_rows, middle_low, preferred_element_type=F32
    ).astype(BF16)
    middle_grad, red_gateup_0 = middle_back_call(
        grad_gateup_rows, w_gateup, grad_gateup_part, SPANS[0], share_rows
    )
    middle_grad = middle_grad + deep_alpha * grad_h2
    grad_h1, grad_gain_one, grad_bias_one = norm_backward(
        middle_grad, normed_one, inv_one, w_norm[0]
    )
    grad_attended, grad_out_part, red_gateup_1 = out_back_call(
        grad_h1.astype(BF16), w_out, attended, grad_gateup_part, SPANS[1]
    )
    grad_attended = grad_attended.reshape(token_count, -1)
    norm_terms = jnp.stack([grad_gain_one, grad_bias_one, grad_gain_two, grad_bias_two])
    grad_proj, grad_norm, red_out, red_gateup_2 = attention_back_call(
        queries,
        key_rows,
        value_rows,
        probs,
        attended,
        grad_attended,
        cos_table,
        sin_table,
        norm_terms,
        grad_out_part,
        grad_gateup_part,
        SPANS[2],
    )
    red_gateup = jnp.swapaxes(
        jnp.concatenate([red_gateup_0, red_gateup_1, red_gateup_2], axis=1), 1, 2
    )
    grad_qkv_part = jnp.einsum("td,jtc->jdc", block_input, grad_proj, preferred_element_type=F32).astype(BF16)
    input_share_grad, red_qkv = input_back_call(grad_proj, w_qkv, grad_qkv_part, share_rows)
    grad_input = (input_share_grad + deep_alpha * grad_h1).astype(BF16)

    step_value = step_count[0].astype(F32)
    rate_qkv = D ** (-0.5)
    rate_out = max(HEADS * HEAD_DIM // 512, 1) ** (-0.5)
    rate_gateup = D ** (-0.5)
    rate_down = max(FF // 64, 1) ** (-0.5)
    rate_norm = 1.0
    new_qkv, new_first_qkv, new_second_qkv = adamw_step(
        master_qkv, first_qkv, second_qkv, red_qkv, rate_qkv, step_value
    )
    new_out, new_first_out, new_second_out = adamw_step(
        master_out, first_out, second_out, red_out, rate_out, step_value
    )
    new_gateup, new_first_gateup, new_second_gateup = adamw_step(
        master_gateup, first_gateup, second_gateup, red_gateup, rate_gateup, step_value
    )
    new_down, new_first_down, new_second_down = adamw_step(
        master_down, first_down, second_down, red_down, rate_down, step_value
    )
    new_norm, new_first_norm, new_second_norm = adamw_step(
        master_norm, first_norm, second_norm, grad_norm, rate_norm, step_value
    )
    return (
        block_output,
        grad_input,
        red_qkv,
        new_qkv,
        new_first_qkv,
        new_second_qkv,
        red_out,
        new_out,
        new_first_out,
        new_second_out,
        red_gateup,
        new_gateup,
        new_first_gateup,
        new_second_gateup,
        red_down,
        new_down,
        new_first_down,
        new_second_down,
        grad_norm,
        new_norm,
        new_first_norm,
        new_second_norm,
    )


def solution(mesh):
    placed = (
        P("dp", None),
        P(("dp", "mp"), None),
        P("dp"),
        P(),
        P("dp"),
        P(),
        P(None, "dp", "mp"),
        P(None, "dp", "mp"),
        P(None, "dp", "mp"),
        P("mp", "dp"),
        P("mp", "dp"),
        P("mp", "dp"),
        P(None, "dp", "mp"),
        P(None, "dp", "mp"),
        P(None, "dp", "mp"),
        P("mp", "dp"),
        P("mp", "dp"),
        P("mp", "dp"),
        P(),
        P(),
        P(),
    )
    ring = mesh.shape["dp"] == 4 and mesh.shape["mp"] == 8
    return jax.shard_map(
        body_ring if ring else body_plain,
        mesh=mesh,
        in_specs=placed,
        out_specs=(
            P(("dp", "mp"), None),
            P(("dp", "mp"), None),
            P(None, "dp", "mp"),
            P(None, "dp", "mp"),
            P(None, "dp", "mp"),
            P(None, "dp", "mp"),
            P("mp", "dp"),
            P("mp", "dp"),
            P("mp", "dp"),
            P("mp", "dp"),
            P(None, "dp", "mp"),
            P(None, "dp", "mp"),
            P(None, "dp", "mp"),
            P(None, "dp", "mp"),
            P("mp", "dp"),
            P("mp", "dp"),
            P("mp", "dp"),
            P("mp", "dp"),
            P(),
            P(),
            P(),
            P(),
        ),
        check_vma=False,
    )
```

```python
import functools
import math

import jax
import jax.numpy as jnp
from jax import lax
from jax.experimental import pallas as pl
from jax.experimental.pallas import tpu as pltpu
from jax.sharding import PartitionSpec as P

D = 2048
HEADS = 16
HEAD_DIM = 128
FF = 5632
DEPTH = 24
LEN = 896


beta_one = 0.9
beta_two = 0.95
adam_epsilon = 1e-08
decay_weight = 0.1
norm_epsilon = 1e-05


def norm_forward(hidden_rows, gain, offset):
    centre = hidden_rows - jnp.mean(hidden_rows, axis=-1, keepdims=True)
    inv_std = lax.rsqrt(jnp.mean(centre * centre, axis=-1, keepdims=True) + norm_epsilon)
    normed = centre * inv_std
    return (normed * gain + offset, normed, inv_std)


def norm_backward(grad_rows, normed, inv_std, gain):
    grad_normed = grad_rows * gain
    first_term = jnp.mean(grad_normed, axis=-1, keepdims=True)
    second_term = jnp.mean(grad_normed * normed, axis=-1, keepdims=True)
    grad_hidden = inv_std * (grad_normed - first_term - normed * second_term)
    return (grad_hidden, jnp.sum(grad_rows * normed, axis=0), jnp.sum(grad_rows, axis=0))


def rotate_half(values):
    middle = values.shape[-1] // 2
    return jnp.concatenate([-values[..., middle:], values[..., :middle]], axis=-1)


def rotate_back(values):
    middle = values.shape[-1] // 2
    return jnp.concatenate([values[..., middle:], -values[..., :middle]], axis=-1)


def rope_tables(positions):
    ladder = jnp.arange(HEAD_DIM // 2, dtype=jnp.float32)
    inverse = jnp.exp(ladder * (-2.0 * math.log(10000.0) / HEAD_DIM))
    angles = positions.astype(jnp.float32)[:, None] * inverse[None, :]
    cos_half = jnp.cos(angles)
    sin_half = jnp.sin(angles)
    return (
        jnp.concatenate([cos_half, cos_half], axis=-1),
        jnp.concatenate([sin_half, sin_half], axis=-1),
    )


def apply_rope(values, cos_table, sin_table):
    return values * cos_table[:, None, :] + rotate_half(values) * sin_table[:, None, :]


def rope_back(grads, cos_table, sin_table):
    return grads * cos_table[:, None, :] + rotate_back(grads * sin_table[:, None, :])


def gelu_tanh(values):
    return jax.nn.gelu(values, approximate=True)


def adamw_step(old_master, old_first, old_second, grad_sum, learn_rate, step_value):
    first_new = beta_one * old_first + (1.0 - beta_one) * grad_sum
    second_new = beta_two * old_second + (1.0 - beta_two) * grad_sum * grad_sum
    fix_first = 1.0 - jnp.power(beta_one, step_value)
    fix_second = 1.0 - jnp.power(beta_two, step_value)
    update = (
        first_new / fix_first / (jnp.sqrt(second_new / fix_second) + adam_epsilon)
        + decay_weight * old_master
    )
    return (old_master - learn_rate * update, first_new, second_new)


def body_plain(
    block_input,
    cotangent,
    prefix_len,
    cluster_id,
    positions,
    step_count,
    master_qkv,
    first_qkv,
    second_qkv,
    master_out,
    first_out,
    second_out,
    master_gateup,
    first_gateup,
    second_gateup,
    master_down,
    first_down,
    second_down,
    master_norm,
    first_norm,
    second_norm,
):
    w_qkv, w_out, w_gateup, w_down = (
        lax.all_gather(master_qkv.astype(jnp.bfloat16), "dp", axis=1, tiled=True),
        lax.all_gather(master_out.astype(jnp.bfloat16), "dp", axis=1, tiled=True),
        lax.all_gather(master_gateup.astype(jnp.bfloat16), "dp", axis=1, tiled=True),
        lax.all_gather(master_down.astype(jnp.bfloat16), "dp", axis=1, tiled=True),
    )
    w_norm = lax.optimization_barrier(master_norm.astype(jnp.bfloat16)).astype(jnp.float32)
    token_count = block_input.shape[0]
    protein_count = token_count // LEN
    share_rows = cotangent.shape[0]
    share_start = lax.axis_index("mp") * share_rows
    head_count = w_qkv.shape[2] // HEAD_DIM
    width_heads = head_count * HEAD_DIM
    deep_alpha = math.sqrt(2.0 * DEPTH)
    score_scale = 1.0 / math.sqrt(HEAD_DIM)
    cos_table, sin_table = rope_tables(positions)
    projected = jnp.einsum("td,jdc->jtc", block_input, w_qkv, preferred_element_type=jnp.float32)
    shaped = projected.reshape(3, token_count, head_count, HEAD_DIM)
    queries = (apply_rope(shaped[0], cos_table, sin_table) * score_scale).astype(jnp.bfloat16)
    key_rows = apply_rope(shaped[1], cos_table, sin_table).astype(jnp.bfloat16)
    value_rows = shaped[2].astype(jnp.bfloat16)
    row_ids = jnp.arange(LEN)[:, None]
    col_ids = jnp.arange(LEN)[None, :]
    attended_parts = []
    log_totals = []
    for protein in range(protein_count):
        row_slice = slice(protein * LEN, (protein + 1) * LEN)
        visible = (col_ids < prefix_len[protein]) | (col_ids <= row_ids)
        scores = jnp.einsum(
            "qhd,khd->hqk",
            queries[row_slice],
            key_rows[row_slice],
            preferred_element_type=jnp.float32,
        )
        scores = jnp.where(visible[None], scores, -1e30)
        row_peak = jnp.max(scores, axis=-1, keepdims=True)
        expo_rows = jnp.exp(scores - row_peak)
        totals = jnp.sum(expo_rows, axis=-1, keepdims=True)
        attn_probs = (expo_rows / totals).astype(jnp.bfloat16)
        attended_parts.append(
            jnp.einsum(
                "hqk,khd->qhd",
                attn_probs,
                value_rows[row_slice],
                preferred_element_type=jnp.float32,
            )
        )
        log_totals.append(row_peak + jnp.log(totals))
    attended = (
        jnp.concatenate(attended_parts, axis=0)
        .reshape(token_count, width_heads)
        .astype(jnp.bfloat16)
    )
    attn_part = jnp.dot(attended, w_out, preferred_element_type=jnp.float32)
    input_share = lax.dynamic_slice_in_dim(block_input, share_start, share_rows, 0).astype(
        jnp.float32
    )
    attn_share = lax.psum_scatter(
        attn_part.astype(jnp.bfloat16), "mp", scatter_dimension=0, tiled=True
    ).astype(jnp.float32)
    middle_share, normed_one, inv_one = norm_forward(
        deep_alpha * input_share + attn_share, w_norm[0], w_norm[1]
    )
    middle_low = lax.all_gather(middle_share.astype(jnp.bfloat16), "mp", axis=0, tiled=True)
    gateup = jnp.einsum("td,jdf->jtf", middle_low, w_gateup, preferred_element_type=jnp.float32)
    gate_rows = gateup[0]
    up_rows = gateup[1]
    activated, gelu_pull = jax.vjp(gelu_tanh, gate_rows)
    hidden = (activated * up_rows).astype(jnp.bfloat16)
    ffn_part = jnp.dot(hidden, w_down, preferred_element_type=jnp.float32)
    ffn_share = lax.psum_scatter(
        ffn_part.astype(jnp.bfloat16), "mp", scatter_dimension=0, tiled=True
    ).astype(jnp.float32)
    out_share, normed_two, inv_two = norm_forward(
        deep_alpha * middle_share + ffn_share, w_norm[2], w_norm[3]
    )
    block_output = out_share.astype(jnp.bfloat16)
    matches = (cluster_id[:, None] == cluster_id[None, :]).astype(jnp.float32)
    counts = jnp.sum(matches, axis=1)
    group_counts = lax.dynamic_slice_in_dim(
        counts, lax.axis_index("dp") * protein_count, protein_count, 0
    )
    row_protein = (share_start + jnp.arange(share_rows)) // LEN
    one_hot = (row_protein[:, None] == jnp.arange(protein_count)[None, :]).astype(jnp.float32)
    row_weight = jnp.sum(one_hot * (1.0 / group_counts)[None, :], axis=1)
    grad_output = cotangent.astype(jnp.float32) * row_weight[:, None]
    grad_h2, grad_gain_two, grad_bias_two = norm_backward(
        grad_output, normed_two, inv_two, w_norm[2]
    )
    ffn_grad_full = lax.all_gather(grad_h2.astype(jnp.bfloat16), "mp", axis=0, tiled=True)
    grad_down_part = jnp.einsum(
        "tf,td->fd", hidden, ffn_grad_full, preferred_element_type=jnp.float32
    )
    grad_hidden = jnp.einsum("td,fd->tf", ffn_grad_full, w_down, preferred_element_type=jnp.float32)
    grad_gate = gelu_pull(grad_hidden * up_rows)[0]
    grad_up = grad_hidden * activated
    grad_gateup_rows = jnp.stack([grad_gate, grad_up]).astype(jnp.bfloat16)
    grad_gateup_part = jnp.einsum(
        "td,jtf->jdf", middle_low, grad_gateup_rows, preferred_element_type=jnp.float32
    )
    middle_grad_part = jnp.einsum(
        "jtf,jdf->td", grad_gateup_rows, w_gateup, preferred_element_type=jnp.float32
    )
    middle_grad = (
        lax.psum_scatter(
            middle_grad_part.astype(jnp.bfloat16), "mp", scatter_dimension=0, tiled=True
        ).astype(jnp.float32)
        + deep_alpha * grad_h2
    )
    grad_h1, grad_gain_one, grad_bias_one = norm_backward(
        middle_grad, normed_one, inv_one, w_norm[0]
    )
    attn_grad_full = lax.all_gather(grad_h1.astype(jnp.bfloat16), "mp", axis=0, tiled=True)
    grad_out_part = jnp.einsum(
        "tc,td->cd", attended, attn_grad_full, preferred_element_type=jnp.float32
    )
    grad_attended = (
        jnp.einsum("td,cd->tc", attn_grad_full, w_out, preferred_element_type=jnp.float32)
        .astype(jnp.bfloat16)
        .reshape(token_count, head_count, HEAD_DIM)
    )
    query_grads = []
    key_grads = []
    value_grads = []
    for protein in range(protein_count):
        row_slice = slice(protein * LEN, (protein + 1) * LEN)
        visible = (col_ids < prefix_len[protein]) | (col_ids <= row_ids)
        scores = jnp.einsum(
            "qhd,khd->hqk",
            queries[row_slice],
            key_rows[row_slice],
            preferred_element_type=jnp.float32,
        )
        scores = jnp.where(visible[None], scores, -1e30)
        probs_full = jnp.exp(scores - log_totals[protein])
        probs_low = probs_full.astype(jnp.bfloat16)
        grad_slice = grad_attended[row_slice]
        value_grads.append(
            jnp.einsum("hqk,qhd->khd", probs_low, grad_slice, preferred_element_type=jnp.float32)
        )
        prob_grads = jnp.einsum(
            "qhd,khd->hqk", grad_slice, value_rows[row_slice], preferred_element_type=jnp.float32
        )
        centre_term = jnp.sum(probs_full * prob_grads, axis=-1, keepdims=True)
        score_grads = (probs_full * (prob_grads - centre_term)).astype(jnp.bfloat16)
        query_grads.append(
            jnp.einsum(
                "hqk,khd->qhd", score_grads, key_rows[row_slice], preferred_element_type=jnp.float32
            )
        )
        key_grads.append(
            jnp.einsum(
                "hqk,qhd->khd", score_grads, queries[row_slice], preferred_element_type=jnp.float32
            )
        )
    grad_query = rope_back(jnp.concatenate(query_grads, axis=0), cos_table, sin_table) * score_scale
    grad_key = rope_back(jnp.concatenate(key_grads, axis=0), cos_table, sin_table)
    grad_value = jnp.concatenate(value_grads, axis=0)
    grad_proj = (
        jnp.stack([grad_query, grad_key, grad_value])
        .reshape(3, token_count, width_heads)
        .astype(jnp.bfloat16)
    )
    grad_qkv_part = jnp.einsum(
        "td,jtc->jdc", block_input, grad_proj, preferred_element_type=jnp.float32
    )
    input_grad_part = jnp.einsum(
        "jtc,jdc->td", grad_proj, w_qkv, preferred_element_type=jnp.float32
    )
    input_grad = (
        lax.psum_scatter(
            input_grad_part.astype(jnp.bfloat16), "mp", scatter_dimension=0, tiled=True
        ).astype(jnp.float32)
        + deep_alpha * grad_h1
    )
    grad_input = input_grad.astype(jnp.bfloat16)
    norm_terms = jnp.stack([grad_gain_one, grad_bias_one, grad_gain_two, grad_bias_two])
    grad_norm = lax.psum(norm_terms, ("dp", "mp"))
    red_qkv, red_out, red_gateup, red_down = (
        lax.psum_scatter(
            grad_qkv_part.astype(jnp.bfloat16), "dp", scatter_dimension=1, tiled=True
        ).astype(jnp.float32),
        lax.psum_scatter(
            grad_out_part.astype(jnp.bfloat16), "dp", scatter_dimension=1, tiled=True
        ).astype(jnp.float32),
        lax.psum_scatter(
            grad_gateup_part.astype(jnp.bfloat16), "dp", scatter_dimension=1, tiled=True
        ).astype(jnp.float32),
        lax.psum_scatter(
            grad_down_part.astype(jnp.bfloat16), "dp", scatter_dimension=1, tiled=True
        ).astype(jnp.float32),
    )
    step_value = step_count[0].astype(jnp.float32)
    rate_qkv = D ** (-0.5)
    rate_out = max(HEADS * HEAD_DIM // 512, 1) ** (-0.5)
    rate_gateup = D ** (-0.5)
    rate_down = max(FF // 64, 1) ** (-0.5)
    rate_norm = 1.0
    new_qkv, new_first_qkv, new_second_qkv = adamw_step(
        master_qkv, first_qkv, second_qkv, red_qkv, rate_qkv, step_value
    )
    new_out, new_first_out, new_second_out = adamw_step(
        master_out, first_out, second_out, red_out, rate_out, step_value
    )
    new_gateup, new_first_gateup, new_second_gateup = adamw_step(
        master_gateup, first_gateup, second_gateup, red_gateup, rate_gateup, step_value
    )
    new_down, new_first_down, new_second_down = adamw_step(
        master_down, first_down, second_down, red_down, rate_down, step_value
    )
    new_norm, new_first_norm, new_second_norm = adamw_step(
        master_norm, first_norm, second_norm, grad_norm, rate_norm, step_value
    )
    return (
        block_output,
        grad_input,
        red_qkv,
        new_qkv,
        new_first_qkv,
        new_second_qkv,
        red_out,
        new_out,
        new_first_out,
        new_second_out,
        red_gateup,
        new_gateup,
        new_first_gateup,
        new_second_gateup,
        red_down,
        new_down,
        new_first_down,
        new_second_down,
        grad_norm,
        new_norm,
        new_first_norm,
        new_second_norm,
    )


MESH = pl.DeviceIdType.MESH
VMEM_BYTES = 61 * 1024 * 1024
BF16 = jnp.bfloat16
F32 = jnp.float32
EMIT = 48
NT = (((1,), (1,)), ((), ()))
ANY = pl.BlockSpec(memory_space=pl.ANY)
VM = pl.BlockSpec(memory_space=pltpu.VMEM)


LIGHT = pl.CostEstimate(flops=1 << 20, bytes_accessed=1 << 16, transcendentals=0)


def nt_dot(left, right):
    return lax.dot_general(left, right, NT, preferred_element_type=F32)


class Ring:
    def __init__(self, send, recv, local):
        self.here = lax.axis_index("dp")
        self.right = (self.here + 1) % 4
        self.left = (self.here + 3) % 4
        self.far = (self.here + 2) % 4
        self.send, self.recv, self.local = send, recv, local

    def copy(self, k, src, dst, other):
        return pltpu.make_async_remote_copy(
            src_ref=src,
            dst_ref=dst,
            send_sem=self.send.at[k],
            recv_sem=self.recv.at[k],
            device_id={"dp": other},
            device_id_type=MESH,
        )


class RingGather:
    def __init__(self, ring, first, half_of, place):
        self.plus_0 = ring.copy(first, half_of(0), place(ring.here, 0), ring.right)
        self.minus_1 = ring.copy(first + 1, half_of(1), place(ring.here, 1), ring.left)
        self.plus_1 = ring.copy(first + 2, half_of(1), place(ring.here, 1), ring.right)
        self.minus_0 = ring.copy(first + 3, half_of(0), place(ring.here, 0), ring.left)
        self.far_0 = ring.copy(first + 4, place(ring.left, 0), place(ring.left, 0), ring.right)
        self.far_1 = ring.copy(first + 5, place(ring.right, 1), place(ring.right, 1), ring.left)
        self.own = [
            pltpu.make_async_copy(half_of(h), place(ring.here, h), ring.local.at[first + h])
            for h in range(2)
        ]
        self.remote = (self.plus_0, self.minus_1, self.plus_1, self.minus_0, self.far_0, self.far_1)

    def start(self):
        for copy in self.remote[:4]:
            copy.start()
        for copy in self.own:
            copy.start()

    def forward(self):
        self.plus_0.wait_recv()
        self.far_0.start()
        self.minus_1.wait_recv()
        self.far_1.start()

    def near(self):
        self.plus_1.wait_recv()
        self.minus_0.wait_recv()

    def far(self):
        self.far_0.wait_recv()
        self.far_1.wait_recv()

    def drain(self):
        for copy in self.remote:
            copy.wait_send()

    def finish(self):
        for copy in self.own:
            copy.wait()
        self.near()
        self.far()
        self.drain()


class RingScatter:
    def __init__(self, ring, first, half_at, buf, out):
        self.buf, self.out = buf, out
        self.plus_far = ring.copy(first, half_at(ring.far, 0), buf.at[0], ring.right)
        self.minus_far = ring.copy(first + 1, half_at(ring.far, 1), buf.at[1], ring.left)
        self.plus_near = ring.copy(first + 2, half_at(ring.right, 1), buf.at[2], ring.right)
        self.minus_near = ring.copy(first + 3, half_at(ring.left, 0), buf.at[3], ring.left)
        self.plus_sum = ring.copy(first + 4, buf.at[6], buf.at[4], ring.right)
        self.minus_sum = ring.copy(first + 5, buf.at[7], buf.at[5], ring.left)
        places = ((ring.right, 0), (ring.left, 1), (ring.here, 0), (ring.here, 1))
        self.loads = [
            pltpu.make_async_copy(half_at(*place), buf.at[6 + k], ring.local.at[first + k])
            for k, place in enumerate(places)
        ]
        self.remote = (
            self.plus_far,
            self.minus_far,
            self.plus_near,
            self.minus_near,
            self.plus_sum,
            self.minus_sum,
        )

    def start(self):
        for copy in self.remote[:4]:
            copy.start()
        for copy in self.loads:
            copy.start()

    def forward(self):
        for copy in self.loads:
            copy.wait()
        self.plus_far.wait_recv()
        for_rows(self.buf.shape[1:], lambda at: add_at(self.buf, 6, 0, at))
        self.plus_sum.start()
        self.minus_far.wait_recv()
        for_rows(self.buf.shape[1:], lambda at: add_at(self.buf, 7, 1, at))
        self.minus_sum.start()

    def finish(self):
        for copy in self.remote[2:]:
            copy.wait_recv()
        buf = self.buf
        for half, terms in enumerate(((8, 3, 4), (9, 2, 5))):
            out = self.out(half)

            def total(at, out=out, terms=terms):
                out[at] = sum(buf[(k,) + at].astype(F32) for k in terms)

            for_rows(buf.shape[1:], total)
        for copy in self.remote:
            copy.wait_send()


def add_at(buf, dst, src, at):
    buf[(dst,) + at] = (buf[(dst,) + at].astype(F32) + buf[(src,) + at].astype(F32)).astype(BF16)


def for_rows(shape, visit):
    def step(i, carry):
        rows = pl.ds(pl.multiple_of(i * 16, 16), 16)
        if len(shape) == 2:
            visit((rows, slice(None)))
        else:
            for j in range(shape[0]):
                visit((j, rows, slice(None)))
        return carry

    lax.fori_loop(0, shape[-2] // 16, step, 0)


def ring_sems(count):
    return [pltpu.SemaphoreType.DMA((count,)) for _ in range(3)]


def row_halves(depth):
    half = depth // 2

    def place(ref):
        def at(owner, part):
            return ref.at[:, pl.ds(pl.multiple_of(owner * depth + part * half, half), half), :]

        return at

    return place


def plane_columns(depth):
    def place(ref):
        def at(owner, part):
            return ref.at[part, :, pl.ds(pl.multiple_of(owner * depth, depth), depth)]

        return at

    return place


def column_halves(depth):
    def place(ref):
        half = ref.shape[0] // 2

        def at(owner, part):
            columns = pl.ds(pl.multiple_of(owner * depth, depth), depth)
            return ref.at[pl.ds(part * half, half), columns]

        return at

    return place


def span_scatter(ring, first, ref, span, buf, out):
    at = plane_columns(ref.shape[2] // 4)(ref.at[:, pl.ds(*span), :])
    return RingScatter(ring, first, at, buf, lambda h: out.at[h])


def greet(others):
    sem = pltpu.get_barrier_semaphore()
    for other in others:
        pl.semaphore_signal(sem, inc=1, device_id=other, device_id_type=MESH)
    pl.semaphore_wait(sem, len(others))


class Square:
    def __init__(self, send, recv, rows):
        me = lax.axis_index("mp")
        self.core = me % 2
        self.x = (me // 2) % 2
        self.y = me // 4
        self.xn = (self.y * 2 + (1 - self.x)) * 2 + self.core
        self.yn = ((1 - self.y) * 2 + self.x) * 2 + self.core
        self.peer = (self.y * 2 + self.x) * 2 + (1 - self.core)
        self.own = self.y * 2 + self.x
        self.xc = self.y * 2 + (1 - self.x)
        self.yc = (1 - self.y) * 2 + self.x
        self.dc = (1 - self.y) * 2 + (1 - self.x)
        self.send, self.recv = send, recv
        cut = rows // 2 // 16 * 16
        self.rows = rows
        self.a = pl.ds(0, cut)
        self.b = pl.ds(cut, rows - cut)
        self.na, self.nb, self.cut = cut, rows - cut, cut

        self.others = [{"mp": self.xn}, {"mp": self.yn}, {"mp": self.peer}]

    def copy(self, k, src, dst, other):
        return pltpu.make_async_remote_copy(
            src_ref=src,
            dst_ref=dst,
            send_sem=self.send.at[k],
            recv_sem=self.recv.at[k],
            device_id={"mp": other},
            device_id_type=MESH,
        )


def add_rows(dst, src, count):
    def step(i, carry):
        rows = pl.ds(pl.multiple_of(i * 16, 16), 16)
        dst[rows, :] = (dst[rows, :].astype(F32) + src[rows, :].astype(F32)).astype(BF16)
        return carry

    lax.fori_loop(0, count // 16, step, 0)


def nothing():
    pass


def square_kernel(
    rows,
    sems,
    gather=None,
    scatter=None,
    ring=None,
    start=nothing,
    first=nothing,
    early=nothing,
    later=nothing,
    between=nothing,
    halfway=nothing,
    middle=nothing,
    end=nothing,
    near_first=False,
    greeting=True,
):
    send, recv, lsem = sems
    sq = Square(send, recv, rows)
    core = sq.core
    if greeting:
        greet(sq.others + ([{"dp": ring.left}, {"dp": ring.right}] if ring is not None else []))

    def place(rel, turn):
        chip_y = (sq.y + rel % 2) % 2
        chip_x = (sq.x + ((rel + 1) // 2) % 2) % 2
        return chip_y * 2 + chip_x, (1 - core + turn) % 2

    if gather is not None:
        compute, share, full, gbuf = gather
        c_own = sq.copy(0, share, gbuf.at[sq.own, core], sq.peer)
        x_a = sq.copy(1, share.at[sq.a], gbuf.at[sq.own, core, sq.a], sq.xn)
        y_b = sq.copy(2, share.at[sq.b], gbuf.at[sq.own, core, sq.b], sq.yn)
        f_x = sq.copy(3, gbuf.at[sq.yc, core, sq.b], gbuf.at[sq.yc, core, sq.b], sq.xn)
        f_y = sq.copy(4, gbuf.at[sq.xc, core, sq.a], gbuf.at[sq.xc, core, sq.a], sq.yn)
        x_b = sq.copy(5, share.at[sq.b], gbuf.at[sq.own, core, sq.b], sq.xn)
        y_a = sq.copy(6, share.at[sq.a], gbuf.at[sq.own, core, sq.a], sq.yn)
        c_d = sq.copy(7, gbuf.at[sq.dc, core], gbuf.at[sq.dc, core], sq.peer)
        c_x = sq.copy(8, gbuf.at[sq.xc, core], gbuf.at[sq.xc, core], sq.peer)
        c_y = sq.copy(9, gbuf.at[sq.yc, core], gbuf.at[sq.yc, core], sq.peer)
        local = pltpu.make_async_copy(share, gbuf.at[sq.own, core], lsem.at[8])
        x_a.start()
        y_b.start()
        if near_first:
            x_b.start()
            y_a.start()
        c_own.start()
        local.start()
    start()
    if gather is not None:

        def take_own():
            c_own.wait_recv()
            local.wait()
            first()

        def forward():
            x_a.wait_recv()
            y_b.wait_recv()
            f_x.start()
            f_y.start()
            if not near_first:
                x_b.start()
                y_a.start()
            early()

        def take_far():
            f_x.wait_recv()
            f_y.wait_recv()
            c_d.start()
            c_d.wait_recv()

        def take_near():
            x_b.wait_recv()
            y_a.wait_recv()
            c_x.start()
            c_y.start()
            later()
            c_x.wait_recv()
            c_y.wait_recv()

        def gather_step(t, carry):
            unit = t // 2
            if near_first:
                chip_y = (sq.y + unit // 2) % 2
                chip_x = (sq.x + unit % 2) % 2
                chip, which = chip_y * 2 + chip_x, (1 - core + t % 2) % 2
            else:
                chip, which = place(unit, t % 2)

            pl.when(t == 0)(take_own)

            @pl.when(t == 2)
            def _():
                forward()
                if near_first:
                    take_near()
                else:
                    take_far()

            pl.when(t == (6 if near_first else 4))(take_far if near_first else take_near)

            if full is not None:
                pltpu.make_async_copy(gbuf.at[chip, which], full.at[chip, which], lsem.at[t]).start()
            compute(t, chip, which)
            return carry

        lax.fori_loop(0, 8 if scatter is None else 6, gather_step, 0)
    between()
    if scatter is not None:
        finish_tile, pbuf, (rcore, rxd, ryd, rx, ry), emit = scatter
        x_d = sq.copy(14, pbuf.at[sq.dc, core, sq.a], rxd, sq.xn)
        y_d = sq.copy(15, pbuf.at[sq.dc, core, sq.b], ryd, sq.yn)
        x_ra = sq.copy(16, pbuf.at[sq.xc, core, sq.a], rx.at[sq.a], sq.xn)
        y_rb = sq.copy(17, pbuf.at[sq.yc, core, sq.b], ry.at[sq.b], sq.yn)
        x_rb = sq.copy(18, pbuf.at[sq.xc, core, sq.b], rx.at[sq.b], sq.xn)
        y_ra = sq.copy(19, pbuf.at[sq.yc, core, sq.a], ry.at[sq.a], sq.yn)

        def scatter_step(t, carry):
            turn = t % 2
            rel = (t // 2 + 1) % 4
            chip, which = place(rel, turn)

            @pl.when(t == 4)
            def _():
                halfway()

            finish_tile(t, chip, which)
            to_peer = sq.copy(10 + rel, pbuf.at[chip, which], rcore.at[chip], sq.peer)

            @pl.when(turn == 0)
            def _():
                to_peer.start()

            @pl.when(turn == 1)
            def _():
                to_peer.wait_recv()
                add_rows(pbuf.at[chip, which], rcore.at[chip], rows)

            @pl.when(t == 1)
            def _():
                x_d.start()
                y_d.start()

            @pl.when(t == 3)
            def _():
                x_ra.start()

            @pl.when(t == 5)
            def _():
                y_rb.start()

            return carry

        if gather is None:
            lax.fori_loop(0, 8, scatter_step, 0)
        else:
            lax.fori_loop(0, 2, scatter_step, 0)
            lax.fori_loop(6, 8, gather_step, 0)
            lax.fori_loop(2, 8, scatter_step, 0)
        x_d.wait_recv()
        add_rows(pbuf.at[sq.yc, core, sq.a], rxd, sq.na)
        y_ra.start()
        y_d.wait_recv()
        add_rows(pbuf.at[sq.xc, core, sq.b], ryd, sq.nb)
        x_rb.start()
        middle()
        x_ra.wait_recv()
        y_rb.wait_recv()
        y_ra.wait_recv()
        x_rb.wait_recv()

        def last(i, carry):
            part = pl.ds(pl.multiple_of(i * EMIT, 16), EMIT)
            emit(
                part,
                pbuf[sq.own, core, part, :].astype(F32)
                + rx[part, :].astype(F32)
                + ry[part, :].astype(F32),
            )
            return carry

        lax.fori_loop(0, rows // EMIT, last, 0)
        for k in range(4):
            sq.copy(10 + k, pbuf.at[0, 0], rcore.at[0], sq.peer).wait_send()
        for copy in (x_d, y_d, x_ra, y_rb, x_rb, y_ra):
            copy.wait_send()
    end()
    if gather is not None:
        for copy in (c_own, x_a, y_b, f_x, f_y, x_b, y_a, c_d, c_x, c_y):
            copy.wait_send()
        if full is not None:
            for t in range(8):
                pltpu.make_async_copy(gbuf.at[0, 0], full.at[0, 0], lsem.at[t]).wait()


def row_mean(values):
    return jnp.mean(values, axis=-1, keepdims=True)


def norm_rows(values):
    centre = values - row_mean(values)
    inv_std = lax.rsqrt(row_mean(centre * centre) + norm_epsilon)
    return centre * inv_std, inv_std


def norm_rows_back(grads, normed, inv_std, gain):
    grad_normed = grads * gain
    return inv_std * (grad_normed - row_mean(grad_normed) - normed * row_mean(grad_normed * normed))


def fold(values):
    return sum(values[i : i + 8] for i in range(0, EMIT, 8))


def scatter_scratch(rows, width, with_sums=True):
    cut = rows // 2 // 16 * 16
    return ([pltpu.VMEM((4, 2, rows, width), BF16)] if with_sums else []) + [
        pltpu.VMEM((4, rows, width), BF16),
        pltpu.VMEM((cut, width), BF16),
        pltpu.VMEM((rows - cut, width), BF16),
        pltpu.VMEM((rows, width), BF16),
        pltpu.VMEM((rows, width), BF16),
    ]


SEMS = [
    pltpu.SemaphoreType.DMA((20,)),
    pltpu.SemaphoreType.DMA((20,)),
    pltpu.SemaphoreType.DMA((9,)),
]


def params(collective_id):
    return pltpu.CompilerParams(
        collective_id=collective_id, has_side_effects=True, vmem_limit_bytes=VMEM_BYTES
    )


def whole(shape):
    return pl.BlockSpec(shape, lambda *_: (0,) * len(shape))


def front_call(block_input, low_qkv, low_out, low_gateup, positions, prefix_len, w_norm, rows, spans):
    tokens, width = block_input.shape
    depth, cols = low_qkv.shape[1:]
    tiles = tokens // rows
    heads = cols // HEAD_DIM
    proteins = tokens // LEN
    scale = 1.0 / math.sqrt(HEAD_DIM)
    alpha = math.sqrt(2.0 * DEPTH)
    half = depth // 2
    out_half = cols // 2
    span = spans[-1][0] + spans[-1][1]

    def kernel(
        pre_ref, x_ref, low_ref, lo_ref, lg_ref, pos_ref, norm_ref,
        q_ref, k_ref, v_ref, o_ref, p_ref, cos_ref, sin_ref, w_ref, wo_ref, wg_ref,
        x1_ref, x1b_ref, n1_ref, inv_ref,
        x_buf, w_buf, acc, q_buf, k_buf, v_buf, o_buf, cos_buf, sin_buf, p_buf, wo_buf, xs_buf,
        rcore, rxd, ryd, rx, ry, xsem, psem, ksem, send, recv, lsem, zsend, zrecv, zlocal,
    ):
        ring = Ring(zsend, zrecv, zlocal)
        sems = Square(send, recv, rows)
        gather = RingGather(
            ring, 0, lambda h: low_ref.at[:, pl.ds(h * half, half), :], row_halves(depth)(w_buf)
        )
        gather_out = RingGather(
            ring, 6, lambda h: lo_ref.at[pl.ds(h * out_half, out_half), :], column_halves(depth)(wo_buf)
        )
        gathers = []
        for n, (low, size) in enumerate(spans):
            at = pl.ds(low, size)
            gathers.append(
                RingGather(
                    ring,
                    12 + 6 * n,
                    lambda h, at=at: lg_ref.at[h, at, :],
                    plane_columns(depth)(wg_ref.at[:, at, :]),
                )
            )
        own_rows = pltpu.make_async_copy(x_ref.at[sems.own, sems.core], xs_buf, xsem.at[8])
        kept = ((q_buf, q_ref), (k_buf, k_ref), (v_buf, v_ref), (cos_buf, cos_ref), (sin_buf, sin_ref))
        keeps = [pltpu.make_async_copy(src, dst, ksem.at[n]) for n, (src, dst) in enumerate(kept)]
        keep_w = pltpu.make_async_copy(w_buf, w_ref, ksem.at[5])
        keep_wo = pltpu.make_async_copy(wo_buf, wo_ref, ksem.at[6])
        keep_o = pltpu.make_async_copy(o_buf, o_ref, ksem.at[7])

        def x_copy(t):
            return pltpu.make_async_copy(x_ref.at[t // 2, t % 2], x_buf.at[t // 2, t % 2], xsem.at[t])

        def start_tile(t, carry):
            x_copy(t).start()
            return carry

        lax.fori_loop(0, tiles, start_tile, 0)
        own_rows.start()
        greet(sems.others + [{"dp": ring.left}, {"dp": ring.right}])
        gather.start()
        for copy in gather.own:
            copy.wait()

        def part(t, j, owner):
            depths = pl.ds(pl.multiple_of(owner * depth, depth), depth)
            return jnp.dot(
                x_buf[t // 2, t % 2, :, depths], w_buf[j, depths, :], preferred_element_type=F32
            )

        def tile_rows(t):
            return pl.ds(pl.multiple_of(t * rows, 16), rows)

        def own_tile(t, carry):
            x_copy(t).wait()
            for j in range(3):
                acc[t, j] = part(t, j, ring.here)
            return carry

        lax.fori_loop(0, tiles, own_tile, 0)
        lane = lax.broadcasted_iota(jnp.int32, (1, HEAD_DIM), 1)
        ladder = (lane % (HEAD_DIM // 2)).astype(F32)
        inverse = jnp.exp(ladder * (-2.0 * math.log(10000.0) / HEAD_DIM))
        sign = jnp.where(lane < HEAD_DIM // 2, -1.0, 1.0)

        def table_tile(t, carry):
            angles = pos_ref[t].astype(F32) * inverse
            cos_buf[tile_rows(t), :] = jnp.cos(angles)
            sin_buf[tile_rows(t), :] = jnp.sin(angles) * sign
            return carry

        lax.fori_loop(0, tiles // 2, table_tile, 0)
        gather.forward()
        gather_out.start()
        lax.fori_loop(tiles // 2, tiles, table_tile, 0)
        gather.near()

        def near_tile(t, carry):
            for j in range(3):
                acc[t, j] += part(t, j, ring.left) + part(t, j, ring.right)
            return carry

        lax.fori_loop(0, tiles, near_tile, 0)
        gather.far()
        gathers[0].start()
        keep_w.start()

        def far_tile(t, carry):
            here = tile_rows(t)
            for j, buf in enumerate((q_buf, k_buf)):
                a = acc[t, j] + part(t, j, ring.far)
                for h in range(heads):
                    cut = slice(h * HEAD_DIM, (h + 1) * HEAD_DIM)
                    turned = a[:, cut] * cos_buf[here, :]
                    turned += pltpu.roll(a[:, cut], HEAD_DIM // 2, 1) * sin_buf[here, :]
                    if j == 0:
                        turned = turned * scale
                    buf[here, cut] = turned.astype(BF16)
            v_buf[here, :] = (acc[t, 2] + part(t, 2, ring.far)).astype(BF16)
            return carry

        lax.fori_loop(0, tiles, far_tile, 0)
        gather_out.forward()
        for keep in keeps:
            keep.start()

        def protein(p, carry):
            prefix = pre_ref[p]
            keys = pl.ds(pl.multiple_of(p * LEN, LEN), LEN)

            @pl.when(p == proteins - 1)
            def _():
                gathers[0].forward()
                gathers[1].start()

            for h in range(heads):
                cut = slice(h * HEAD_DIM, (h + 1) * HEAD_DIM)
                store = pltpu.make_async_copy(p_buf.at[h], p_ref.at[p, h], psem.at[h])

                @pl.when(p > 0)
                def _():
                    store.wait()

                for i in range(LEN // BLOCK):
                    here = pl.ds(pl.multiple_of(p * LEN + i * BLOCK, BLOCK), BLOCK)
                    s = nt_dot(q_buf[here, cut], k_buf[keys, cut])
                    col = lax.broadcasted_iota(jnp.int32, s.shape, 1)
                    row = lax.broadcasted_iota(jnp.int32, (BLOCK, 1), 0) + i * BLOCK
                    s = jnp.where(col < jnp.maximum(prefix, row + 1), s, -1e30)
                    e = jnp.exp(s - jnp.max(s, axis=-1, keepdims=True))
                    prob = (e * (1.0 / jnp.sum(e, axis=-1, keepdims=True))).astype(BF16)
                    p_buf[h, i * BLOCK : (i + 1) * BLOCK, :] = prob
                    mixed = jnp.dot(prob, v_buf[keys, cut], preferred_element_type=F32)
                    o_buf[here, cut] = mixed.astype(BF16)
                store.start()
            return carry

        lax.fori_loop(0, proteins, protein, 0)
        for copy in gather_out.own:
            copy.wait()
        gather_out.near()
        gather_out.far()
        keep_wo.start()
        keep_o.start()
        own_rows.wait()

        def compute(t, chip, which):
            tile = o_buf[tile_rows(chip * 2 + which), :]
            x_buf[chip, which] = jnp.dot(tile, wo_buf[...], preferred_element_type=F32).astype(BF16)

        def emit(at, value):
            normed, inv_std = norm_rows(alpha * xs_buf[at, :].astype(F32) + value)
            x1 = normed * norm_ref[0:1, :] + norm_ref[1:2, :]
            x1_ref[at, :] = x1
            x1b_ref[at, :] = x1.astype(BF16)
            n1_ref[at, :] = normed
            inv_ref[at, :] = jnp.broadcast_to(inv_std, (EMIT, HEAD_DIM))

        square_kernel(
            rows,
            (send, recv, lsem),
            scatter=(compute, x_buf, (rcore, rxd, ryd, rx, ry), emit),
            middle=gathers[1].forward,
            greeting=False,
        )
        for other in gathers:
            other.finish()
        gather.drain()
        gather_out.drain()
        for keep in keeps + [keep_w, keep_wo, keep_o]:
            keep.wait()
        for h in range(heads):
            pltpu.make_async_copy(p_buf.at[h], p_ref.at[0, h], psem.at[h]).wait()

    wide = jax.ShapeDtypeStruct((rows, width), F32)
    return pl.pallas_call(
        kernel,
        out_shape=[jax.ShapeDtypeStruct((tokens, cols), BF16)] * 4
        + [jax.ShapeDtypeStruct((proteins, heads, LEN, LEN), BF16)]
        + [jax.ShapeDtypeStruct((tokens, HEAD_DIM), F32)] * 2
        + [
            jax.ShapeDtypeStruct((3, width, cols), BF16),
            jax.ShapeDtypeStruct((cols, width), BF16),
            jax.ShapeDtypeStruct((2, span, width), BF16),
            wide,
            jax.ShapeDtypeStruct((rows, width), BF16),
            wide,
            jax.ShapeDtypeStruct((rows, HEAD_DIM), F32),
        ],
        in_specs=[pl.BlockSpec(memory_space=pltpu.SMEM)] + [ANY] * 4 + [VM, VM],
        out_specs=[ANY] * 10 + [VM] * 4,
        scratch_shapes=[
            pltpu.VMEM((4, 2, rows, width), BF16),
            pltpu.VMEM((3, width, cols), BF16),
            pltpu.VMEM((tiles, 3, rows, cols), F32),
        ]
        + [pltpu.VMEM((tokens, cols), BF16)] * 4
        + [pltpu.VMEM((tokens, HEAD_DIM), F32)] * 2
        + [
            pltpu.VMEM((heads, LEN, LEN), BF16),
            pltpu.VMEM((cols, width), BF16),
            pltpu.VMEM((rows, width), BF16),
        ]
        + scatter_scratch(rows, width, False)
        + [
            pltpu.SemaphoreType.DMA((9,)),
            pltpu.SemaphoreType.DMA((heads,)),
            pltpu.SemaphoreType.DMA((8,)),
        ]
        + SEMS
        + ring_sems(12 + 6 * len(spans)),
        compiler_params=params(0),
        cost_estimate=LIGHT,
        name="front",
    )(
        prefix_len,
        block_input.reshape(4, 2, rows, width),
        low_qkv,
        low_out,
        low_gateup,
        positions.reshape(tiles, rows, 1),
        w_norm,
    )


BLOCK = 128
TN = (((0,), (0,)), ((), ()))


def attention_back_call(
    queries, key_rows, value_rows, probs, attended, grad_attended, cos_table, sin_table, norm_terms,
    grad_out_part,
):
    tokens, cols = queries.shape
    proteins = tokens // LEN
    heads = cols // HEAD_DIM
    scale = 1.0 / math.sqrt(HEAD_DIM)
    last = proteins * heads - 1
    depth = grad_out_part.shape[1] // 4

    def kernel(
        q_ref, k_ref, v_ref, p_ref, o_ref, do_ref, cos_ref, sin_ref, nt_ref, go_ref,
        da_ref, norm_ref, red_o,
        dk_acc, dv_acc, sums, got, nsend, nrecv, buf_o, send, recv, local,
    ):
        step = pl.program_id(0) * heads + pl.program_id(1)
        ring = Ring(send, recv, local)
        part = cols // 2
        side = RingScatter(
            ring, 0, column_halves(depth)(go_ref), buf_o, lambda h: red_o.at[pl.ds(h * part, part), :]
        )
        sq = Square(nsend, nrecv, 32)
        partners = [
            {"mp": sq.peer},
            {"mp": sq.xn},
            {"mp": sq.yn},
            {"dp": ring.here + 1 - 2 * (ring.here % 2)},
            {"dp": 3 - ring.here},
        ]
        swaps = [
            pltpu.make_async_remote_copy(
                src_ref=sums.at[k],
                dst_ref=got.at[k],
                send_sem=nsend.at[k],
                recv_sem=nrecv.at[k],
                device_id=other,
                device_id_type=MESH,
            )
            for k, other in enumerate(partners)
        ]

        @pl.when(step == 0)
        def _():
            sums[0] = nt_ref[...]
            greet(sq.others + [{"dp": ring.left}, {"dp": ring.right}])
            side.start()
            swaps[0].start()

        for k in range(5):

            @pl.when(step == k + 1)
            def _():
                swaps[k].wait()
                if k < 4:
                    sums[k + 1] = sums[k] + got[k]
                    swaps[k + 1].start()
                else:
                    norm_ref[...] = sums[k] + got[k]

        @pl.when(step == last // 2)
        def _():
            side.forward()

        for i in range(LEN // BLOCK):
            rows = slice(i * BLOCK, (i + 1) * BLOCK)
            do = do_ref[rows, :]
            p = p_ref[0, 0, rows, :]
            delta = jnp.sum(do.astype(F32) * o_ref[rows, :].astype(F32), axis=-1, keepdims=True)
            dp = nt_dot(do, v_ref[...])
            ds = (p.astype(F32) * (dp - delta)).astype(BF16)
            dv = lax.dot_general(p, do, TN, preferred_element_type=F32)
            dk = lax.dot_general(ds, q_ref[rows, :], TN, preferred_element_type=F32)
            if i == 0:
                dv_acc[...] = dv
                dk_acc[...] = dk
            else:
                dv_acc[...] += dv
                dk_acc[...] += dk
            dq = jnp.dot(ds, k_ref[...], preferred_element_type=F32)
            turned = dq * cos_ref[rows, :] - pltpu.roll(dq, HEAD_DIM // 2, 1) * sin_ref[rows, :]
            da_ref[0, rows, :] = (turned * scale).astype(BF16)
        dk = dk_acc[...]
        turned = dk * cos_ref[...] - pltpu.roll(dk, HEAD_DIM // 2, 1) * sin_ref[...]
        da_ref[1] = turned.astype(BF16)
        da_ref[2] = dv_acc[...].astype(BF16)

        @pl.when(step == last)
        def _():
            side.finish()

    tile = pl.BlockSpec((LEN, HEAD_DIM), lambda p, h: (p, h))
    table = pl.BlockSpec((LEN, HEAD_DIM), lambda p, h: (p, 0))
    return pl.pallas_call(
        kernel,
        grid=(proteins, heads),
        in_specs=[tile] * 3
        + [pl.BlockSpec((1, 1, LEN, LEN), lambda p, h: (p, h, 0, 0)), tile, tile, table, table]
        + [whole(norm_terms.shape), ANY],
        out_specs=[
            pl.BlockSpec((3, LEN, HEAD_DIM), lambda p, h: (0, p, h)),
            whole(norm_terms.shape),
            whole((cols, depth)),
        ],
        out_shape=[
            jax.ShapeDtypeStruct((3, tokens, cols), BF16),
            jax.ShapeDtypeStruct(norm_terms.shape, F32),
            jax.ShapeDtypeStruct((cols, depth), F32),
        ],
        scratch_shapes=[
            pltpu.VMEM((LEN, HEAD_DIM), F32),
            pltpu.VMEM((LEN, HEAD_DIM), F32),
            pltpu.VMEM((5,) + norm_terms.shape, F32),
            pltpu.VMEM((5,) + norm_terms.shape, F32),
            pltpu.SemaphoreType.DMA((5,)),
            pltpu.SemaphoreType.DMA((5,)),
            pltpu.VMEM((10, cols // 2, depth), BF16),
        ]
        + ring_sems(6),
        compiler_params=params(7),
        cost_estimate=LIGHT,
        name="attention_back",
    )(
        queries,
        key_rows,
        value_rows,
        probs,
        attended,
        grad_attended,
        cos_table,
        sin_table,
        norm_terms,
        grad_out_part,
    )


def ffn_call(middle_low, middle_share, w_gateup, low_down, cotangent, row_weight, w_norm):
    rows = middle_low.shape[0]
    live, depth = low_down.shape
    curve = math.sqrt(2.0 / math.pi)
    alpha = math.sqrt(2.0 * DEPTH)

    def kernel(
        share, x1_ref, wg_ref, ld_ref, cot_ref, rw_ref, norm_ref,
        y_ref, dh_ref, dhb_ref, terms_ref, full, hid_ref, act_ref, pull_ref, wd_ref,
        w_g, w_d, gbuf, hid_buf, stage, pbuf, rcore, rxd, ryd, rx, ry, sums,
        wsem, osem, hsem, send, recv, lsem, zsend, zrecv, zlocal,
    ):
        ring = Ring(zsend, zrecv, zlocal)
        half = live // 2
        gather_d = RingGather(ring, 0, lambda h: ld_ref.at[pl.ds(h * half, half), :], column_halves(depth)(w_d))
        load_g = pltpu.make_async_copy(wg_ref, w_g, wsem.at[0])
        load_g.start()
        keep_d = pltpu.make_async_copy(w_d, wd_ref, wsem.at[1])
        outs = (act_ref, pull_ref)

        def between():
            for copy in gather_d.own:
                copy.wait()
            gather_d.near()
            gather_d.far()
            keep_d.start()

        def compute(t, chip, which):
            slot = t % 2

            @pl.when(t >= 2)
            def _():
                for k, ref in enumerate(outs):
                    pltpu.make_async_copy(stage.at[slot, k], ref.at[chip, which], osem.at[slot, k]).wait()

            tile = gbuf[chip, which]
            gate = nt_dot(tile, w_g[0])
            up = nt_dot(tile, w_g[1])
            square = gate * gate
            bent = jnp.tanh(curve * gate * (1.0 + 0.044715 * square))
            half = 0.5 * (1.0 + bent)
            act = gate * half
            slope = half + 0.5 * curve * gate * (1.0 - bent * bent) * (1.0 + 3.0 * 0.044715 * square)
            hid_buf[chip, which] = (act * up).astype(BF16)
            stage[slot, 0] = act.astype(BF16)
            stage[slot, 1] = (slope * up).astype(BF16)
            for k, ref in enumerate(outs):
                pltpu.make_async_copy(stage.at[slot, k], ref.at[chip, which], osem.at[slot, k]).start()
            pltpu.make_async_copy(hid_buf.at[chip, which], hid_ref.at[chip, which], hsem.at[t]).start()

        def finish_tile(t, chip, which):
            part = jnp.dot(hid_buf[chip, which], w_d[...], preferred_element_type=F32)
            pbuf[chip, which] = part.astype(BF16)

        def emit(at, value):
            normed, inv_std = norm_rows(alpha * x1_ref[at, :] + value)
            gain = norm_ref[2:3, :]
            y_ref[at, :] = (normed * gain + norm_ref[3:4, :]).astype(BF16)
            dy = cot_ref[at, :].astype(F32) * rw_ref[at, :]
            sums[0] += fold(dy * normed)
            sums[1] += fold(dy)
            dh = norm_rows_back(dy, normed, inv_std, gain)
            dh_ref[at, :] = dh
            dhb_ref[at, :] = dh.astype(BF16)

        sums[...] = jnp.zeros_like(sums)

        def end():
            terms_ref[...] = jnp.sum(sums[...], axis=1)
            for slot in range(2):
                for k, ref in enumerate(outs):
                    pltpu.make_async_copy(stage.at[slot, k], ref.at[0, 0], osem.at[slot, k]).wait()
            for t in range(8):
                pltpu.make_async_copy(hid_buf.at[0, 0], hid_ref.at[0, 0], hsem.at[t]).wait()
            keep_d.wait()
            gather_d.drain()

        square_kernel(
            rows,
            (send, recv, lsem),
            gather=(compute, share, full, gbuf),
            scatter=(finish_tile, pbuf, (rcore, rxd, ryd, rx, ry), emit),
            ring=ring,
            start=gather_d.start,
            first=load_g.wait,
            later=gather_d.forward,
            between=between,
            end=end,
        )

    kept = jax.ShapeDtypeStruct((4, 2, rows, live), BF16)
    return pl.pallas_call(
        kernel,
        out_shape=[
            jax.ShapeDtypeStruct((rows, D), BF16),
            jax.ShapeDtypeStruct((rows, D), F32),
            jax.ShapeDtypeStruct((rows, D), BF16),
            jax.ShapeDtypeStruct((2, D), F32),
            jax.ShapeDtypeStruct((4, 2, rows, D), BF16),
            kept,
            kept,
            kept,
            jax.ShapeDtypeStruct((live, D), BF16),
        ],
        in_specs=[ANY, VM, ANY, ANY, VM, VM, VM],
        out_specs=[VM] * 4 + [ANY] * 5,
        scratch_shapes=[
            pltpu.VMEM((2, live, D), BF16),
            pltpu.VMEM((live, D), BF16),
            pltpu.VMEM((4, 2, rows, D), BF16),
            pltpu.VMEM((4, 2, rows, live), BF16),
            pltpu.VMEM((2, 2, rows, live), BF16),
        ]
        + scatter_scratch(rows, D)
        + [
            pltpu.VMEM((2, 8, D), F32),
            pltpu.SemaphoreType.DMA((2,)),
            pltpu.SemaphoreType.DMA((2, 2)),
            pltpu.SemaphoreType.DMA((8,)),
        ]
        + SEMS
        + ring_sems(6),
        compiler_params=params(1),
        cost_estimate=LIGHT,
        name="ffn",
    )(middle_low, middle_share, w_gateup, low_down, cotangent, row_weight, w_norm)


def ffn_back_call(ffn_grad, act, pull, w_down):
    rows = ffn_grad.shape[0]
    live = w_down.shape[0]

    def kernel(share, act_ref, pull_ref, wd_ref, full, dg_ref, w_d, gbuf, load, stage, wsem, isem, osem, send, recv, lsem):
        weight = pltpu.make_async_copy(wd_ref, w_d, wsem.at[0])
        weight.start()

        def compute(t, chip, which):
            slot = t % 2
            loads = [
                pltpu.make_async_copy(ref.at[chip, which], load.at[k], isem.at[k])
                for k, ref in enumerate((act_ref, pull_ref))
            ]
            stores = [
                pltpu.make_async_copy(stage.at[slot, k], dg_ref.at[k, chip, which], osem.at[slot, k])
                for k in range(2)
            ]
            for copy in loads:
                copy.start()

            @pl.when(t >= 2)
            def _():
                for copy in stores:
                    copy.wait()

            dh = nt_dot(gbuf[chip, which], w_d[...])
            for copy in loads:
                copy.wait()
            stage[slot, 0] = (dh * load[1].astype(F32)).astype(BF16)
            stage[slot, 1] = (dh * load[0].astype(F32)).astype(BF16)
            for copy in stores:
                copy.start()

        def end():
            for slot in range(2):
                for k in range(2):
                    pltpu.make_async_copy(stage.at[slot, k], dg_ref.at[k, 0, 0], osem.at[slot, k]).wait()

        square_kernel(
            rows,
            (send, recv, lsem),
            gather=(compute, share, full, gbuf),
            first=weight.wait,
            end=end,
            near_first=True,
        )

    return pl.pallas_call(
        kernel,
        out_shape=[
            jax.ShapeDtypeStruct((4, 2, rows, D), BF16),
            jax.ShapeDtypeStruct((2, 4, 2, rows, live), BF16),
        ],
        in_specs=[ANY] * 4,
        out_specs=[ANY, ANY],
        scratch_shapes=[
            pltpu.VMEM((live, D), BF16),
            pltpu.VMEM((4, 2, rows, D), BF16),
            pltpu.VMEM((2, rows, live), BF16),
            pltpu.VMEM((2, 2, rows, live), BF16),
            pltpu.SemaphoreType.DMA((1,)),
            pltpu.SemaphoreType.DMA((2,)),
            pltpu.SemaphoreType.DMA((2, 2)),
        ]
        + SEMS,
        compiler_params=params(2),
        cost_estimate=LIGHT,
        name="ffn_back",
    )(ffn_grad, act, pull, w_down)


def middle_back_call(grad_gateup_rows, w_gateup, grad_gateup_part, spans, grad_h2, normed, inv_std, w_norm):
    rows = grad_h2.shape[0]
    alpha = math.sqrt(2.0 * DEPTH)
    live, width = grad_gateup_part.shape[1:]
    depth = width // 4

    def kernel(
        dg_ref, wg_ref, gg_ref, dh2_ref, n1_ref, inv_ref, norm_ref, dh_ref, dhb_ref, terms_ref, red_0, red_1,
        w_g, load, buf_0, buf_1, pbuf, rcore, rxd, ryd, rx, ry, sums, wsem, isem, send, recv, lsem, zsend, zrecv, zlocal,
    ):
        ring = Ring(zsend, zrecv, zlocal)
        early = span_scatter(ring, 0, gg_ref, spans[0], buf_0, red_0)
        late = span_scatter(ring, 6, gg_ref, spans[1], buf_1, red_1)
        weight = pltpu.make_async_copy(wg_ref, w_g, wsem.at[0])
        weight.start()
        me = lax.axis_index("mp")
        core, x, y = me % 2, (me // 2) % 2, me // 4

        def loads(t):
            rel = (t // 2 + 1) % 4
            chip = ((y + rel % 2) % 2) * 2 + (x + ((rel + 1) // 2) % 2) % 2
            which = (1 - core + t % 2) % 2
            return [
                pltpu.make_async_copy(dg_ref.at[k, chip, which], load.at[t % 2, k], isem.at[t % 2, k])
                for k in range(2)
            ]

        for copy in loads(0):
            copy.start()

        def compute(t, chip, which):
            @pl.when(t < 7)
            def _():
                for copy in loads(t + 1):
                    copy.start()

            for copy in loads(t):
                copy.wait()
            slot = t % 2
            part = jnp.dot(load[slot, 0], w_g[0], preferred_element_type=F32)
            part += jnp.dot(load[slot, 1], w_g[1], preferred_element_type=F32)
            pbuf[chip, which] = part.astype(BF16)

        sums[...] = jnp.zeros_like(sums)

        def emit(at, value):
            grads = value + alpha * dh2_ref[at, :]
            normed = n1_ref[at, :]
            sums[0] += fold(grads * normed)
            sums[1] += fold(grads)
            dh = norm_rows_back(grads, normed, inv_ref[at, 0:1], norm_ref[0:1, :])
            dh_ref[at, :] = dh
            dhb_ref[at, :] = dh.astype(BF16)

        def end():
            terms_ref[...] = jnp.sum(sums[...], axis=1)
            early.finish()
            late.finish()

        square_kernel(
            rows,
            (send, recv, lsem),
            scatter=(compute, pbuf, (rcore, rxd, ryd, rx, ry), emit),
            ring=ring,
            start=lambda: (early.start(), weight.wait()),
            halfway=lambda: (early.forward(), late.start()),
            middle=late.forward,
            end=end,
        )

    return pl.pallas_call(
        kernel,
        out_shape=[
            jax.ShapeDtypeStruct((rows, D), F32),
            jax.ShapeDtypeStruct((rows, D), BF16),
            jax.ShapeDtypeStruct((2, D), F32),
            jax.ShapeDtypeStruct((2, spans[0][1], depth), F32),
            jax.ShapeDtypeStruct((2, spans[1][1], depth), F32),
        ],
        in_specs=[ANY] * 3 + [VM] * 4,
        out_specs=[VM] * 5,
        scratch_shapes=[
            pltpu.VMEM((2, live, D), BF16),
            pltpu.VMEM((2, 2, rows, live), BF16),
            pltpu.VMEM((10, spans[0][1], depth), BF16),
            pltpu.VMEM((10, spans[1][1], depth), BF16),
        ]
        + scatter_scratch(rows, D)
        + [pltpu.VMEM((2, 8, D), F32)]
        + [pltpu.SemaphoreType.DMA((1,)), pltpu.SemaphoreType.DMA((2, 2))]
        + SEMS
        + ring_sems(12),
        compiler_params=params(8),
        cost_estimate=LIGHT,
        name="middle_back",
    )(grad_gateup_rows, w_gateup, grad_gateup_part, grad_h2, normed, inv_std, w_norm)


def out_back_call(attn_grad, w_out, attended, grad_gateup_part, span):
    rows = attn_grad.shape[0]
    cols = w_out.shape[0]
    depth = grad_gateup_part.shape[2] // 4

    def kernel(
        share, w_ref, o_ref, gg_ref, dout, go_ref, red,
        w_buf, gbuf, buf, acc, wsem, send, recv, lsem, zsend, zrecv, zlocal,
    ):
        ring = Ring(zsend, zrecv, zlocal)
        side = span_scatter(ring, 0, gg_ref, span, buf, red)
        weight = pltpu.make_async_copy(w_ref, w_buf, wsem.at[0])
        weight.start()

        def compute(t, chip, which):
            tile = gbuf[chip, which]
            dout[chip, which] = nt_dot(tile, w_buf[...]).astype(BF16)
            part = lax.dot_general(o_ref[chip, which], tile, TN, preferred_element_type=F32)

            @pl.when(t == 0)
            def _():
                acc[...] = part

            @pl.when(t > 0)
            def _():
                acc[...] += part

        def end():
            go_ref[...] = acc[...].astype(BF16)
            side.finish()

        square_kernel(
            rows,
            (send, recv, lsem),
            gather=(compute, share, None, gbuf),
            ring=ring,
            start=side.start,
            first=weight.wait,
            early=side.forward,
            end=end,
            near_first=True,
        )

    return pl.pallas_call(
        kernel,
        out_shape=[
            jax.ShapeDtypeStruct((4, 2, rows, cols), BF16),
            jax.ShapeDtypeStruct((cols, D), BF16),
            jax.ShapeDtypeStruct((2, span[1], depth), F32),
        ],
        in_specs=[ANY, ANY, VM, ANY],
        out_specs=[VM, VM, VM],
        scratch_shapes=[
            pltpu.VMEM((cols, D), BF16),
            pltpu.VMEM((4, 2, rows, D), BF16),
            pltpu.VMEM((10, span[1], depth), BF16),
            pltpu.VMEM((cols, D), F32),
            pltpu.SemaphoreType.DMA((1,)),
        ]
        + SEMS
        + ring_sems(6),
        compiler_params=params(3),
        cost_estimate=LIGHT,
        name="out_back",
    )(attn_grad, w_out, attended.reshape(4, 2, rows, cols), grad_gateup_part)


def input_back_call(grad_proj, w_qkv, grad_qkv_part, grad_h1):
    rows = grad_h1.shape[0]
    alpha = math.sqrt(2.0 * DEPTH)
    width, cols = w_qkv.shape[1:]
    depth = width // 4

    def kernel(
        da_ref, w_ref, gq_ref, dh_ref, out, red_q,
        w_buf, buf_q, pbuf, rcore, rxd, ryd, rx, ry, wsem, send, recv, lsem, zsend, zrecv, zlocal,
    ):
        ring = Ring(zsend, zrecv, zlocal)
        half = depth // 2
        side = RingScatter(
            ring, 0, row_halves(depth)(gq_ref), buf_q, lambda h: red_q.at[:, pl.ds(h * half, half), :]
        )
        weight = pltpu.make_async_copy(w_ref, w_buf, wsem.at[0])
        weight.start()

        def start():
            side.start()
            weight.wait()

        def compute(t, chip, which):
            part = nt_dot(da_ref[0, chip, which], w_buf[0])
            part += nt_dot(da_ref[1, chip, which], w_buf[1])
            part += nt_dot(da_ref[2, chip, which], w_buf[2])
            pbuf[chip, which] = part.astype(BF16)

        def emit(at, value):
            out[at, :] = (value + alpha * dh_ref[at, :]).astype(BF16)

        square_kernel(
            rows,
            (send, recv, lsem),
            scatter=(compute, pbuf, (rcore, rxd, ryd, rx, ry), emit),
            ring=ring,
            start=start,
            middle=side.forward,
            end=side.finish,
        )

    return pl.pallas_call(
        kernel,
        out_shape=[
            jax.ShapeDtypeStruct((rows, D), BF16),
            jax.ShapeDtypeStruct((3, depth, cols), F32),
        ],
        in_specs=[VM, ANY, ANY, VM],
        out_specs=[VM, VM],
        scratch_shapes=[
            pltpu.VMEM((3, D, cols), BF16),
            pltpu.VMEM((10, 3, depth // 2, cols), BF16),
        ]
        + scatter_scratch(rows, D)
        + [pltpu.SemaphoreType.DMA((1,))]
        + SEMS
        + ring_sems(6),
        compiler_params=params(4),
        cost_estimate=LIGHT,
        name="input_back",
    )(grad_proj.reshape(3, 4, 2, rows, cols), w_qkv, grad_qkv_part, grad_h1)


FRONT_SPANS = ((0, 240), (240, 464))
SPANS = ((0, 144), (144, 144), (288, 416))


def body_ring(
    block_input,
    cotangent,
    prefix_len,
    cluster_id,
    positions,
    step_count,
    master_qkv,
    first_qkv,
    second_qkv,
    master_out,
    first_out,
    second_out,
    master_gateup,
    first_gateup,
    second_gateup,
    master_down,
    first_down,
    second_down,
    master_norm,
    first_norm,
    second_norm,
):
    token_count = block_input.shape[0]
    protein_count = token_count // LEN
    share_rows = cotangent.shape[0]
    share_start = lax.axis_index("mp") * share_rows

    low_qkv = master_qkv.astype(BF16)
    low_out = master_out.astype(BF16)
    low_gateup = jnp.swapaxes(master_gateup, 1, 2).astype(BF16)
    low_down = master_down.astype(BF16)
    w_norm = lax.optimization_barrier(master_norm.astype(BF16)).astype(F32)

    (
        queries, key_rows, value_rows, attended, probs, cos_table, sin_table, w_qkv, w_out, w_gateup,
        middle_share, middle_low, normed_one, inv_one,
    ) = front_call(
        block_input, low_qkv, low_out, low_gateup, positions, prefix_len, w_norm, share_rows, FRONT_SPANS
    )
    matches = (cluster_id[:, None] == cluster_id[None, :]).astype(F32)
    counts = jnp.sum(matches, axis=1)
    group_counts = lax.dynamic_slice_in_dim(
        counts, lax.axis_index("dp") * protein_count, protein_count, 0
    )
    row_protein = (share_start + jnp.arange(share_rows)) // LEN
    one_hot = (row_protein[:, None] == jnp.arange(protein_count)[None, :]).astype(F32)
    row_weight = jnp.sum(one_hot * (1.0 / group_counts)[None, :], axis=1)
    block_output, grad_h2, grad_h2_low, terms_two, middle_low, hidden, act, pull, w_down = ffn_call(
        middle_low, middle_share, w_gateup, low_down, cotangent, row_weight[:, None], w_norm
    )
    ffn_grad, grad_gateup_rows = ffn_back_call(grad_h2_low, act, pull, w_down)
    hidden = hidden.reshape(token_count, -1)
    middle_low = middle_low.reshape(token_count, D)
    ffn_grad = ffn_grad.reshape(token_count, D)
    gateup_rows = grad_gateup_rows.reshape(2, token_count, -1)
    grad_down_part = jnp.einsum("tf,td->fd", hidden, ffn_grad, preferred_element_type=F32).astype(BF16)
    red_down = lax.psum_scatter(grad_down_part, "dp", scatter_dimension=1, tiled=True).astype(F32)
    gateup_rows, grad_gateup_rows, grad_down_part = lax.optimization_barrier(
        (gateup_rows, grad_gateup_rows, grad_down_part)
    )
    grad_gateup_part = jnp.einsum(
        "jtf,td->jfd", gateup_rows, middle_low, preferred_element_type=F32
    ).astype(BF16)
    grad_h1, grad_h1_low, terms_one, red_gateup_0, red_gateup_1 = middle_back_call(
        grad_gateup_rows, w_gateup, grad_gateup_part, SPANS[:2], grad_h2, normed_one, inv_one, w_norm
    )
    grad_attended, grad_out_part, red_gateup_2 = out_back_call(
        grad_h1_low, w_out, attended, grad_gateup_part, SPANS[2]
    )
    grad_attended = grad_attended.reshape(token_count, -1)
    norm_terms = jnp.concatenate([terms_one, terms_two])
    grad_proj, grad_norm, red_out = attention_back_call(
        queries,
        key_rows,
        value_rows,
        probs,
        attended,
        grad_attended,
        cos_table,
        sin_table,
        norm_terms,
        grad_out_part,
    )
    red_gateup = jnp.swapaxes(
        jnp.concatenate([red_gateup_0, red_gateup_1, red_gateup_2], axis=1), 1, 2
    )
    grad_qkv_part = jnp.einsum("td,jtc->jdc", block_input, grad_proj, preferred_element_type=F32).astype(BF16)
    grad_input, red_qkv = input_back_call(grad_proj, w_qkv, grad_qkv_part, grad_h1)

    step_value = step_count[0].astype(F32)
    rate_qkv = D ** (-0.5)
    rate_out = max(HEADS * HEAD_DIM // 512, 1) ** (-0.5)
    rate_gateup = D ** (-0.5)
    rate_down = max(FF // 64, 1) ** (-0.5)
    rate_norm = 1.0
    new_qkv, new_first_qkv, new_second_qkv = adamw_step(
        master_qkv, first_qkv, second_qkv, red_qkv, rate_qkv, step_value
    )
    new_out, new_first_out, new_second_out = adamw_step(
        master_out, first_out, second_out, red_out, rate_out, step_value
    )
    new_gateup, new_first_gateup, new_second_gateup = adamw_step(
        master_gateup, first_gateup, second_gateup, red_gateup, rate_gateup, step_value
    )
    new_down, new_first_down, new_second_down = adamw_step(
        master_down, first_down, second_down, red_down, rate_down, step_value
    )
    new_norm, new_first_norm, new_second_norm = adamw_step(
        master_norm, first_norm, second_norm, grad_norm, rate_norm, step_value
    )
    return (
        block_output,
        grad_input,
        red_qkv,
        new_qkv,
        new_first_qkv,
        new_second_qkv,
        red_out,
        new_out,
        new_first_out,
        new_second_out,
        red_gateup,
        new_gateup,
        new_first_gateup,
        new_second_gateup,
        red_down,
        new_down,
        new_first_down,
        new_second_down,
        grad_norm,
        new_norm,
        new_first_norm,
        new_second_norm,
    )


def solution(mesh):
    placed = (
        P("dp", None),
        P(("dp", "mp"), None),
        P("dp"),
        P(),
        P("dp"),
        P(),
        P(None, "dp", "mp"),
        P(None, "dp", "mp"),
        P(None, "dp", "mp"),
        P("mp", "dp"),
        P("mp", "dp"),
        P("mp", "dp"),
        P(None, "dp", "mp"),
        P(None, "dp", "mp"),
        P(None, "dp", "mp"),
        P("mp", "dp"),
        P("mp", "dp"),
        P("mp", "dp"),
        P(),
        P(),
        P(),
    )
    ring = mesh.shape["dp"] == 4 and mesh.shape["mp"] == 8
    return jax.shard_map(
        body_ring if ring else body_plain,
        mesh=mesh,
        in_specs=placed,
        out_specs=(
            P(("dp", "mp"), None),
            P(("dp", "mp"), None),
            P(None, "dp", "mp"),
            P(None, "dp", "mp"),
            P(None, "dp", "mp"),
            P(None, "dp", "mp"),
            P("mp", "dp"),
            P("mp", "dp"),
            P("mp", "dp"),
            P("mp", "dp"),
            P(None, "dp", "mp"),
            P(None, "dp", "mp"),
            P(None, "dp", "mp"),
            P(None, "dp", "mp"),
            P("mp", "dp"),
            P("mp", "dp"),
            P("mp", "dp"),
            P("mp", "dp"),
            P(),
            P(),
            P(),
            P(),
        ),
        check_vma=False,
    )
```

```python
import functools
import math

import jax
import jax.numpy as jnp
from jax import lax
from jax.experimental import pallas as pl
from jax.experimental.pallas import tpu as pltpu
from jax.sharding import PartitionSpec as P

D = 2048
HEADS = 16
HEAD_DIM = 128
FF = 5632
DEPTH = 24
LEN = 896


beta_one = 0.9
beta_two = 0.95
adam_epsilon = 1e-08
decay_weight = 0.1
norm_epsilon = 1e-05


def norm_forward(hidden_rows, gain, offset):
    centre = hidden_rows - jnp.mean(hidden_rows, axis=-1, keepdims=True)
    inv_std = lax.rsqrt(jnp.mean(centre * centre, axis=-1, keepdims=True) + norm_epsilon)
    normed = centre * inv_std
    return (normed * gain + offset, normed, inv_std)


def norm_backward(grad_rows, normed, inv_std, gain):
    grad_normed = grad_rows * gain
    first_term = jnp.mean(grad_normed, axis=-1, keepdims=True)
    second_term = jnp.mean(grad_normed * normed, axis=-1, keepdims=True)
    grad_hidden = inv_std * (grad_normed - first_term - normed * second_term)
    return (grad_hidden, jnp.sum(grad_rows * normed, axis=0), jnp.sum(grad_rows, axis=0))


def rotate_half(values):
    middle = values.shape[-1] // 2
    return jnp.concatenate([-values[..., middle:], values[..., :middle]], axis=-1)


def rotate_back(values):
    middle = values.shape[-1] // 2
    return jnp.concatenate([values[..., middle:], -values[..., :middle]], axis=-1)


def rope_tables(positions):
    ladder = jnp.arange(HEAD_DIM // 2, dtype=jnp.float32)
    inverse = jnp.exp(ladder * (-2.0 * math.log(10000.0) / HEAD_DIM))
    angles = positions.astype(jnp.float32)[:, None] * inverse[None, :]
    cos_half = jnp.cos(angles)
    sin_half = jnp.sin(angles)
    return (
        jnp.concatenate([cos_half, cos_half], axis=-1),
        jnp.concatenate([sin_half, sin_half], axis=-1),
    )


def apply_rope(values, cos_table, sin_table):
    return values * cos_table[:, None, :] + rotate_half(values) * sin_table[:, None, :]


def rope_back(grads, cos_table, sin_table):
    return grads * cos_table[:, None, :] + rotate_back(grads * sin_table[:, None, :])


def gelu_tanh(values):
    return jax.nn.gelu(values, approximate=True)


def adamw_step(old_master, old_first, old_second, grad_sum, learn_rate, step_value):
    first_new = beta_one * old_first + (1.0 - beta_one) * grad_sum
    second_new = beta_two * old_second + (1.0 - beta_two) * grad_sum * grad_sum
    fix_first = 1.0 - jnp.power(beta_one, step_value)
    fix_second = 1.0 - jnp.power(beta_two, step_value)
    update = (
        first_new / fix_first / (jnp.sqrt(second_new / fix_second) + adam_epsilon)
        + decay_weight * old_master
    )
    return (old_master - learn_rate * update, first_new, second_new)


def body_plain(
    block_input,
    cotangent,
    prefix_len,
    cluster_id,
    positions,
    step_count,
    master_qkv,
    first_qkv,
    second_qkv,
    master_out,
    first_out,
    second_out,
    master_gateup,
    first_gateup,
    second_gateup,
    master_down,
    first_down,
    second_down,
    master_norm,
    first_norm,
    second_norm,
):
    w_qkv, w_out, w_gateup, w_down = (
        lax.all_gather(master_qkv.astype(jnp.bfloat16), "dp", axis=1, tiled=True),
        lax.all_gather(master_out.astype(jnp.bfloat16), "dp", axis=1, tiled=True),
        lax.all_gather(master_gateup.astype(jnp.bfloat16), "dp", axis=1, tiled=True),
        lax.all_gather(master_down.astype(jnp.bfloat16), "dp", axis=1, tiled=True),
    )
    w_norm = lax.optimization_barrier(master_norm.astype(jnp.bfloat16)).astype(jnp.float32)
    token_count = block_input.shape[0]
    protein_count = token_count // LEN
    share_rows = cotangent.shape[0]
    share_start = lax.axis_index("mp") * share_rows
    head_count = w_qkv.shape[2] // HEAD_DIM
    width_heads = head_count * HEAD_DIM
    deep_alpha = math.sqrt(2.0 * DEPTH)
    score_scale = 1.0 / math.sqrt(HEAD_DIM)
    cos_table, sin_table = rope_tables(positions)
    projected = jnp.einsum("td,jdc->jtc", block_input, w_qkv, preferred_element_type=jnp.float32)
    shaped = projected.reshape(3, token_count, head_count, HEAD_DIM)
    queries = (apply_rope(shaped[0], cos_table, sin_table) * score_scale).astype(jnp.bfloat16)
    key_rows = apply_rope(shaped[1], cos_table, sin_table).astype(jnp.bfloat16)
    value_rows = shaped[2].astype(jnp.bfloat16)
    row_ids = jnp.arange(LEN)[:, None]
    col_ids = jnp.arange(LEN)[None, :]
    attended_parts = []
    log_totals = []
    for protein in range(protein_count):
        row_slice = slice(protein * LEN, (protein + 1) * LEN)
        visible = (col_ids < prefix_len[protein]) | (col_ids <= row_ids)
        scores = jnp.einsum(
            "qhd,khd->hqk",
            queries[row_slice],
            key_rows[row_slice],
            preferred_element_type=jnp.float32,
        )
        scores = jnp.where(visible[None], scores, -1e30)
        row_peak = jnp.max(scores, axis=-1, keepdims=True)
        expo_rows = jnp.exp(scores - row_peak)
        totals = jnp.sum(expo_rows, axis=-1, keepdims=True)
        attn_probs = (expo_rows / totals).astype(jnp.bfloat16)
        attended_parts.append(
            jnp.einsum(
                "hqk,khd->qhd",
                attn_probs,
                value_rows[row_slice],
                preferred_element_type=jnp.float32,
            )
        )
        log_totals.append(row_peak + jnp.log(totals))
    attended = (
        jnp.concatenate(attended_parts, axis=0)
        .reshape(token_count, width_heads)
        .astype(jnp.bfloat16)
    )
    attn_part = jnp.dot(attended, w_out, preferred_element_type=jnp.float32)
    input_share = lax.dynamic_slice_in_dim(block_input, share_start, share_rows, 0).astype(
        jnp.float32
    )
    attn_share = lax.psum_scatter(
        attn_part.astype(jnp.bfloat16), "mp", scatter_dimension=0, tiled=True
    ).astype(jnp.float32)
    middle_share, normed_one, inv_one = norm_forward(
        deep_alpha * input_share + attn_share, w_norm[0], w_norm[1]
    )
    middle_low = lax.all_gather(middle_share.astype(jnp.bfloat16), "mp", axis=0, tiled=True)
    gateup = jnp.einsum("td,jdf->jtf", middle_low, w_gateup, preferred_element_type=jnp.float32)
    gate_rows = gateup[0]
    up_rows = gateup[1]
    activated, gelu_pull = jax.vjp(gelu_tanh, gate_rows)
    hidden = (activated * up_rows).astype(jnp.bfloat16)
    ffn_part = jnp.dot(hidden, w_down, preferred_element_type=jnp.float32)
    ffn_share = lax.psum_scatter(
        ffn_part.astype(jnp.bfloat16), "mp", scatter_dimension=0, tiled=True
    ).astype(jnp.float32)
    out_share, normed_two, inv_two = norm_forward(
        deep_alpha * middle_share + ffn_share, w_norm[2], w_norm[3]
    )
    block_output = out_share.astype(jnp.bfloat16)
    matches = (cluster_id[:, None] == cluster_id[None, :]).astype(jnp.float32)
    counts = jnp.sum(matches, axis=1)
    group_counts = lax.dynamic_slice_in_dim(
        counts, lax.axis_index("dp") * protein_count, protein_count, 0
    )
    row_protein = (share_start + jnp.arange(share_rows)) // LEN
    one_hot = (row_protein[:, None] == jnp.arange(protein_count)[None, :]).astype(jnp.float32)
    row_weight = jnp.sum(one_hot * (1.0 / group_counts)[None, :], axis=1)
    grad_output = cotangent.astype(jnp.float32) * row_weight[:, None]
    grad_h2, grad_gain_two, grad_bias_two = norm_backward(
        grad_output, normed_two, inv_two, w_norm[2]
    )
    ffn_grad_full = lax.all_gather(grad_h2.astype(jnp.bfloat16), "mp", axis=0, tiled=True)
    grad_down_part = jnp.einsum(
        "tf,td->fd", hidden, ffn_grad_full, preferred_element_type=jnp.float32
    )
    grad_hidden = jnp.einsum("td,fd->tf", ffn_grad_full, w_down, preferred_element_type=jnp.float32)
    grad_gate = gelu_pull(grad_hidden * up_rows)[0]
    grad_up = grad_hidden * activated
    grad_gateup_rows = jnp.stack([grad_gate, grad_up]).astype(jnp.bfloat16)
    grad_gateup_part = jnp.einsum(
        "td,jtf->jdf", middle_low, grad_gateup_rows, preferred_element_type=jnp.float32
    )
    middle_grad_part = jnp.einsum(
        "jtf,jdf->td", grad_gateup_rows, w_gateup, preferred_element_type=jnp.float32
    )
    middle_grad = (
        lax.psum_scatter(
            middle_grad_part.astype(jnp.bfloat16), "mp", scatter_dimension=0, tiled=True
        ).astype(jnp.float32)
        + deep_alpha * grad_h2
    )
    grad_h1, grad_gain_one, grad_bias_one = norm_backward(
        middle_grad, normed_one, inv_one, w_norm[0]
    )
    attn_grad_full = lax.all_gather(grad_h1.astype(jnp.bfloat16), "mp", axis=0, tiled=True)
    grad_out_part = jnp.einsum(
        "tc,td->cd", attended, attn_grad_full, preferred_element_type=jnp.float32
    )
    grad_attended = (
        jnp.einsum("td,cd->tc", attn_grad_full, w_out, preferred_element_type=jnp.float32)
        .astype(jnp.bfloat16)
        .reshape(token_count, head_count, HEAD_DIM)
    )
    query_grads = []
    key_grads = []
    value_grads = []
    for protein in range(protein_count):
        row_slice = slice(protein * LEN, (protein + 1) * LEN)
        visible = (col_ids < prefix_len[protein]) | (col_ids <= row_ids)
        scores = jnp.einsum(
            "qhd,khd->hqk",
            queries[row_slice],
            key_rows[row_slice],
            preferred_element_type=jnp.float32,
        )
        scores = jnp.where(visible[None], scores, -1e30)
        probs_full = jnp.exp(scores - log_totals[protein])
        probs_low = probs_full.astype(jnp.bfloat16)
        grad_slice = grad_attended[row_slice]
        value_grads.append(
            jnp.einsum("hqk,qhd->khd", probs_low, grad_slice, preferred_element_type=jnp.float32)
        )
        prob_grads = jnp.einsum(
            "qhd,khd->hqk", grad_slice, value_rows[row_slice], preferred_element_type=jnp.float32
        )
        centre_term = jnp.sum(probs_full * prob_grads, axis=-1, keepdims=True)
        score_grads = (probs_full * (prob_grads - centre_term)).astype(jnp.bfloat16)
        query_grads.append(
            jnp.einsum(
                "hqk,khd->qhd", score_grads, key_rows[row_slice], preferred_element_type=jnp.float32
            )
        )
        key_grads.append(
            jnp.einsum(
                "hqk,qhd->khd", score_grads, queries[row_slice], preferred_element_type=jnp.float32
            )
        )
    grad_query = rope_back(jnp.concatenate(query_grads, axis=0), cos_table, sin_table) * score_scale
    grad_key = rope_back(jnp.concatenate(key_grads, axis=0), cos_table, sin_table)
    grad_value = jnp.concatenate(value_grads, axis=0)
    grad_proj = (
        jnp.stack([grad_query, grad_key, grad_value])
        .reshape(3, token_count, width_heads)
        .astype(jnp.bfloat16)
    )
    grad_qkv_part = jnp.einsum(
        "td,jtc->jdc", block_input, grad_proj, preferred_element_type=jnp.float32
    )
    input_grad_part = jnp.einsum(
        "jtc,jdc->td", grad_proj, w_qkv, preferred_element_type=jnp.float32
    )
    input_grad = (
        lax.psum_scatter(
            input_grad_part.astype(jnp.bfloat16), "mp", scatter_dimension=0, tiled=True
        ).astype(jnp.float32)
        + deep_alpha * grad_h1
    )
    grad_input = input_grad.astype(jnp.bfloat16)
    norm_terms = jnp.stack([grad_gain_one, grad_bias_one, grad_gain_two, grad_bias_two])
    grad_norm = lax.psum(norm_terms, ("dp", "mp"))
    red_qkv, red_out, red_gateup, red_down = (
        lax.psum_scatter(
            grad_qkv_part.astype(jnp.bfloat16), "dp", scatter_dimension=1, tiled=True
        ).astype(jnp.float32),
        lax.psum_scatter(
            grad_out_part.astype(jnp.bfloat16), "dp", scatter_dimension=1, tiled=True
        ).astype(jnp.float32),
        lax.psum_scatter(
            grad_gateup_part.astype(jnp.bfloat16), "dp", scatter_dimension=1, tiled=True
        ).astype(jnp.float32),
        lax.psum_scatter(
            grad_down_part.astype(jnp.bfloat16), "dp", scatter_dimension=1, tiled=True
        ).astype(jnp.float32),
    )
    step_value = step_count[0].astype(jnp.float32)
    rate_qkv = D ** (-0.5)
    rate_out = max(HEADS * HEAD_DIM // 512, 1) ** (-0.5)
    rate_gateup = D ** (-0.5)
    rate_down = max(FF // 64, 1) ** (-0.5)
    rate_norm = 1.0
    new_qkv, new_first_qkv, new_second_qkv = adamw_step(
        master_qkv, first_qkv, second_qkv, red_qkv, rate_qkv, step_value
    )
    new_out, new_first_out, new_second_out = adamw_step(
        master_out, first_out, second_out, red_out, rate_out, step_value
    )
    new_gateup, new_first_gateup, new_second_gateup = adamw_step(
        master_gateup, first_gateup, second_gateup, red_gateup, rate_gateup, step_value
    )
    new_down, new_first_down, new_second_down = adamw_step(
        master_down, first_down, second_down, red_down, rate_down, step_value
    )
    new_norm, new_first_norm, new_second_norm = adamw_step(
        master_norm, first_norm, second_norm, grad_norm, rate_norm, step_value
    )
    return (
        block_output,
        grad_input,
        red_qkv,
        new_qkv,
        new_first_qkv,
        new_second_qkv,
        red_out,
        new_out,
        new_first_out,
        new_second_out,
        red_gateup,
        new_gateup,
        new_first_gateup,
        new_second_gateup,
        red_down,
        new_down,
        new_first_down,
        new_second_down,
        grad_norm,
        new_norm,
        new_first_norm,
        new_second_norm,
    )


MESH = pl.DeviceIdType.MESH
VMEM_BYTES = 61 * 1024 * 1024
BF16 = jnp.bfloat16
F32 = jnp.float32
EMIT = 48
NT = (((1,), (1,)), ((), ()))
ANY = pl.BlockSpec(memory_space=pl.ANY)
VM = pl.BlockSpec(memory_space=pltpu.VMEM)


LIGHT = pl.CostEstimate(flops=1 << 20, bytes_accessed=1 << 16, transcendentals=0)


def nt_dot(left, right):
    return lax.dot_general(left, right, NT, preferred_element_type=F32)


class Ring:
    def __init__(self, send, recv, local):
        self.here = lax.axis_index("dp")
        self.right = (self.here + 1) % 4
        self.left = (self.here + 3) % 4
        self.far = (self.here + 2) % 4
        self.send, self.recv, self.local = send, recv, local

    def copy(self, k, src, dst, other):
        return pltpu.make_async_remote_copy(
            src_ref=src,
            dst_ref=dst,
            send_sem=self.send.at[k],
            recv_sem=self.recv.at[k],
            device_id={"dp": other},
            device_id_type=MESH,
        )


class RingGather:
    def __init__(self, ring, first, half_of, place):
        self.plus_0 = ring.copy(first, half_of(0), place(ring.here, 0), ring.right)
        self.minus_1 = ring.copy(first + 1, half_of(1), place(ring.here, 1), ring.left)
        self.plus_1 = ring.copy(first + 2, half_of(1), place(ring.here, 1), ring.right)
        self.minus_0 = ring.copy(first + 3, half_of(0), place(ring.here, 0), ring.left)
        self.far_0 = ring.copy(first + 4, place(ring.left, 0), place(ring.left, 0), ring.right)
        self.far_1 = ring.copy(first + 5, place(ring.right, 1), place(ring.right, 1), ring.left)
        self.own = [
            pltpu.make_async_copy(half_of(h), place(ring.here, h), ring.local.at[first + h])
            for h in range(2)
        ]
        self.remote = (self.plus_0, self.minus_1, self.plus_1, self.minus_0, self.far_0, self.far_1)

    def start(self):
        for copy in self.remote[:4]:
            copy.start()
        for copy in self.own:
            copy.start()

    def forward(self):
        self.plus_0.wait_recv()
        self.far_0.start()
        self.minus_1.wait_recv()
        self.far_1.start()

    def near(self):
        self.plus_1.wait_recv()
        self.minus_0.wait_recv()

    def far(self):
        self.far_0.wait_recv()
        self.far_1.wait_recv()

    def drain(self):
        for copy in self.remote:
            copy.wait_send()

    def finish(self):
        for copy in self.own:
            copy.wait()
        self.near()
        self.far()
        self.drain()


class RingScatter:
    def __init__(self, ring, first, half_at, buf, out):
        self.buf, self.out = buf, out
        self.plus_far = ring.copy(first, half_at(ring.far, 0), buf.at[0], ring.right)
        self.minus_far = ring.copy(first + 1, half_at(ring.far, 1), buf.at[1], ring.left)
        self.plus_near = ring.copy(first + 2, half_at(ring.right, 1), buf.at[2], ring.right)
        self.minus_near = ring.copy(first + 3, half_at(ring.left, 0), buf.at[3], ring.left)
        self.plus_sum = ring.copy(first + 4, buf.at[6], buf.at[4], ring.right)
        self.minus_sum = ring.copy(first + 5, buf.at[7], buf.at[5], ring.left)
        places = ((ring.right, 0), (ring.left, 1), (ring.here, 0), (ring.here, 1))
        self.loads = [
            pltpu.make_async_copy(half_at(*place), buf.at[6 + k], ring.local.at[first + k])
            for k, place in enumerate(places)
        ]
        self.remote = (
            self.plus_far,
            self.minus_far,
            self.plus_near,
            self.minus_near,
            self.plus_sum,
            self.minus_sum,
        )

    def start(self):
        for copy in self.remote[:4]:
            copy.start()
        for copy in self.loads:
            copy.start()

    def forward(self):
        for copy in self.loads:
            copy.wait()
        self.plus_far.wait_recv()
        for_rows(self.buf.shape[1:], lambda at: add_at(self.buf, 6, 0, at))
        self.plus_sum.start()
        self.minus_far.wait_recv()
        for_rows(self.buf.shape[1:], lambda at: add_at(self.buf, 7, 1, at))
        self.minus_sum.start()

    def finish(self):
        for copy in self.remote[2:]:
            copy.wait_recv()
        buf = self.buf
        for half, terms in enumerate(((8, 3, 4), (9, 2, 5))):
            out = self.out(half)

            def total(at, out=out, terms=terms):
                out[at] = sum(buf[(k,) + at].astype(F32) for k in terms)

            for_rows(buf.shape[1:], total)
        for copy in self.remote:
            copy.wait_send()


def add_at(buf, dst, src, at):
    buf[(dst,) + at] = (buf[(dst,) + at].astype(F32) + buf[(src,) + at].astype(F32)).astype(BF16)


def for_rows(shape, visit):
    def step(i, carry):
        rows = pl.ds(pl.multiple_of(i * 16, 16), 16)
        if len(shape) == 2:
            visit((rows, slice(None)))
        else:
            for j in range(shape[0]):
                visit((j, rows, slice(None)))
        return carry

    lax.fori_loop(0, shape[-2] // 16, step, 0)


def ring_sems(count):
    return [pltpu.SemaphoreType.DMA((count,)) for _ in range(3)]


def row_halves(depth):
    half = depth // 2

    def place(ref):
        def at(owner, part):
            return ref.at[:, pl.ds(pl.multiple_of(owner * depth + part * half, half), half), :]

        return at

    return place


def plane_columns(depth):
    def place(ref):
        def at(owner, part):
            return ref.at[part, :, pl.ds(pl.multiple_of(owner * depth, depth), depth)]

        return at

    return place


def column_halves(depth):
    def place(ref):
        half = ref.shape[0] // 2

        def at(owner, part):
            columns = pl.ds(pl.multiple_of(owner * depth, depth), depth)
            return ref.at[pl.ds(part * half, half), columns]

        return at

    return place


def span_scatter(ring, first, ref, span, buf, out):
    at = plane_columns(ref.shape[2] // 4)(ref.at[:, pl.ds(*span), :])
    return RingScatter(ring, first, at, buf, lambda h: out.at[h])


def greet(others):
    sem = pltpu.get_barrier_semaphore()
    for other in others:
        pl.semaphore_signal(sem, inc=1, device_id=other, device_id_type=MESH)
    pl.semaphore_wait(sem, len(others))


class Square:
    def __init__(self, send, recv, rows):
        me = lax.axis_index("mp")
        self.core = me % 2
        self.x = (me // 2) % 2
        self.y = me // 4
        self.xn = (self.y * 2 + (1 - self.x)) * 2 + self.core
        self.yn = ((1 - self.y) * 2 + self.x) * 2 + self.core
        self.peer = (self.y * 2 + self.x) * 2 + (1 - self.core)
        self.own = self.y * 2 + self.x
        self.xc = self.y * 2 + (1 - self.x)
        self.yc = (1 - self.y) * 2 + self.x
        self.dc = (1 - self.y) * 2 + (1 - self.x)
        self.send, self.recv = send, recv
        cut = rows // 2 // 16 * 16
        self.rows = rows
        self.a = pl.ds(0, cut)
        self.b = pl.ds(cut, rows - cut)
        self.na, self.nb, self.cut = cut, rows - cut, cut

        self.others = [{"mp": self.xn}, {"mp": self.yn}, {"mp": self.peer}]

    def copy(self, k, src, dst, other):
        return pltpu.make_async_remote_copy(
            src_ref=src,
            dst_ref=dst,
            send_sem=self.send.at[k],
            recv_sem=self.recv.at[k],
            device_id={"mp": other},
            device_id_type=MESH,
        )


def add_rows(dst, src, count):
    def step(i, carry):
        rows = pl.ds(pl.multiple_of(i * 16, 16), 16)
        dst[rows, :] = (dst[rows, :].astype(F32) + src[rows, :].astype(F32)).astype(BF16)
        return carry

    lax.fori_loop(0, count // 16, step, 0)


def nothing():
    pass


def square_kernel(
    rows,
    sems,
    gather=None,
    scatter=None,
    ring=None,
    start=nothing,
    first=nothing,
    early=nothing,
    later=nothing,
    between=nothing,
    halfway=nothing,
    middle=nothing,
    end=nothing,
    near_first=False,
    greeting=True,
):
    send, recv, lsem = sems
    sq = Square(send, recv, rows)
    core = sq.core
    if greeting:
        greet(sq.others + ([{"dp": ring.left}, {"dp": ring.right}] if ring is not None else []))

    def place(rel, turn):
        chip_y = (sq.y + rel % 2) % 2
        chip_x = (sq.x + ((rel + 1) // 2) % 2) % 2
        return chip_y * 2 + chip_x, (1 - core + turn) % 2

    if gather is not None:
        compute, share, full, gbuf = gather
        c_own = sq.copy(0, share, gbuf.at[sq.own, core], sq.peer)
        x_a = sq.copy(1, share.at[sq.a], gbuf.at[sq.own, core, sq.a], sq.xn)
        y_b = sq.copy(2, share.at[sq.b], gbuf.at[sq.own, core, sq.b], sq.yn)
        f_x = sq.copy(3, gbuf.at[sq.yc, core, sq.b], gbuf.at[sq.yc, core, sq.b], sq.xn)
        f_y = sq.copy(4, gbuf.at[sq.xc, core, sq.a], gbuf.at[sq.xc, core, sq.a], sq.yn)
        x_b = sq.copy(5, share.at[sq.b], gbuf.at[sq.own, core, sq.b], sq.xn)
        y_a = sq.copy(6, share.at[sq.a], gbuf.at[sq.own, core, sq.a], sq.yn)
        c_d = sq.copy(7, gbuf.at[sq.dc, core], gbuf.at[sq.dc, core], sq.peer)
        c_x = sq.copy(8, gbuf.at[sq.xc, core], gbuf.at[sq.xc, core], sq.peer)
        c_y = sq.copy(9, gbuf.at[sq.yc, core], gbuf.at[sq.yc, core], sq.peer)
        local = pltpu.make_async_copy(share, gbuf.at[sq.own, core], lsem.at[8])
        x_a.start()
        y_b.start()
        if near_first:
            x_b.start()
            y_a.start()
        c_own.start()
        local.start()
    start()
    if gather is not None:

        def take_own():
            c_own.wait_recv()
            local.wait()
            first()

        def forward():
            x_a.wait_recv()
            y_b.wait_recv()
            f_x.start()
            f_y.start()
            if not near_first:
                x_b.start()
                y_a.start()
            early()

        def take_far():
            f_x.wait_recv()
            f_y.wait_recv()
            c_d.start()
            c_d.wait_recv()

        def take_near():
            x_b.wait_recv()
            y_a.wait_recv()
            c_x.start()
            c_y.start()
            later()
            c_x.wait_recv()
            c_y.wait_recv()

        def gather_step(t, carry):
            unit = t // 2
            if near_first:
                chip_y = (sq.y + unit // 2) % 2
                chip_x = (sq.x + unit % 2) % 2
                chip, which = chip_y * 2 + chip_x, (1 - core + t % 2) % 2
            else:
                chip, which = place(unit, t % 2)

            pl.when(t == 0)(take_own)

            @pl.when(t == 2)
            def _():
                forward()
                if near_first:
                    take_near()
                else:
                    take_far()

            pl.when(t == (6 if near_first else 4))(take_far if near_first else take_near)

            if full is not None:
                pltpu.make_async_copy(gbuf.at[chip, which], full.at[chip, which], lsem.at[t]).start()
            compute(t, chip, which)
            return carry

        lax.fori_loop(0, 8 if scatter is None else 6, gather_step, 0)
    between()
    if scatter is not None:
        finish_tile, pbuf, (rcore, rxd, ryd, rx, ry), emit = scatter
        x_d = sq.copy(14, pbuf.at[sq.dc, core, sq.a], rxd, sq.xn)
        y_d = sq.copy(15, pbuf.at[sq.dc, core, sq.b], ryd, sq.yn)
        x_ra = sq.copy(16, pbuf.at[sq.xc, core, sq.a], rx.at[sq.a], sq.xn)
        y_rb = sq.copy(17, pbuf.at[sq.yc, core, sq.b], ry.at[sq.b], sq.yn)
        x_rb = sq.copy(18, pbuf.at[sq.xc, core, sq.b], rx.at[sq.b], sq.xn)
        y_ra = sq.copy(19, pbuf.at[sq.yc, core, sq.a], ry.at[sq.a], sq.yn)

        def scatter_step(t, carry):
            turn = t % 2
            rel = (t // 2 + 1) % 4
            chip, which = place(rel, turn)

            @pl.when(t == 4)
            def _():
                halfway()

            finish_tile(t, chip, which)
            to_peer = sq.copy(10 + rel, pbuf.at[chip, which], rcore.at[chip], sq.peer)

            @pl.when(turn == 0)
            def _():
                to_peer.start()

            @pl.when(turn == 1)
            def _():
                to_peer.wait_recv()
                add_rows(pbuf.at[chip, which], rcore.at[chip], rows)

            @pl.when(t == 1)
            def _():
                x_d.start()
                y_d.start()

            @pl.when(t == 3)
            def _():
                x_ra.start()

            @pl.when(t == 5)
            def _():
                y_rb.start()

            return carry

        if gather is None:
            lax.fori_loop(0, 8, scatter_step, 0)
        else:
            lax.fori_loop(0, 2, scatter_step, 0)
            lax.fori_loop(6, 8, gather_step, 0)
            lax.fori_loop(2, 8, scatter_step, 0)
        x_d.wait_recv()
        add_rows(pbuf.at[sq.yc, core, sq.a], rxd, sq.na)
        y_ra.start()
        y_d.wait_recv()
        add_rows(pbuf.at[sq.xc, core, sq.b], ryd, sq.nb)
        x_rb.start()
        middle()
        x_ra.wait_recv()
        y_rb.wait_recv()
        y_ra.wait_recv()
        x_rb.wait_recv()

        def last(i, carry):
            part = pl.ds(pl.multiple_of(i * EMIT, 16), EMIT)
            emit(
                part,
                pbuf[sq.own, core, part, :].astype(F32)
                + rx[part, :].astype(F32)
                + ry[part, :].astype(F32),
            )
            return carry

        lax.fori_loop(0, rows // EMIT, last, 0)
        for k in range(4):
            sq.copy(10 + k, pbuf.at[0, 0], rcore.at[0], sq.peer).wait_send()
        for copy in (x_d, y_d, x_ra, y_rb, x_rb, y_ra):
            copy.wait_send()
    end()
    if gather is not None:
        for copy in (c_own, x_a, y_b, f_x, f_y, x_b, y_a, c_d, c_x, c_y):
            copy.wait_send()
        if full is not None:
            for t in range(8):
                pltpu.make_async_copy(gbuf.at[0, 0], full.at[0, 0], lsem.at[t]).wait()


def row_mean(values):
    return jnp.mean(values, axis=-1, keepdims=True)


def norm_rows(values):
    centre = values - row_mean(values)
    inv_std = lax.rsqrt(row_mean(centre * centre) + norm_epsilon)
    return centre * inv_std, inv_std


def norm_rows_back(grads, normed, inv_std, gain):
    grad_normed = grads * gain
    return inv_std * (grad_normed - row_mean(grad_normed) - normed * row_mean(grad_normed * normed))


def fold(values):
    return sum(values[i : i + 8] for i in range(0, EMIT, 8))


def scatter_scratch(rows, width, with_sums=True):
    cut = rows // 2 // 16 * 16
    return ([pltpu.VMEM((4, 2, rows, width), BF16)] if with_sums else []) + [
        pltpu.VMEM((4, rows, width), BF16),
        pltpu.VMEM((cut, width), BF16),
        pltpu.VMEM((rows - cut, width), BF16),
        pltpu.VMEM((rows, width), BF16),
        pltpu.VMEM((rows, width), BF16),
    ]


SEMS = [
    pltpu.SemaphoreType.DMA((20,)),
    pltpu.SemaphoreType.DMA((20,)),
    pltpu.SemaphoreType.DMA((9,)),
]


def params(collective_id):
    return pltpu.CompilerParams(
        collective_id=collective_id, has_side_effects=True, vmem_limit_bytes=VMEM_BYTES
    )


def whole(shape):
    return pl.BlockSpec(shape, lambda *_: (0,) * len(shape))


def front_call(block_input, low_qkv, low_out, gateup, positions, prefix_len, w_norm, rows, spans):
    tokens, width = block_input.shape
    depth, cols = low_qkv.shape[1:]
    tiles = tokens // rows
    heads = cols // HEAD_DIM
    proteins = tokens // LEN
    scale = 1.0 / math.sqrt(HEAD_DIM)
    alpha = math.sqrt(2.0 * DEPTH)
    half = depth // 2
    out_half = cols // 2
    span = spans[-1][0] + spans[-1][1]
    live = gateup.shape[1]

    def kernel(
        pre_ref, x_ref, low_ref, lo_ref, lg_ref, pos_ref, norm_ref,
        q_ref, k_ref, v_ref, o_ref, p_ref, cos_ref, sin_ref, w_ref, wo_ref, wg_ref,
        x1_ref, x1b_ref, n1_ref, inv_ref,
        x_buf, w_buf, acc, q_buf, k_buf, v_buf, o_buf, cos_buf, sin_buf, p_buf, wo_buf, xs_buf, wide_g, low_g,
        rcore, rxd, ryd, rx, ry, xsem, psem, ksem, send, recv, lsem, zsend, zrecv, zlocal,
    ):
        ring = Ring(zsend, zrecv, zlocal)
        sems = Square(send, recv, rows)
        gather = RingGather(
            ring, 0, lambda h: low_ref.at[:, pl.ds(h * half, half), :], row_halves(depth)(w_buf)
        )
        gather_out = RingGather(
            ring, 6, lambda h: lo_ref.at[pl.ds(h * out_half, out_half), :], column_halves(depth)(wo_buf)
        )
        gathers = []
        for n, (low, size) in enumerate(spans):
            at = pl.ds(low, size)
            gathers.append(
                RingGather(
                    ring,
                    12 + 6 * n,
                    lambda h, at=at: low_g.at[h, at, :],
                    plane_columns(depth)(wg_ref.at[:, at, :]),
                )
            )
        own_rows = pltpu.make_async_copy(x_ref.at[sems.own, sems.core], xs_buf, xsem.at[8])
        load_g = pltpu.make_async_copy(lg_ref, wide_g, xsem.at[9])
        kept = ((q_buf, q_ref), (k_buf, k_ref), (v_buf, v_ref), (cos_buf, cos_ref), (sin_buf, sin_ref))
        keeps = [pltpu.make_async_copy(src, dst, ksem.at[n]) for n, (src, dst) in enumerate(kept)]
        keep_w = pltpu.make_async_copy(w_buf, w_ref, ksem.at[5])
        keep_wo = pltpu.make_async_copy(wo_buf, wo_ref, ksem.at[6])
        keep_o = pltpu.make_async_copy(o_buf, o_ref, ksem.at[7])

        def x_copy(t):
            return pltpu.make_async_copy(x_ref.at[t // 2, t % 2], x_buf.at[t // 2, t % 2], xsem.at[t])

        def start_tile(t, carry):
            x_copy(t).start()
            return carry

        lax.fori_loop(0, tiles, start_tile, 0)
        own_rows.start()
        load_g.start()
        greet(sems.others + [{"dp": ring.left}, {"dp": ring.right}])
        gather.start()
        for copy in gather.own:
            copy.wait()

        def part(t, j, owner):
            depths = pl.ds(pl.multiple_of(owner * depth, depth), depth)
            return jnp.dot(
                x_buf[t // 2, t % 2, :, depths], w_buf[j, depths, :], preferred_element_type=F32
            )

        def tile_rows(t):
            return pl.ds(pl.multiple_of(t * rows, 16), rows)

        def own_tile(t, carry):
            x_copy(t).wait()
            for j in range(3):
                acc[t, j] = part(t, j, ring.here)
            return carry

        lax.fori_loop(0, tiles, own_tile, 0)
        rung = lax.broadcasted_iota(jnp.int32, (HEAD_DIM, 1), 0)
        ladder = (rung % (HEAD_DIM // 2)).astype(F32)
        inverse = jnp.exp(ladder * (-2.0 * math.log(10000.0) / HEAD_DIM))
        sign = jnp.where(rung < HEAD_DIM // 2, -1.0, 1.0)

        def table_tile(b, carry):
            angles = inverse * pos_ref[pl.ds(b, 1), :].astype(F32)
            here = pl.ds(pl.multiple_of(b * HEAD_DIM, HEAD_DIM), HEAD_DIM)
            cos_buf[here, :] = jnp.cos(angles).T
            sin_buf[here, :] = (jnp.sin(angles) * sign).T
            return carry

        blocks = tokens // HEAD_DIM
        lax.fori_loop(0, blocks // 2, table_tile, 0)
        gather.forward()
        gather_out.start()
        lax.fori_loop(blocks // 2, blocks, table_tile, 0)
        load_g.wait()

        def round_rows(i, carry):
            here = pl.ds(pl.multiple_of(i * 16, 16), 16)
            for h in range(2):
                low_g[h, here, :] = wide_g[h, here, :].astype(BF16)
            return carry

        lax.fori_loop(0, live // 16, round_rows, 0)
        gather.near()

        def near_tile(t, carry):
            for j in range(3):
                acc[t, j] += part(t, j, ring.left) + part(t, j, ring.right)
            return carry

        lax.fori_loop(0, tiles, near_tile, 0)
        gather.far()
        gathers[0].start()
        keep_w.start()

        def far_tile(t, carry):
            here = tile_rows(t)
            for j, buf in enumerate((q_buf, k_buf)):
                a = acc[t, j] + part(t, j, ring.far)
                for h in range(heads):
                    cut = slice(h * HEAD_DIM, (h + 1) * HEAD_DIM)
                    turned = a[:, cut] * cos_buf[here, :]
                    turned += pltpu.roll(a[:, cut], HEAD_DIM // 2, 1) * sin_buf[here, :]
                    if j == 0:
                        turned = turned * scale
                    buf[here, cut] = turned.astype(BF16)
            v_buf[here, :] = (acc[t, 2] + part(t, 2, ring.far)).astype(BF16)
            return carry

        lax.fori_loop(0, tiles, far_tile, 0)
        gather_out.forward()
        for keep in keeps:
            keep.start()

        def protein(p, carry):
            prefix = pre_ref[p]
            keys = pl.ds(pl.multiple_of(p * LEN, LEN), LEN)

            @pl.when(p == proteins - 1)
            def _():
                gathers[0].forward()
                gathers[1].start()

            for h in range(heads):
                cut = slice(h * HEAD_DIM, (h + 1) * HEAD_DIM)
                store = pltpu.make_async_copy(p_buf.at[h], p_ref.at[p, h], psem.at[h])

                @pl.when(p > 0)
                def _():
                    store.wait()

                for i in range(LEN // BLOCK):
                    here = pl.ds(pl.multiple_of(p * LEN + i * BLOCK, BLOCK), BLOCK)
                    s = nt_dot(q_buf[here, cut], k_buf[keys, cut])
                    col = lax.broadcasted_iota(jnp.int32, s.shape, 1)
                    row = lax.broadcasted_iota(jnp.int32, (BLOCK, 1), 0) + i * BLOCK
                    s = jnp.where(col < jnp.maximum(prefix, row + 1), s, -1e30)
                    e = jnp.exp(s - jnp.max(s, axis=-1, keepdims=True))
                    prob = (e * (1.0 / jnp.sum(e, axis=-1, keepdims=True))).astype(BF16)
                    p_buf[h, i * BLOCK : (i + 1) * BLOCK, :] = prob
                    mixed = jnp.dot(prob, v_buf[keys, cut], preferred_element_type=F32)
                    o_buf[here, cut] = mixed.astype(BF16)
                store.start()
            return carry

        lax.fori_loop(0, proteins, protein, 0)
        for copy in gather_out.own:
            copy.wait()
        gather_out.near()
        gather_out.far()
        keep_wo.start()
        keep_o.start()
        own_rows.wait()

        def compute(t, chip, which):
            tile = o_buf[tile_rows(chip * 2 + which), :]
            x_buf[chip, which] = jnp.dot(tile, wo_buf[...], preferred_element_type=F32).astype(BF16)

        def emit(at, value):
            normed, inv_std = norm_rows(alpha * xs_buf[at, :].astype(F32) + value)
            x1 = normed * norm_ref[0:1, :] + norm_ref[1:2, :]
            x1_ref[at, :] = x1
            x1b_ref[at, :] = x1.astype(BF16)
            n1_ref[at, :] = normed
            inv_ref[at, :] = jnp.broadcast_to(inv_std, (EMIT, HEAD_DIM))

        square_kernel(
            rows,
            (send, recv, lsem),
            scatter=(compute, x_buf, (rcore, rxd, ryd, rx, ry), emit),
            middle=gathers[1].forward,
            greeting=False,
        )
        for other in gathers:
            other.finish()
        gather.drain()
        gather_out.drain()
        for keep in keeps + [keep_w, keep_wo, keep_o]:
            keep.wait()
        for h in range(heads):
            pltpu.make_async_copy(p_buf.at[h], p_ref.at[0, h], psem.at[h]).wait()

    wide = jax.ShapeDtypeStruct((rows, width), F32)
    return pl.pallas_call(
        kernel,
        out_shape=[jax.ShapeDtypeStruct((tokens, cols), BF16)] * 4
        + [jax.ShapeDtypeStruct((proteins, heads, LEN, LEN), BF16)]
        + [jax.ShapeDtypeStruct((tokens, HEAD_DIM), F32)] * 2
        + [
            jax.ShapeDtypeStruct((3, width, cols), BF16),
            jax.ShapeDtypeStruct((cols, width), BF16),
            jax.ShapeDtypeStruct((2, span, width), BF16),
            wide,
            jax.ShapeDtypeStruct((rows, width), BF16),
            wide,
            jax.ShapeDtypeStruct((rows, HEAD_DIM), F32),
        ],
        in_specs=[pl.BlockSpec(memory_space=pltpu.SMEM)] + [ANY] * 4 + [VM, VM],
        out_specs=[ANY] * 10 + [VM] * 4,
        scratch_shapes=[
            pltpu.VMEM((4, 2, rows, width), BF16),
            pltpu.VMEM((3, width, cols), BF16),
            pltpu.VMEM((tiles, 3, rows, cols), F32),
        ]
        + [pltpu.VMEM((tokens, cols), BF16)] * 4
        + [pltpu.VMEM((tokens, HEAD_DIM), F32)] * 2
        + [
            pltpu.VMEM((heads, LEN, LEN), BF16),
            pltpu.VMEM((cols, width), BF16),
            pltpu.VMEM((rows, width), BF16),
            pltpu.VMEM(gateup.shape, F32),
            pltpu.VMEM(gateup.shape, BF16),
        ]
        + scatter_scratch(rows, width, False)
        + [
            pltpu.SemaphoreType.DMA((10,)),
            pltpu.SemaphoreType.DMA((heads,)),
            pltpu.SemaphoreType.DMA((8,)),
        ]
        + SEMS
        + ring_sems(12 + 6 * len(spans)),
        compiler_params=params(0),
        cost_estimate=LIGHT,
        name="front",
    )(
        prefix_len,
        block_input.reshape(4, 2, rows, width),
        low_qkv,
        low_out,
        gateup,
        positions.reshape(tokens // HEAD_DIM, HEAD_DIM),
        w_norm,
    )


BLOCK = 128
TN = (((0,), (0,)), ((), ()))


def attention_back_call(
    queries, key_rows, value_rows, probs, attended, grad_attended, cos_table, sin_table, norm_terms,
    grad_out_part,
):
    tokens, cols = queries.shape
    proteins = tokens // LEN
    heads = cols // HEAD_DIM
    scale = 1.0 / math.sqrt(HEAD_DIM)
    last = proteins * heads - 1
    depth = grad_out_part.shape[1] // 4

    def kernel(
        q_ref, k_ref, v_ref, p_ref, o_ref, do_ref, cos_ref, sin_ref, nt_ref, go_ref,
        da_ref, norm_ref, red_o,
        dk_acc, dv_acc, sums, got, nsend, nrecv, buf_o, send, recv, local,
    ):
        step = pl.program_id(0) * heads + pl.program_id(1)
        ring = Ring(send, recv, local)
        part = cols // 2
        side = RingScatter(
            ring, 0, column_halves(depth)(go_ref), buf_o, lambda h: red_o.at[pl.ds(h * part, part), :]
        )
        sq = Square(nsend, nrecv, 32)
        partners = [
            {"mp": sq.peer},
            {"mp": sq.xn},
            {"mp": sq.yn},
            {"dp": ring.here + 1 - 2 * (ring.here % 2)},
            {"dp": 3 - ring.here},
        ]
        swaps = [
            pltpu.make_async_remote_copy(
                src_ref=sums.at[k],
                dst_ref=got.at[k],
                send_sem=nsend.at[k],
                recv_sem=nrecv.at[k],
                device_id=other,
                device_id_type=MESH,
            )
            for k, other in enumerate(partners)
        ]

        @pl.when(step == 0)
        def _():
            sums[0] = nt_ref[...]
            greet(sq.others + [{"dp": ring.left}, {"dp": ring.right}])
            side.start()
            swaps[0].start()

        for k in range(5):

            @pl.when(step == k + 1)
            def _():
                swaps[k].wait()
                if k < 4:
                    sums[k + 1] = sums[k] + got[k]
                    swaps[k + 1].start()
                else:
                    norm_ref[...] = sums[k] + got[k]

        @pl.when(step == last // 2)
        def _():
            side.forward()

        for i in range(LEN // BLOCK):
            rows = slice(i * BLOCK, (i + 1) * BLOCK)
            do = do_ref[rows, :]
            p = p_ref[0, 0, rows, :]
            delta = jnp.sum(do.astype(F32) * o_ref[rows, :].astype(F32), axis=-1, keepdims=True)
            dp = nt_dot(do, v_ref[...])
            ds = (p.astype(F32) * (dp - delta)).astype(BF16)
            dv = lax.dot_general(p, do, TN, preferred_element_type=F32)
            dk = lax.dot_general(ds, q_ref[rows, :], TN, preferred_element_type=F32)
            if i == 0:
                dv_acc[...] = dv
                dk_acc[...] = dk
            else:
                dv_acc[...] += dv
                dk_acc[...] += dk
            dq = jnp.dot(ds, k_ref[...], preferred_element_type=F32)
            turned = dq * cos_ref[rows, :] - pltpu.roll(dq, HEAD_DIM // 2, 1) * sin_ref[rows, :]
            da_ref[0, rows, :] = (turned * scale).astype(BF16)
        dk = dk_acc[...]
        turned = dk * cos_ref[...] - pltpu.roll(dk, HEAD_DIM // 2, 1) * sin_ref[...]
        da_ref[1] = turned.astype(BF16)
        da_ref[2] = dv_acc[...].astype(BF16)

        @pl.when(step == last)
        def _():
            side.finish()

    tile = pl.BlockSpec((LEN, HEAD_DIM), lambda p, h: (p, h))
    table = pl.BlockSpec((LEN, HEAD_DIM), lambda p, h: (p, 0))
    return pl.pallas_call(
        kernel,
        grid=(proteins, heads),
        in_specs=[tile] * 3
        + [pl.BlockSpec((1, 1, LEN, LEN), lambda p, h: (p, h, 0, 0)), tile, tile, table, table]
        + [whole(norm_terms.shape), ANY],
        out_specs=[
            pl.BlockSpec((3, LEN, HEAD_DIM), lambda p, h: (0, p, h)),
            whole(norm_terms.shape),
            whole((cols, depth)),
        ],
        out_shape=[
            jax.ShapeDtypeStruct((3, tokens, cols), BF16),
            jax.ShapeDtypeStruct(norm_terms.shape, F32),
            jax.ShapeDtypeStruct((cols, depth), F32),
        ],
        scratch_shapes=[
            pltpu.VMEM((LEN, HEAD_DIM), F32),
            pltpu.VMEM((LEN, HEAD_DIM), F32),
            pltpu.VMEM((5,) + norm_terms.shape, F32),
            pltpu.VMEM((5,) + norm_terms.shape, F32),
            pltpu.SemaphoreType.DMA((5,)),
            pltpu.SemaphoreType.DMA((5,)),
            pltpu.VMEM((10, cols // 2, depth), BF16),
        ]
        + ring_sems(6),
        compiler_params=params(7),
        cost_estimate=LIGHT,
        name="attention_back",
    )(
        queries,
        key_rows,
        value_rows,
        probs,
        attended,
        grad_attended,
        cos_table,
        sin_table,
        norm_terms,
        grad_out_part,
    )


def ffn_call(middle_low, middle_share, w_gateup, low_down, cotangent, row_weight, w_norm):
    rows = middle_low.shape[0]
    live, depth = low_down.shape
    curve = math.sqrt(2.0 / math.pi)
    alpha = math.sqrt(2.0 * DEPTH)

    def kernel(
        share, x1_ref, wg_ref, ld_ref, cot_ref, rw_ref, norm_ref,
        y_ref, dh_ref, dhb_ref, terms_ref, full, hid_ref, act_ref, pull_ref, wd_ref,
        w_g, w_d, gbuf, hid_buf, stage, pbuf, rcore, rxd, ryd, rx, ry, sums,
        wsem, osem, hsem, send, recv, lsem, zsend, zrecv, zlocal,
    ):
        ring = Ring(zsend, zrecv, zlocal)
        half = live // 2
        gather_d = RingGather(ring, 0, lambda h: ld_ref.at[pl.ds(h * half, half), :], column_halves(depth)(w_d))
        load_g = pltpu.make_async_copy(wg_ref, w_g, wsem.at[0])
        load_g.start()
        keep_d = pltpu.make_async_copy(w_d, wd_ref, wsem.at[1])
        outs = (act_ref, pull_ref)

        def between():
            for copy in gather_d.own:
                copy.wait()
            gather_d.near()
            gather_d.far()
            keep_d.start()

        def compute(t, chip, which):
            slot = t % 2

            @pl.when(t >= 2)
            def _():
                for k, ref in enumerate(outs):
                    pltpu.make_async_copy(stage.at[slot, k], ref.at[chip, which], osem.at[slot, k]).wait()

            tile = gbuf[chip, which]
            gate = nt_dot(tile, w_g[0])
            up = nt_dot(tile, w_g[1])
            square = gate * gate
            bent = jnp.tanh(curve * gate * (1.0 + 0.044715 * square))
            half = 0.5 * (1.0 + bent)
            act = gate * half
            slope = half + 0.5 * curve * gate * (1.0 - bent * bent) * (1.0 + 3.0 * 0.044715 * square)
            hid_buf[chip, which] = (act * up).astype(BF16)
            stage[slot, 0] = act.astype(BF16)
            stage[slot, 1] = (slope * up).astype(BF16)
            for k, ref in enumerate(outs):
                pltpu.make_async_copy(stage.at[slot, k], ref.at[chip, which], osem.at[slot, k]).start()
            pltpu.make_async_copy(hid_buf.at[chip, which], hid_ref.at[chip, which], hsem.at[t]).start()

        def finish_tile(t, chip, which):
            part = jnp.dot(hid_buf[chip, which], w_d[...], preferred_element_type=F32)
            pbuf[chip, which] = part.astype(BF16)

        def emit(at, value):
            normed, inv_std = norm_rows(alpha * x1_ref[at, :] + value)
            gain = norm_ref[2:3, :]
            y_ref[at, :] = (normed * gain + norm_ref[3:4, :]).astype(BF16)
            dy = cot_ref[at, :].astype(F32) * rw_ref[at, :]
            sums[0] += fold(dy * normed)
            sums[1] += fold(dy)
            dh = norm_rows_back(dy, normed, inv_std, gain)
            dh_ref[at, :] = dh
            dhb_ref[at, :] = dh.astype(BF16)

        sums[...] = jnp.zeros_like(sums)

        def end():
            terms_ref[...] = jnp.sum(sums[...], axis=1)
            for slot in range(2):
                for k, ref in enumerate(outs):
                    pltpu.make_async_copy(stage.at[slot, k], ref.at[0, 0], osem.at[slot, k]).wait()
            for t in range(8):
                pltpu.make_async_copy(hid_buf.at[0, 0], hid_ref.at[0, 0], hsem.at[t]).wait()
            keep_d.wait()
            gather_d.drain()

        square_kernel(
            rows,
            (send, recv, lsem),
            gather=(compute, share, full, gbuf),
            scatter=(finish_tile, pbuf, (rcore, rxd, ryd, rx, ry), emit),
            ring=ring,
            start=gather_d.start,
            first=load_g.wait,
            early=gather_d.forward,
            between=between,
            end=end,
        )

    kept = jax.ShapeDtypeStruct((4, 2, rows, live), BF16)
    return pl.pallas_call(
        kernel,
        out_shape=[
            jax.ShapeDtypeStruct((rows, D), BF16),
            jax.ShapeDtypeStruct((rows, D), F32),
            jax.ShapeDtypeStruct((rows, D), BF16),
            jax.ShapeDtypeStruct((2, D), F32),
            jax.ShapeDtypeStruct((4, 2, rows, D), BF16),
            kept,
            kept,
            kept,
            jax.ShapeDtypeStruct((live, D), BF16),
        ],
        in_specs=[ANY, VM, ANY, ANY, VM, VM, VM],
        out_specs=[VM] * 4 + [ANY] * 5,
        scratch_shapes=[
            pltpu.VMEM((2, live, D), BF16),
            pltpu.VMEM((live, D), BF16),
            pltpu.VMEM((4, 2, rows, D), BF16),
            pltpu.VMEM((4, 2, rows, live), BF16),
            pltpu.VMEM((2, 2, rows, live), BF16),
        ]
        + scatter_scratch(rows, D)
        + [
            pltpu.VMEM((2, 8, D), F32),
            pltpu.SemaphoreType.DMA((2,)),
            pltpu.SemaphoreType.DMA((2, 2)),
            pltpu.SemaphoreType.DMA((8,)),
        ]
        + SEMS
        + ring_sems(6),
        compiler_params=params(1),
        cost_estimate=LIGHT,
        name="ffn",
    )(middle_low, middle_share, w_gateup, low_down, cotangent, row_weight, w_norm)


def ffn_back_call(ffn_grad, act, pull, w_down):
    rows = ffn_grad.shape[0]
    live = w_down.shape[0]

    def kernel(share, act_ref, pull_ref, wd_ref, full, dg_ref, w_d, gbuf, load, stage, wsem, isem, osem, send, recv, lsem):
        weight = pltpu.make_async_copy(wd_ref, w_d, wsem.at[0])
        weight.start()

        def compute(t, chip, which):
            slot = t % 2
            loads = [
                pltpu.make_async_copy(ref.at[chip, which], load.at[k], isem.at[k])
                for k, ref in enumerate((act_ref, pull_ref))
            ]
            stores = [
                pltpu.make_async_copy(stage.at[slot, k], dg_ref.at[k, chip, which], osem.at[slot, k])
                for k in range(2)
            ]
            for copy in loads:
                copy.start()

            @pl.when(t >= 2)
            def _():
                for copy in stores:
                    copy.wait()

            dh = nt_dot(gbuf[chip, which], w_d[...])
            for copy in loads:
                copy.wait()
            stage[slot, 0] = (dh * load[1].astype(F32)).astype(BF16)
            stage[slot, 1] = (dh * load[0].astype(F32)).astype(BF16)
            for copy in stores:
                copy.start()

        def end():
            for slot in range(2):
                for k in range(2):
                    pltpu.make_async_copy(stage.at[slot, k], dg_ref.at[k, 0, 0], osem.at[slot, k]).wait()

        square_kernel(
            rows,
            (send, recv, lsem),
            gather=(compute, share, full, gbuf),
            first=weight.wait,
            end=end,
            near_first=True,
        )

    return pl.pallas_call(
        kernel,
        out_shape=[
            jax.ShapeDtypeStruct((4, 2, rows, D), BF16),
            jax.ShapeDtypeStruct((2, 4, 2, rows, live), BF16),
        ],
        in_specs=[ANY] * 4,
        out_specs=[ANY, ANY],
        scratch_shapes=[
            pltpu.VMEM((live, D), BF16),
            pltpu.VMEM((4, 2, rows, D), BF16),
            pltpu.VMEM((2, rows, live), BF16),
            pltpu.VMEM((2, 2, rows, live), BF16),
            pltpu.SemaphoreType.DMA((1,)),
            pltpu.SemaphoreType.DMA((2,)),
            pltpu.SemaphoreType.DMA((2, 2)),
        ]
        + SEMS,
        compiler_params=params(2),
        cost_estimate=LIGHT,
        name="ffn_back",
    )(ffn_grad, act, pull, w_down)


def middle_back_call(grad_gateup_rows, w_gateup, grad_gateup_part, spans, grad_h2, normed, inv_std, w_norm):
    rows = grad_h2.shape[0]
    alpha = math.sqrt(2.0 * DEPTH)
    live, width = grad_gateup_part.shape[1:]
    depth = width // 4

    def kernel(
        dg_ref, wg_ref, gg_ref, dh2_ref, n1_ref, inv_ref, norm_ref, dh_ref, dhb_ref, terms_ref, red_0, red_1,
        w_g, load, buf_0, buf_1, pbuf, rcore, rxd, ryd, rx, ry, sums, wsem, isem, send, recv, lsem, zsend, zrecv, zlocal,
    ):
        ring = Ring(zsend, zrecv, zlocal)
        early = span_scatter(ring, 0, gg_ref, spans[0], buf_0, red_0)
        late = span_scatter(ring, 6, gg_ref, spans[1], buf_1, red_1)
        weight = pltpu.make_async_copy(wg_ref, w_g, wsem.at[0])
        weight.start()
        me = lax.axis_index("mp")
        core, x, y = me % 2, (me // 2) % 2, me // 4

        def loads(t):
            rel = (t // 2 + 1) % 4
            chip = ((y + rel % 2) % 2) * 2 + (x + ((rel + 1) // 2) % 2) % 2
            which = (1 - core + t % 2) % 2
            return [
                pltpu.make_async_copy(dg_ref.at[k, chip, which], load.at[t % 2, k], isem.at[t % 2, k])
                for k in range(2)
            ]

        for copy in loads(0):
            copy.start()

        def compute(t, chip, which):
            @pl.when(t < 7)
            def _():
                for copy in loads(t + 1):
                    copy.start()

            for copy in loads(t):
                copy.wait()
            slot = t % 2
            part = jnp.dot(load[slot, 0], w_g[0], preferred_element_type=F32)
            part += jnp.dot(load[slot, 1], w_g[1], preferred_element_type=F32)
            pbuf[chip, which] = part.astype(BF16)

        sums[...] = jnp.zeros_like(sums)

        def emit(at, value):
            grads = value + alpha * dh2_ref[at, :]
            normed = n1_ref[at, :]
            sums[0] += fold(grads * normed)
            sums[1] += fold(grads)
            dh = norm_rows_back(grads, normed, inv_ref[at, 0:1], norm_ref[0:1, :])
            dh_ref[at, :] = dh
            dhb_ref[at, :] = dh.astype(BF16)

        def end():
            terms_ref[...] = jnp.sum(sums[...], axis=1)
            early.finish()
            late.finish()

        square_kernel(
            rows,
            (send, recv, lsem),
            scatter=(compute, pbuf, (rcore, rxd, ryd, rx, ry), emit),
            ring=ring,
            start=lambda: (early.start(), weight.wait()),
            halfway=lambda: (early.forward(), late.start()),
            middle=late.forward,
            end=end,
        )

    return pl.pallas_call(
        kernel,
        out_shape=[
            jax.ShapeDtypeStruct((rows, D), F32),
            jax.ShapeDtypeStruct((rows, D), BF16),
            jax.ShapeDtypeStruct((2, D), F32),
            jax.ShapeDtypeStruct((2, spans[0][1], depth), F32),
            jax.ShapeDtypeStruct((2, spans[1][1], depth), F32),
        ],
        in_specs=[ANY] * 3 + [VM] * 4,
        out_specs=[VM] * 5,
        scratch_shapes=[
            pltpu.VMEM((2, live, D), BF16),
            pltpu.VMEM((2, 2, rows, live), BF16),
            pltpu.VMEM((10, spans[0][1], depth), BF16),
            pltpu.VMEM((10, spans[1][1], depth), BF16),
        ]
        + scatter_scratch(rows, D)
        + [pltpu.VMEM((2, 8, D), F32)]
        + [pltpu.SemaphoreType.DMA((1,)), pltpu.SemaphoreType.DMA((2, 2))]
        + SEMS
        + ring_sems(12),
        compiler_params=params(8),
        cost_estimate=LIGHT,
        name="middle_back",
    )(grad_gateup_rows, w_gateup, grad_gateup_part, grad_h2, normed, inv_std, w_norm)


def out_back_call(attn_grad, w_out, attended, grad_gateup_part, span):
    rows = attn_grad.shape[0]
    cols = w_out.shape[0]
    depth = grad_gateup_part.shape[2] // 4

    def kernel(
        share, w_ref, o_ref, gg_ref, dout, go_ref, red,
        w_buf, gbuf, buf, acc, wsem, send, recv, lsem, zsend, zrecv, zlocal,
    ):
        ring = Ring(zsend, zrecv, zlocal)
        side = span_scatter(ring, 0, gg_ref, span, buf, red)
        weight = pltpu.make_async_copy(w_ref, w_buf, wsem.at[0])
        weight.start()

        def compute(t, chip, which):
            tile = gbuf[chip, which]
            dout[chip, which] = nt_dot(tile, w_buf[...]).astype(BF16)
            part = lax.dot_general(o_ref[chip, which], tile, TN, preferred_element_type=F32)

            @pl.when(t == 0)
            def _():
                acc[...] = part

            @pl.when(t > 0)
            def _():
                acc[...] += part

        def end():
            go_ref[...] = acc[...].astype(BF16)
            side.finish()

        square_kernel(
            rows,
            (send, recv, lsem),
            gather=(compute, share, None, gbuf),
            ring=ring,
            start=side.start,
            first=weight.wait,
            early=side.forward,
            end=end,
            near_first=True,
        )

    return pl.pallas_call(
        kernel,
        out_shape=[
            jax.ShapeDtypeStruct((4, 2, rows, cols), BF16),
            jax.ShapeDtypeStruct((cols, D), BF16),
            jax.ShapeDtypeStruct((2, span[1], depth), F32),
        ],
        in_specs=[ANY, ANY, VM, ANY],
        out_specs=[VM, VM, VM],
        scratch_shapes=[
            pltpu.VMEM((cols, D), BF16),
            pltpu.VMEM((4, 2, rows, D), BF16),
            pltpu.VMEM((10, span[1], depth), BF16),
            pltpu.VMEM((cols, D), F32),
            pltpu.SemaphoreType.DMA((1,)),
        ]
        + SEMS
        + ring_sems(6),
        compiler_params=params(3),
        cost_estimate=LIGHT,
        name="out_back",
    )(attn_grad, w_out, attended.reshape(4, 2, rows, cols), grad_gateup_part)


def input_back_call(grad_proj, w_qkv, block_input, grad_gateup_part, span, grad_h1):
    rows = grad_h1.shape[0]
    alpha = math.sqrt(2.0 * DEPTH)
    width, cols = w_qkv.shape[1:]
    depth = width // 4
    tokens = block_input.shape[0]

    def kernel(
        da_ref, w_ref, x_ref, gg_ref, dh_ref, out, red_q, red_g,
        w_buf, x_buf, gq_buf, buf_q, buf_g, pbuf, rcore, rxd, ryd, rx, ry,
        wsem, send, recv, lsem, zsend, zrecv, zlocal,
    ):
        ring = Ring(zsend, zrecv, zlocal)
        half = depth // 2
        side_g = span_scatter(ring, 0, gg_ref, span, buf_g, red_g)
        side_q = RingScatter(
            ring, 6, row_halves(depth)(gq_buf), buf_q, lambda h: red_q.at[:, pl.ds(h * half, half), :]
        )
        weight = pltpu.make_async_copy(w_ref, w_buf, wsem.at[0])
        load = pltpu.make_async_copy(x_ref, x_buf, wsem.at[1])
        load.start()
        weight.start()

        def product(n, carry):
            depths = pl.ds(pl.multiple_of(n * depth, depth), depth)
            left = x_buf[:, :, :, depths].reshape(tokens, depth)
            for j in range(3):
                right = da_ref[j].reshape(tokens, cols)
                gq_buf[j, depths, :] = lax.dot_general(left, right, TN, preferred_element_type=F32).astype(BF16)
            return carry

        def start():
            side_g.start()
            load.wait()
            lax.fori_loop(0, 4, product, 0)
            side_g.forward()
            side_q.start()
            weight.wait()

        def compute(t, chip, which):
            part = nt_dot(da_ref[0, chip, which], w_buf[0])
            part += nt_dot(da_ref[1, chip, which], w_buf[1])
            part += nt_dot(da_ref[2, chip, which], w_buf[2])
            pbuf[chip, which] = part.astype(BF16)

        def emit(at, value):
            out[at, :] = (value + alpha * dh_ref[at, :]).astype(BF16)

        def end():
            side_g.finish()
            side_q.finish()

        square_kernel(
            rows,
            (send, recv, lsem),
            scatter=(compute, pbuf, (rcore, rxd, ryd, rx, ry), emit),
            ring=ring,
            start=start,
            middle=side_q.forward,
            end=end,
        )

    return pl.pallas_call(
        kernel,
        out_shape=[
            jax.ShapeDtypeStruct((rows, D), BF16),
            jax.ShapeDtypeStruct((3, depth, cols), F32),
            jax.ShapeDtypeStruct((2, span[1], depth), F32),
        ],
        in_specs=[VM, ANY, ANY, ANY, VM],
        out_specs=[VM, VM, VM],
        scratch_shapes=[
            pltpu.VMEM((3, D, cols), BF16),
            pltpu.VMEM((4, 2, rows, width), BF16),
            pltpu.VMEM((3, width, cols), BF16),
            pltpu.VMEM((10, 3, depth // 2, cols), BF16),
            pltpu.VMEM((10, span[1], depth), BF16),
        ]
        + scatter_scratch(rows, D)
        + [pltpu.SemaphoreType.DMA((2,))]
        + SEMS
        + ring_sems(12),
        compiler_params=params(4),
        cost_estimate=LIGHT,
        name="input_back",
    )(
        grad_proj.reshape(3, 4, 2, rows, cols),
        w_qkv,
        block_input.reshape(4, 2, rows, width),
        grad_gateup_part,
        grad_h1,
    )


FRONT_SPANS = ((0, 240), (240, 464))
SPANS = ((0, 96), (96, 112), (208, 384), (592, 112))


def body_ring(
    block_input,
    cotangent,
    prefix_len,
    cluster_id,
    positions,
    step_count,
    master_qkv,
    first_qkv,
    second_qkv,
    master_out,
    first_out,
    second_out,
    master_gateup,
    first_gateup,
    second_gateup,
    master_down,
    first_down,
    second_down,
    master_norm,
    first_norm,
    second_norm,
):
    token_count = block_input.shape[0]
    protein_count = token_count // LEN
    share_rows = cotangent.shape[0]
    share_start = lax.axis_index("mp") * share_rows

    low_qkv = master_qkv.astype(BF16)
    low_out = master_out.astype(BF16)
    low_down = master_down.astype(BF16)
    w_norm = lax.optimization_barrier(master_norm.astype(BF16)).astype(F32)

    (
        queries, key_rows, value_rows, attended, probs, cos_table, sin_table, w_qkv, w_out, w_gateup,
        middle_share, middle_low, normed_one, inv_one,
    ) = front_call(
        block_input, low_qkv, low_out, jnp.swapaxes(master_gateup, 1, 2), positions, prefix_len, w_norm, share_rows, FRONT_SPANS
    )
    matches = (cluster_id[:, None] == cluster_id[None, :]).astype(F32)
    counts = jnp.sum(matches, axis=1)
    group_counts = lax.dynamic_slice_in_dim(
        counts, lax.axis_index("dp") * protein_count, protein_count, 0
    )
    row_protein = (share_start + jnp.arange(share_rows)) // LEN
    one_hot = (row_protein[:, None] == jnp.arange(protein_count)[None, :]).astype(F32)
    row_weight = jnp.sum(one_hot * (1.0 / group_counts)[None, :], axis=1)
    block_output, grad_h2, grad_h2_low, terms_two, middle_low, hidden, act, pull, w_down = ffn_call(
        middle_low, middle_share, w_gateup, low_down, cotangent, row_weight[:, None], w_norm
    )
    ffn_grad, grad_gateup_rows = ffn_back_call(grad_h2_low, act, pull, w_down)
    hidden = hidden.reshape(token_count, -1)
    middle_low = middle_low.reshape(token_count, D)
    ffn_grad = ffn_grad.reshape(token_count, D)
    gateup_rows = grad_gateup_rows.reshape(2, token_count, -1)
    grad_down_part = jnp.einsum("tf,td->fd", hidden, ffn_grad, preferred_element_type=F32).astype(BF16)
    red_down = lax.psum_scatter(grad_down_part, "dp", scatter_dimension=1, tiled=True).astype(F32)
    gateup_rows, grad_gateup_rows, grad_down_part = lax.optimization_barrier(
        (gateup_rows, grad_gateup_rows, grad_down_part)
    )
    grad_gateup_part = jnp.einsum(
        "jtf,td->jfd", gateup_rows, middle_low, preferred_element_type=F32
    ).astype(BF16)
    grad_h1, grad_h1_low, terms_one, red_gateup_0, red_gateup_1 = middle_back_call(
        grad_gateup_rows, w_gateup, grad_gateup_part, SPANS[:2], grad_h2, normed_one, inv_one, w_norm
    )
    grad_attended, grad_out_part, red_gateup_2 = out_back_call(
        grad_h1_low, w_out, attended, grad_gateup_part, SPANS[2]
    )
    grad_attended = grad_attended.reshape(token_count, -1)
    norm_terms = jnp.concatenate([terms_one, terms_two])
    grad_proj, grad_norm, red_out = attention_back_call(
        queries,
        key_rows,
        value_rows,
        probs,
        attended,
        grad_attended,
        cos_table,
        sin_table,
        norm_terms,
        grad_out_part,
    )
    grad_input, red_qkv, red_gateup_3 = input_back_call(
        grad_proj, w_qkv, block_input, grad_gateup_part, SPANS[3], grad_h1
    )
    red_gateup = jnp.swapaxes(
        jnp.concatenate([red_gateup_0, red_gateup_1, red_gateup_2, red_gateup_3], axis=1), 1, 2
    )

    step_value = step_count[0].astype(F32)
    rate_qkv = D ** (-0.5)
    rate_out = max(HEADS * HEAD_DIM // 512, 1) ** (-0.5)
    rate_gateup = D ** (-0.5)
    rate_down = max(FF // 64, 1) ** (-0.5)
    rate_norm = 1.0
    new_qkv, new_first_qkv, new_second_qkv = adamw_step(
        master_qkv, first_qkv, second_qkv, red_qkv, rate_qkv, step_value
    )
    new_out, new_first_out, new_second_out = adamw_step(
        master_out, first_out, second_out, red_out, rate_out, step_value
    )
    new_gateup, new_first_gateup, new_second_gateup = adamw_step(
        master_gateup, first_gateup, second_gateup, red_gateup, rate_gateup, step_value
    )
    new_down, new_first_down, new_second_down = adamw_step(
        master_down, first_down, second_down, red_down, rate_down, step_value
    )
    new_norm, new_first_norm, new_second_norm = adamw_step(
        master_norm, first_norm, second_norm, grad_norm, rate_norm, step_value
    )
    return (
        block_output,
        grad_input,
        red_qkv,
        new_qkv,
        new_first_qkv,
        new_second_qkv,
        red_out,
        new_out,
        new_first_out,
        new_second_out,
        red_gateup,
        new_gateup,
        new_first_gateup,
        new_second_gateup,
        red_down,
        new_down,
        new_first_down,
        new_second_down,
        grad_norm,
        new_norm,
        new_first_norm,
        new_second_norm,
    )


def solution(mesh):
    placed = (
        P("dp", None),
        P(("dp", "mp"), None),
        P("dp"),
        P(),
        P("dp"),
        P(),
        P(None, "dp", "mp"),
        P(None, "dp", "mp"),
        P(None, "dp", "mp"),
        P("mp", "dp"),
        P("mp", "dp"),
        P("mp", "dp"),
        P(None, "dp", "mp"),
        P(None, "dp", "mp"),
        P(None, "dp", "mp"),
        P("mp", "dp"),
        P("mp", "dp"),
        P("mp", "dp"),
        P(),
        P(),
        P(),
    )
    ring = mesh.shape["dp"] == 4 and mesh.shape["mp"] == 8
    return jax.shard_map(
        body_ring if ring else body_plain,
        mesh=mesh,
        in_specs=placed,
        out_specs=(
            P(("dp", "mp"), None),
            P(("dp", "mp"), None),
            P(None, "dp", "mp"),
            P(None, "dp", "mp"),
            P(None, "dp", "mp"),
            P(None, "dp", "mp"),
            P("mp", "dp"),
            P("mp", "dp"),
            P("mp", "dp"),
            P("mp", "dp"),
            P(None, "dp", "mp"),
            P(None, "dp", "mp"),
            P(None, "dp", "mp"),
            P(None, "dp", "mp"),
            P("mp", "dp"),
            P("mp", "dp"),
            P("mp", "dp"),
            P("mp", "dp"),
            P(),
            P(),
            P(),
            P(),
        ),
        check_vma=False,
    )
```

```python
import functools
import math

import jax
import jax.numpy as jnp
from jax import lax
from jax.experimental import pallas as pl
from jax.experimental.pallas import tpu as pltpu
from jax.sharding import PartitionSpec as P

D = 2048
HEADS = 16
HEAD_DIM = 128
FF = 5632
DEPTH = 24
LEN = 896


beta_one = 0.9
beta_two = 0.95
adam_epsilon = 1e-08
decay_weight = 0.1
norm_epsilon = 1e-05


def norm_forward(hidden_rows, gain, offset):
    centre = hidden_rows - jnp.mean(hidden_rows, axis=-1, keepdims=True)
    inv_std = lax.rsqrt(jnp.mean(centre * centre, axis=-1, keepdims=True) + norm_epsilon)
    normed = centre * inv_std
    return (normed * gain + offset, normed, inv_std)


def norm_backward(grad_rows, normed, inv_std, gain):
    grad_normed = grad_rows * gain
    first_term = jnp.mean(grad_normed, axis=-1, keepdims=True)
    second_term = jnp.mean(grad_normed * normed, axis=-1, keepdims=True)
    grad_hidden = inv_std * (grad_normed - first_term - normed * second_term)
    return (grad_hidden, jnp.sum(grad_rows * normed, axis=0), jnp.sum(grad_rows, axis=0))


def rotate_half(values):
    middle = values.shape[-1] // 2
    return jnp.concatenate([-values[..., middle:], values[..., :middle]], axis=-1)


def rotate_back(values):
    middle = values.shape[-1] // 2
    return jnp.concatenate([values[..., middle:], -values[..., :middle]], axis=-1)


def rope_tables(positions):
    ladder = jnp.arange(HEAD_DIM // 2, dtype=jnp.float32)
    inverse = jnp.exp(ladder * (-2.0 * math.log(10000.0) / HEAD_DIM))
    angles = positions.astype(jnp.float32)[:, None] * inverse[None, :]
    cos_half = jnp.cos(angles)
    sin_half = jnp.sin(angles)
    return (
        jnp.concatenate([cos_half, cos_half], axis=-1),
        jnp.concatenate([sin_half, sin_half], axis=-1),
    )


def apply_rope(values, cos_table, sin_table):
    return values * cos_table[:, None, :] + rotate_half(values) * sin_table[:, None, :]


def rope_back(grads, cos_table, sin_table):
    return grads * cos_table[:, None, :] + rotate_back(grads * sin_table[:, None, :])


def gelu_tanh(values):
    return jax.nn.gelu(values, approximate=True)


def adamw_step(old_master, old_first, old_second, grad_sum, learn_rate, step_value):
    first_new = beta_one * old_first + (1.0 - beta_one) * grad_sum
    second_new = beta_two * old_second + (1.0 - beta_two) * grad_sum * grad_sum
    fix_first = 1.0 - jnp.power(beta_one, step_value)
    fix_second = 1.0 - jnp.power(beta_two, step_value)
    update = (
        first_new / fix_first / (jnp.sqrt(second_new / fix_second) + adam_epsilon)
        + decay_weight * old_master
    )
    return (old_master - learn_rate * update, first_new, second_new)


def body_plain(
    block_input,
    cotangent,
    prefix_len,
    cluster_id,
    positions,
    step_count,
    master_qkv,
    first_qkv,
    second_qkv,
    master_out,
    first_out,
    second_out,
    master_gateup,
    first_gateup,
    second_gateup,
    master_down,
    first_down,
    second_down,
    master_norm,
    first_norm,
    second_norm,
):
    w_qkv, w_out, w_gateup, w_down = (
        lax.all_gather(master_qkv.astype(jnp.bfloat16), "dp", axis=1, tiled=True),
        lax.all_gather(master_out.astype(jnp.bfloat16), "dp", axis=1, tiled=True),
        lax.all_gather(master_gateup.astype(jnp.bfloat16), "dp", axis=1, tiled=True),
        lax.all_gather(master_down.astype(jnp.bfloat16), "dp", axis=1, tiled=True),
    )
    w_norm = lax.optimization_barrier(master_norm.astype(jnp.bfloat16)).astype(jnp.float32)
    token_count = block_input.shape[0]
    protein_count = token_count // LEN
    share_rows = cotangent.shape[0]
    share_start = lax.axis_index("mp") * share_rows
    head_count = w_qkv.shape[2] // HEAD_DIM
    width_heads = head_count * HEAD_DIM
    deep_alpha = math.sqrt(2.0 * DEPTH)
    score_scale = 1.0 / math.sqrt(HEAD_DIM)
    cos_table, sin_table = rope_tables(positions)
    projected = jnp.einsum("td,jdc->jtc", block_input, w_qkv, preferred_element_type=jnp.float32)
    shaped = projected.reshape(3, token_count, head_count, HEAD_DIM)
    queries = (apply_rope(shaped[0], cos_table, sin_table) * score_scale).astype(jnp.bfloat16)
    key_rows = apply_rope(shaped[1], cos_table, sin_table).astype(jnp.bfloat16)
    value_rows = shaped[2].astype(jnp.bfloat16)
    row_ids = jnp.arange(LEN)[:, None]
    col_ids = jnp.arange(LEN)[None, :]
    attended_parts = []
    log_totals = []
    for protein in range(protein_count):
        row_slice = slice(protein * LEN, (protein + 1) * LEN)
        visible = (col_ids < prefix_len[protein]) | (col_ids <= row_ids)
        scores = jnp.einsum(
            "qhd,khd->hqk",
            queries[row_slice],
            key_rows[row_slice],
            preferred_element_type=jnp.float32,
        )
        scores = jnp.where(visible[None], scores, -1e30)
        row_peak = jnp.max(scores, axis=-1, keepdims=True)
        expo_rows = jnp.exp(scores - row_peak)
        totals = jnp.sum(expo_rows, axis=-1, keepdims=True)
        attn_probs = (expo_rows / totals).astype(jnp.bfloat16)
        attended_parts.append(
            jnp.einsum(
                "hqk,khd->qhd",
                attn_probs,
                value_rows[row_slice],
                preferred_element_type=jnp.float32,
            )
        )
        log_totals.append(row_peak + jnp.log(totals))
    attended = (
        jnp.concatenate(attended_parts, axis=0)
        .reshape(token_count, width_heads)
        .astype(jnp.bfloat16)
    )
    attn_part = jnp.dot(attended, w_out, preferred_element_type=jnp.float32)
    input_share = lax.dynamic_slice_in_dim(block_input, share_start, share_rows, 0).astype(
        jnp.float32
    )
    attn_share = lax.psum_scatter(
        attn_part.astype(jnp.bfloat16), "mp", scatter_dimension=0, tiled=True
    ).astype(jnp.float32)
    middle_share, normed_one, inv_one = norm_forward(
        deep_alpha * input_share + attn_share, w_norm[0], w_norm[1]
    )
    middle_low = lax.all_gather(middle_share.astype(jnp.bfloat16), "mp", axis=0, tiled=True)
    gateup = jnp.einsum("td,jdf->jtf", middle_low, w_gateup, preferred_element_type=jnp.float32)
    gate_rows = gateup[0]
    up_rows = gateup[1]
    activated, gelu_pull = jax.vjp(gelu_tanh, gate_rows)
    hidden = (activated * up_rows).astype(jnp.bfloat16)
    ffn_part = jnp.dot(hidden, w_down, preferred_element_type=jnp.float32)
    ffn_share = lax.psum_scatter(
        ffn_part.astype(jnp.bfloat16), "mp", scatter_dimension=0, tiled=True
    ).astype(jnp.float32)
    out_share, normed_two, inv_two = norm_forward(
        deep_alpha * middle_share + ffn_share, w_norm[2], w_norm[3]
    )
    block_output = out_share.astype(jnp.bfloat16)
    matches = (cluster_id[:, None] == cluster_id[None, :]).astype(jnp.float32)
    counts = jnp.sum(matches, axis=1)
    group_counts = lax.dynamic_slice_in_dim(
        counts, lax.axis_index("dp") * protein_count, protein_count, 0
    )
    row_protein = (share_start + jnp.arange(share_rows)) // LEN
    one_hot = (row_protein[:, None] == jnp.arange(protein_count)[None, :]).astype(jnp.float32)
    row_weight = jnp.sum(one_hot * (1.0 / group_counts)[None, :], axis=1)
    grad_output = cotangent.astype(jnp.float32) * row_weight[:, None]
    grad_h2, grad_gain_two, grad_bias_two = norm_backward(
        grad_output, normed_two, inv_two, w_norm[2]
    )
    ffn_grad_full = lax.all_gather(grad_h2.astype(jnp.bfloat16), "mp", axis=0, tiled=True)
    grad_down_part = jnp.einsum(
        "tf,td->fd", hidden, ffn_grad_full, preferred_element_type=jnp.float32
    )
    grad_hidden = jnp.einsum("td,fd->tf", ffn_grad_full, w_down, preferred_element_type=jnp.float32)
    grad_gate = gelu_pull(grad_hidden * up_rows)[0]
    grad_up = grad_hidden * activated
    grad_gateup_rows = jnp.stack([grad_gate, grad_up]).astype(jnp.bfloat16)
    grad_gateup_part = jnp.einsum(
        "td,jtf->jdf", middle_low, grad_gateup_rows, preferred_element_type=jnp.float32
    )
    middle_grad_part = jnp.einsum(
        "jtf,jdf->td", grad_gateup_rows, w_gateup, preferred_element_type=jnp.float32
    )
    middle_grad = (
        lax.psum_scatter(
            middle_grad_part.astype(jnp.bfloat16), "mp", scatter_dimension=0, tiled=True
        ).astype(jnp.float32)
        + deep_alpha * grad_h2
    )
    grad_h1, grad_gain_one, grad_bias_one = norm_backward(
        middle_grad, normed_one, inv_one, w_norm[0]
    )
    attn_grad_full = lax.all_gather(grad_h1.astype(jnp.bfloat16), "mp", axis=0, tiled=True)
    grad_out_part = jnp.einsum(
        "tc,td->cd", attended, attn_grad_full, preferred_element_type=jnp.float32
    )
    grad_attended = (
        jnp.einsum("td,cd->tc", attn_grad_full, w_out, preferred_element_type=jnp.float32)
        .astype(jnp.bfloat16)
        .reshape(token_count, head_count, HEAD_DIM)
    )
    query_grads = []
    key_grads = []
    value_grads = []
    for protein in range(protein_count):
        row_slice = slice(protein * LEN, (protein + 1) * LEN)
        visible = (col_ids < prefix_len[protein]) | (col_ids <= row_ids)
        scores = jnp.einsum(
            "qhd,khd->hqk",
            queries[row_slice],
            key_rows[row_slice],
            preferred_element_type=jnp.float32,
        )
        scores = jnp.where(visible[None], scores, -1e30)
        probs_full = jnp.exp(scores - log_totals[protein])
        probs_low = probs_full.astype(jnp.bfloat16)
        grad_slice = grad_attended[row_slice]
        value_grads.append(
            jnp.einsum("hqk,qhd->khd", probs_low, grad_slice, preferred_element_type=jnp.float32)
        )
        prob_grads = jnp.einsum(
            "qhd,khd->hqk", grad_slice, value_rows[row_slice], preferred_element_type=jnp.float32
        )
        centre_term = jnp.sum(probs_full * prob_grads, axis=-1, keepdims=True)
        score_grads = (probs_full * (prob_grads - centre_term)).astype(jnp.bfloat16)
        query_grads.append(
            jnp.einsum(
                "hqk,khd->qhd", score_grads, key_rows[row_slice], preferred_element_type=jnp.float32
            )
        )
        key_grads.append(
            jnp.einsum(
                "hqk,qhd->khd", score_grads, queries[row_slice], preferred_element_type=jnp.float32
            )
        )
    grad_query = rope_back(jnp.concatenate(query_grads, axis=0), cos_table, sin_table) * score_scale
    grad_key = rope_back(jnp.concatenate(key_grads, axis=0), cos_table, sin_table)
    grad_value = jnp.concatenate(value_grads, axis=0)
    grad_proj = (
        jnp.stack([grad_query, grad_key, grad_value])
        .reshape(3, token_count, width_heads)
        .astype(jnp.bfloat16)
    )
    grad_qkv_part = jnp.einsum(
        "td,jtc->jdc", block_input, grad_proj, preferred_element_type=jnp.float32
    )
    input_grad_part = jnp.einsum(
        "jtc,jdc->td", grad_proj, w_qkv, preferred_element_type=jnp.float32
    )
    input_grad = (
        lax.psum_scatter(
            input_grad_part.astype(jnp.bfloat16), "mp", scatter_dimension=0, tiled=True
        ).astype(jnp.float32)
        + deep_alpha * grad_h1
    )
    grad_input = input_grad.astype(jnp.bfloat16)
    norm_terms = jnp.stack([grad_gain_one, grad_bias_one, grad_gain_two, grad_bias_two])
    grad_norm = lax.psum(norm_terms, ("dp", "mp"))
    red_qkv, red_out, red_gateup, red_down = (
        lax.psum_scatter(
            grad_qkv_part.astype(jnp.bfloat16), "dp", scatter_dimension=1, tiled=True
        ).astype(jnp.float32),
        lax.psum_scatter(
            grad_out_part.astype(jnp.bfloat16), "dp", scatter_dimension=1, tiled=True
        ).astype(jnp.float32),
        lax.psum_scatter(
            grad_gateup_part.astype(jnp.bfloat16), "dp", scatter_dimension=1, tiled=True
        ).astype(jnp.float32),
        lax.psum_scatter(
            grad_down_part.astype(jnp.bfloat16), "dp", scatter_dimension=1, tiled=True
        ).astype(jnp.float32),
    )
    step_value = step_count[0].astype(jnp.float32)
    rate_qkv = D ** (-0.5)
    rate_out = max(HEADS * HEAD_DIM // 512, 1) ** (-0.5)
    rate_gateup = D ** (-0.5)
    rate_down = max(FF // 64, 1) ** (-0.5)
    rate_norm = 1.0
    new_qkv, new_first_qkv, new_second_qkv = adamw_step(
        master_qkv, first_qkv, second_qkv, red_qkv, rate_qkv, step_value
    )
    new_out, new_first_out, new_second_out = adamw_step(
        master_out, first_out, second_out, red_out, rate_out, step_value
    )
    new_gateup, new_first_gateup, new_second_gateup = adamw_step(
        master_gateup, first_gateup, second_gateup, red_gateup, rate_gateup, step_value
    )
    new_down, new_first_down, new_second_down = adamw_step(
        master_down, first_down, second_down, red_down, rate_down, step_value
    )
    new_norm, new_first_norm, new_second_norm = adamw_step(
        master_norm, first_norm, second_norm, grad_norm, rate_norm, step_value
    )
    return (
        block_output,
        grad_input,
        red_qkv,
        new_qkv,
        new_first_qkv,
        new_second_qkv,
        red_out,
        new_out,
        new_first_out,
        new_second_out,
        red_gateup,
        new_gateup,
        new_first_gateup,
        new_second_gateup,
        red_down,
        new_down,
        new_first_down,
        new_second_down,
        grad_norm,
        new_norm,
        new_first_norm,
        new_second_norm,
    )


MESH = pl.DeviceIdType.MESH
VMEM_BYTES = 61 * 1024 * 1024
BF16 = jnp.bfloat16
F32 = jnp.float32
EMIT = 112
NT = (((1,), (1,)), ((), ()))
ANY = pl.BlockSpec(memory_space=pl.ANY)
VM = pl.BlockSpec(memory_space=pltpu.VMEM)


LIGHT = pl.CostEstimate(flops=1 << 20, bytes_accessed=1 << 16, transcendentals=0)


def nt_dot(left, right):
    return lax.dot_general(left, right, NT, preferred_element_type=F32)


class Ring:
    def __init__(self, send, recv, local):
        self.here = lax.axis_index("dp")
        self.right = (self.here + 1) % 4
        self.left = (self.here + 3) % 4
        self.far = (self.here + 2) % 4
        self.send, self.recv, self.local = send, recv, local

    def copy(self, k, src, dst, other):
        return pltpu.make_async_remote_copy(
            src_ref=src,
            dst_ref=dst,
            send_sem=self.send.at[k],
            recv_sem=self.recv.at[k],
            device_id={"dp": other},
            device_id_type=MESH,
        )


class RingGather:
    def __init__(self, ring, first, half_of, place):
        self.plus_0 = ring.copy(first, half_of(0), place(ring.here, 0), ring.right)
        self.minus_1 = ring.copy(first + 1, half_of(1), place(ring.here, 1), ring.left)
        self.plus_1 = ring.copy(first + 2, half_of(1), place(ring.here, 1), ring.right)
        self.minus_0 = ring.copy(first + 3, half_of(0), place(ring.here, 0), ring.left)
        self.far_0 = ring.copy(first + 4, place(ring.left, 0), place(ring.left, 0), ring.right)
        self.far_1 = ring.copy(first + 5, place(ring.right, 1), place(ring.right, 1), ring.left)
        self.own = [
            pltpu.make_async_copy(half_of(h), place(ring.here, h), ring.local.at[first + h])
            for h in range(2)
        ]
        self.remote = (self.plus_0, self.minus_1, self.plus_1, self.minus_0, self.far_0, self.far_1)

    def start(self):
        for copy in self.remote[:4]:
            copy.start()
        for copy in self.own:
            copy.start()

    def forward(self):
        self.plus_0.wait_recv()
        self.far_0.start()
        self.minus_1.wait_recv()
        self.far_1.start()

    def near(self):
        self.plus_1.wait_recv()
        self.minus_0.wait_recv()

    def far(self):
        self.far_0.wait_recv()
        self.far_1.wait_recv()

    def drain(self):
        for copy in self.remote:
            copy.wait_send()

    def finish(self):
        for copy in self.own:
            copy.wait()
        self.near()
        self.far()
        self.drain()


class RingScatter:
    def __init__(self, ring, first, half_at, buf, out):
        self.buf, self.out = buf, out
        self.plus_far = ring.copy(first, half_at(ring.far, 0), buf.at[0], ring.right)
        self.minus_far = ring.copy(first + 1, half_at(ring.far, 1), buf.at[1], ring.left)
        self.plus_near = ring.copy(first + 2, half_at(ring.right, 1), buf.at[2], ring.right)
        self.minus_near = ring.copy(first + 3, half_at(ring.left, 0), buf.at[3], ring.left)
        self.plus_sum = ring.copy(first + 4, buf.at[6], buf.at[4], ring.right)
        self.minus_sum = ring.copy(first + 5, buf.at[7], buf.at[5], ring.left)
        places = ((ring.right, 0), (ring.left, 1), (ring.here, 0), (ring.here, 1))
        self.loads = [
            pltpu.make_async_copy(half_at(*place), buf.at[6 + k], ring.local.at[first + k])
            for k, place in enumerate(places)
        ]
        self.remote = (
            self.plus_far,
            self.minus_far,
            self.plus_near,
            self.minus_near,
            self.plus_sum,
            self.minus_sum,
        )

    def start_far(self):
        self.plus_far.start()
        self.minus_far.start()

    def start_near(self):
        self.plus_near.start()
        self.minus_near.start()

    def load(self):
        for copy in self.loads:
            copy.start()

    def start(self):
        self.start_far()
        self.start_near()
        self.load()

    def forward(self):
        for copy in self.loads:
            copy.wait()
        self.plus_far.wait_recv()
        for_rows(self.buf.shape[1:], lambda at: add_at(self.buf, 6, 0, at))
        self.plus_sum.start()
        self.minus_far.wait_recv()
        for_rows(self.buf.shape[1:], lambda at: add_at(self.buf, 7, 1, at))
        self.minus_sum.start()

    def finish(self):
        for copy in self.remote[2:]:
            copy.wait_recv()
        buf = self.buf
        for half, terms in enumerate(((8, 3, 4), (9, 2, 5))):
            out = self.out(half)

            def total(at, out=out, terms=terms):
                out[at] = sum(buf[(k,) + at].astype(F32) for k in terms)

            for_rows(buf.shape[1:], total)
        for copy in self.remote:
            copy.wait_send()


def add_at(buf, dst, src, at):
    buf[(dst,) + at] = (buf[(dst,) + at].astype(F32) + buf[(src,) + at].astype(F32)).astype(BF16)


def for_rows(shape, visit):
    def step(i, carry):
        rows = pl.ds(pl.multiple_of(i * 16, 16), 16)
        if len(shape) == 2:
            visit((rows, slice(None)))
        else:
            for j in range(shape[0]):
                visit((j, rows, slice(None)))
        return carry

    lax.fori_loop(0, shape[-2] // 16, step, 0)


def ring_sems(count):
    return [pltpu.SemaphoreType.DMA((count,)) for _ in range(3)]


def row_halves(depth):
    half = depth // 2

    def place(ref):
        def at(owner, part):
            return ref.at[:, pl.ds(pl.multiple_of(owner * depth + part * half, half), half), :]

        return at

    return place


def plane_columns(depth):
    def place(ref):
        def at(owner, part):
            return ref.at[part, :, pl.ds(pl.multiple_of(owner * depth, depth), depth)]

        return at

    return place


def column_halves(depth):
    def place(ref):
        half = ref.shape[0] // 2

        def at(owner, part):
            columns = pl.ds(pl.multiple_of(owner * depth, depth), depth)
            return ref.at[pl.ds(part * half, half), columns]

        return at

    return place


def span_scatter(ring, first, ref, span, buf, out):
    at = plane_columns(ref.shape[2] // 4)(ref.at[:, pl.ds(*span), :])
    return RingScatter(ring, first, at, buf, lambda h: out.at[h])


def greet(others):
    sem = pltpu.get_barrier_semaphore()
    for other in others:
        pl.semaphore_signal(sem, inc=1, device_id=other, device_id_type=MESH)
    pl.semaphore_wait(sem, len(others))


class Square:
    def __init__(self, send, recv, rows):
        me = lax.axis_index("mp")
        self.core = me % 2
        self.x = (me // 2) % 2
        self.y = me // 4
        self.xn = (self.y * 2 + (1 - self.x)) * 2 + self.core
        self.yn = ((1 - self.y) * 2 + self.x) * 2 + self.core
        self.peer = (self.y * 2 + self.x) * 2 + (1 - self.core)
        self.own = self.y * 2 + self.x
        self.xc = self.y * 2 + (1 - self.x)
        self.yc = (1 - self.y) * 2 + self.x
        self.dc = (1 - self.y) * 2 + (1 - self.x)
        self.send, self.recv = send, recv
        cut = rows // 2 // 16 * 16
        self.rows = rows
        self.a = pl.ds(0, cut)
        self.b = pl.ds(cut, rows - cut)
        self.na, self.nb, self.cut = cut, rows - cut, cut

        self.others = [{"mp": self.xn}, {"mp": self.yn}, {"mp": self.peer}]

    def copy(self, k, src, dst, other):
        return pltpu.make_async_remote_copy(
            src_ref=src,
            dst_ref=dst,
            send_sem=self.send.at[k],
            recv_sem=self.recv.at[k],
            device_id={"mp": other},
            device_id_type=MESH,
        )


def add_rows(dst, src, count):
    def step(i, carry):
        rows = pl.ds(pl.multiple_of(i * 16, 16), 16)
        dst[rows, :] = (dst[rows, :].astype(F32) + src[rows, :].astype(F32)).astype(BF16)
        return carry

    lax.fori_loop(0, count // 16, step, 0)


def nothing():
    pass


def square_kernel(
    rows,
    sems,
    gather=None,
    scatter=None,
    ring=None,
    start=nothing,
    first=nothing,
    early=nothing,
    later=nothing,
    between=nothing,
    halfway=nothing,
    half=4,
    middle=nothing,
    end=nothing,
    near_first=False,
    greeting=True,
):
    send, recv, lsem = sems
    sq = Square(send, recv, rows)
    core = sq.core
    if greeting:
        greet(sq.others + ([{"dp": ring.left}, {"dp": ring.right}] if ring is not None else []))

    def place(rel, turn):
        chip_y = (sq.y + rel % 2) % 2
        chip_x = (sq.x + ((rel + 1) // 2) % 2) % 2
        return chip_y * 2 + chip_x, (1 - core + turn) % 2

    if gather is not None:
        compute, share, full, gbuf = gather
        c_own = sq.copy(0, share, gbuf.at[sq.own, core], sq.peer)
        x_a = sq.copy(1, share.at[sq.a], gbuf.at[sq.own, core, sq.a], sq.xn)
        y_b = sq.copy(2, share.at[sq.b], gbuf.at[sq.own, core, sq.b], sq.yn)
        f_x = sq.copy(3, gbuf.at[sq.yc, core, sq.b], gbuf.at[sq.yc, core, sq.b], sq.xn)
        f_y = sq.copy(4, gbuf.at[sq.xc, core, sq.a], gbuf.at[sq.xc, core, sq.a], sq.yn)
        x_b = sq.copy(5, share.at[sq.b], gbuf.at[sq.own, core, sq.b], sq.xn)
        y_a = sq.copy(6, share.at[sq.a], gbuf.at[sq.own, core, sq.a], sq.yn)
        c_d = sq.copy(7, gbuf.at[sq.dc, core], gbuf.at[sq.dc, core], sq.peer)
        c_x = sq.copy(8, gbuf.at[sq.xc, core], gbuf.at[sq.xc, core], sq.peer)
        c_y = sq.copy(9, gbuf.at[sq.yc, core], gbuf.at[sq.yc, core], sq.peer)
        local = pltpu.make_async_copy(share, gbuf.at[sq.own, core], lsem.at[8])
        x_a.start()
        y_b.start()
        if near_first:
            x_b.start()
            y_a.start()
        c_own.start()
        local.start()
    start()
    if gather is not None:

        def take_own():
            c_own.wait_recv()
            local.wait()
            first()

        def forward():
            x_a.wait_recv()
            y_b.wait_recv()
            f_x.start()
            f_y.start()
            if not near_first:
                x_b.start()
                y_a.start()
            early()

        def take_far():
            f_x.wait_recv()
            f_y.wait_recv()
            c_d.start()
            c_d.wait_recv()

        def take_near():
            x_b.wait_recv()
            y_a.wait_recv()
            c_x.start()
            c_y.start()
            later()
            c_x.wait_recv()
            c_y.wait_recv()

        def gather_step(t, carry):
            unit = t // 2
            if near_first:
                chip_y = (sq.y + unit // 2) % 2
                chip_x = (sq.x + unit % 2) % 2
                chip, which = chip_y * 2 + chip_x, (1 - core + t % 2) % 2
            else:
                chip, which = place(unit, t % 2)

            pl.when(t == 0)(take_own)

            @pl.when(t == 2)
            def _():
                forward()
                if near_first:
                    take_near()
                else:
                    take_far()

            pl.when(t == (6 if near_first else 4))(take_far if near_first else take_near)

            if full is not None:
                pltpu.make_async_copy(gbuf.at[chip, which], full.at[chip, which], lsem.at[t]).start()
            compute(t, chip, which)
            return carry

        lax.fori_loop(0, 8 if scatter is None else 6, gather_step, 0)
    between()
    if scatter is not None:
        finish_tile, pbuf, (rcore, rxd, ryd, rx, ry), emit = scatter
        x_d = sq.copy(14, pbuf.at[sq.dc, core, sq.a], rxd, sq.xn)
        y_d = sq.copy(15, pbuf.at[sq.dc, core, sq.b], ryd, sq.yn)
        x_ra = sq.copy(16, pbuf.at[sq.xc, core, sq.a], rx.at[sq.a], sq.xn)
        y_rb = sq.copy(17, pbuf.at[sq.yc, core, sq.b], ry.at[sq.b], sq.yn)
        x_rb = sq.copy(18, pbuf.at[sq.xc, core, sq.b], rx.at[sq.b], sq.xn)
        y_ra = sq.copy(19, pbuf.at[sq.yc, core, sq.a], ry.at[sq.a], sq.yn)

        def scatter_step(t, carry):
            turn = t % 2
            rel = (t // 2 + 1) % 4
            chip, which = place(rel, turn)

            @pl.when(t == half)
            def _():
                halfway()

            finish_tile(t, chip, which)
            to_peer = sq.copy(10 + rel, pbuf.at[chip, which], rcore.at[chip], sq.peer)

            @pl.when(turn == 0)
            def _():
                to_peer.start()

            @pl.when(turn == 1)
            def _():
                to_peer.wait_recv()
                add_rows(pbuf.at[chip, which], rcore.at[chip], rows)

            @pl.when(t == 1)
            def _():
                x_d.start()
                y_d.start()

            @pl.when(t == 3)
            def _():
                x_ra.start()

            @pl.when(t == 5)
            def _():
                y_rb.start()

            return carry

        if gather is None:
            lax.fori_loop(0, 8, scatter_step, 0)
        else:
            lax.fori_loop(0, 2, scatter_step, 0)
            lax.fori_loop(6, 8, gather_step, 0)
            lax.fori_loop(2, 8, scatter_step, 0)
        x_d.wait_recv()
        add_rows(pbuf.at[sq.yc, core, sq.a], rxd, sq.na)
        y_ra.start()
        y_d.wait_recv()
        add_rows(pbuf.at[sq.xc, core, sq.b], ryd, sq.nb)
        x_rb.start()
        middle()
        x_ra.wait_recv()
        y_rb.wait_recv()
        y_ra.wait_recv()
        x_rb.wait_recv()

        def last(i, carry):
            part = pl.ds(pl.multiple_of(i * EMIT, 16), EMIT)
            emit(
                part,
                pbuf[sq.own, core, part, :].astype(F32)
                + rx[part, :].astype(F32)
                + ry[part, :].astype(F32),
            )
            return carry

        lax.fori_loop(0, rows // EMIT, last, 0)
        for k in range(4):
            sq.copy(10 + k, pbuf.at[0, 0], rcore.at[0], sq.peer).wait_send()
        for copy in (x_d, y_d, x_ra, y_rb, x_rb, y_ra):
            copy.wait_send()
    end()
    if gather is not None:
        for copy in (c_own, x_a, y_b, f_x, f_y, x_b, y_a, c_d, c_x, c_y):
            copy.wait_send()
        if full is not None:
            for t in range(8):
                pltpu.make_async_copy(gbuf.at[0, 0], full.at[0, 0], lsem.at[t]).wait()


def row_mean(values):
    return jnp.mean(values, axis=-1, keepdims=True)


def norm_rows(values):
    centre = values - row_mean(values)
    inv_std = lax.rsqrt(row_mean(centre * centre) + norm_epsilon)
    return centre * inv_std, inv_std


def norm_rows_back(grads, normed, inv_std, gain):
    grad_normed = grads * gain
    return inv_std * (grad_normed - row_mean(grad_normed) - normed * row_mean(grad_normed * normed))


def fold(values):
    return sum(values[i : i + 8] for i in range(0, EMIT, 8))


def scatter_scratch(rows, width, with_sums=True):
    cut = rows // 2 // 16 * 16
    return ([pltpu.VMEM((4, 2, rows, width), BF16)] if with_sums else []) + [
        pltpu.VMEM((4, rows, width), BF16),
        pltpu.VMEM((cut, width), BF16),
        pltpu.VMEM((rows - cut, width), BF16),
        pltpu.VMEM((rows, width), BF16),
        pltpu.VMEM((rows, width), BF16),
    ]


SEMS = [
    pltpu.SemaphoreType.DMA((20,)),
    pltpu.SemaphoreType.DMA((20,)),
    pltpu.SemaphoreType.DMA((9,)),
]


def params(collective_id):
    return pltpu.CompilerParams(
        collective_id=collective_id, has_side_effects=True, vmem_limit_bytes=VMEM_BYTES
    )


def whole(shape):
    return pl.BlockSpec(shape, lambda *_: (0,) * len(shape))


def front_call(block_input, low_qkv, low_out, gateup, positions, prefix_len, w_norm, rows, spans):
    tokens, width = block_input.shape
    depth, cols = low_qkv.shape[1:]
    tiles = tokens // rows
    heads = cols // HEAD_DIM
    proteins = tokens // LEN
    scale = 1.0 / math.sqrt(HEAD_DIM)
    alpha = math.sqrt(2.0 * DEPTH)
    half = depth // 2
    out_half = cols // 2
    span = spans[-1][0] + spans[-1][1]
    live = gateup.shape[1]

    def kernel(
        pre_ref, x_ref, low_ref, lo_ref, lg_ref, pos_ref, norm_ref,
        q_ref, k_ref, v_ref, o_ref, p_ref, cos_ref, sin_ref, w_ref, wo_ref, wg_ref,
        x1_ref, x1b_ref, n1_ref, inv_ref,
        x_buf, w_buf, acc, q_buf, k_buf, v_buf, o_buf, cos_buf, sin_buf, p_buf, wo_buf, xs_buf, wide_g, low_g,
        rcore, rxd, ryd, rx, ry, xsem, psem, ksem, send, recv, lsem, zsend, zrecv, zlocal,
    ):
        ring = Ring(zsend, zrecv, zlocal)
        sems = Square(send, recv, rows)
        gather = RingGather(
            ring, 0, lambda h: low_ref.at[:, pl.ds(h * half, half), :], row_halves(depth)(w_buf)
        )
        gather_out = RingGather(
            ring, 6, lambda h: lo_ref.at[pl.ds(h * out_half, out_half), :], column_halves(depth)(wo_buf)
        )
        gathers = []
        for n, (low, size) in enumerate(spans):
            at = pl.ds(low, size)
            gathers.append(
                RingGather(
                    ring,
                    12 + 6 * n,
                    lambda h, at=at: low_g.at[h, at, :],
                    plane_columns(depth)(wg_ref.at[:, at, :]),
                )
            )
        own_rows = pltpu.make_async_copy(x_ref.at[sems.own, sems.core], xs_buf, xsem.at[8])
        load_g = pltpu.make_async_copy(lg_ref, wide_g, xsem.at[9])
        kept = ((q_buf, q_ref), (k_buf, k_ref), (v_buf, v_ref), (cos_buf, cos_ref), (sin_buf, sin_ref))
        keeps = [pltpu.make_async_copy(src, dst, ksem.at[n]) for n, (src, dst) in enumerate(kept)]
        keep_w = pltpu.make_async_copy(w_buf, w_ref, ksem.at[5])
        keep_wo = pltpu.make_async_copy(wo_buf, wo_ref, ksem.at[6])
        keep_o = pltpu.make_async_copy(o_buf, o_ref, ksem.at[7])

        def x_copy(t):
            return pltpu.make_async_copy(x_ref.at[t // 2, t % 2], x_buf.at[t // 2, t % 2], xsem.at[t])

        def start_tile(t, carry):
            x_copy(t).start()
            return carry

        lax.fori_loop(0, tiles, start_tile, 0)
        own_rows.start()
        load_g.start()
        greet(sems.others + [{"dp": ring.left}, {"dp": ring.right}])
        gather.start()
        for copy in gather.own:
            copy.wait()

        def part(t, j, owner):
            depths = pl.ds(pl.multiple_of(owner * depth, depth), depth)
            return jnp.dot(
                x_buf[t // 2, t % 2, :, depths], w_buf[j, depths, :], preferred_element_type=F32
            )

        def tile_rows(t):
            return pl.ds(pl.multiple_of(t * rows, 16), rows)

        def own_tile(t, carry):
            x_copy(t).wait()
            for j in range(3):
                acc[t, j] = part(t, j, ring.here)
            return carry

        lax.fori_loop(0, tiles, own_tile, 0)
        rung = lax.broadcasted_iota(jnp.int32, (HEAD_DIM, 1), 0)
        ladder = (rung % (HEAD_DIM // 2)).astype(F32)
        inverse = jnp.exp(ladder * (-2.0 * math.log(10000.0) / HEAD_DIM))
        sign = jnp.where(rung < HEAD_DIM // 2, -1.0, 1.0)

        def table_tile(b, carry):
            angles = inverse * pos_ref[pl.ds(b, 1), :].astype(F32)
            here = pl.ds(pl.multiple_of(b * HEAD_DIM, HEAD_DIM), HEAD_DIM)
            cos_buf[here, :] = jnp.cos(angles).T
            sin_buf[here, :] = (jnp.sin(angles) * sign).T
            return carry

        blocks = tokens // HEAD_DIM
        lax.fori_loop(0, blocks // 2, table_tile, 0)
        gather.forward()
        gather_out.start()
        lax.fori_loop(blocks // 2, blocks, table_tile, 0)
        load_g.wait()

        def round_rows(i, carry):
            here = pl.ds(pl.multiple_of(i * 16, 16), 16)
            for h in range(2):
                low_g[h, here, :] = wide_g[h, here, :].astype(BF16)
            return carry

        lax.fori_loop(0, live // 16, round_rows, 0)
        gather.near()

        def near_tile(t, carry):
            for j in range(3):
                acc[t, j] += part(t, j, ring.left) + part(t, j, ring.right)
            return carry

        lax.fori_loop(0, tiles, near_tile, 0)
        gather.far()
        gathers[0].start()
        keep_w.start()

        def far_tile(t, carry):
            here = tile_rows(t)
            for j, buf in enumerate((q_buf, k_buf)):
                a = acc[t, j] + part(t, j, ring.far)
                for h in range(heads):
                    cut = slice(h * HEAD_DIM, (h + 1) * HEAD_DIM)
                    turned = a[:, cut] * cos_buf[here, :]
                    turned += pltpu.roll(a[:, cut], HEAD_DIM // 2, 1) * sin_buf[here, :]
                    if j == 0:
                        turned = turned * scale
                    buf[here, cut] = turned.astype(BF16)
            v_buf[here, :] = (acc[t, 2] + part(t, 2, ring.far)).astype(BF16)
            return carry

        lax.fori_loop(0, tiles, far_tile, 0)
        gather_out.forward()
        for keep in keeps:
            keep.start()

        def protein(p, carry):
            prefix = pre_ref[p]
            keys = pl.ds(pl.multiple_of(p * LEN, LEN), LEN)

            @pl.when(p == proteins - 1)
            def _():
                gathers[0].forward()
                gathers[1].start()

            for h in range(heads):
                cut = slice(h * HEAD_DIM, (h + 1) * HEAD_DIM)
                store = pltpu.make_async_copy(p_buf.at[h], p_ref.at[p, h], psem.at[h])

                @pl.when(p > 0)
                def _():
                    store.wait()

                for i in range(LEN // BLOCK):
                    here = pl.ds(pl.multiple_of(p * LEN + i * BLOCK, BLOCK), BLOCK)
                    s = nt_dot(q_buf[here, cut], k_buf[keys, cut])
                    col = lax.broadcasted_iota(jnp.int32, s.shape, 1)
                    row = lax.broadcasted_iota(jnp.int32, (BLOCK, 1), 0) + i * BLOCK
                    s = jnp.where(col < jnp.maximum(prefix, row + 1), s, -1e30)
                    e = jnp.exp(s - jnp.max(s, axis=-1, keepdims=True))
                    prob = (e * (1.0 / jnp.sum(e, axis=-1, keepdims=True))).astype(BF16)
                    p_buf[h, i * BLOCK : (i + 1) * BLOCK, :] = prob
                    mixed = jnp.dot(prob, v_buf[keys, cut], preferred_element_type=F32)
                    o_buf[here, cut] = mixed.astype(BF16)
                store.start()
            return carry

        lax.fori_loop(0, proteins, protein, 0)
        for copy in gather_out.own:
            copy.wait()
        gather_out.near()
        gather_out.far()
        keep_wo.start()
        keep_o.start()
        own_rows.wait()

        def compute(t, chip, which):
            tile = o_buf[tile_rows(chip * 2 + which), :]
            x_buf[chip, which] = jnp.dot(tile, wo_buf[...], preferred_element_type=F32).astype(BF16)

        def emit(at, value):
            normed, inv_std = norm_rows(alpha * xs_buf[at, :].astype(F32) + value)
            x1 = normed * norm_ref[0:1, :] + norm_ref[1:2, :]
            x1_ref[at, :] = x1
            x1b_ref[at, :] = x1.astype(BF16)
            n1_ref[at, :] = normed
            inv_ref[at, :] = jnp.broadcast_to(inv_std, (EMIT, HEAD_DIM))

        square_kernel(
            rows,
            (send, recv, lsem),
            scatter=(compute, x_buf, (rcore, rxd, ryd, rx, ry), emit),
            middle=gathers[1].forward,
            greeting=False,
        )
        for other in gathers:
            other.finish()
        gather.drain()
        gather_out.drain()
        for keep in keeps + [keep_w, keep_wo, keep_o]:
            keep.wait()
        for h in range(heads):
            pltpu.make_async_copy(p_buf.at[h], p_ref.at[0, h], psem.at[h]).wait()

    wide = jax.ShapeDtypeStruct((rows, width), F32)
    return pl.pallas_call(
        kernel,
        out_shape=[jax.ShapeDtypeStruct((tokens, cols), BF16)] * 4
        + [jax.ShapeDtypeStruct((proteins, heads, LEN, LEN), BF16)]
        + [jax.ShapeDtypeStruct((tokens, HEAD_DIM), F32)] * 2
        + [
            jax.ShapeDtypeStruct((3, width, cols), BF16),
            jax.ShapeDtypeStruct((cols, width), BF16),
            jax.ShapeDtypeStruct((2, span, width), BF16),
            wide,
            jax.ShapeDtypeStruct((rows, width), BF16),
            wide,
            jax.ShapeDtypeStruct((rows, HEAD_DIM), F32),
        ],
        in_specs=[pl.BlockSpec(memory_space=pltpu.SMEM)] + [ANY] * 4 + [VM, VM],
        out_specs=[ANY] * 10 + [VM] * 4,
        scratch_shapes=[
            pltpu.VMEM((4, 2, rows, width), BF16),
            pltpu.VMEM((3, width, cols), BF16),
            pltpu.VMEM((tiles, 3, rows, cols), F32),
        ]
        + [pltpu.VMEM((tokens, cols), BF16)] * 4
        + [pltpu.VMEM((tokens, HEAD_DIM), F32)] * 2
        + [
            pltpu.VMEM((heads, LEN, LEN), BF16),
            pltpu.VMEM((cols, width), BF16),
            pltpu.VMEM((rows, width), BF16),
            pltpu.VMEM(gateup.shape, F32),
            pltpu.VMEM(gateup.shape, BF16),
        ]
        + scatter_scratch(rows, width, False)
        + [
            pltpu.SemaphoreType.DMA((10,)),
            pltpu.SemaphoreType.DMA((heads,)),
            pltpu.SemaphoreType.DMA((8,)),
        ]
        + SEMS
        + ring_sems(12 + 6 * len(spans)),
        compiler_params=params(0),
        cost_estimate=LIGHT,
        name="front",
    )(
        prefix_len,
        block_input.reshape(4, 2, rows, width),
        low_qkv,
        low_out,
        gateup,
        positions.reshape(tokens // HEAD_DIM, HEAD_DIM),
        w_norm,
    )


BLOCK = 128
BACK_BLOCK = 448
TN = (((0,), (0,)), ((), ()))


def attention_back_call(
    queries, key_rows, value_rows, probs, attended, grad_attended, cos_table, sin_table, norm_terms,
    grad_out_part,
):
    tokens, cols = queries.shape
    proteins = tokens // LEN
    heads = cols // HEAD_DIM
    scale = 1.0 / math.sqrt(HEAD_DIM)
    last = proteins * heads - 1
    depth = grad_out_part.shape[1] // 4

    def kernel(
        q_ref, k_ref, v_ref, p_ref, o_ref, do_ref, cos_ref, sin_ref, nt_ref, go_ref,
        da_ref, norm_ref, red_o,
        ds_buf, sums, got, nsend, nrecv, buf_o, send, recv, local,
    ):
        step = pl.program_id(0) * heads + pl.program_id(1)
        ring = Ring(send, recv, local)
        part = cols // 2
        side = RingScatter(
            ring, 0, column_halves(depth)(go_ref), buf_o, lambda h: red_o.at[pl.ds(h * part, part), :]
        )
        sq = Square(nsend, nrecv, 32)
        partners = [
            {"mp": sq.peer},
            {"mp": sq.xn},
            {"mp": sq.yn},
            {"dp": ring.here + 1 - 2 * (ring.here % 2)},
            {"dp": 3 - ring.here},
        ]
        swaps = [
            pltpu.make_async_remote_copy(
                src_ref=sums.at[k],
                dst_ref=got.at[k],
                send_sem=nsend.at[k],
                recv_sem=nrecv.at[k],
                device_id=other,
                device_id_type=MESH,
            )
            for k, other in enumerate(partners)
        ]

        @pl.when(step == 0)
        def _():
            sums[0] = nt_ref[...]
            greet(sq.others + [{"dp": ring.left}, {"dp": ring.right}])
            side.start()
            swaps[0].start()

        for k in range(5):

            @pl.when(step == k + 1)
            def _():
                swaps[k].wait()
                if k < 4:
                    sums[k + 1] = sums[k] + got[k]
                    swaps[k + 1].start()
                else:
                    norm_ref[...] = sums[k] + got[k]

        @pl.when(step == last // 2)
        def _():
            side.forward()

        for i in range(LEN // BACK_BLOCK):
            rows = slice(i * BACK_BLOCK, (i + 1) * BACK_BLOCK)
            do = do_ref[rows, :]
            delta = jnp.sum(do.astype(F32) * o_ref[rows, :].astype(F32), axis=-1, keepdims=True)
            dp = nt_dot(do, v_ref[...])
            ds = (p_ref[0, 0, rows, :].astype(F32) * (dp - delta)).astype(BF16)
            ds_buf[rows, :] = ds
            dq = jnp.dot(ds, k_ref[...], preferred_element_type=F32)
            turned = dq * cos_ref[rows, :] - pltpu.roll(dq, HEAD_DIM // 2, 1) * sin_ref[rows, :]
            da_ref[0, rows, :] = (turned * scale).astype(BF16)
        da_ref[2] = lax.dot_general(p_ref[0, 0], do_ref[...], TN, preferred_element_type=F32).astype(BF16)
        dk = lax.dot_general(ds_buf[...], q_ref[...], TN, preferred_element_type=F32)
        turned = dk * cos_ref[...] - pltpu.roll(dk, HEAD_DIM // 2, 1) * sin_ref[...]
        da_ref[1] = turned.astype(BF16)

        @pl.when(step == last)
        def _():
            side.finish()

    tile = pl.BlockSpec((LEN, HEAD_DIM), lambda p, h: (p, h))
    table = pl.BlockSpec((LEN, HEAD_DIM), lambda p, h: (p, 0))
    return pl.pallas_call(
        kernel,
        grid=(proteins, heads),
        in_specs=[tile] * 3
        + [pl.BlockSpec((1, 1, LEN, LEN), lambda p, h: (p, h, 0, 0)), tile, tile, table, table]
        + [whole(norm_terms.shape), ANY],
        out_specs=[
            pl.BlockSpec((3, LEN, HEAD_DIM), lambda p, h: (0, p, h)),
            whole(norm_terms.shape),
            whole((cols, depth)),
        ],
        out_shape=[
            jax.ShapeDtypeStruct((3, tokens, cols), BF16),
            jax.ShapeDtypeStruct(norm_terms.shape, F32),
            jax.ShapeDtypeStruct((cols, depth), F32),
        ],
        scratch_shapes=[
            pltpu.VMEM((LEN, LEN), BF16),
            pltpu.VMEM((5,) + norm_terms.shape, F32),
            pltpu.VMEM((5,) + norm_terms.shape, F32),
            pltpu.SemaphoreType.DMA((5,)),
            pltpu.SemaphoreType.DMA((5,)),
            pltpu.VMEM((10, cols // 2, depth), BF16),
        ]
        + ring_sems(6),
        compiler_params=params(7),
        cost_estimate=LIGHT,
        name="attention_back",
    )(
        queries,
        key_rows,
        value_rows,
        probs,
        attended,
        grad_attended,
        cos_table,
        sin_table,
        norm_terms,
        grad_out_part,
    )


def ffn_call(middle_low, middle_share, w_gateup, low_down, cotangent, row_weight, w_norm):
    rows = middle_low.shape[0]
    live, depth = low_down.shape
    curve = math.sqrt(2.0 / math.pi)
    alpha = math.sqrt(2.0 * DEPTH)

    def kernel(
        share, x1_ref, wg_ref, ld_ref, cot_ref, rw_ref, norm_ref,
        y_ref, dh_ref, dhb_ref, terms_ref, full, hid_ref, act_ref, pull_ref, wd_ref,
        w_g, w_d, gbuf, hid_buf, stage, pbuf, rcore, rxd, ryd, rx, ry, sums,
        wsem, osem, hsem, send, recv, lsem, zsend, zrecv, zlocal,
    ):
        ring = Ring(zsend, zrecv, zlocal)
        half = live // 2
        gather_d = RingGather(ring, 0, lambda h: ld_ref.at[pl.ds(h * half, half), :], column_halves(depth)(w_d))
        load_g = pltpu.make_async_copy(wg_ref, w_g, wsem.at[0])
        load_g.start()
        keep_d = pltpu.make_async_copy(w_d, wd_ref, wsem.at[1])
        outs = (act_ref, pull_ref)

        def between():
            for copy in gather_d.own:
                copy.wait()
            gather_d.near()
            gather_d.far()
            keep_d.start()

        def compute(t, chip, which):
            slot = t % 2

            @pl.when(t >= 2)
            def _():
                for k, ref in enumerate(outs):
                    pltpu.make_async_copy(stage.at[slot, k], ref.at[chip, which], osem.at[slot, k]).wait()

            tile = gbuf[chip, which]
            gate = nt_dot(tile, w_g[0])
            up = nt_dot(tile, w_g[1])
            square = gate * gate
            bent = jnp.tanh(curve * gate * (1.0 + 0.044715 * square))
            half = 0.5 * (1.0 + bent)
            act = gate * half
            slope = half + 0.5 * curve * gate * (1.0 - bent * bent) * (1.0 + 3.0 * 0.044715 * square)
            hid_buf[chip, which] = (act * up).astype(BF16)
            stage[slot, 0] = act.astype(BF16)
            stage[slot, 1] = (slope * up).astype(BF16)
            for k, ref in enumerate(outs):
                pltpu.make_async_copy(stage.at[slot, k], ref.at[chip, which], osem.at[slot, k]).start()
            pltpu.make_async_copy(hid_buf.at[chip, which], hid_ref.at[chip, which], hsem.at[t]).start()

        def finish_tile(t, chip, which):
            part = jnp.dot(hid_buf[chip, which], w_d[...], preferred_element_type=F32)
            pbuf[chip, which] = part.astype(BF16)

        def emit(at, value):
            normed, inv_std = norm_rows(alpha * x1_ref[at, :] + value)
            gain = norm_ref[2:3, :]
            y_ref[at, :] = (normed * gain + norm_ref[3:4, :]).astype(BF16)
            dy = cot_ref[at, :].astype(F32) * rw_ref[at, :]
            sums[0] += fold(dy * normed)
            sums[1] += fold(dy)
            dh = norm_rows_back(dy, normed, inv_std, gain)
            dh_ref[at, :] = dh
            dhb_ref[at, :] = dh.astype(BF16)

        sums[...] = jnp.zeros_like(sums)

        def end():
            terms_ref[...] = jnp.sum(sums[...], axis=1)
            for slot in range(2):
                for k, ref in enumerate(outs):
                    pltpu.make_async_copy(stage.at[slot, k], ref.at[0, 0], osem.at[slot, k]).wait()
            for t in range(8):
                pltpu.make_async_copy(hid_buf.at[0, 0], hid_ref.at[0, 0], hsem.at[t]).wait()
            keep_d.wait()
            gather_d.drain()

        square_kernel(
            rows,
            (send, recv, lsem),
            gather=(compute, share, full, gbuf),
            scatter=(finish_tile, pbuf, (rcore, rxd, ryd, rx, ry), emit),
            ring=ring,
            start=gather_d.start,
            first=load_g.wait,
            early=gather_d.forward,
            between=between,
            end=end,
        )

    kept = jax.ShapeDtypeStruct((4, 2, rows, live), BF16)
    return pl.pallas_call(
        kernel,
        out_shape=[
            jax.ShapeDtypeStruct((rows, D), BF16),
            jax.ShapeDtypeStruct((rows, D), F32),
            jax.ShapeDtypeStruct((rows, D), BF16),
            jax.ShapeDtypeStruct((2, D), F32),
            jax.ShapeDtypeStruct((4, 2, rows, D), BF16),
            kept,
            kept,
            kept,
            jax.ShapeDtypeStruct((live, D), BF16),
        ],
        in_specs=[ANY, VM, ANY, ANY, VM, VM, VM],
        out_specs=[VM] * 4 + [ANY] * 5,
        scratch_shapes=[
            pltpu.VMEM((2, live, D), BF16),
            pltpu.VMEM((live, D), BF16),
            pltpu.VMEM((4, 2, rows, D), BF16),
            pltpu.VMEM((4, 2, rows, live), BF16),
            pltpu.VMEM((2, 2, rows, live), BF16),
        ]
        + scatter_scratch(rows, D)
        + [
            pltpu.VMEM((2, 8, D), F32),
            pltpu.SemaphoreType.DMA((2,)),
            pltpu.SemaphoreType.DMA((2, 2)),
            pltpu.SemaphoreType.DMA((8,)),
        ]
        + SEMS
        + ring_sems(6),
        compiler_params=params(1),
        cost_estimate=LIGHT,
        name="ffn",
    )(middle_low, middle_share, w_gateup, low_down, cotangent, row_weight, w_norm)


def ffn_back_call(ffn_grad, act, pull, w_down):
    rows = ffn_grad.shape[0]
    live = w_down.shape[0]

    def kernel(share, act_ref, pull_ref, wd_ref, full, dg_ref, w_d, gbuf, load, stage, wsem, isem, osem, send, recv, lsem):
        weight = pltpu.make_async_copy(wd_ref, w_d, wsem.at[0])
        weight.start()

        def compute(t, chip, which):
            slot = t % 2
            loads = [
                pltpu.make_async_copy(ref.at[chip, which], load.at[k], isem.at[k])
                for k, ref in enumerate((act_ref, pull_ref))
            ]
            stores = [
                pltpu.make_async_copy(stage.at[slot, k], dg_ref.at[k, chip, which], osem.at[slot, k])
                for k in range(2)
            ]
            for copy in loads:
                copy.start()

            @pl.when(t >= 2)
            def _():
                for copy in stores:
                    copy.wait()

            dh = nt_dot(gbuf[chip, which], w_d[...])
            for copy in loads:
                copy.wait()
            stage[slot, 0] = (dh * load[1].astype(F32)).astype(BF16)
            stage[slot, 1] = (dh * load[0].astype(F32)).astype(BF16)
            for copy in stores:
                copy.start()

        def end():
            for slot in range(2):
                for k in range(2):
                    pltpu.make_async_copy(stage.at[slot, k], dg_ref.at[k, 0, 0], osem.at[slot, k]).wait()

        square_kernel(
            rows,
            (send, recv, lsem),
            gather=(compute, share, full, gbuf),
            first=weight.wait,
            end=end,
            near_first=True,
        )

    return pl.pallas_call(
        kernel,
        out_shape=[
            jax.ShapeDtypeStruct((4, 2, rows, D), BF16),
            jax.ShapeDtypeStruct((2, 4, 2, rows, live), BF16),
        ],
        in_specs=[ANY] * 4,
        out_specs=[ANY, ANY],
        scratch_shapes=[
            pltpu.VMEM((live, D), BF16),
            pltpu.VMEM((4, 2, rows, D), BF16),
            pltpu.VMEM((2, rows, live), BF16),
            pltpu.VMEM((2, 2, rows, live), BF16),
            pltpu.SemaphoreType.DMA((1,)),
            pltpu.SemaphoreType.DMA((2,)),
            pltpu.SemaphoreType.DMA((2, 2)),
        ]
        + SEMS,
        compiler_params=params(2),
        cost_estimate=LIGHT,
        name="ffn_back",
    )(ffn_grad, act, pull, w_down)


def middle_back_call(grad_gateup_rows, w_gateup, grad_gateup_part, spans, grad_h2, normed, inv_std, w_norm):
    rows = grad_h2.shape[0]
    alpha = math.sqrt(2.0 * DEPTH)
    live, width = grad_gateup_part.shape[1:]
    depth = width // 4

    def kernel(
        dg_ref, wg_ref, gg_ref, dh2_ref, n1_ref, inv_ref, norm_ref, dh_ref, dhb_ref, terms_ref, red_0, red_1,
        w_g, load, buf_0, buf_1, pbuf, rcore, rxd, ryd, rx, ry, sums, wsem, isem, send, recv, lsem, zsend, zrecv, zlocal,
    ):
        ring = Ring(zsend, zrecv, zlocal)
        early = span_scatter(ring, 0, gg_ref, spans[0], buf_0, red_0)
        late = span_scatter(ring, 6, gg_ref, spans[1], buf_1, red_1)
        weight = pltpu.make_async_copy(wg_ref, w_g, wsem.at[0])
        weight.start()
        me = lax.axis_index("mp")
        core, x, y = me % 2, (me // 2) % 2, me // 4

        def loads(t):
            rel = (t // 2 + 1) % 4
            chip = ((y + rel % 2) % 2) * 2 + (x + ((rel + 1) // 2) % 2) % 2
            which = (1 - core + t % 2) % 2
            return [
                pltpu.make_async_copy(dg_ref.at[k, chip, which], load.at[t % 2, k], isem.at[t % 2, k])
                for k in range(2)
            ]

        for copy in loads(0):
            copy.start()

        def compute(t, chip, which):
            @pl.when(t < 7)
            def _():
                for copy in loads(t + 1):
                    copy.start()

            for copy in loads(t):
                copy.wait()
            slot = t % 2
            part = jnp.dot(load[slot, 0], w_g[0], preferred_element_type=F32)
            part += jnp.dot(load[slot, 1], w_g[1], preferred_element_type=F32)
            pbuf[chip, which] = part.astype(BF16)

        sums[...] = jnp.zeros_like(sums)

        def emit(at, value):
            grads = value + alpha * dh2_ref[at, :]
            normed = n1_ref[at, :]
            sums[0] += fold(grads * normed)
            sums[1] += fold(grads)
            dh = norm_rows_back(grads, normed, inv_ref[at, 0:1], norm_ref[0:1, :])
            dh_ref[at, :] = dh
            dhb_ref[at, :] = dh.astype(BF16)

        def end():
            terms_ref[...] = jnp.sum(sums[...], axis=1)
            early.finish()
            late.finish()

        square_kernel(
            rows,
            (send, recv, lsem),
            scatter=(compute, pbuf, (rcore, rxd, ryd, rx, ry), emit),
            ring=ring,
            start=lambda: (early.start(), weight.wait()),
            halfway=lambda: (early.forward(), late.start()),
            middle=late.forward,
            end=end,
        )

    return pl.pallas_call(
        kernel,
        out_shape=[
            jax.ShapeDtypeStruct((rows, D), F32),
            jax.ShapeDtypeStruct((rows, D), BF16),
            jax.ShapeDtypeStruct((2, D), F32),
            jax.ShapeDtypeStruct((2, spans[0][1], depth), F32),
            jax.ShapeDtypeStruct((2, spans[1][1], depth), F32),
        ],
        in_specs=[ANY] * 3 + [VM] * 4,
        out_specs=[VM] * 5,
        scratch_shapes=[
            pltpu.VMEM((2, live, D), BF16),
            pltpu.VMEM((2, 2, rows, live), BF16),
            pltpu.VMEM((10, spans[0][1], depth), BF16),
            pltpu.VMEM((10, spans[1][1], depth), BF16),
        ]
        + scatter_scratch(rows, D)
        + [pltpu.VMEM((2, 8, D), F32)]
        + [pltpu.SemaphoreType.DMA((1,)), pltpu.SemaphoreType.DMA((2, 2))]
        + SEMS
        + ring_sems(12),
        compiler_params=params(8),
        cost_estimate=LIGHT,
        name="middle_back",
    )(grad_gateup_rows, w_gateup, grad_gateup_part, grad_h2, normed, inv_std, w_norm)


def out_back_call(attn_grad, w_out, attended, grad_gateup_part, span):
    rows = attn_grad.shape[0]
    cols = w_out.shape[0]
    depth = grad_gateup_part.shape[2] // 4

    def kernel(
        share, w_ref, o_ref, gg_ref, dout, go_ref, red,
        w_buf, gbuf, buf, acc, wsem, send, recv, lsem, zsend, zrecv, zlocal,
    ):
        ring = Ring(zsend, zrecv, zlocal)
        side = span_scatter(ring, 0, gg_ref, span, buf, red)
        weight = pltpu.make_async_copy(w_ref, w_buf, wsem.at[0])
        weight.start()

        def compute(t, chip, which):
            tile = gbuf[chip, which]
            dout[chip, which] = nt_dot(tile, w_buf[...]).astype(BF16)
            part = lax.dot_general(o_ref[chip, which], tile, TN, preferred_element_type=F32)

            @pl.when(t == 0)
            def _():
                acc[...] = part

            @pl.when(t > 0)
            def _():
                acc[...] += part

        def end():
            go_ref[...] = acc[...].astype(BF16)
            side.finish()

        square_kernel(
            rows,
            (send, recv, lsem),
            gather=(compute, share, None, gbuf),
            ring=ring,
            start=side.start,
            first=weight.wait,
            early=side.forward,
            end=end,
            near_first=True,
        )

    return pl.pallas_call(
        kernel,
        out_shape=[
            jax.ShapeDtypeStruct((4, 2, rows, cols), BF16),
            jax.ShapeDtypeStruct((cols, D), BF16),
            jax.ShapeDtypeStruct((2, span[1], depth), F32),
        ],
        in_specs=[ANY, ANY, VM, ANY],
        out_specs=[VM, VM, VM],
        scratch_shapes=[
            pltpu.VMEM((cols, D), BF16),
            pltpu.VMEM((4, 2, rows, D), BF16),
            pltpu.VMEM((10, span[1], depth), BF16),
            pltpu.VMEM((cols, D), F32),
            pltpu.SemaphoreType.DMA((1,)),
        ]
        + SEMS
        + ring_sems(6),
        compiler_params=params(3),
        cost_estimate=LIGHT,
        name="out_back",
    )(attn_grad, w_out, attended.reshape(4, 2, rows, cols), grad_gateup_part)


def input_back_call(grad_proj, w_qkv, block_input, grad_gateup_part, span, grad_h1):
    rows = grad_h1.shape[0]
    alpha = math.sqrt(2.0 * DEPTH)
    width, cols = w_qkv.shape[1:]
    depth = width // 4
    tokens = block_input.shape[0]

    def kernel(
        da_ref, w_ref, x_ref, gg_ref, dh_ref, out, red_q, red_g,
        w_buf, x_buf, gq_buf, buf_q, buf_g, pbuf, rcore, rxd, ryd, rx, ry,
        wsem, send, recv, lsem, zsend, zrecv, zlocal,
    ):
        ring = Ring(zsend, zrecv, zlocal)
        half = depth // 2
        side_g = span_scatter(ring, 0, gg_ref, span, buf_g, red_g)
        side_q = RingScatter(
            ring, 6, row_halves(depth)(gq_buf), buf_q, lambda h: red_q.at[:, pl.ds(h * half, half), :]
        )
        weight = pltpu.make_async_copy(w_ref, w_buf, wsem.at[0])
        load = pltpu.make_async_copy(x_ref, x_buf, wsem.at[1])
        load.start()
        weight.start()

        def product(n):
            depths = pl.ds(pl.multiple_of(n * depth, depth), depth)
            left = x_buf[:, :, :, depths].reshape(tokens, depth)
            for j in range(3):
                right = da_ref[j].reshape(tokens, cols)
                gq_buf[j, depths, :] = lax.dot_general(left, right, TN, preferred_element_type=F32).astype(BF16)

        def start():
            side_g.start()
            load.wait()
            product(ring.far)
            side_q.start_far()
            weight.wait()

        def halfway():
            product(ring.right)
            product(ring.left)
            side_q.start_near()
            side_g.forward()
            product(ring.here)
            side_q.load()

        def compute(t, chip, which):
            part = nt_dot(da_ref[0, chip, which], w_buf[0])
            part += nt_dot(da_ref[1, chip, which], w_buf[1])
            part += nt_dot(da_ref[2, chip, which], w_buf[2])
            pbuf[chip, which] = part.astype(BF16)

        def emit(at, value):
            out[at, :] = (value + alpha * dh_ref[at, :]).astype(BF16)

        def end():
            side_g.finish()
            side_q.finish()

        square_kernel(
            rows,
            (send, recv, lsem),
            scatter=(compute, pbuf, (rcore, rxd, ryd, rx, ry), emit),
            ring=ring,
            start=start,
            halfway=halfway,
            half=2,
            middle=side_q.forward,
            end=end,
        )

    return pl.pallas_call(
        kernel,
        out_shape=[
            jax.ShapeDtypeStruct((rows, D), BF16),
            jax.ShapeDtypeStruct((3, depth, cols), F32),
            jax.ShapeDtypeStruct((2, span[1], depth), F32),
        ],
        in_specs=[VM, ANY, ANY, ANY, VM],
        out_specs=[VM, VM, VM],
        scratch_shapes=[
            pltpu.VMEM((3, D, cols), BF16),
            pltpu.VMEM((4, 2, rows, width), BF16),
            pltpu.VMEM((3, width, cols), BF16),
            pltpu.VMEM((10, 3, depth // 2, cols), BF16),
            pltpu.VMEM((10, span[1], depth), BF16),
        ]
        + scatter_scratch(rows, D)
        + [pltpu.SemaphoreType.DMA((2,))]
        + SEMS
        + ring_sems(12),
        compiler_params=params(4),
        cost_estimate=LIGHT,
        name="input_back",
    )(
        grad_proj.reshape(3, 4, 2, rows, cols),
        w_qkv,
        block_input.reshape(4, 2, rows, width),
        grad_gateup_part,
        grad_h1,
    )


FRONT_SPANS = ((0, 240), (240, 464))
SPANS = ((0, 96), (96, 112), (208, 384), (592, 112))


def body_ring(
    block_input,
    cotangent,
    prefix_len,
    cluster_id,
    positions,
    step_count,
    master_qkv,
    first_qkv,
    second_qkv,
    master_out,
    first_out,
    second_out,
    master_gateup,
    first_gateup,
    second_gateup,
    master_down,
    first_down,
    second_down,
    master_norm,
    first_norm,
    second_norm,
):
    token_count = block_input.shape[0]
    protein_count = token_count // LEN
    share_rows = cotangent.shape[0]
    share_start = lax.axis_index("mp") * share_rows

    low_qkv = master_qkv.astype(BF16)
    low_out = master_out.astype(BF16)
    low_down = master_down.astype(BF16)
    w_norm = lax.optimization_barrier(master_norm.astype(BF16)).astype(F32)

    (
        queries, key_rows, value_rows, attended, probs, cos_table, sin_table, w_qkv, w_out, w_gateup,
        middle_share, middle_low, normed_one, inv_one,
    ) = front_call(
        block_input, low_qkv, low_out, jnp.swapaxes(master_gateup, 1, 2), positions, prefix_len, w_norm, share_rows, FRONT_SPANS
    )
    matches = (cluster_id[:, None] == cluster_id[None, :]).astype(F32)
    counts = jnp.sum(matches, axis=1)
    group_counts = lax.dynamic_slice_in_dim(
        counts, lax.axis_index("dp") * protein_count, protein_count, 0
    )
    row_protein = (share_start + jnp.arange(share_rows)) // LEN
    one_hot = (row_protein[:, None] == jnp.arange(protein_count)[None, :]).astype(F32)
    row_weight = jnp.sum(one_hot * (1.0 / group_counts)[None, :], axis=1)
    block_output, grad_h2, grad_h2_low, terms_two, middle_low, hidden, act, pull, w_down = ffn_call(
        middle_low, middle_share, w_gateup, low_down, cotangent, row_weight[:, None], w_norm
    )
    ffn_grad, grad_gateup_rows = ffn_back_call(grad_h2_low, act, pull, w_down)
    hidden = hidden.reshape(token_count, -1)
    middle_low = middle_low.reshape(token_count, D)
    ffn_grad = ffn_grad.reshape(token_count, D)
    gateup_rows = grad_gateup_rows.reshape(2, token_count, -1)
    grad_down_part = jnp.einsum("tf,td->fd", hidden, ffn_grad, preferred_element_type=F32).astype(BF16)
    red_down = lax.psum_scatter(grad_down_part, "dp", scatter_dimension=1, tiled=True).astype(F32)
    gateup_rows, grad_gateup_rows, grad_down_part = lax.optimization_barrier(
        (gateup_rows, grad_gateup_rows, grad_down_part)
    )
    grad_gateup_part = jnp.einsum(
        "jtf,td->jfd", gateup_rows, middle_low, preferred_element_type=F32
    ).astype(BF16)
    grad_h1, grad_h1_low, terms_one, red_gateup_0, red_gateup_1 = middle_back_call(
        grad_gateup_rows, w_gateup, grad_gateup_part, SPANS[:2], grad_h2, normed_one, inv_one, w_norm
    )
    grad_attended, grad_out_part, red_gateup_2 = out_back_call(
        grad_h1_low, w_out, attended, grad_gateup_part, SPANS[2]
    )
    grad_attended = grad_attended.reshape(token_count, -1)
    norm_terms = jnp.concatenate([terms_one, terms_two])
    grad_proj, grad_norm, red_out = attention_back_call(
        queries,
        key_rows,
        value_rows,
        probs,
        attended,
        grad_attended,
        cos_table,
        sin_table,
        norm_terms,
        grad_out_part,
    )
    grad_input, red_qkv, red_gateup_3 = input_back_call(
        grad_proj, w_qkv, block_input, grad_gateup_part, SPANS[3], grad_h1
    )
    red_gateup = jnp.swapaxes(
        jnp.concatenate([red_gateup_0, red_gateup_1, red_gateup_2, red_gateup_3], axis=1), 1, 2
    )

    step_value = step_count[0].astype(F32)
    rate_qkv = D ** (-0.5)
    rate_out = max(HEADS * HEAD_DIM // 512, 1) ** (-0.5)
    rate_gateup = D ** (-0.5)
    rate_down = max(FF // 64, 1) ** (-0.5)
    rate_norm = 1.0
    new_qkv, new_first_qkv, new_second_qkv = adamw_step(
        master_qkv, first_qkv, second_qkv, red_qkv, rate_qkv, step_value
    )
    new_out, new_first_out, new_second_out = adamw_step(
        master_out, first_out, second_out, red_out, rate_out, step_value
    )
    new_gateup, new_first_gateup, new_second_gateup = adamw_step(
        master_gateup, first_gateup, second_gateup, red_gateup, rate_gateup, step_value
    )
    new_down, new_first_down, new_second_down = adamw_step(
        master_down, first_down, second_down, red_down, rate_down, step_value
    )
    new_norm, new_first_norm, new_second_norm = adamw_step(
        master_norm, first_norm, second_norm, grad_norm, rate_norm, step_value
    )
    return (
        block_output,
        grad_input,
        red_qkv,
        new_qkv,
        new_first_qkv,
        new_second_qkv,
        red_out,
        new_out,
        new_first_out,
        new_second_out,
        red_gateup,
        new_gateup,
        new_first_gateup,
        new_second_gateup,
        red_down,
        new_down,
        new_first_down,
        new_second_down,
        grad_norm,
        new_norm,
        new_first_norm,
        new_second_norm,
    )


def solution(mesh):
    placed = (
        P("dp", None),
        P(("dp", "mp"), None),
        P("dp"),
        P(),
        P("dp"),
        P(),
        P(None, "dp", "mp"),
        P(None, "dp", "mp"),
        P(None, "dp", "mp"),
        P("mp", "dp"),
        P("mp", "dp"),
        P("mp", "dp"),
        P(None, "dp", "mp"),
        P(None, "dp", "mp"),
        P(None, "dp", "mp"),
        P("mp", "dp"),
        P("mp", "dp"),
        P("mp", "dp"),
        P(),
        P(),
        P(),
    )
    ring = mesh.shape["dp"] == 4 and mesh.shape["mp"] == 8
    return jax.shard_map(
        body_ring if ring else body_plain,
        mesh=mesh,
        in_specs=placed,
        out_specs=(
            P(("dp", "mp"), None),
            P(("dp", "mp"), None),
            P(None, "dp", "mp"),
            P(None, "dp", "mp"),
            P(None, "dp", "mp"),
            P(None, "dp", "mp"),
            P("mp", "dp"),
            P("mp", "dp"),
            P("mp", "dp"),
            P("mp", "dp"),
            P(None, "dp", "mp"),
            P(None, "dp", "mp"),
            P(None, "dp", "mp"),
            P(None, "dp", "mp"),
            P("mp", "dp"),
            P("mp", "dp"),
            P("mp", "dp"),
            P("mp", "dp"),
            P(),
            P(),
            P(),
            P(),
        ),
        check_vma=False,
    )
```

```python
import functools
import math

import jax
import jax.numpy as jnp
from jax import lax
from jax.experimental import pallas as pl
from jax.experimental.pallas import tpu as pltpu
from jax.sharding import PartitionSpec as P

D = 2048
HEADS = 16
HEAD_DIM = 128
FF = 5632
DEPTH = 24
LEN = 896


beta_one = 0.9
beta_two = 0.95
adam_epsilon = 1e-08
decay_weight = 0.1
norm_epsilon = 1e-05


def norm_forward(hidden_rows, gain, offset):
    centre = hidden_rows - jnp.mean(hidden_rows, axis=-1, keepdims=True)
    inv_std = lax.rsqrt(jnp.mean(centre * centre, axis=-1, keepdims=True) + norm_epsilon)
    normed = centre * inv_std
    return (normed * gain + offset, normed, inv_std)


def norm_backward(grad_rows, normed, inv_std, gain):
    grad_normed = grad_rows * gain
    first_term = jnp.mean(grad_normed, axis=-1, keepdims=True)
    second_term = jnp.mean(grad_normed * normed, axis=-1, keepdims=True)
    grad_hidden = inv_std * (grad_normed - first_term - normed * second_term)
    return (grad_hidden, jnp.sum(grad_rows * normed, axis=0), jnp.sum(grad_rows, axis=0))


def rotate_half(values):
    middle = values.shape[-1] // 2
    return jnp.concatenate([-values[..., middle:], values[..., :middle]], axis=-1)


def rotate_back(values):
    middle = values.shape[-1] // 2
    return jnp.concatenate([values[..., middle:], -values[..., :middle]], axis=-1)


def rope_tables(positions):
    ladder = jnp.arange(HEAD_DIM // 2, dtype=jnp.float32)
    inverse = jnp.exp(ladder * (-2.0 * math.log(10000.0) / HEAD_DIM))
    angles = positions.astype(jnp.float32)[:, None] * inverse[None, :]
    cos_half = jnp.cos(angles)
    sin_half = jnp.sin(angles)
    return (
        jnp.concatenate([cos_half, cos_half], axis=-1),
        jnp.concatenate([sin_half, sin_half], axis=-1),
    )


def apply_rope(values, cos_table, sin_table):
    return values * cos_table[:, None, :] + rotate_half(values) * sin_table[:, None, :]


def rope_back(grads, cos_table, sin_table):
    return grads * cos_table[:, None, :] + rotate_back(grads * sin_table[:, None, :])


def gelu_tanh(values):
    return jax.nn.gelu(values, approximate=True)


def adamw_step(old_master, old_first, old_second, grad_sum, learn_rate, step_value):
    first_new = beta_one * old_first + (1.0 - beta_one) * grad_sum
    second_new = beta_two * old_second + (1.0 - beta_two) * grad_sum * grad_sum
    fix_first = 1.0 - jnp.power(beta_one, step_value)
    fix_second = 1.0 - jnp.power(beta_two, step_value)
    update = (
        first_new / fix_first / (jnp.sqrt(second_new / fix_second) + adam_epsilon)
        + decay_weight * old_master
    )
    return (old_master - learn_rate * update, first_new, second_new)


def body_plain(
    block_input,
    cotangent,
    prefix_len,
    cluster_id,
    positions,
    step_count,
    master_qkv,
    first_qkv,
    second_qkv,
    master_out,
    first_out,
    second_out,
    master_gateup,
    first_gateup,
    second_gateup,
    master_down,
    first_down,
    second_down,
    master_norm,
    first_norm,
    second_norm,
):
    w_qkv, w_out, w_gateup, w_down = (
        lax.all_gather(master_qkv.astype(jnp.bfloat16), "dp", axis=1, tiled=True),
        lax.all_gather(master_out.astype(jnp.bfloat16), "dp", axis=1, tiled=True),
        lax.all_gather(master_gateup.astype(jnp.bfloat16), "dp", axis=1, tiled=True),
        lax.all_gather(master_down.astype(jnp.bfloat16), "dp", axis=1, tiled=True),
    )
    w_norm = lax.optimization_barrier(master_norm.astype(jnp.bfloat16)).astype(jnp.float32)
    token_count = block_input.shape[0]
    protein_count = token_count // LEN
    share_rows = cotangent.shape[0]
    share_start = lax.axis_index("mp") * share_rows
    head_count = w_qkv.shape[2] // HEAD_DIM
    width_heads = head_count * HEAD_DIM
    deep_alpha = math.sqrt(2.0 * DEPTH)
    score_scale = 1.0 / math.sqrt(HEAD_DIM)
    cos_table, sin_table = rope_tables(positions)
    projected = jnp.einsum("td,jdc->jtc", block_input, w_qkv, preferred_element_type=jnp.float32)
    shaped = projected.reshape(3, token_count, head_count, HEAD_DIM)
    queries = (apply_rope(shaped[0], cos_table, sin_table) * score_scale).astype(jnp.bfloat16)
    key_rows = apply_rope(shaped[1], cos_table, sin_table).astype(jnp.bfloat16)
    value_rows = shaped[2].astype(jnp.bfloat16)
    row_ids = jnp.arange(LEN)[:, None]
    col_ids = jnp.arange(LEN)[None, :]
    attended_parts = []
    log_totals = []
    for protein in range(protein_count):
        row_slice = slice(protein * LEN, (protein + 1) * LEN)
        visible = (col_ids < prefix_len[protein]) | (col_ids <= row_ids)
        scores = jnp.einsum(
            "qhd,khd->hqk",
            queries[row_slice],
            key_rows[row_slice],
            preferred_element_type=jnp.float32,
        )
        scores = jnp.where(visible[None], scores, -1e30)
        row_peak = jnp.max(scores, axis=-1, keepdims=True)
        expo_rows = jnp.exp(scores - row_peak)
        totals = jnp.sum(expo_rows, axis=-1, keepdims=True)
        attn_probs = (expo_rows / totals).astype(jnp.bfloat16)
        attended_parts.append(
            jnp.einsum(
                "hqk,khd->qhd",
                attn_probs,
                value_rows[row_slice],
                preferred_element_type=jnp.float32,
            )
        )
        log_totals.append(row_peak + jnp.log(totals))
    attended = (
        jnp.concatenate(attended_parts, axis=0)
        .reshape(token_count, width_heads)
        .astype(jnp.bfloat16)
    )
    attn_part = jnp.dot(attended, w_out, preferred_element_type=jnp.float32)
    input_share = lax.dynamic_slice_in_dim(block_input, share_start, share_rows, 0).astype(
        jnp.float32
    )
    attn_share = lax.psum_scatter(
        attn_part.astype(jnp.bfloat16), "mp", scatter_dimension=0, tiled=True
    ).astype(jnp.float32)
    middle_share, normed_one, inv_one = norm_forward(
        deep_alpha * input_share + attn_share, w_norm[0], w_norm[1]
    )
    middle_low = lax.all_gather(middle_share.astype(jnp.bfloat16), "mp", axis=0, tiled=True)
    gateup = jnp.einsum("td,jdf->jtf", middle_low, w_gateup, preferred_element_type=jnp.float32)
    gate_rows = gateup[0]
    up_rows = gateup[1]
    activated, gelu_pull = jax.vjp(gelu_tanh, gate_rows)
    hidden = (activated * up_rows).astype(jnp.bfloat16)
    ffn_part = jnp.dot(hidden, w_down, preferred_element_type=jnp.float32)
    ffn_share = lax.psum_scatter(
        ffn_part.astype(jnp.bfloat16), "mp", scatter_dimension=0, tiled=True
    ).astype(jnp.float32)
    out_share, normed_two, inv_two = norm_forward(
        deep_alpha * middle_share + ffn_share, w_norm[2], w_norm[3]
    )
    block_output = out_share.astype(jnp.bfloat16)
    matches = (cluster_id[:, None] == cluster_id[None, :]).astype(jnp.float32)
    counts = jnp.sum(matches, axis=1)
    group_counts = lax.dynamic_slice_in_dim(
        counts, lax.axis_index("dp") * protein_count, protein_count, 0
    )
    row_protein = (share_start + jnp.arange(share_rows)) // LEN
    one_hot = (row_protein[:, None] == jnp.arange(protein_count)[None, :]).astype(jnp.float32)
    row_weight = jnp.sum(one_hot * (1.0 / group_counts)[None, :], axis=1)
    grad_output = cotangent.astype(jnp.float32) * row_weight[:, None]
    grad_h2, grad_gain_two, grad_bias_two = norm_backward(
        grad_output, normed_two, inv_two, w_norm[2]
    )
    ffn_grad_full = lax.all_gather(grad_h2.astype(jnp.bfloat16), "mp", axis=0, tiled=True)
    grad_down_part = jnp.einsum(
        "tf,td->fd", hidden, ffn_grad_full, preferred_element_type=jnp.float32
    )
    grad_hidden = jnp.einsum("td,fd->tf", ffn_grad_full, w_down, preferred_element_type=jnp.float32)
    grad_gate = gelu_pull(grad_hidden * up_rows)[0]
    grad_up = grad_hidden * activated
    grad_gateup_rows = jnp.stack([grad_gate, grad_up]).astype(jnp.bfloat16)
    grad_gateup_part = jnp.einsum(
        "td,jtf->jdf", middle_low, grad_gateup_rows, preferred_element_type=jnp.float32
    )
    middle_grad_part = jnp.einsum(
        "jtf,jdf->td", grad_gateup_rows, w_gateup, preferred_element_type=jnp.float32
    )
    middle_grad = (
        lax.psum_scatter(
            middle_grad_part.astype(jnp.bfloat16), "mp", scatter_dimension=0, tiled=True
        ).astype(jnp.float32)
        + deep_alpha * grad_h2
    )
    grad_h1, grad_gain_one, grad_bias_one = norm_backward(
        middle_grad, normed_one, inv_one, w_norm[0]
    )
    attn_grad_full = lax.all_gather(grad_h1.astype(jnp.bfloat16), "mp", axis=0, tiled=True)
    grad_out_part = jnp.einsum(
        "tc,td->cd", attended, attn_grad_full, preferred_element_type=jnp.float32
    )
    grad_attended = (
        jnp.einsum("td,cd->tc", attn_grad_full, w_out, preferred_element_type=jnp.float32)
        .astype(jnp.bfloat16)
        .reshape(token_count, head_count, HEAD_DIM)
    )
    query_grads = []
    key_grads = []
    value_grads = []
    for protein in range(protein_count):
        row_slice = slice(protein * LEN, (protein + 1) * LEN)
        visible = (col_ids < prefix_len[protein]) | (col_ids <= row_ids)
        scores = jnp.einsum(
            "qhd,khd->hqk",
            queries[row_slice],
            key_rows[row_slice],
            preferred_element_type=jnp.float32,
        )
        scores = jnp.where(visible[None], scores, -1e30)
        probs_full = jnp.exp(scores - log_totals[protein])
        probs_low = probs_full.astype(jnp.bfloat16)
        grad_slice = grad_attended[row_slice]
        value_grads.append(
            jnp.einsum("hqk,qhd->khd", probs_low, grad_slice, preferred_element_type=jnp.float32)
        )
        prob_grads = jnp.einsum(
            "qhd,khd->hqk", grad_slice, value_rows[row_slice], preferred_element_type=jnp.float32
        )
        centre_term = jnp.sum(probs_full * prob_grads, axis=-1, keepdims=True)
        score_grads = (probs_full * (prob_grads - centre_term)).astype(jnp.bfloat16)
        query_grads.append(
            jnp.einsum(
                "hqk,khd->qhd", score_grads, key_rows[row_slice], preferred_element_type=jnp.float32
            )
        )
        key_grads.append(
            jnp.einsum(
                "hqk,qhd->khd", score_grads, queries[row_slice], preferred_element_type=jnp.float32
            )
        )
    grad_query = rope_back(jnp.concatenate(query_grads, axis=0), cos_table, sin_table) * score_scale
    grad_key = rope_back(jnp.concatenate(key_grads, axis=0), cos_table, sin_table)
    grad_value = jnp.concatenate(value_grads, axis=0)
    grad_proj = (
        jnp.stack([grad_query, grad_key, grad_value])
        .reshape(3, token_count, width_heads)
        .astype(jnp.bfloat16)
    )
    grad_qkv_part = jnp.einsum(
        "td,jtc->jdc", block_input, grad_proj, preferred_element_type=jnp.float32
    )
    input_grad_part = jnp.einsum(
        "jtc,jdc->td", grad_proj, w_qkv, preferred_element_type=jnp.float32
    )
    input_grad = (
        lax.psum_scatter(
            input_grad_part.astype(jnp.bfloat16), "mp", scatter_dimension=0, tiled=True
        ).astype(jnp.float32)
        + deep_alpha * grad_h1
    )
    grad_input = input_grad.astype(jnp.bfloat16)
    norm_terms = jnp.stack([grad_gain_one, grad_bias_one, grad_gain_two, grad_bias_two])
    grad_norm = lax.psum(norm_terms, ("dp", "mp"))
    red_qkv, red_out, red_gateup, red_down = (
        lax.psum_scatter(
            grad_qkv_part.astype(jnp.bfloat16), "dp", scatter_dimension=1, tiled=True
        ).astype(jnp.float32),
        lax.psum_scatter(
            grad_out_part.astype(jnp.bfloat16), "dp", scatter_dimension=1, tiled=True
        ).astype(jnp.float32),
        lax.psum_scatter(
            grad_gateup_part.astype(jnp.bfloat16), "dp", scatter_dimension=1, tiled=True
        ).astype(jnp.float32),
        lax.psum_scatter(
            grad_down_part.astype(jnp.bfloat16), "dp", scatter_dimension=1, tiled=True
        ).astype(jnp.float32),
    )
    step_value = step_count[0].astype(jnp.float32)
    rate_qkv = D ** (-0.5)
    rate_out = max(HEADS * HEAD_DIM // 512, 1) ** (-0.5)
    rate_gateup = D ** (-0.5)
    rate_down = max(FF // 64, 1) ** (-0.5)
    rate_norm = 1.0
    new_qkv, new_first_qkv, new_second_qkv = adamw_step(
        master_qkv, first_qkv, second_qkv, red_qkv, rate_qkv, step_value
    )
    new_out, new_first_out, new_second_out = adamw_step(
        master_out, first_out, second_out, red_out, rate_out, step_value
    )
    new_gateup, new_first_gateup, new_second_gateup = adamw_step(
        master_gateup, first_gateup, second_gateup, red_gateup, rate_gateup, step_value
    )
    new_down, new_first_down, new_second_down = adamw_step(
        master_down, first_down, second_down, red_down, rate_down, step_value
    )
    new_norm, new_first_norm, new_second_norm = adamw_step(
        master_norm, first_norm, second_norm, grad_norm, rate_norm, step_value
    )
    return (
        block_output,
        grad_input,
        red_qkv,
        new_qkv,
        new_first_qkv,
        new_second_qkv,
        red_out,
        new_out,
        new_first_out,
        new_second_out,
        red_gateup,
        new_gateup,
        new_first_gateup,
        new_second_gateup,
        red_down,
        new_down,
        new_first_down,
        new_second_down,
        grad_norm,
        new_norm,
        new_first_norm,
        new_second_norm,
    )


MESH = pl.DeviceIdType.MESH
VMEM_BYTES = 61 * 1024 * 1024
BF16 = jnp.bfloat16
F32 = jnp.float32
EMIT = 112
NT = (((1,), (1,)), ((), ()))
ANY = pl.BlockSpec(memory_space=pl.ANY)
VM = pl.BlockSpec(memory_space=pltpu.VMEM)


LIGHT = pl.CostEstimate(flops=1 << 20, bytes_accessed=1 << 16, transcendentals=0)


def nt_dot(left, right):
    return lax.dot_general(left, right, NT, preferred_element_type=F32)


class Ring:
    def __init__(self, send, recv, local):
        self.here = lax.axis_index("dp")
        self.right = (self.here + 1) % 4
        self.left = (self.here + 3) % 4
        self.far = (self.here + 2) % 4
        self.send, self.recv, self.local = send, recv, local

    def copy(self, k, src, dst, other):
        return pltpu.make_async_remote_copy(
            src_ref=src,
            dst_ref=dst,
            send_sem=self.send.at[k],
            recv_sem=self.recv.at[k],
            device_id={"dp": other},
            device_id_type=MESH,
        )


class RingGather:
    def __init__(self, ring, first, half_of, place):
        self.plus_0 = ring.copy(first, half_of(0), place(ring.here, 0), ring.right)
        self.minus_1 = ring.copy(first + 1, half_of(1), place(ring.here, 1), ring.left)
        self.plus_1 = ring.copy(first + 2, half_of(1), place(ring.here, 1), ring.right)
        self.minus_0 = ring.copy(first + 3, half_of(0), place(ring.here, 0), ring.left)
        self.far_0 = ring.copy(first + 4, place(ring.left, 0), place(ring.left, 0), ring.right)
        self.far_1 = ring.copy(first + 5, place(ring.right, 1), place(ring.right, 1), ring.left)
        self.own = [
            pltpu.make_async_copy(half_of(h), place(ring.here, h), ring.local.at[first + h])
            for h in range(2)
        ]
        self.remote = (self.plus_0, self.minus_1, self.plus_1, self.minus_0, self.far_0, self.far_1)

    def start(self):
        for copy in self.remote[:4]:
            copy.start()
        for copy in self.own:
            copy.start()

    def forward(self):
        self.plus_0.wait_recv()
        self.far_0.start()
        self.minus_1.wait_recv()
        self.far_1.start()

    def near(self):
        self.plus_1.wait_recv()
        self.minus_0.wait_recv()

    def far(self):
        self.far_0.wait_recv()
        self.far_1.wait_recv()

    def drain(self):
        for copy in self.remote:
            copy.wait_send()

    def finish(self):
        for copy in self.own:
            copy.wait()
        self.near()
        self.far()
        self.drain()


class RingScatter:
    def __init__(self, ring, first, half_at, buf, out):
        self.buf, self.out = buf, out
        self.plus_far = ring.copy(first, half_at(ring.far, 0), buf.at[0], ring.right)
        self.minus_far = ring.copy(first + 1, half_at(ring.far, 1), buf.at[1], ring.left)
        self.plus_near = ring.copy(first + 2, half_at(ring.right, 1), buf.at[2], ring.right)
        self.minus_near = ring.copy(first + 3, half_at(ring.left, 0), buf.at[3], ring.left)
        self.plus_sum = ring.copy(first + 4, buf.at[6], buf.at[4], ring.right)
        self.minus_sum = ring.copy(first + 5, buf.at[7], buf.at[5], ring.left)
        places = ((ring.right, 0), (ring.left, 1), (ring.here, 0), (ring.here, 1))
        self.loads = [
            pltpu.make_async_copy(half_at(*place), buf.at[6 + k], ring.local.at[first + k])
            for k, place in enumerate(places)
        ]
        self.remote = (
            self.plus_far,
            self.minus_far,
            self.plus_near,
            self.minus_near,
            self.plus_sum,
            self.minus_sum,
        )

    def start_far(self):
        self.plus_far.start()
        self.minus_far.start()

    def start_near(self):
        self.plus_near.start()
        self.minus_near.start()

    def load(self):
        for copy in self.loads:
            copy.start()

    def start(self):
        self.start_far()
        self.start_near()
        self.load()

    def forward(self):
        for copy in self.loads:
            copy.wait()
        self.plus_far.wait_recv()
        for_rows(self.buf.shape[1:], lambda at: add_at(self.buf, 6, 0, at))
        self.plus_sum.start()
        self.minus_far.wait_recv()
        for_rows(self.buf.shape[1:], lambda at: add_at(self.buf, 7, 1, at))
        self.minus_sum.start()

    def finish(self):
        for copy in self.remote[2:]:
            copy.wait_recv()
        buf = self.buf
        for half, terms in enumerate(((8, 3, 4), (9, 2, 5))):
            out = self.out(half)

            def total(at, out=out, terms=terms):
                out[at] = sum(buf[(k,) + at].astype(F32) for k in terms)

            for_rows(buf.shape[1:], total)
        for copy in self.remote:
            copy.wait_send()


def add_at(buf, dst, src, at):
    buf[(dst,) + at] = (buf[(dst,) + at].astype(F32) + buf[(src,) + at].astype(F32)).astype(BF16)


def for_rows(shape, visit):
    def step(i, carry):
        rows = pl.ds(pl.multiple_of(i * 16, 16), 16)
        if len(shape) == 2:
            visit((rows, slice(None)))
        else:
            for j in range(shape[0]):
                visit((j, rows, slice(None)))
        return carry

    lax.fori_loop(0, shape[-2] // 16, step, 0)


def ring_sems(count):
    return [pltpu.SemaphoreType.DMA((count,)) for _ in range(3)]


def row_halves(depth):
    half = depth // 2

    def place(ref):
        def at(owner, part):
            return ref.at[:, pl.ds(pl.multiple_of(owner * depth + part * half, half), half), :]

        return at

    return place


def plane_columns(depth):
    def place(ref):
        def at(owner, part):
            return ref.at[part, :, pl.ds(pl.multiple_of(owner * depth, depth), depth)]

        return at

    return place


def column_halves(depth):
    def place(ref):
        half = ref.shape[0] // 2

        def at(owner, part):
            columns = pl.ds(pl.multiple_of(owner * depth, depth), depth)
            return ref.at[pl.ds(part * half, half), columns]

        return at

    return place


def span_scatter(ring, first, ref, span, buf, out):
    at = plane_columns(ref.shape[2] // 4)(ref.at[:, pl.ds(*span), :])
    return RingScatter(ring, first, at, buf, lambda h: out.at[h])


def greet(others):
    sem = pltpu.get_barrier_semaphore()
    for other in others:
        pl.semaphore_signal(sem, inc=1, device_id=other, device_id_type=MESH)
    pl.semaphore_wait(sem, len(others))


class Square:
    def __init__(self, send, recv, rows):
        me = lax.axis_index("mp")
        self.core = me % 2
        self.x = (me // 2) % 2
        self.y = me // 4
        self.xn = (self.y * 2 + (1 - self.x)) * 2 + self.core
        self.yn = ((1 - self.y) * 2 + self.x) * 2 + self.core
        self.peer = (self.y * 2 + self.x) * 2 + (1 - self.core)
        self.own = self.y * 2 + self.x
        self.xc = self.y * 2 + (1 - self.x)
        self.yc = (1 - self.y) * 2 + self.x
        self.dc = (1 - self.y) * 2 + (1 - self.x)
        self.send, self.recv = send, recv
        cut = rows // 2 // 16 * 16
        self.rows = rows
        self.a = pl.ds(0, cut)
        self.b = pl.ds(cut, rows - cut)
        self.na, self.nb, self.cut = cut, rows - cut, cut

        self.others = [{"mp": self.xn}, {"mp": self.yn}, {"mp": self.peer}]

    def copy(self, k, src, dst, other):
        return pltpu.make_async_remote_copy(
            src_ref=src,
            dst_ref=dst,
            send_sem=self.send.at[k],
            recv_sem=self.recv.at[k],
            device_id={"mp": other},
            device_id_type=MESH,
        )


def add_rows(dst, src, count):
    def step(i, carry):
        rows = pl.ds(pl.multiple_of(i * 16, 16), 16)
        dst[rows, :] = (dst[rows, :].astype(F32) + src[rows, :].astype(F32)).astype(BF16)
        return carry

    lax.fori_loop(0, count // 16, step, 0)


def nothing():
    pass


def square_kernel(
    rows,
    sems,
    gather=None,
    scatter=None,
    ring=None,
    start=nothing,
    first=nothing,
    early=nothing,
    later=nothing,
    between=nothing,
    halfway=nothing,
    half=4,
    middle=nothing,
    end=nothing,
    near_first=False,
    greeting=True,
):
    send, recv, lsem = sems
    sq = Square(send, recv, rows)
    core = sq.core
    if greeting:
        greet(sq.others + ([{"dp": ring.left}, {"dp": ring.right}] if ring is not None else []))

    def place(rel, turn):
        chip_y = (sq.y + rel % 2) % 2
        chip_x = (sq.x + ((rel + 1) // 2) % 2) % 2
        return chip_y * 2 + chip_x, (1 - core + turn) % 2

    if gather is not None:
        compute, share, full, gbuf = gather
        c_own = sq.copy(0, share, gbuf.at[sq.own, core], sq.peer)
        x_a = sq.copy(1, share.at[sq.a], gbuf.at[sq.own, core, sq.a], sq.xn)
        y_b = sq.copy(2, share.at[sq.b], gbuf.at[sq.own, core, sq.b], sq.yn)
        f_x = sq.copy(3, gbuf.at[sq.yc, core, sq.b], gbuf.at[sq.yc, core, sq.b], sq.xn)
        f_y = sq.copy(4, gbuf.at[sq.xc, core, sq.a], gbuf.at[sq.xc, core, sq.a], sq.yn)
        x_b = sq.copy(5, share.at[sq.b], gbuf.at[sq.own, core, sq.b], sq.xn)
        y_a = sq.copy(6, share.at[sq.a], gbuf.at[sq.own, core, sq.a], sq.yn)
        c_d = sq.copy(7, gbuf.at[sq.dc, core], gbuf.at[sq.dc, core], sq.peer)
        c_x = sq.copy(8, gbuf.at[sq.xc, core], gbuf.at[sq.xc, core], sq.peer)
        c_y = sq.copy(9, gbuf.at[sq.yc, core], gbuf.at[sq.yc, core], sq.peer)
        local = pltpu.make_async_copy(share, gbuf.at[sq.own, core], lsem.at[8])
        x_a.start()
        y_b.start()
        if near_first:
            x_b.start()
            y_a.start()
        c_own.start()
        local.start()
    start()
    if gather is not None:

        def take_own():
            c_own.wait_recv()
            local.wait()
            first()

        def forward():
            x_a.wait_recv()
            y_b.wait_recv()
            f_x.start()
            f_y.start()
            if not near_first:
                x_b.start()
                y_a.start()
            early()

        def take_far():
            f_x.wait_recv()
            f_y.wait_recv()
            c_d.start()
            c_d.wait_recv()

        def take_near():
            x_b.wait_recv()
            y_a.wait_recv()
            c_x.start()
            c_y.start()
            later()
            c_x.wait_recv()
            c_y.wait_recv()

        def gather_step(t, carry):
            unit = t // 2
            if near_first:
                chip_y = (sq.y + unit // 2) % 2
                chip_x = (sq.x + unit % 2) % 2
                chip, which = chip_y * 2 + chip_x, (1 - core + t % 2) % 2
            else:
                chip, which = place(unit, t % 2)

            pl.when(t == 0)(take_own)

            @pl.when(t == 2)
            def _():
                forward()
                if near_first:
                    take_near()
                else:
                    take_far()

            pl.when(t == (6 if near_first else 4))(take_far if near_first else take_near)

            if full is not None:
                pltpu.make_async_copy(gbuf.at[chip, which], full.at[chip, which], lsem.at[t]).start()
            compute(t, chip, which)
            return carry

        lax.fori_loop(0, 8 if scatter is None else 6, gather_step, 0)
    between()
    if scatter is not None:
        finish_tile, pbuf, (rcore, rxd, ryd, rx, ry), emit = scatter
        x_d = sq.copy(14, pbuf.at[sq.dc, core, sq.a], rxd, sq.xn)
        y_d = sq.copy(15, pbuf.at[sq.dc, core, sq.b], ryd, sq.yn)
        x_ra = sq.copy(16, pbuf.at[sq.xc, core, sq.a], rx.at[sq.a], sq.xn)
        y_rb = sq.copy(17, pbuf.at[sq.yc, core, sq.b], ry.at[sq.b], sq.yn)
        x_rb = sq.copy(18, pbuf.at[sq.xc, core, sq.b], rx.at[sq.b], sq.xn)
        y_ra = sq.copy(19, pbuf.at[sq.yc, core, sq.a], ry.at[sq.a], sq.yn)

        def scatter_step(t, carry):
            turn = t % 2
            rel = (t // 2 + 1) % 4
            chip, which = place(rel, turn)

            @pl.when(t == half)
            def _():
                halfway()

            finish_tile(t, chip, which)
            to_peer = sq.copy(10 + rel, pbuf.at[chip, which], rcore.at[chip], sq.peer)

            @pl.when(turn == 0)
            def _():
                to_peer.start()

            @pl.when(turn == 1)
            def _():
                to_peer.wait_recv()
                add_rows(pbuf.at[chip, which], rcore.at[chip], rows)

            @pl.when(t == 1)
            def _():
                x_d.start()
                y_d.start()

            @pl.when(t == 3)
            def _():
                x_ra.start()

            @pl.when(t == 5)
            def _():
                y_rb.start()

            return carry

        if gather is None:
            lax.fori_loop(0, 8, scatter_step, 0)
        else:
            lax.fori_loop(0, 2, scatter_step, 0)
            lax.fori_loop(6, 8, gather_step, 0)
            lax.fori_loop(2, 8, scatter_step, 0)
        x_d.wait_recv()
        add_rows(pbuf.at[sq.yc, core, sq.a], rxd, sq.na)
        y_ra.start()
        y_d.wait_recv()
        add_rows(pbuf.at[sq.xc, core, sq.b], ryd, sq.nb)
        x_rb.start()
        middle()
        x_ra.wait_recv()
        y_rb.wait_recv()
        y_ra.wait_recv()
        x_rb.wait_recv()

        def last(i, carry):
            part = pl.ds(pl.multiple_of(i * EMIT, 16), EMIT)
            emit(
                part,
                pbuf[sq.own, core, part, :].astype(F32)
                + rx[part, :].astype(F32)
                + ry[part, :].astype(F32),
            )
            return carry

        lax.fori_loop(0, rows // EMIT, last, 0)
        for k in range(4):
            sq.copy(10 + k, pbuf.at[0, 0], rcore.at[0], sq.peer).wait_send()
        for copy in (x_d, y_d, x_ra, y_rb, x_rb, y_ra):
            copy.wait_send()
    end()
    if gather is not None:
        for copy in (c_own, x_a, y_b, f_x, f_y, x_b, y_a, c_d, c_x, c_y):
            copy.wait_send()
        if full is not None:
            for t in range(8):
                pltpu.make_async_copy(gbuf.at[0, 0], full.at[0, 0], lsem.at[t]).wait()


def row_mean(values):
    return jnp.mean(values, axis=-1, keepdims=True)


def norm_rows(values):
    centre = values - row_mean(values)
    inv_std = lax.rsqrt(row_mean(centre * centre) + norm_epsilon)
    return centre * inv_std, inv_std


def norm_rows_back(grads, normed, inv_std, gain):
    grad_normed = grads * gain
    return inv_std * (grad_normed - row_mean(grad_normed) - normed * row_mean(grad_normed * normed))


def fold(values):
    return sum(values[i : i + 8] for i in range(0, EMIT, 8))


def scatter_scratch(rows, width, with_sums=True):
    cut = rows // 2 // 16 * 16
    return ([pltpu.VMEM((4, 2, rows, width), BF16)] if with_sums else []) + [
        pltpu.VMEM((4, rows, width), BF16),
        pltpu.VMEM((cut, width), BF16),
        pltpu.VMEM((rows - cut, width), BF16),
        pltpu.VMEM((rows, width), BF16),
        pltpu.VMEM((rows, width), BF16),
    ]


SEMS = [
    pltpu.SemaphoreType.DMA((20,)),
    pltpu.SemaphoreType.DMA((20,)),
    pltpu.SemaphoreType.DMA((9,)),
]


def params(collective_id):
    return pltpu.CompilerParams(
        collective_id=collective_id, has_side_effects=True, vmem_limit_bytes=VMEM_BYTES
    )


def whole(shape):
    return pl.BlockSpec(shape, lambda *_: (0,) * len(shape))


def front_call(block_input, low_qkv, low_out, gateup, positions, prefix_len, w_norm, rows, spans):
    tokens, width = block_input.shape
    depth, cols = low_qkv.shape[1:]
    tiles = tokens // rows
    heads = cols // HEAD_DIM
    proteins = tokens // LEN
    scale = 1.0 / math.sqrt(HEAD_DIM)
    alpha = math.sqrt(2.0 * DEPTH)
    half = depth // 2
    out_half = cols // 2
    span = spans[-1][0] + spans[-1][1]
    live = gateup.shape[1]

    def kernel(
        pre_ref, x_ref, low_ref, lo_ref, lg_ref, pos_ref, norm_ref,
        q_ref, k_ref, v_ref, o_ref, p_ref, cos_ref, sin_ref, w_ref, wo_ref, wg_ref,
        x1_ref, x1b_ref, n1_ref, inv_ref,
        x_buf, w_buf, acc, q_buf, k_buf, v_buf, o_buf, cos_buf, sin_buf, p_buf, wo_buf, xs_buf, wide_g, low_g,
        rcore, rxd, ryd, rx, ry, xsem, psem, ksem, send, recv, lsem, zsend, zrecv, zlocal,
    ):
        ring = Ring(zsend, zrecv, zlocal)
        sems = Square(send, recv, rows)
        gather = RingGather(
            ring, 0, lambda h: low_ref.at[:, pl.ds(h * half, half), :], row_halves(depth)(w_buf)
        )
        gather_out = RingGather(
            ring, 6, lambda h: lo_ref.at[pl.ds(h * out_half, out_half), :], column_halves(depth)(wo_buf)
        )
        gathers = []
        for n, (low, size) in enumerate(spans):
            at = pl.ds(low, size)
            gathers.append(
                RingGather(
                    ring,
                    12 + 6 * n,
                    lambda h, at=at: low_g.at[h, at, :],
                    plane_columns(depth)(wg_ref.at[:, at, :]),
                )
            )
        own_rows = pltpu.make_async_copy(x_ref.at[sems.own, sems.core], xs_buf, xsem.at[8])
        load_g = pltpu.make_async_copy(lg_ref, wide_g, xsem.at[9])
        kept = ((q_buf, q_ref), (k_buf, k_ref), (v_buf, v_ref), (cos_buf, cos_ref), (sin_buf, sin_ref))
        keeps = [pltpu.make_async_copy(src, dst, ksem.at[n]) for n, (src, dst) in enumerate(kept)]
        keep_w = pltpu.make_async_copy(w_buf, w_ref, ksem.at[5])
        keep_wo = pltpu.make_async_copy(wo_buf, wo_ref, ksem.at[6])
        keep_o = pltpu.make_async_copy(o_buf, o_ref, ksem.at[7])

        def x_copy(t):
            return pltpu.make_async_copy(x_ref.at[t // 2, t % 2], x_buf.at[t // 2, t % 2], xsem.at[t])

        def start_tile(t, carry):
            x_copy(t).start()
            return carry

        lax.fori_loop(0, tiles, start_tile, 0)
        own_rows.start()
        load_g.start()
        greet(sems.others + [{"dp": ring.left}, {"dp": ring.right}])
        gather.start()
        for copy in gather.own:
            copy.wait()

        def part(t, j, owner):
            depths = pl.ds(pl.multiple_of(owner * depth, depth), depth)
            return jnp.dot(
                x_buf[t // 2, t % 2, :, depths], w_buf[j, depths, :], preferred_element_type=F32
            )

        def tile_rows(t):
            return pl.ds(pl.multiple_of(t * rows, 16), rows)

        def own_tile(t, carry):
            x_copy(t).wait()
            for j in range(3):
                acc[t, j] = part(t, j, ring.here)
            return carry

        lax.fori_loop(0, tiles, own_tile, 0)
        rung = lax.broadcasted_iota(jnp.int32, (HEAD_DIM, 1), 0)
        ladder = (rung % (HEAD_DIM // 2)).astype(F32)
        inverse = jnp.exp(ladder * (-2.0 * math.log(10000.0) / HEAD_DIM))
        sign = jnp.where(rung < HEAD_DIM // 2, -1.0, 1.0)

        def table_tile(b, carry):
            angles = inverse * pos_ref[pl.ds(b, 1), :].astype(F32)
            here = pl.ds(pl.multiple_of(b * HEAD_DIM, HEAD_DIM), HEAD_DIM)
            cos_buf[here, :] = jnp.cos(angles).T
            sin_buf[here, :] = (jnp.sin(angles) * sign).T
            return carry

        blocks = tokens // HEAD_DIM
        lax.fori_loop(0, blocks // 2, table_tile, 0)
        gather.forward()
        gather_out.start()
        lax.fori_loop(blocks // 2, blocks, table_tile, 0)
        load_g.wait()

        def round_rows(i, carry):
            here = pl.ds(pl.multiple_of(i * 16, 16), 16)
            for h in range(2):
                low_g[h, here, :] = wide_g[h, here, :].astype(BF16)
            return carry

        lax.fori_loop(0, live // 16, round_rows, 0)
        gather.near()

        def near_tile(t, carry):
            for j in range(3):
                acc[t, j] += part(t, j, ring.left) + part(t, j, ring.right)
            return carry

        lax.fori_loop(0, tiles, near_tile, 0)
        gather.far()
        gathers[0].start()
        keep_w.start()

        def far_tile(t, carry):
            here = tile_rows(t)
            for j, buf in enumerate((q_buf, k_buf)):
                a = acc[t, j] + part(t, j, ring.far)
                for h in range(heads):
                    cut = slice(h * HEAD_DIM, (h + 1) * HEAD_DIM)
                    turned = a[:, cut] * cos_buf[here, :]
                    turned += pltpu.roll(a[:, cut], HEAD_DIM // 2, 1) * sin_buf[here, :]
                    if j == 0:
                        turned = turned * scale
                    buf[here, cut] = turned.astype(BF16)
            v_buf[here, :] = (acc[t, 2] + part(t, 2, ring.far)).astype(BF16)
            return carry

        lax.fori_loop(0, tiles, far_tile, 0)
        gather_out.forward()
        for keep in keeps:
            keep.start()

        def protein(p, carry):
            prefix = pre_ref[p]
            keys = pl.ds(pl.multiple_of(p * LEN, LEN), LEN)

            @pl.when(p == proteins - 1)
            def _():
                gathers[0].forward()
                gathers[1].start()

            for h in range(heads):
                cut = slice(h * HEAD_DIM, (h + 1) * HEAD_DIM)
                store = pltpu.make_async_copy(p_buf.at[h], p_ref.at[p, h], psem.at[h])

                @pl.when(p > 0)
                def _():
                    store.wait()

                for i in range(LEN // BLOCK):
                    here = pl.ds(pl.multiple_of(p * LEN + i * BLOCK, BLOCK), BLOCK)
                    s = nt_dot(q_buf[here, cut], k_buf[keys, cut])
                    col = lax.broadcasted_iota(jnp.int32, s.shape, 1)
                    row = lax.broadcasted_iota(jnp.int32, (BLOCK, 1), 0) + i * BLOCK
                    s = jnp.where(col < jnp.maximum(prefix, row + 1), s, -1e30)
                    e = jnp.exp(s - jnp.max(s, axis=-1, keepdims=True))
                    prob = (e * (1.0 / jnp.sum(e, axis=-1, keepdims=True))).astype(BF16)
                    p_buf[h, i * BLOCK : (i + 1) * BLOCK, :] = prob
                    mixed = jnp.dot(prob, v_buf[keys, cut], preferred_element_type=F32)
                    o_buf[here, cut] = mixed.astype(BF16)
                store.start()
            return carry

        lax.fori_loop(0, proteins, protein, 0)
        for copy in gather_out.own:
            copy.wait()
        gather_out.near()
        gather_out.far()
        keep_wo.start()
        keep_o.start()
        own_rows.wait()

        def compute(t, chip, which):
            tile = o_buf[tile_rows(chip * 2 + which), :]
            x_buf[chip, which] = jnp.dot(tile, wo_buf[...], preferred_element_type=F32).astype(BF16)

        def emit(at, value):
            normed, inv_std = norm_rows(alpha * xs_buf[at, :].astype(F32) + value)
            x1 = normed * norm_ref[0:1, :] + norm_ref[1:2, :]
            x1_ref[at, :] = x1
            x1b_ref[at, :] = x1.astype(BF16)
            n1_ref[at, :] = normed
            inv_ref[at, :] = jnp.broadcast_to(inv_std, (EMIT, HEAD_DIM))

        square_kernel(
            rows,
            (send, recv, lsem),
            scatter=(compute, x_buf, (rcore, rxd, ryd, rx, ry), emit),
            middle=gathers[1].forward,
            greeting=False,
        )
        for other in gathers:
            other.finish()
        gather.drain()
        gather_out.drain()
        for keep in keeps + [keep_w, keep_wo, keep_o]:
            keep.wait()
        for h in range(heads):
            pltpu.make_async_copy(p_buf.at[h], p_ref.at[0, h], psem.at[h]).wait()

    wide = jax.ShapeDtypeStruct((rows, width), F32)
    return pl.pallas_call(
        kernel,
        out_shape=[jax.ShapeDtypeStruct((tokens, cols), BF16)] * 4
        + [jax.ShapeDtypeStruct((proteins, heads, LEN, LEN), BF16)]
        + [jax.ShapeDtypeStruct((tokens, HEAD_DIM), F32)] * 2
        + [
            jax.ShapeDtypeStruct((3, width, cols), BF16),
            jax.ShapeDtypeStruct((cols, width), BF16),
            jax.ShapeDtypeStruct((2, span, width), BF16),
            wide,
            jax.ShapeDtypeStruct((rows, width), BF16),
            wide,
            jax.ShapeDtypeStruct((rows, HEAD_DIM), F32),
        ],
        in_specs=[pl.BlockSpec(memory_space=pltpu.SMEM)] + [ANY] * 4 + [VM, VM],
        out_specs=[ANY] * 10 + [VM] * 4,
        scratch_shapes=[
            pltpu.VMEM((4, 2, rows, width), BF16),
            pltpu.VMEM((3, width, cols), BF16),
            pltpu.VMEM((tiles, 3, rows, cols), F32),
        ]
        + [pltpu.VMEM((tokens, cols), BF16)] * 4
        + [pltpu.VMEM((tokens, HEAD_DIM), F32)] * 2
        + [
            pltpu.VMEM((heads, LEN, LEN), BF16),
            pltpu.VMEM((cols, width), BF16),
            pltpu.VMEM((rows, width), BF16),
            pltpu.VMEM(gateup.shape, F32),
            pltpu.VMEM(gateup.shape, BF16),
        ]
        + scatter_scratch(rows, width, False)
        + [
            pltpu.SemaphoreType.DMA((10,)),
            pltpu.SemaphoreType.DMA((heads,)),
            pltpu.SemaphoreType.DMA((8,)),
        ]
        + SEMS
        + ring_sems(12 + 6 * len(spans)),
        compiler_params=params(0),
        cost_estimate=LIGHT,
        name="front",
    )(
        prefix_len,
        block_input.reshape(4, 2, rows, width),
        low_qkv,
        low_out,
        gateup,
        positions.reshape(tokens // HEAD_DIM, HEAD_DIM),
        w_norm,
    )


BLOCK = 128
BACK_BLOCK = 448
TN = (((0,), (0,)), ((), ()))


def attention_back_call(
    queries, key_rows, value_rows, probs, attended, grad_attended, cos_table, sin_table, norm_terms,
    grad_out_part,
):
    tokens, cols = queries.shape
    proteins = tokens // LEN
    heads = cols // HEAD_DIM
    scale = 1.0 / math.sqrt(HEAD_DIM)
    last = proteins * heads - 1
    depth = grad_out_part.shape[1] // 4

    def kernel(
        q_ref, k_ref, v_ref, p_ref, o_ref, do_ref, cos_ref, sin_ref, nt_ref, go_ref,
        da_ref, norm_ref, red_o,
        ds_buf, sums, got, nsend, nrecv, buf_o, send, recv, local,
    ):
        step = pl.program_id(0) * heads + pl.program_id(1)
        ring = Ring(send, recv, local)
        part = cols // 2
        side = RingScatter(
            ring, 0, column_halves(depth)(go_ref), buf_o, lambda h: red_o.at[pl.ds(h * part, part), :]
        )
        sq = Square(nsend, nrecv, 32)
        partners = [
            {"mp": sq.peer},
            {"mp": sq.xn},
            {"mp": sq.yn},
            {"dp": ring.here + 1 - 2 * (ring.here % 2)},
            {"dp": 3 - ring.here},
        ]
        swaps = [
            pltpu.make_async_remote_copy(
                src_ref=sums.at[k],
                dst_ref=got.at[k],
                send_sem=nsend.at[k],
                recv_sem=nrecv.at[k],
                device_id=other,
                device_id_type=MESH,
            )
            for k, other in enumerate(partners)
        ]

        @pl.when(step == 0)
        def _():
            sums[0] = nt_ref[...]
            greet(sq.others + [{"dp": ring.left}, {"dp": ring.right}])
            side.start()
            swaps[0].start()

        for k in range(5):

            @pl.when(step == k + 1)
            def _():
                swaps[k].wait()
                if k < 4:
                    sums[k + 1] = sums[k] + got[k]
                    swaps[k + 1].start()
                else:
                    norm_ref[...] = sums[k] + got[k]

        @pl.when(step == last // 2)
        def _():
            side.forward()

        for i in range(LEN // BACK_BLOCK):
            rows = slice(i * BACK_BLOCK, (i + 1) * BACK_BLOCK)
            do = do_ref[rows, :]
            delta = jnp.sum(do.astype(F32) * o_ref[rows, :].astype(F32), axis=-1, keepdims=True)
            dp = nt_dot(do, v_ref[...])
            ds = (p_ref[0, 0, rows, :].astype(F32) * (dp - delta)).astype(BF16)
            ds_buf[rows, :] = ds
            dq = jnp.dot(ds, k_ref[...], preferred_element_type=F32)
            turned = dq * cos_ref[rows, :] - pltpu.roll(dq, HEAD_DIM // 2, 1) * sin_ref[rows, :]
            da_ref[0, rows, :] = (turned * scale).astype(BF16)
        da_ref[2] = lax.dot_general(p_ref[0, 0], do_ref[...], TN, preferred_element_type=F32).astype(BF16)
        dk = lax.dot_general(ds_buf[...], q_ref[...], TN, preferred_element_type=F32)
        turned = dk * cos_ref[...] - pltpu.roll(dk, HEAD_DIM // 2, 1) * sin_ref[...]
        da_ref[1] = turned.astype(BF16)

        @pl.when(step == last)
        def _():
            side.finish()

    tile = pl.BlockSpec((LEN, HEAD_DIM), lambda p, h: (p, h))
    table = pl.BlockSpec((LEN, HEAD_DIM), lambda p, h: (p, 0))
    return pl.pallas_call(
        kernel,
        grid=(proteins, heads),
        in_specs=[tile] * 3
        + [pl.BlockSpec((1, 1, LEN, LEN), lambda p, h: (p, h, 0, 0)), tile, tile, table, table]
        + [whole(norm_terms.shape), ANY],
        out_specs=[
            pl.BlockSpec((3, LEN, HEAD_DIM), lambda p, h: (0, p, h)),
            whole(norm_terms.shape),
            whole((cols, depth)),
        ],
        out_shape=[
            jax.ShapeDtypeStruct((3, tokens, cols), BF16),
            jax.ShapeDtypeStruct(norm_terms.shape, F32),
            jax.ShapeDtypeStruct((cols, depth), F32),
        ],
        scratch_shapes=[
            pltpu.VMEM((LEN, LEN), BF16),
            pltpu.VMEM((5,) + norm_terms.shape, F32),
            pltpu.VMEM((5,) + norm_terms.shape, F32),
            pltpu.SemaphoreType.DMA((5,)),
            pltpu.SemaphoreType.DMA((5,)),
            pltpu.VMEM((10, cols // 2, depth), BF16),
        ]
        + ring_sems(6),
        compiler_params=params(7),
        cost_estimate=LIGHT,
        name="attention_back",
    )(
        queries,
        key_rows,
        value_rows,
        probs,
        attended,
        grad_attended,
        cos_table,
        sin_table,
        norm_terms,
        grad_out_part,
    )


def ffn_call(middle_low, middle_share, w_gateup, low_down, cotangent, row_weight, w_norm):
    rows = middle_low.shape[0]
    live, depth = low_down.shape
    curve = math.sqrt(2.0 / math.pi)
    alpha = math.sqrt(2.0 * DEPTH)

    def kernel(
        share, x1_ref, wg_ref, ld_ref, cot_ref, rw_ref, norm_ref,
        y_ref, dh_ref, dhb_ref, terms_ref, full, hid_ref, act_ref, pull_ref, wd_ref,
        w_g, w_d, gbuf, hid_buf, stage, pbuf, rcore, rxd, ryd, rx, ry, sums,
        wsem, osem, hsem, send, recv, lsem, zsend, zrecv, zlocal,
    ):
        ring = Ring(zsend, zrecv, zlocal)
        half = live // 2
        gather_d = RingGather(ring, 0, lambda h: ld_ref.at[pl.ds(h * half, half), :], column_halves(depth)(w_d))
        load_g = pltpu.make_async_copy(wg_ref, w_g, wsem.at[0])
        load_g.start()
        keep_d = pltpu.make_async_copy(w_d, wd_ref, wsem.at[1])
        outs = (act_ref, pull_ref)

        def between():
            for copy in gather_d.own:
                copy.wait()
            gather_d.near()
            gather_d.far()
            keep_d.start()

        def compute(t, chip, which):
            slot = t % 2

            @pl.when(t >= 2)
            def _():
                for k, ref in enumerate(outs):
                    pltpu.make_async_copy(stage.at[slot, k], ref.at[chip, which], osem.at[slot, k]).wait()

            tile = gbuf[chip, which]
            gate = nt_dot(tile, w_g[0])
            up = nt_dot(tile, w_g[1])
            square = gate * gate
            bent = jnp.tanh(curve * gate * (1.0 + 0.044715 * square))
            half = 0.5 * (1.0 + bent)
            act = gate * half
            slope = half + 0.5 * curve * gate * (1.0 - bent * bent) * (1.0 + 3.0 * 0.044715 * square)
            hid_buf[chip, which] = (act * up).astype(BF16)
            stage[slot, 0] = act.astype(BF16)
            stage[slot, 1] = (slope * up).astype(BF16)
            for k, ref in enumerate(outs):
                pltpu.make_async_copy(stage.at[slot, k], ref.at[chip, which], osem.at[slot, k]).start()
            pltpu.make_async_copy(hid_buf.at[chip, which], hid_ref.at[chip, which], hsem.at[t]).start()

        def finish_tile(t, chip, which):
            part = jnp.dot(hid_buf[chip, which], w_d[...], preferred_element_type=F32)
            pbuf[chip, which] = part.astype(BF16)

        def emit(at, value):
            normed, inv_std = norm_rows(alpha * x1_ref[at, :] + value)
            gain = norm_ref[2:3, :]
            y_ref[at, :] = (normed * gain + norm_ref[3:4, :]).astype(BF16)
            dy = cot_ref[at, :].astype(F32) * rw_ref[at, :]
            sums[0] += fold(dy * normed)
            sums[1] += fold(dy)
            dh = norm_rows_back(dy, normed, inv_std, gain)
            dh_ref[at, :] = dh
            dhb_ref[at, :] = dh.astype(BF16)

        sums[...] = jnp.zeros_like(sums)

        def end():
            terms_ref[...] = jnp.sum(sums[...], axis=1)
            for slot in range(2):
                for k, ref in enumerate(outs):
                    pltpu.make_async_copy(stage.at[slot, k], ref.at[0, 0], osem.at[slot, k]).wait()
            for t in range(8):
                pltpu.make_async_copy(hid_buf.at[0, 0], hid_ref.at[0, 0], hsem.at[t]).wait()
            keep_d.wait()
            gather_d.drain()

        square_kernel(
            rows,
            (send, recv, lsem),
            gather=(compute, share, full, gbuf),
            scatter=(finish_tile, pbuf, (rcore, rxd, ryd, rx, ry), emit),
            ring=ring,
            start=gather_d.start,
            first=load_g.wait,
            early=gather_d.forward,
            between=between,
            end=end,
        )

    kept = jax.ShapeDtypeStruct((4, 2, rows, live), BF16)
    return pl.pallas_call(
        kernel,
        out_shape=[
            jax.ShapeDtypeStruct((rows, D), BF16),
            jax.ShapeDtypeStruct((rows, D), F32),
            jax.ShapeDtypeStruct((rows, D), BF16),
            jax.ShapeDtypeStruct((2, D), F32),
            jax.ShapeDtypeStruct((4, 2, rows, D), BF16),
            kept,
            kept,
            kept,
            jax.ShapeDtypeStruct((live, D), BF16),
        ],
        in_specs=[ANY, VM, ANY, ANY, VM, VM, VM],
        out_specs=[VM] * 4 + [ANY] * 5,
        scratch_shapes=[
            pltpu.VMEM((2, live, D), BF16),
            pltpu.VMEM((live, D), BF16),
            pltpu.VMEM((4, 2, rows, D), BF16),
            pltpu.VMEM((4, 2, rows, live), BF16),
            pltpu.VMEM((2, 2, rows, live), BF16),
        ]
        + scatter_scratch(rows, D)
        + [
            pltpu.VMEM((2, 8, D), F32),
            pltpu.SemaphoreType.DMA((2,)),
            pltpu.SemaphoreType.DMA((2, 2)),
            pltpu.SemaphoreType.DMA((8,)),
        ]
        + SEMS
        + ring_sems(6),
        compiler_params=params(1),
        cost_estimate=LIGHT,
        name="ffn",
    )(middle_low, middle_share, w_gateup, low_down, cotangent, row_weight, w_norm)


def ffn_back_call(ffn_grad, act, pull, w_down):
    rows = ffn_grad.shape[0]
    live = w_down.shape[0]

    def kernel(share, act_ref, pull_ref, wd_ref, full, dg_ref, w_d, gbuf, load, stage, wsem, isem, osem, send, recv, lsem):
        weight = pltpu.make_async_copy(wd_ref, w_d, wsem.at[0])
        weight.start()

        def compute(t, chip, which):
            slot = t % 2
            loads = [
                pltpu.make_async_copy(ref.at[chip, which], load.at[k], isem.at[k])
                for k, ref in enumerate((act_ref, pull_ref))
            ]
            stores = [
                pltpu.make_async_copy(stage.at[slot, k], dg_ref.at[k, chip, which], osem.at[slot, k])
                for k in range(2)
            ]
            for copy in loads:
                copy.start()

            @pl.when(t >= 2)
            def _():
                for copy in stores:
                    copy.wait()

            dh = nt_dot(gbuf[chip, which], w_d[...])
            for copy in loads:
                copy.wait()
            stage[slot, 0] = (dh * load[1].astype(F32)).astype(BF16)
            stage[slot, 1] = (dh * load[0].astype(F32)).astype(BF16)
            for copy in stores:
                copy.start()

        def end():
            for slot in range(2):
                for k in range(2):
                    pltpu.make_async_copy(stage.at[slot, k], dg_ref.at[k, 0, 0], osem.at[slot, k]).wait()

        square_kernel(
            rows,
            (send, recv, lsem),
            gather=(compute, share, full, gbuf),
            first=weight.wait,
            end=end,
            near_first=True,
        )

    return pl.pallas_call(
        kernel,
        out_shape=[
            jax.ShapeDtypeStruct((4, 2, rows, D), BF16),
            jax.ShapeDtypeStruct((2, 4, 2, rows, live), BF16),
        ],
        in_specs=[ANY] * 4,
        out_specs=[ANY, ANY],
        scratch_shapes=[
            pltpu.VMEM((live, D), BF16),
            pltpu.VMEM((4, 2, rows, D), BF16),
            pltpu.VMEM((2, rows, live), BF16),
            pltpu.VMEM((2, 2, rows, live), BF16),
            pltpu.SemaphoreType.DMA((1,)),
            pltpu.SemaphoreType.DMA((2,)),
            pltpu.SemaphoreType.DMA((2, 2)),
        ]
        + SEMS,
        compiler_params=params(2),
        cost_estimate=LIGHT,
        name="ffn_back",
    )(ffn_grad, act, pull, w_down)


def middle_back_call(grad_gateup_rows, w_gateup, grad_gateup_part, spans, grad_h2, normed, inv_std, w_norm):
    rows = grad_h2.shape[0]
    alpha = math.sqrt(2.0 * DEPTH)
    live, width = grad_gateup_part.shape[1:]
    depth = width // 4

    def kernel(
        dg_ref, wg_ref, gg_ref, dh2_ref, n1_ref, inv_ref, norm_ref, dh_ref, dhb_ref, terms_ref, red_0, red_1,
        w_g, load, buf_0, buf_1, pbuf, rcore, rxd, ryd, rx, ry, sums, wsem, isem, send, recv, lsem, zsend, zrecv, zlocal,
    ):
        ring = Ring(zsend, zrecv, zlocal)
        early = span_scatter(ring, 0, gg_ref, spans[0], buf_0, red_0)
        late = span_scatter(ring, 6, gg_ref, spans[1], buf_1, red_1)
        weight = pltpu.make_async_copy(wg_ref, w_g, wsem.at[0])
        weight.start()
        me = lax.axis_index("mp")
        core, x, y = me % 2, (me // 2) % 2, me // 4

        def loads(t):
            rel = (t // 2 + 1) % 4
            chip = ((y + rel % 2) % 2) * 2 + (x + ((rel + 1) // 2) % 2) % 2
            which = (1 - core + t % 2) % 2
            return [
                pltpu.make_async_copy(dg_ref.at[k, chip, which], load.at[t % 2, k], isem.at[t % 2, k])
                for k in range(2)
            ]

        for copy in loads(0):
            copy.start()

        def compute(t, chip, which):
            @pl.when(t < 7)
            def _():
                for copy in loads(t + 1):
                    copy.start()

            for copy in loads(t):
                copy.wait()
            slot = t % 2
            part = jnp.dot(load[slot, 0], w_g[0], preferred_element_type=F32)
            part += jnp.dot(load[slot, 1], w_g[1], preferred_element_type=F32)
            pbuf[chip, which] = part.astype(BF16)

        sums[...] = jnp.zeros_like(sums)

        def emit(at, value):
            grads = value + alpha * dh2_ref[at, :]
            normed = n1_ref[at, :]
            sums[0] += fold(grads * normed)
            sums[1] += fold(grads)
            dh = norm_rows_back(grads, normed, inv_ref[at, 0:1], norm_ref[0:1, :])
            dh_ref[at, :] = dh
            dhb_ref[at, :] = dh.astype(BF16)

        def end():
            terms_ref[...] = jnp.sum(sums[...], axis=1)
            early.finish()
            late.finish()

        square_kernel(
            rows,
            (send, recv, lsem),
            scatter=(compute, pbuf, (rcore, rxd, ryd, rx, ry), emit),
            ring=ring,
            start=lambda: (early.start(), weight.wait()),
            halfway=lambda: (early.forward(), late.start()),
            middle=late.forward,
            end=end,
        )

    return pl.pallas_call(
        kernel,
        out_shape=[
            jax.ShapeDtypeStruct((rows, D), F32),
            jax.ShapeDtypeStruct((rows, D), BF16),
            jax.ShapeDtypeStruct((2, D), F32),
            jax.ShapeDtypeStruct((2, spans[0][1], depth), F32),
            jax.ShapeDtypeStruct((2, spans[1][1], depth), F32),
        ],
        in_specs=[ANY] * 3 + [VM] * 4,
        out_specs=[VM] * 5,
        scratch_shapes=[
            pltpu.VMEM((2, live, D), BF16),
            pltpu.VMEM((2, 2, rows, live), BF16),
            pltpu.VMEM((10, spans[0][1], depth), BF16),
            pltpu.VMEM((10, spans[1][1], depth), BF16),
        ]
        + scatter_scratch(rows, D)
        + [pltpu.VMEM((2, 8, D), F32)]
        + [pltpu.SemaphoreType.DMA((1,)), pltpu.SemaphoreType.DMA((2, 2))]
        + SEMS
        + ring_sems(12),
        compiler_params=params(8),
        cost_estimate=LIGHT,
        name="middle_back",
    )(grad_gateup_rows, w_gateup, grad_gateup_part, grad_h2, normed, inv_std, w_norm)


def out_back_call(attn_grad, w_out, attended, grad_gateup_part, span):
    rows = attn_grad.shape[0]
    cols = w_out.shape[0]
    depth = grad_gateup_part.shape[2] // 4

    def kernel(
        share, w_ref, o_ref, gg_ref, dout, go_ref, red,
        w_buf, gbuf, buf, acc, wsem, send, recv, lsem, zsend, zrecv, zlocal,
    ):
        ring = Ring(zsend, zrecv, zlocal)
        side = span_scatter(ring, 0, gg_ref, span, buf, red)
        weight = pltpu.make_async_copy(w_ref, w_buf, wsem.at[0])
        weight.start()

        def compute(t, chip, which):
            tile = gbuf[chip, which]
            dout[chip, which] = nt_dot(tile, w_buf[...]).astype(BF16)
            part = lax.dot_general(o_ref[chip, which], tile, TN, preferred_element_type=F32)

            @pl.when(t == 0)
            def _():
                acc[...] = part

            @pl.when(t > 0)
            def _():
                acc[...] += part

        def end():
            go_ref[...] = acc[...].astype(BF16)
            side.finish()

        square_kernel(
            rows,
            (send, recv, lsem),
            gather=(compute, share, None, gbuf),
            ring=ring,
            start=side.start,
            first=weight.wait,
            early=side.forward,
            end=end,
            near_first=True,
        )

    return pl.pallas_call(
        kernel,
        out_shape=[
            jax.ShapeDtypeStruct((4, 2, rows, cols), BF16),
            jax.ShapeDtypeStruct((cols, D), BF16),
            jax.ShapeDtypeStruct((2, span[1], depth), F32),
        ],
        in_specs=[ANY, ANY, VM, ANY],
        out_specs=[VM, VM, VM],
        scratch_shapes=[
            pltpu.VMEM((cols, D), BF16),
            pltpu.VMEM((4, 2, rows, D), BF16),
            pltpu.VMEM((10, span[1], depth), BF16),
            pltpu.VMEM((cols, D), F32),
            pltpu.SemaphoreType.DMA((1,)),
        ]
        + SEMS
        + ring_sems(6),
        compiler_params=params(3),
        cost_estimate=LIGHT,
        name="out_back",
    )(attn_grad, w_out, attended.reshape(4, 2, rows, cols), grad_gateup_part)


def input_back_call(grad_proj, w_qkv, block_input, grad_gateup_part, span, grad_h1):
    rows = grad_h1.shape[0]
    alpha = math.sqrt(2.0 * DEPTH)
    width, cols = w_qkv.shape[1:]
    depth = width // 4
    tokens = block_input.shape[0]

    def kernel(
        da_ref, w_ref, x_ref, gg_ref, dh_ref, out, red_q, red_g,
        w_buf, x_buf, gq_buf, buf_q, buf_g, pbuf, rcore, rxd, ryd, rx, ry,
        wsem, send, recv, lsem, zsend, zrecv, zlocal,
    ):
        ring = Ring(zsend, zrecv, zlocal)
        half = depth // 2
        side_g = span_scatter(ring, 0, gg_ref, span, buf_g, red_g)
        side_q = RingScatter(
            ring, 6, row_halves(depth)(gq_buf), buf_q, lambda h: red_q.at[:, pl.ds(h * half, half), :]
        )
        weight = pltpu.make_async_copy(w_ref, w_buf, wsem.at[0])
        load = pltpu.make_async_copy(x_ref, x_buf, wsem.at[1])
        load.start()
        weight.start()

        def product(n):
            depths = pl.ds(pl.multiple_of(n * depth, depth), depth)
            left = x_buf[:, :, :, depths].reshape(tokens, depth)
            for j in range(3):
                right = da_ref[j].reshape(tokens, cols)
                gq_buf[j, depths, :] = lax.dot_general(left, right, TN, preferred_element_type=F32).astype(BF16)

        def start():
            side_g.start()
            load.wait()
            product(ring.far)
            side_q.start_far()
            weight.wait()

        def halfway():
            product(ring.right)
            product(ring.left)
            side_q.start_near()
            side_g.forward()
            product(ring.here)
            side_q.load()

        def compute(t, chip, which):
            part = nt_dot(da_ref[0, chip, which], w_buf[0])
            part += nt_dot(da_ref[1, chip, which], w_buf[1])
            part += nt_dot(da_ref[2, chip, which], w_buf[2])
            pbuf[chip, which] = part.astype(BF16)

        def emit(at, value):
            out[at, :] = (value + alpha * dh_ref[at, :]).astype(BF16)

        def end():
            side_g.finish()
            side_q.finish()

        square_kernel(
            rows,
            (send, recv, lsem),
            scatter=(compute, pbuf, (rcore, rxd, ryd, rx, ry), emit),
            ring=ring,
            start=start,
            halfway=halfway,
            half=2,
            middle=side_q.forward,
            end=end,
        )

    return pl.pallas_call(
        kernel,
        out_shape=[
            jax.ShapeDtypeStruct((rows, D), BF16),
            jax.ShapeDtypeStruct((3, depth, cols), F32),
            jax.ShapeDtypeStruct((2, span[1], depth), F32),
        ],
        in_specs=[VM, ANY, ANY, ANY, VM],
        out_specs=[VM, VM, VM],
        scratch_shapes=[
            pltpu.VMEM((3, D, cols), BF16),
            pltpu.VMEM((4, 2, rows, width), BF16),
            pltpu.VMEM((3, width, cols), BF16),
            pltpu.VMEM((10, 3, depth // 2, cols), BF16),
            pltpu.VMEM((10, span[1], depth), BF16),
        ]
        + scatter_scratch(rows, D)
        + [pltpu.SemaphoreType.DMA((2,))]
        + SEMS
        + ring_sems(12),
        compiler_params=params(4),
        cost_estimate=LIGHT,
        name="input_back",
    )(
        grad_proj.reshape(3, 4, 2, rows, cols),
        w_qkv,
        block_input.reshape(4, 2, rows, width),
        grad_gateup_part,
        grad_h1,
    )


FRONT_SPANS = ((0, 240), (240, 464))
SPANS = ((0, 96), (96, 128), (224, 400), (624, 80))


def body_ring(
    block_input,
    cotangent,
    prefix_len,
    cluster_id,
    positions,
    step_count,
    master_qkv,
    first_qkv,
    second_qkv,
    master_out,
    first_out,
    second_out,
    master_gateup,
    first_gateup,
    second_gateup,
    master_down,
    first_down,
    second_down,
    master_norm,
    first_norm,
    second_norm,
):
    token_count = block_input.shape[0]
    protein_count = token_count // LEN
    share_rows = cotangent.shape[0]
    share_start = lax.axis_index("mp") * share_rows

    low_qkv = master_qkv.astype(BF16)
    low_out = master_out.astype(BF16)
    low_down = master_down.astype(BF16)
    w_norm = lax.optimization_barrier(master_norm.astype(BF16)).astype(F32)

    (
        queries, key_rows, value_rows, attended, probs, cos_table, sin_table, w_qkv, w_out, w_gateup,
        middle_share, middle_low, normed_one, inv_one,
    ) = front_call(
        block_input, low_qkv, low_out, jnp.swapaxes(master_gateup, 1, 2), positions, prefix_len, w_norm, share_rows, FRONT_SPANS
    )
    matches = (cluster_id[:, None] == cluster_id[None, :]).astype(F32)
    counts = jnp.sum(matches, axis=1)
    group_counts = lax.dynamic_slice_in_dim(
        counts, lax.axis_index("dp") * protein_count, protein_count, 0
    )
    row_protein = (share_start + jnp.arange(share_rows)) // LEN
    one_hot = (row_protein[:, None] == jnp.arange(protein_count)[None, :]).astype(F32)
    row_weight = jnp.sum(one_hot * (1.0 / group_counts)[None, :], axis=1)
    block_output, grad_h2, grad_h2_low, terms_two, middle_low, hidden, act, pull, w_down = ffn_call(
        middle_low, middle_share, w_gateup, low_down, cotangent, row_weight[:, None], w_norm
    )
    ffn_grad, grad_gateup_rows = ffn_back_call(grad_h2_low, act, pull, w_down)
    hidden = hidden.reshape(token_count, -1)
    middle_low = middle_low.reshape(token_count, D)
    ffn_grad = ffn_grad.reshape(token_count, D)
    gateup_rows = grad_gateup_rows.reshape(2, token_count, -1)
    grad_down_part = jnp.einsum("tf,td->fd", hidden, ffn_grad, preferred_element_type=F32).astype(BF16)
    red_down = lax.psum_scatter(grad_down_part, "dp", scatter_dimension=1, tiled=True).astype(F32)
    gateup_rows, grad_gateup_rows, grad_down_part = lax.optimization_barrier(
        (gateup_rows, grad_gateup_rows, grad_down_part)
    )
    grad_gateup_part = jnp.einsum(
        "jtf,td->jfd", gateup_rows, middle_low, preferred_element_type=F32
    ).astype(BF16)
    grad_h1, grad_h1_low, terms_one, red_gateup_0, red_gateup_1 = middle_back_call(
        grad_gateup_rows, w_gateup, grad_gateup_part, SPANS[:2], grad_h2, normed_one, inv_one, w_norm
    )
    grad_attended, grad_out_part, red_gateup_2 = out_back_call(
        grad_h1_low, w_out, attended, grad_gateup_part, SPANS[2]
    )
    grad_attended = grad_attended.reshape(token_count, -1)
    norm_terms = jnp.concatenate([terms_one, terms_two])
    grad_proj, grad_norm, red_out = attention_back_call(
        queries,
        key_rows,
        value_rows,
        probs,
        attended,
        grad_attended,
        cos_table,
        sin_table,
        norm_terms,
        grad_out_part,
    )
    grad_input, red_qkv, red_gateup_3 = input_back_call(
        grad_proj, w_qkv, block_input, grad_gateup_part, SPANS[3], grad_h1
    )
    red_gateup = jnp.swapaxes(
        jnp.concatenate([red_gateup_0, red_gateup_1, red_gateup_2, red_gateup_3], axis=1), 1, 2
    )

    step_value = step_count[0].astype(F32)
    rate_qkv = D ** (-0.5)
    rate_out = max(HEADS * HEAD_DIM // 512, 1) ** (-0.5)
    rate_gateup = D ** (-0.5)
    rate_down = max(FF // 64, 1) ** (-0.5)
    rate_norm = 1.0
    new_qkv, new_first_qkv, new_second_qkv = adamw_step(
        master_qkv, first_qkv, second_qkv, red_qkv, rate_qkv, step_value
    )
    new_out, new_first_out, new_second_out = adamw_step(
        master_out, first_out, second_out, red_out, rate_out, step_value
    )
    new_gateup, new_first_gateup, new_second_gateup = adamw_step(
        master_gateup, first_gateup, second_gateup, red_gateup, rate_gateup, step_value
    )
    new_down, new_first_down, new_second_down = adamw_step(
        master_down, first_down, second_down, red_down, rate_down, step_value
    )
    new_norm, new_first_norm, new_second_norm = adamw_step(
        master_norm, first_norm, second_norm, grad_norm, rate_norm, step_value
    )
    return (
        block_output,
        grad_input,
        red_qkv,
        new_qkv,
        new_first_qkv,
        new_second_qkv,
        red_out,
        new_out,
        new_first_out,
        new_second_out,
        red_gateup,
        new_gateup,
        new_first_gateup,
        new_second_gateup,
        red_down,
        new_down,
        new_first_down,
        new_second_down,
        grad_norm,
        new_norm,
        new_first_norm,
        new_second_norm,
    )


def solution(mesh):
    placed = (
        P("dp", None),
        P(("dp", "mp"), None),
        P("dp"),
        P(),
        P("dp"),
        P(),
        P(None, "dp", "mp"),
        P(None, "dp", "mp"),
        P(None, "dp", "mp"),
        P("mp", "dp"),
        P("mp", "dp"),
        P("mp", "dp"),
        P(None, "dp", "mp"),
        P(None, "dp", "mp"),
        P(None, "dp", "mp"),
        P("mp", "dp"),
        P("mp", "dp"),
        P("mp", "dp"),
        P(),
        P(),
        P(),
    )
    ring = mesh.shape["dp"] == 4 and mesh.shape["mp"] == 8
    return jax.shard_map(
        body_ring if ring else body_plain,
        mesh=mesh,
        in_specs=placed,
        out_specs=(
            P(("dp", "mp"), None),
            P(("dp", "mp"), None),
            P(None, "dp", "mp"),
            P(None, "dp", "mp"),
            P(None, "dp", "mp"),
            P(None, "dp", "mp"),
            P("mp", "dp"),
            P("mp", "dp"),
            P("mp", "dp"),
            P("mp", "dp"),
            P(None, "dp", "mp"),
            P(None, "dp", "mp"),
            P(None, "dp", "mp"),
            P(None, "dp", "mp"),
            P("mp", "dp"),
            P("mp", "dp"),
            P("mp", "dp"),
            P("mp", "dp"),
            P(),
            P(),
            P(),
            P(),
        ),
        check_vma=False,
    )
```
